128 devices in a mesh: dp: 4 (over x), grid: 32 (over z, y, core).
Axes of the slice: x: 4, y: 4, z: 4, core: 2. Of those that a mesh axis runs over, the one named last changes fastest.
Arguments:
- intensities: bfloat16 [8192, 32, 128], P(('dp', 'grid')), may hold values from -6 to 6
- gridding: bfloat16 [8192, 32, 512], P(('dp', 'grid')), may hold values from -0.0625 to 0.0625
- dest_slab: int32 [8192, 1], P(('dp', 'grid')), may hold values from 0 to 31; in each aligned block of 64 rows (0 to 63, 64 to 127, ...) at most 4 rows name the same one
- spectral_weights: float32 [4, 128, 128, 128], P('dp', None, 'grid'), may hold values from 0.05 to 2
Outputs:
- solution_field: float32 [128, 128, 128], P('grid')
- residual: float32 [128, 128, 128], P('grid')
The draws below stay inside these ranges and needn't reach their ends.
Inputs may be any that keep to these rules, and one draw needn't show every extreme that they name: `dest_slab`: at most 4 of one device's 64 snapshots name the same slab, and in every draw some device has exactly 4 that name one slab.
All inputs are finite; a program needn't handle non-finite values.
Results may differ from the reference program's by a relative error of at most 0.0003.
Values may be sent and summed in bfloat16 or wider, within the bound.
No kernel may reach another device: no remote copies, remote signals or barrier semaphores. Data moves between devices by JAX's collectives and lax.ppermute only.
A program may use at most 128 MiB of HBM per device.

```python
import math
import jax
import jax.numpy as jnp
import numpy as np
from jax import lax

M = 128
R = 32
NENT = 64
ITERS = 8
SLAB = 4
CAP = 4
ENTRIES = 8192
GROUPS = 4
N_DP = 4
N_GRID = 32


def block_scale(rng, shape, pieces, least, high):
    loudness = 1.0
    for axis_at, blocks in pieces:
        draws = jax.random.uniform(jax.random.fold_in(jax.random.fold_in(rng, 6), axis_at), (blocks,), jnp.float32, least / len(pieces), high / len(pieces))
        loudness = loudness * jnp.repeat(jnp.exp(draws), shape[axis_at] // blocks).reshape((-1,) + (1,) * (len(shape) - 1 - axis_at))
    return loudness


def deal_out(own_key, own, number, rows, count, top, most, slope):
    sequence = jax.random.permutation(own_key, count)
    heavy_load, common = portions_of(count, rows * top, most, slope, True), portions_of(count, rows * top, most, slope, False)
    places = jnp.arange(count)

    def named(lengths, turn):
        used = int((lengths > 0).sum())
        fixed = max(1, used // 4)
        moved = fixed + (places - fixed + turn * (used - fixed)) % max(1, count - fixed)
        return jnp.zeros((count,), jnp.int32).at[sequence[jnp.where(places < fixed, places, moved)]].set(jnp.asarray(lengths, jnp.int32))

    lengths = jnp.where(number % 4 == 0, named(heavy_load, number // 4), named(common, number - number // 4 - 1))
    mixed = jax.random.permutation(jax.random.fold_in(own, 3), count)
    source_of, taker = mixed[0:count // 2 * 2:2], mixed[1:count // 2 * 2:2]
    margin = jnp.minimum(lengths[source_of] - 1, most - lengths[taker]) // 2
    margin = jnp.where((source_of == sequence[0]) | (taker == sequence[0]) | (lengths[taker] == 0), 0, jnp.maximum(margin, 0))
    moved = jax.random.randint(jax.random.fold_in(own, 4), (count // 2,), 0, 1 << 20) % (margin + 1)
    lengths = lengths.at[source_of].add(-moved).at[taker].add(moved)
    labels = jnp.searchsorted(jnp.cumsum(lengths), jnp.arange(rows * top), side="right").astype(jnp.int32)
    table = labels.reshape(top, rows).T
    table = table[jax.random.permutation(jax.random.fold_in(own, 1), rows)]
    turn = jax.random.randint(jax.random.fold_in(own, 2), (rows, 1), 0, top)
    return jnp.take_along_axis(table, (jnp.arange(top)[None, :] + turn) % top, axis=1)


def portions_of(amount, total, limit, skew, full):
    weights = [(1 << 20) // math.isqrt(grade ** skew) + 1 for grade in range(1, amount + 1)]
    largest = limit if full else min(limit, max(-(-total // amount), total * weights[0] // sum(weights)))
    least = 1 if total - largest >= amount - 1 else 0
    holding, rest = [largest] + [least] * (amount - 1), total - largest - least * (amount - 1)
    while rest > 0:
        candidates = [i for i in range(1, amount) if holding[i] < largest] or [i for i in range(1, amount) if holding[i] < limit]
        mass, left = sum([weights[i] for i in candidates]), rest
        for i in candidates:
            extra = min(limit - holding[i], max(1, left * weights[i] // mass), rest)
            holding[i] = holding[i] + extra
            rest = rest - extra
    return np.array(holding)


def scatter_about(own_key, shape, scale, bound, cuts=(), kind=jnp.bfloat16):
    array = scale * jax.random.normal(own_key, shape, jnp.float32)
    if cuts:
        array = array * block_scale(own_key, shape, cuts, -0.22, 0.18)
    return jnp.clip(array, -bound, bound).astype(kind)


def setup_inputs(seed: int = 0) -> dict:
    key_of = jax.random.split(jax.random.key(seed), 5)
    intensities = scatter_about(key_of[0], (ENTRIES, R, M), 1.0, 6.0, ((0, 128),))
    gridding = scatter_about(key_of[1], (ENTRIES, R, SLAB * M), (R * N_DP * NENT) ** -0.5, 0.0625, ((0, 128),))
    dest_slab_keys = jax.random.split(jax.random.fold_in(key_of[2], 1), ENTRIES // NENT)
    dest_slab_turns = jax.random.permutation(jax.random.fold_in(key_of[2], 3), ENTRIES // NENT)
    dest_slab = jax.vmap(lambda own, number: deal_out(jax.random.fold_in(key_of[2], 2), own, number, NENT, N_GRID, 1, CAP, 2))(dest_slab_keys, dest_slab_turns).reshape((ENTRIES, 1))
    spectral_weights = jnp.clip(jnp.exp(math.log(2.0) - 3.6888794 * jax.random.uniform(key_of[3], (GROUPS, M, M, M), jnp.float32) ** block_scale(key_of[3], (GROUPS, M, M, M), ((0, 4), (2, 32)), -0.2, 0.2)), 0.05, 2.0)
    return dict(intensities=intensities, gridding=gridding, dest_slab=dest_slab, spectral_weights=spectral_weights)


def operate(field, weight_sum):
    spectrum = jnp.fft.fftn(field)
    return jnp.real(jnp.fft.ifftn(weight_sum * spectrum)).astype(field.dtype)


def reference(intensities, gridding, dest_slab, spectral_weights):
    blocks = ENTRIES // NENT
    vals = intensities.reshape(blocks, NENT, R, M)
    mats = gridding.reshape(blocks, NENT, R, SLAB * M)
    targets = dest_slab.reshape(blocks, NENT).astype(jnp.int32)

    def add_block(total, block):
        block_vals, block_mats, block_dest = block
        contrib = jnp.einsum("krq,krz->kqz", block_mats.astype(jnp.float32), block_vals.astype(jnp.float32))
        return total.at[block_dest].add(contrib), None

    start = jnp.zeros((N_GRID, SLAB * M, M), jnp.float32)
    total, _ = lax.scan(add_block, start, (vals, mats, targets))
    right_side = total.reshape(M, M, M)
    weight_sum = jnp.sum(spectral_weights, axis=0)
    solution_field = jnp.zeros_like(right_side)
    residual, direction = right_side, right_side
    norm_now = jnp.sum(residual * residual)
    for step in range(ITERS):
        image = operate(direction, weight_sum)
        alpha = norm_now / jnp.sum(direction * image)
        solution_field = solution_field + alpha * direction
        residual = residual - alpha * image
        norm_next = jnp.sum(residual * residual)
        direction = residual + (norm_next / norm_now) * direction
        norm_now = norm_next
    return solution_field, residual
```

```python
import functools

import jax
import jax.numpy as jnp
import numpy as np
from jax import lax
from jax.experimental import pallas as pl
from jax.experimental.pallas import tpu as pltpu
from jax.sharding import PartitionSpec as P

ITERS = 8
MOMENTS = 2 * ITERS + 1
LOW_LANE = 64
ALL = ("dp", "grid")
HIGHEST = lax.Precision.HIGHEST


def two_sum(a, b):
    s = a + b
    v = s - a
    return s, (a - (s - v)) + (b - v)


def quick_sum(a, b):
    s = a + b
    return s, b - (s - a)


def halves(a):
    c = a * 4097.0
    high = c - (c - a)
    return high, a - high


def two_prod(a, b, a_parts=None, b_parts=None):
    p = a * b
    ah, al = a_parts or halves(a)
    bh, bl = b_parts or halves(b)
    return p, ((ah * bh - p) + ah * bl + al * bh) + al * bl


def dd_add(a, b):
    s, e = two_sum(a[0], b[0])
    t, f = two_sum(a[1], b[1])
    s, e = quick_sum(s, e + t)
    return quick_sum(s, e + f)


def dd_mul(a, b):
    p, e = two_prod(a[0], b[0])
    return quick_sum(p, e + (a[0] * b[1] + a[1] * b[0]))


def dd_scale(a, factor):
    return a[0] * factor, a[1] * factor


def dd_neg(a):
    return -a[0], -a[1]


def dd_div(a, b):
    first = a[0] / b[0]
    rest = dd_add(a, dd_neg(dd_mul((first, jnp.zeros_like(first)), b)))
    second = rest[0] / b[0]
    rest = dd_add(rest, dd_neg(dd_mul((second, jnp.zeros_like(second)), b)))
    third = rest[0] / b[0]
    high, low = quick_sum(first, second)
    return quick_sum(high, low + third)


def dot(a, b):
    return jax.lax.dot_general(
        a, b, (((1,), (0,)), ((), ())), precision=HIGHEST, preferred_element_type=jnp.float32
    )


def owner_order(size, ndp):
    slots = size // ndp
    d = np.arange(size)
    return ndp * (d % slots) + d // slots


def dft_tables(size, ndp):
    index = np.arange(size)
    angle = 2.0 * np.pi * ((index[:, None] * index[None, :]) % size) / size
    cos, sin = np.cos(angle), np.sin(angle)
    order = owner_order(size, ndp)
    as_f32 = lambda a: np.ascontiguousarray(a, dtype=np.float32)
    return dict(
        lanes=as_f32(np.concatenate([cos, sin], 1)),
        own_rows=as_f32(np.concatenate([cos[order], sin[order]], 0)),
        own_cols=as_f32(np.concatenate([cos[:, order], sin[:, order]], 0)),
        back_rows=as_f32(np.concatenate([cos, sin], 0)),
        back_own=as_f32(np.concatenate([cos[:, order], sin[:, order]], 0)),
        mirror=as_f32(((index[:, None] + index[None, :]) % size) == 0),
    )


def plane_kernel(plane_ref, own_ref, mirrored_ref, lanes_ref, rows_ref, out_ref, sym_ref):
    size = plane_ref.shape[0]
    sym = (own_ref[...] + mirrored_ref[...]) * 0.5
    sym_ref[...] = sym
    low = jnp.min(jnp.min(sym, axis=0, keepdims=True), axis=1, keepdims=True)
    high = jnp.max(jnp.max(sym, axis=0, keepdims=True), axis=1, keepdims=True)
    first = dot(plane_ref[...], lanes_ref[...])
    both = dot(rows_ref[...], first)
    real = both[:size, :size] - both[size:, size:]
    imag = -(both[size:, :size] + both[:size, size:])
    out_ref[:, 0, :] = real
    out_ref[:, 1, :] = imag
    out_ref[:, 2, :] = jnp.broadcast_to(low, (size, size))
    out_ref[:, 3, :] = jnp.broadcast_to(high, (size, size))


def sublane_total(a):
    for shift in (4, 2, 1):
        a = dd_add(a, (pltpu.roll(a[0], shift, 0), pltpu.roll(a[1], shift, 0)))
    return a


def lane_total(a):
    for shift in (64, 32, 16, 8, 4, 2, 1):
        a = dd_add(a, (pltpu.roll(a[0], shift, 1), pltpu.roll(a[1], shift, 1)))
    return a


def moment_kernel(columns_ref, sym_ref, cols_ref, real_ref, imag_ref, scaled_ref, range_ref, send_ref):
    size = sym_ref.shape[0]
    low = jnp.min(jnp.min(columns_ref[:, 2, :], axis=0, keepdims=True), axis=1, keepdims=True)
    high = jnp.max(jnp.max(columns_ref[:, 3, :], axis=0, keepdims=True), axis=1, keepdims=True)
    half = jnp.maximum((high - low) * 0.5, high * 1e-4)
    half = jnp.broadcast_to(half, (1, size))
    centre = jnp.broadcast_to((high + low) * 0.5, (1, size)) / half
    range_ref[0:1, :] = half
    range_ref[1:2, :] = centre
    range_ref[2:8, :] = jnp.zeros((6, size), jnp.float32)
    given = jnp.concatenate([columns_ref[:, 0, :], columns_ref[:, 1, :]], axis=1)
    both = dot(cols_ref[...], given)
    real = both[:size, :size] + both[size:, size:]
    imag = both[:size, size:] - both[size:, :size]
    real_ref[...] = real
    imag_ref[...] = imag
    scaled = sym_ref[...] / half
    scaled_ref[...] = scaled
    power = real * real + imag * imag
    chunk = 32
    totals = [None] * MOMENTS
    for start in range(0, size, chunk):
        t = scaled[start : start + chunk] - centre
        p = power[start : start + chunk]
        p_parts = halves(p)
        t2 = t * 2.0
        t2_parts = halves(t2)
        zero = jnp.zeros_like(t)
        before, here = (jnp.ones_like(t), zero), (t, zero)
        for order in range(MOMENTS):
            value = before
            v_parts = halves(value[0])
            term, low_term = two_prod(value[0], p, v_parts, p_parts)
            term = (term, low_term + value[1] * p)
            rows = [(term[0][i : i + 8], term[1][i : i + 8]) for i in range(0, chunk, 8)]
            while len(rows) > 1:
                rows = [dd_add(rows[i], rows[i + 1]) for i in range(0, len(rows), 2)]
            totals[order] = rows[0] if totals[order] is None else dd_add(totals[order], rows[0])
            if order + 1 < MOMENTS:
                up, low_up = two_prod(here[0], t2, None, t2_parts)
                up, low_up = quick_sum(up, low_up + here[1] * t2)
                following = dd_add((up, low_up), dd_neg(before))
                before, here = here, following
    row = lax.broadcasted_iota(jnp.int32, (8, size), 0)
    lane = lax.broadcasted_iota(jnp.int32, (8, size), 1)
    out = jnp.zeros((8, size), jnp.float32)
    for base in range(0, MOMENTS, 8):
        high_rows = jnp.zeros((8, size), jnp.float32)
        low_rows = jnp.zeros((8, size), jnp.float32)
        for order in range(base, min(base + 8, MOMENTS)):
            total = sublane_total(totals[order])
            high_rows = jnp.where(row == order - base, total[0], high_rows)
            low_rows = jnp.where(row == order - base, total[1], low_rows)
        high_rows, low_rows = lane_total((high_rows, low_rows))
        out = jnp.where(lane == row + base, high_rows, out)
        out = jnp.where(lane == row + (base + LOW_LANE), low_rows, out)
    line = jnp.sum(out, axis=0, keepdims=True)
    send_ref[...] = jnp.broadcast_to(line, (size, size))


def lane_of(a, lane):
    pick = lambda v: jnp.broadcast_to(v[:, lane : lane + 1], v.shape)
    return pick(a[0]), pick(a[1])


def solve_kernel(sums_ref, range_ref, scaled_ref, real_ref, imag_ref, rows_ref, out_ref, gain_ref, *, scale):
    size = scaled_ref.shape[0]
    given = sums_ref[...]
    low = pltpu.roll(given, size - LOW_LANE, 1)
    rows = [(given[i : i + 8], low[i : i + 8]) for i in range(0, given.shape[0], 8)]
    while len(rows) > 1:
        rows = [dd_add(rows[i], rows[i + 1]) for i in range(0, len(rows), 2)]
    moments = sublane_total(rows[0])
    half = range_ref[0:1, :]
    centre = jnp.broadcast_to(range_ref[1:2, :], moments[0].shape)
    centre = (centre, jnp.zeros_like(centre))
    lane = lax.broadcasted_iota(jnp.int32, moments[0].shape, 1)
    resid, direct = moments, moments
    steps, turns = [], []
    decay = jnp.ones((1, size), jnp.float32)
    for k in range(ITERS):
        after = tuple(pltpu.roll(v, size - 1, 1) for v in direct)
        prior = tuple(pltpu.roll(v, 1, 1) for v in direct)
        prior = tuple(jnp.where(lane == 0, a, p) for a, p in zip(after, prior))
        image = dd_add(dd_mul(direct, centre), dd_scale(dd_add(after, prior), 0.5))
        alpha = dd_div(lane_of(resid, k), lane_of(image, k))
        fresh = dd_add(resid, dd_neg(dd_mul(alpha, image)))
        beta = dd_mul(alpha, dd_div(lane_of(fresh, k + 1), lane_of(resid, k)))
        beta = dd_scale(beta, -1.0 if k == 0 else -0.5)
        direct = dd_add(fresh, dd_mul(beta, direct))
        resid = fresh
        steps.append(alpha[0][0:1])
        turns.append(beta[0][0:1])
        decay = decay * beta[0][0:1]
    gain = lax.rsqrt(jnp.maximum(jnp.abs(decay), 1e-30)) / centre[0][0:1]
    gain_ref[...] = jnp.broadcast_to(gain, gain_ref.shape)
    scaled = scaled_ref[...]
    field = steps[0]
    solved = jnp.broadcast_to(field, scaled.shape)
    left = 1.0 - field * scaled
    toward = left + turns[0]
    for k in range(1, ITERS):
        solved = solved + steps[k] * toward
        left = left - steps[k] * (scaled * toward)
        if k + 1 < ITERS:
            toward = left + turns[k] * toward
    solved = solved * (scale / half)
    left = left * (gain * scale)
    real, imag = real_ref[...], imag_ref[...]
    back_real = solved * real - left * imag
    back_imag = solved * imag + left * real
    both = dot(rows_ref[...], jnp.concatenate([back_real, back_imag], axis=1))
    out_ref[0] = both[:size, :size] - both[size:, size:]
    out_ref[1] = both[:size, size:] + both[size:, :size]


def output_kernel(given_ref, gain_ref, own_ref, lanes_ref, field_ref, resid_ref):
    planes, size = field_ref.shape[0], field_ref.shape[1]
    wide = jnp.concatenate([given_ref[:, i, :] for i in range(2 * planes)], axis=1)
    both = dot(own_ref[...], wide)
    shrink = 1.0 / gain_ref[0:1, :]
    for j in range(planes):
        at = 2 * j * size
        real = both[:size, at : at + size] - both[size:, at + size : at + 2 * size]
        imag = both[:size, at + size : at + 2 * size] + both[size:, at : at + size]
        ends = dot(jnp.concatenate([real, imag], axis=0), lanes_ref[...])
        field_ref[j] = ends[:size, :size] - ends[size:, size:]
        resid_ref[j] = (ends[size:, :size] + ends[:size, size:]) * shrink


def call(kernel, name, shapes, *args):
    whole = pl.BlockSpec(memory_space=pltpu.VMEM)
    return pl.pallas_call(
        kernel,
        out_shape=[jax.ShapeDtypeStruct(s, jnp.float32) for s in shapes],
        in_specs=[whole] * len(args),
        out_specs=[whole] * len(shapes),
        name=name,
    )(*args)


def grid_sums(intensities, gridding, dest_slab, ngrid):
    nent, rows, size = intensities.shape
    slab_rows = gridding.shape[2]
    capacity = max(2, 2 * nent // ngrid)
    target = dest_slab[:, 0]
    member = (target[:, None] == jnp.arange(ngrid, dtype=jnp.int32)[None, :]).astype(jnp.int32)
    before = jnp.sum((jnp.cumsum(member, axis=0) - member) * member, axis=1)
    slot = target * capacity + before
    value_slots = jnp.zeros((ngrid * capacity, rows, size), intensities.dtype).at[slot].set(intensities)
    matrix_slots = jnp.zeros((ngrid * capacity, rows, slab_rows), gridding.dtype).at[slot].set(gridding)
    return lax.dot_general(
        matrix_slots.reshape(ngrid, capacity * rows, slab_rows),
        value_slots.reshape(ngrid, capacity * rows, size),
        (((1,), (1,)), ((0,), (0,))),
        preferred_element_type=jnp.float32,
    )


def body(intensities, gridding, dest_slab, spectral_weights):
    ngrid = lax.axis_size("grid")
    ndp = lax.axis_size("dp")
    size = intensities.shape[2]
    slab_rows = gridding.shape[2]
    planes = slab_rows // size
    count = ngrid * ndp
    table = dft_tables(size, ndp)

    pieces = jnp.moveaxis(spectral_weights[0], 1, 0)
    arrived = lax.all_to_all(pieces, "dp", 0, 0, tiled=True)
    own = jnp.sum(arrived, axis=0)
    flip = lambda w: jnp.roll(jnp.flip(w, (0, 1)), (1, 1), (0, 1))
    ky = owner_order(size, ndp)
    holder = np.argsort(ky)
    mirrored = lax.ppermute(flip(own), ALL, [(d, int(holder[(-ky[d]) % size])) for d in range(count)])

    product = grid_sums(intensities, gridding, dest_slab, ngrid)
    partial = lax.psum_scatter(product.reshape(slab_rows * ngrid, size), "grid", scatter_dimension=0, tiled=True)
    plane = lax.psum_scatter(partial, "dp", scatter_dimension=0, tiled=True)

    forward, sym = call(
        plane_kernel, "plane", [(size, 4, size), (size, size)],
        plane, own, mirrored, table["lanes"], table["own_rows"],
    )
    columns = lax.all_to_all(forward, ALL, 0, 0, tiled=True)
    square = (size, size)
    real, imag, scaled, ends, send = call(
        moment_kernel, "moments", [square, square, square, (8, size), square],
        columns, sym, table["own_cols"],
    )
    sums = lax.all_to_all(send.reshape(count, 1, size), ALL, 0, 0, tiled=True).reshape(count, size)
    back, gain = call(
        functools.partial(solve_kernel, scale=1.0 / size**3), "solve", [(2, size, size), (8, size)],
        sums, ends, scaled, real, imag, table["back_rows"],
    )
    spread = jnp.transpose(back.reshape(2, ngrid, planes, size), (1, 2, 0, 3)).reshape(1, ngrid, 2 * planes, size)
    spread = jnp.broadcast_to(spread, (ndp, ngrid, 2 * planes, size)).reshape(count, 2 * planes, size)
    given = lax.all_to_all(spread, ALL, 0, 0, tiled=True)
    return tuple(
        call(
            output_kernel, "planes_back", [(planes, size, size)] * 2,
            given, gain, table["back_own"], table["lanes"],
        )
    )


def solution(mesh):
    return jax.shard_map(
        body,
        mesh=mesh,
        in_specs=(
            P(("dp", "grid"), None, None),
            P(("dp", "grid"), None, None),
            P(("dp", "grid"), None),
            P("dp", None, "grid", None),
        ),
        out_specs=(P("grid", None, None), P("grid", None, None)),
        check_vma=False,
    )
```

```python
import functools

import jax
import jax.numpy as jnp
import numpy as np
from jax import lax
from jax.experimental import pallas as pl
from jax.experimental.pallas import tpu as pltpu
from jax.sharding import PartitionSpec as P


ITERS = 8
MOMENTS = 2 * ITERS + 1
LOW_LANE = 64
ALL = ("dp", "grid")
HIGHEST = lax.Precision.HIGHEST


def two_sum(a, b):
    s = a + b
    v = s - a
    return s, (a - (s - v)) + (b - v)


def quick_sum(a, b):
    s = a + b
    return s, b - (s - a)


def halves(a):
    c = a * 4097.0
    high = c - (c - a)
    return high, a - high


def two_prod(a, b, a_parts=None, b_parts=None):
    p = a * b
    ah, al = a_parts or halves(a)
    bh, bl = b_parts or halves(b)
    return p, ((ah * bh - p) + ah * bl + al * bh) + al * bl


def dd_add(a, b):
    s, e = two_sum(a[0], b[0])
    t, f = two_sum(a[1], b[1])
    s, e = quick_sum(s, e + t)
    return quick_sum(s, e + f)


def dd_mul(a, b):
    p, e = two_prod(a[0], b[0])
    return quick_sum(p, e + (a[0] * b[1] + a[1] * b[0]))


def dd_scale(a, factor):
    return a[0] * factor, a[1] * factor


def dd_neg(a):
    return -a[0], -a[1]


def dd_div(a, b):
    first = a[0] / b[0]
    rest = dd_add(a, dd_neg(dd_mul((first, jnp.zeros_like(first)), b)))
    second = rest[0] / b[0]
    rest = dd_add(rest, dd_neg(dd_mul((second, jnp.zeros_like(second)), b)))
    third = rest[0] / b[0]
    high, low = quick_sum(first, second)
    return quick_sum(high, low + third)


def dot(a, b):
    return jax.lax.dot_general(
        a, b, (((1,), (0,)), ((), ())), precision=HIGHEST, preferred_element_type=jnp.float32
    )


def owner_order(size, ndp):
    slots = size // ndp
    d = np.arange(size)
    return ndp * (d % slots) + d // slots


def dft_tables(size, ndp):
    index = np.arange(size)
    angle = 2.0 * np.pi * ((index[:, None] * index[None, :]) % size) / size
    cos, sin = np.cos(angle), np.sin(angle)
    order = owner_order(size, ndp)
    as_f32 = lambda a: np.ascontiguousarray(a, dtype=np.float32)
    return dict(
        lanes=as_f32(np.concatenate([cos, sin], 1)),
        own_rows=as_f32(np.concatenate([cos[order], sin[order]], 0)),
        own_cols=as_f32(np.concatenate([cos[:, order], sin[:, order]], 0)),
        back_rows=as_f32(np.concatenate([cos, sin], 0)),
        back_own=as_f32(np.concatenate([cos[:, order], sin[:, order]], 0)),
        mirror=as_f32(((index[:, None] + index[None, :]) % size) == 0),
    )


def plane_kernel(plane_ref, own_ref, mirrored_ref, lanes_ref, rows_ref, out_ref, sym_ref):
    size = plane_ref.shape[0]
    sym = (own_ref[...] + mirrored_ref[...]) * 0.5
    sym_ref[...] = sym
    low = jnp.min(jnp.min(sym, axis=0, keepdims=True), axis=1, keepdims=True)
    high = jnp.max(jnp.max(sym, axis=0, keepdims=True), axis=1, keepdims=True)
    first = dot(plane_ref[...].T, lanes_ref[...])
    both = dot(rows_ref[...], first)
    real = both[:size, :size] - both[size:, size:]
    imag = -(both[size:, :size] + both[:size, size:])
    out_ref[:, 0, :] = real
    out_ref[:, 1, :] = imag
    out_ref[:, 2, :] = jnp.broadcast_to(low, (size, size))
    out_ref[:, 3, :] = jnp.broadcast_to(high, (size, size))


def sublane_total(a):
    for shift in (4, 2, 1):
        a = dd_add(a, (pltpu.roll(a[0], shift, 0), pltpu.roll(a[1], shift, 0)))
    return a


def lane_total(a):
    for shift in (64, 32, 16, 8, 4, 2, 1):
        a = dd_add(a, (pltpu.roll(a[0], shift, 1), pltpu.roll(a[1], shift, 1)))
    return a


def moment_kernel(columns_ref, sym_ref, cols_ref, real_ref, imag_ref, scaled_ref, range_ref, send_ref):
    size = sym_ref.shape[0]
    low = jnp.min(jnp.min(columns_ref[:, 2, :], axis=0, keepdims=True), axis=1, keepdims=True)
    high = jnp.max(jnp.max(columns_ref[:, 3, :], axis=0, keepdims=True), axis=1, keepdims=True)
    half = jnp.maximum((high - low) * 0.5, high * 1e-4)
    half = jnp.broadcast_to(half, (1, size))
    centre = jnp.broadcast_to((high + low) * 0.5, (1, size)) / half
    range_ref[0:1, :] = half
    range_ref[1:2, :] = centre
    range_ref[2:8, :] = jnp.zeros((6, size), jnp.float32)
    given = jnp.concatenate([columns_ref[:, 0, :], columns_ref[:, 1, :]], axis=1)
    both = dot(cols_ref[...], given)
    real = both[:size, :size] + both[size:, size:]
    imag = both[:size, size:] - both[size:, :size]
    real_ref[...] = real
    imag_ref[...] = imag
    scaled = sym_ref[...] / half
    scaled_ref[...] = scaled
    power = real * real + imag * imag
    chunk = 32
    totals = [None] * MOMENTS
    for start in range(0, size, chunk):
        t = scaled[start : start + chunk] - centre
        p = power[start : start + chunk]
        p_parts = halves(p)
        t2 = t * 2.0
        t2_parts = halves(t2)
        zero = jnp.zeros_like(t)
        before, here = (jnp.ones_like(t), zero), (t, zero)
        for order in range(MOMENTS):
            value = before
            v_parts = halves(value[0])
            term, low_term = two_prod(value[0], p, v_parts, p_parts)
            term = (term, low_term + value[1] * p)
            rows = [(term[0][i : i + 8], term[1][i : i + 8]) for i in range(0, chunk, 8)]
            while len(rows) > 1:
                rows = [dd_add(rows[i], rows[i + 1]) for i in range(0, len(rows), 2)]
            totals[order] = rows[0] if totals[order] is None else dd_add(totals[order], rows[0])
            if order + 1 < MOMENTS:
                up, low_up = two_prod(here[0], t2, None, t2_parts)
                up, low_up = quick_sum(up, low_up + here[1] * t2)
                following = dd_add((up, low_up), dd_neg(before))
                before, here = here, following
    row = lax.broadcasted_iota(jnp.int32, (8, size), 0)
    lane = lax.broadcasted_iota(jnp.int32, (8, size), 1)
    out = jnp.zeros((8, size), jnp.float32)
    for base in range(0, MOMENTS, 8):
        high_rows = jnp.zeros((8, size), jnp.float32)
        low_rows = jnp.zeros((8, size), jnp.float32)
        for order in range(base, min(base + 8, MOMENTS)):
            total = sublane_total(totals[order])
            high_rows = jnp.where(row == order - base, total[0], high_rows)
            low_rows = jnp.where(row == order - base, total[1], low_rows)
        high_rows, low_rows = lane_total((high_rows, low_rows))
        out = jnp.where(lane == row + base, high_rows, out)
        out = jnp.where(lane == row + (base + LOW_LANE), low_rows, out)
    line = jnp.sum(out, axis=0, keepdims=True)
    send_ref[...] = jnp.broadcast_to(line, (size, size))


def lane_of(a, lane):
    pick = lambda v: jnp.broadcast_to(v[:, lane : lane + 1], v.shape)
    return pick(a[0]), pick(a[1])


def solve_kernel(sums_ref, range_ref, scaled_ref, real_ref, imag_ref, rows_ref, out_ref, gain_ref, *, scale):
    size = scaled_ref.shape[0]
    given = sums_ref[...]
    low = pltpu.roll(given, size - LOW_LANE, 1)
    rows = [(given[i : i + 8], low[i : i + 8]) for i in range(0, given.shape[0], 8)]
    while len(rows) > 1:
        rows = [dd_add(rows[i], rows[i + 1]) for i in range(0, len(rows), 2)]
    moments = sublane_total(rows[0])
    half = range_ref[0:1, :]
    centre = jnp.broadcast_to(range_ref[1:2, :], moments[0].shape)
    centre = (centre, jnp.zeros_like(centre))
    lane = lax.broadcasted_iota(jnp.int32, moments[0].shape, 1)
    resid, direct = moments, moments
    steps, turns = [], []
    decay = jnp.ones((1, size), jnp.float32)
    for k in range(ITERS):
        after = tuple(pltpu.roll(v, size - 1, 1) for v in direct)
        prior = tuple(pltpu.roll(v, 1, 1) for v in direct)
        prior = tuple(jnp.where(lane == 0, a, p) for a, p in zip(after, prior))
        image = dd_add(dd_mul(direct, centre), dd_scale(dd_add(after, prior), 0.5))
        alpha = dd_div(lane_of(resid, k), lane_of(image, k))
        fresh = dd_add(resid, dd_neg(dd_mul(alpha, image)))
        beta = dd_mul(alpha, dd_div(lane_of(fresh, k + 1), lane_of(resid, k)))
        beta = dd_scale(beta, -1.0 if k == 0 else -0.5)
        direct = dd_add(fresh, dd_mul(beta, direct))
        resid = fresh
        steps.append(alpha[0][0:1])
        turns.append(beta[0][0:1])
        decay = decay * beta[0][0:1]
    gain = lax.rsqrt(jnp.maximum(jnp.abs(decay), 1e-30)) / centre[0][0:1]
    gain_ref[...] = jnp.broadcast_to(gain, gain_ref.shape)
    scaled = scaled_ref[...]
    field = steps[0]
    solved = jnp.broadcast_to(field, scaled.shape)
    left = 1.0 - field * scaled
    toward = left + turns[0]
    for k in range(1, ITERS):
        solved = solved + steps[k] * toward
        left = left - steps[k] * (scaled * toward)
        if k + 1 < ITERS:
            toward = left + turns[k] * toward
    solved = solved * (scale / half)
    left = left * (gain * scale)
    real, imag = real_ref[...], imag_ref[...]
    back_real = solved * real - left * imag
    back_imag = solved * imag + left * real
    both = dot(rows_ref[...], jnp.concatenate([back_real, back_imag], axis=1))
    out_ref[0] = both[:size, :size] - both[size:, size:]
    out_ref[1] = both[:size, size:] + both[size:, :size]


def output_kernel(given_ref, gain_ref, own_ref, lanes_ref, field_ref, resid_ref):
    planes, size = field_ref.shape[0], field_ref.shape[1]
    wide = jnp.concatenate([given_ref[:, i, :] for i in range(2 * planes)], axis=1)
    both = dot(own_ref[...], wide)
    shrink = 1.0 / gain_ref[0:1, :]
    for j in range(planes):
        at = 2 * j * size
        real = both[:size, at : at + size] - both[size:, at + size : at + 2 * size]
        imag = both[:size, at + size : at + 2 * size] + both[size:, at : at + size]
        ends = dot(jnp.concatenate([real, imag], axis=0), lanes_ref[...])
        field_ref[j] = ends[:size, :size] - ends[size:, size:]
        resid_ref[j] = (ends[size:, :size] + ends[:size, size:]) * shrink


def call(kernel, name, shapes, *args):
    whole = pl.BlockSpec(memory_space=pltpu.VMEM)
    return pl.pallas_call(
        kernel,
        out_shape=[jax.ShapeDtypeStruct(s, jnp.float32) for s in shapes],
        in_specs=[whole] * len(args),
        out_specs=[whole] * len(shapes),
        name=name,
    )(*args)


SIDE = 4
CORES = 2
PARTS = ((0, 48), (48, 88), (88, 128))
ORDERS = ((0, 1, 2), (1, 2, 0), (2, 0, 1))


def place_of(device):
    return device // 32, (device // 2) % SIDE, (device // 8) % SIDE, device % CORES


def device_at(x, y, z, core):
    return ((x * SIDE + z) * SIDE + y) * CORES + core


def shift_pairs(axis, hop):
    pairs = []
    for device in range(SIDE**3 * CORES):
        place = list(place_of(device))
        place[axis] = (place[axis] + hop) % (CORES if axis == 3 else SIDE)
        pairs.append((device, device_at(*place)))
    return pairs


def grid_kernel(dest_ref, place_ref, values_ref, matrix_ref, *rest):
    outs, (count_ref, list_ref) = rest[:3], rest[3:]
    nent, rows, size = values_ref.shape
    nslab = count_ref.shape[0]
    capacity = list_ref.shape[0] // nslab
    x, y, z, core = (place_ref[i] for i in range(4))

    def clear(s, _):
        count_ref[s] = 0
        return 0

    def enter(e, _):
        slab = dest_ref[e]
        taken = count_ref[slab]
        list_ref[slab * capacity + taken] = e
        count_ref[slab] = taken + 1
        return 0

    lax.fori_loop(0, nslab, clear, 0)
    lax.fori_loop(0, nent, enter, 0)
    for zr in range(SIDE):
        for yr in range(SIDE):
            slab = ((z + zr) % SIDE) * (SIDE * CORES) + ((y + yr) % SIDE) * CORES + core
            taken = count_ref[slab]
            values, matrices = [], []
            for m in range(capacity):
                entry = jnp.where(m < taken, list_ref[slab * capacity + m], 0)
                value = values_ref[entry]
                values.append(jnp.where(m < taken, value, jnp.zeros_like(value)))
                matrices.append(
                    jnp.concatenate(
                        [
                            matrix_ref[entry, :, pl.ds(pl.multiple_of(((x + pr) % SIDE) * size, size), size)]
                            for pr in range(SIDE)
                        ],
                        axis=1,
                    )
                )
            product = lax.dot_general(
                jnp.concatenate(values, 0),
                jnp.concatenate(matrices, 0),
                (((0,), (0,)), ((), ())),
                preferred_element_type=jnp.float32,
            )
            for pr in range(SIDE):
                relative = (pr, yr, zr)
                for out_ref, (start, stop), order in zip(outs, PARTS, ORDERS):
                    index = tuple(relative[axis] for axis in order)
                    out_ref[index] = product[start:stop, pr * size : (pr + 1) * size]


def grid_blocks(dest, place, values, matrix, nslab):
    whole = pl.BlockSpec(memory_space=pltpu.VMEM)
    scalars = pl.BlockSpec(memory_space=pltpu.SMEM)
    size = values.shape[2]
    nent = values.shape[0]
    capacity = max(2, 2 * nent // nslab)
    return pl.pallas_call(
        grid_kernel,
        out_shape=[
            jax.ShapeDtypeStruct((SIDE, SIDE, SIDE, stop - start, size), jnp.float32) for start, stop in PARTS
        ],
        in_specs=[scalars, scalars, whole, whole],
        out_specs=[whole] * len(PARTS),
        scratch_shapes=[pltpu.SMEM((nslab,), jnp.int32), pltpu.SMEM((nslab * capacity,), jnp.int32)],
        name="gridding",
    )(dest, place, values, matrix)


def exchange(parts, axis):
    arrived = [lax.ppermute(parts[r], ALL, shift_pairs(axis, r)) for r in range(1, SIDE)]
    return ((parts[0] + arrived[0]) + arrived[1]) + arrived[2]


def scattered_sum(intensities, gridding, dest_slab, nslab):
    grid_at = lax.axis_index("grid")
    x, z, y, core = lax.axis_index("dp"), grid_at // 8, (grid_at // 2) % SIDE, grid_at % CORES
    dest = dest_slab[:, 0]
    place = lambda c: jnp.stack([x, y, z, c]).astype(jnp.int32)
    away = grid_blocks(dest, place(1 - core), intensities, gridding, nslab)
    arrived = [lax.ppermute(a, ALL, shift_pairs(3, 1)) for a in away]
    kept = grid_blocks(dest, place(core), intensities, gridding, nslab)
    pieces = []
    for own, other, order in zip(kept, arrived, ORDERS):
        total = exchange([own[r] + other[r] for r in range(SIDE)], order[0])
        total = exchange([total[r] for r in range(SIDE)], order[1])
        total = exchange([total[r] for r in range(SIDE)], order[2])
        pieces.append(total)
    return jnp.concatenate(pieces, 0)


def body(intensities, gridding, dest_slab, spectral_weights):
    ngrid = lax.axis_size("grid")
    ndp = lax.axis_size("dp")
    size = intensities.shape[2]
    slab_rows = gridding.shape[2]
    planes = slab_rows // size
    count = ngrid * ndp
    table = dft_tables(size, ndp)

    mine = lax.axis_index("dp")
    pieces = [
        lax.dynamic_index_in_dim(spectral_weights[0], (mine + r) % SIDE, 1, keepdims=False) for r in range(SIDE)
    ]
    own = exchange(pieces, 0)
    flip = lambda w: jnp.roll(jnp.flip(w, (0, 1)), (1, 1), (0, 1))
    ky = owner_order(size, ndp)
    holder = np.argsort(ky)
    mirrored = lax.ppermute(flip(own), ALL, [(d, int(holder[(-ky[d]) % size])) for d in range(count)])

    plane = scattered_sum(intensities, gridding, dest_slab, ngrid)

    forward, sym = call(
        plane_kernel, "plane", [(size, 4, size), (size, size)],
        plane, own, mirrored, table["lanes"], table["own_rows"],
    )
    columns = lax.all_to_all(forward, ALL, 0, 0, tiled=True)
    square = (size, size)
    real, imag, scaled, ends, send = call(
        moment_kernel, "moments", [square, square, square, (8, size), square],
        columns, sym, table["own_cols"],
    )
    sums = lax.all_to_all(send.reshape(count, 1, size), ALL, 0, 0, tiled=True).reshape(count, size)
    back, gain = call(
        functools.partial(solve_kernel, scale=1.0 / size**3), "solve", [(2, size, size), (8, size)],
        sums, ends, scaled, real, imag, table["back_rows"],
    )
    spread = jnp.transpose(back.reshape(2, ngrid, planes, size), (1, 2, 0, 3)).reshape(1, ngrid, 2 * planes, size)
    spread = jnp.broadcast_to(spread, (ndp, ngrid, 2 * planes, size)).reshape(count, 2 * planes, size)
    given = lax.all_to_all(spread, ALL, 0, 0, tiled=True)
    return tuple(
        call(
            output_kernel, "planes_back", [(planes, size, size)] * 2,
            given, gain, table["back_own"], table["lanes"],
        )
    )


def solution(mesh):
    return jax.shard_map(
        body,
        mesh=mesh,
        in_specs=(
            P(("dp", "grid"), None, None),
            P(("dp", "grid"), None, None),
            P(("dp", "grid"), None),
            P("dp", None, "grid", None),
        ),
        out_specs=(P("grid", None, None), P("grid", None, None)),
        check_vma=False,
    )
```

```python
import functools

import jax
import jax.numpy as jnp
import numpy as np
from jax import lax
from jax.experimental import pallas as pl
from jax.experimental.pallas import tpu as pltpu
from jax.sharding import PartitionSpec as P


ITERS = 8
MOMENTS = 2 * ITERS + 1
LOW_LANE = 64
ALL = ("dp", "grid")
HIGHEST = lax.Precision.HIGHEST


def two_sum(a, b):
    s = a + b
    v = s - a
    return s, (a - (s - v)) + (b - v)


def quick_sum(a, b):
    s = a + b
    return s, b - (s - a)


def halves(a):
    c = a * 4097.0
    high = c - (c - a)
    return high, a - high


def two_prod(a, b, a_parts=None, b_parts=None):
    p = a * b
    ah, al = a_parts or halves(a)
    bh, bl = b_parts or halves(b)
    return p, ((ah * bh - p) + ah * bl + al * bh) + al * bl


def dd_add(a, b):
    s, e = two_sum(a[0], b[0])
    t, f = two_sum(a[1], b[1])
    s, e = quick_sum(s, e + t)
    return quick_sum(s, e + f)


def dd_mul(a, b):
    p, e = two_prod(a[0], b[0])
    return quick_sum(p, e + (a[0] * b[1] + a[1] * b[0]))


def dd_scale(a, factor):
    return a[0] * factor, a[1] * factor


def dd_neg(a):
    return -a[0], -a[1]


def dd_div(a, b):
    first = a[0] / b[0]
    rest = dd_add(a, dd_neg(dd_mul((first, jnp.zeros_like(first)), b)))
    second = rest[0] / b[0]
    rest = dd_add(rest, dd_neg(dd_mul((second, jnp.zeros_like(second)), b)))
    third = rest[0] / b[0]
    high, low = quick_sum(first, second)
    return quick_sum(high, low + third)


def dot(a, b):
    return jax.lax.dot_general(
        a, b, (((1,), (0,)), ((), ())), precision=HIGHEST, preferred_element_type=jnp.float32
    )


def owner_order(size, ndp):
    slots = size // ndp
    d = np.arange(size)
    return ndp * (d % slots) + d // slots


def dft_tables(size, ndp):
    index = np.arange(size)
    angle = 2.0 * np.pi * ((index[:, None] * index[None, :]) % size) / size
    cos, sin = np.cos(angle), np.sin(angle)
    order = owner_order(size, ndp)
    as_f32 = lambda a: np.ascontiguousarray(a, dtype=np.float32)
    return dict(
        lanes=as_f32(np.concatenate([cos, sin], 1)),
        own_rows=as_f32(np.concatenate([cos[order], sin[order]], 0)),
        own_cols=as_f32(np.concatenate([cos[:, order], sin[:, order]], 0)),
        back_rows=as_f32(np.concatenate([cos, sin], 0)),
        back_own=as_f32(np.concatenate([cos[:, order], sin[:, order]], 0)),
        mirror=as_f32(((index[:, None] + index[None, :]) % size) == 0),
    )


def plane_kernel(plane_ref, own_ref, mirrored_ref, lanes_ref, rows_ref, out_ref, sym_ref):
    size = plane_ref.shape[0]
    sym = (own_ref[...] + mirrored_ref[...]) * 0.5
    sym_ref[...] = sym
    low = jnp.min(jnp.min(sym, axis=0, keepdims=True), axis=1, keepdims=True)
    high = jnp.max(jnp.max(sym, axis=0, keepdims=True), axis=1, keepdims=True)
    first = dot(plane_ref[...].T, lanes_ref[...])
    both = dot(rows_ref[...], first)
    real = both[:size, :size] - both[size:, size:]
    imag = -(both[size:, :size] + both[:size, size:])
    out_ref[:, 0, :] = real
    out_ref[:, 1, :] = imag
    out_ref[:, 2, :] = jnp.broadcast_to(low, (size, size))
    out_ref[:, 3, :] = jnp.broadcast_to(high, (size, size))


def sublane_total(a):
    for shift in (4, 2, 1):
        a = dd_add(a, (pltpu.roll(a[0], shift, 0), pltpu.roll(a[1], shift, 0)))
    return a


def lane_total(a):
    for shift in (64, 32, 16, 8, 4, 2, 1):
        a = dd_add(a, (pltpu.roll(a[0], shift, 1), pltpu.roll(a[1], shift, 1)))
    return a


def moment_kernel(columns_ref, sym_ref, cols_ref, real_ref, imag_ref, scaled_ref, range_ref, send_ref):
    size = sym_ref.shape[0]
    low = jnp.min(jnp.min(columns_ref[:, 2, :], axis=0, keepdims=True), axis=1, keepdims=True)
    high = jnp.max(jnp.max(columns_ref[:, 3, :], axis=0, keepdims=True), axis=1, keepdims=True)
    half = jnp.maximum((high - low) * 0.5, high * 1e-4)
    half = jnp.broadcast_to(half, (1, size))
    centre = jnp.broadcast_to((high + low) * 0.5, (1, size)) / half
    range_ref[0:1, :] = half
    range_ref[1:2, :] = centre
    range_ref[2:8, :] = jnp.zeros((6, size), jnp.float32)
    given = jnp.concatenate([columns_ref[:, 0, :], columns_ref[:, 1, :]], axis=1)
    both = dot(cols_ref[...], given)
    real = both[:size, :size] + both[size:, size:]
    imag = both[:size, size:] - both[size:, :size]
    real_ref[...] = real
    imag_ref[...] = imag
    scaled = sym_ref[...] / half
    scaled_ref[...] = scaled
    power = real * real + imag * imag
    chunk = 32
    totals = [None] * MOMENTS
    for start in range(0, size, chunk):
        t = scaled[start : start + chunk] - centre
        p = power[start : start + chunk]
        p_parts = halves(p)
        t2 = t * 2.0
        t2_parts = halves(t2)
        zero = jnp.zeros_like(t)
        before, here = (jnp.ones_like(t), zero), (t, zero)
        for order in range(MOMENTS):
            value = before
            v_parts = halves(value[0])
            term, low_term = two_prod(value[0], p, v_parts, p_parts)
            term = (term, low_term + value[1] * p)
            rows = [(term[0][i : i + 8], term[1][i : i + 8]) for i in range(0, chunk, 8)]
            while len(rows) > 1:
                rows = [dd_add(rows[i], rows[i + 1]) for i in range(0, len(rows), 2)]
            totals[order] = rows[0] if totals[order] is None else dd_add(totals[order], rows[0])
            if order + 1 < MOMENTS:
                up, low_up = two_prod(here[0], t2, None, t2_parts)
                up, low_up = quick_sum(up, low_up + here[1] * t2)
                following = dd_add((up, low_up), dd_neg(before))
                before, here = here, following
    row = lax.broadcasted_iota(jnp.int32, (8, size), 0)
    lane = lax.broadcasted_iota(jnp.int32, (8, size), 1)
    out = jnp.zeros((8, size), jnp.float32)
    for base in range(0, MOMENTS, 8):
        high_rows = jnp.zeros((8, size), jnp.float32)
        low_rows = jnp.zeros((8, size), jnp.float32)
        for order in range(base, min(base + 8, MOMENTS)):
            total = sublane_total(totals[order])
            high_rows = jnp.where(row == order - base, total[0], high_rows)
            low_rows = jnp.where(row == order - base, total[1], low_rows)
        high_rows, low_rows = lane_total((high_rows, low_rows))
        out = jnp.where(lane == row + base, high_rows, out)
        out = jnp.where(lane == row + (base + LOW_LANE), low_rows, out)
    line = jnp.sum(out, axis=0, keepdims=True)
    send_ref[...] = jnp.broadcast_to(line, (size, size))


def lane_of(a, lane):
    pick = lambda v: jnp.broadcast_to(v[:, lane : lane + 1], v.shape)
    return pick(a[0]), pick(a[1])


def solve_kernel(sums_ref, range_ref, scaled_ref, real_ref, imag_ref, rows_ref, out_ref, gain_ref, *, scale):
    size = scaled_ref.shape[0]
    given = sums_ref[...]
    low = pltpu.roll(given, size - LOW_LANE, 1)
    rows = [(given[i : i + 8], low[i : i + 8]) for i in range(0, given.shape[0], 8)]
    while len(rows) > 1:
        rows = [dd_add(rows[i], rows[i + 1]) for i in range(0, len(rows), 2)]
    moments = sublane_total(rows[0])
    half = range_ref[0:1, :]
    centre = jnp.broadcast_to(range_ref[1:2, :], moments[0].shape)
    centre = (centre, jnp.zeros_like(centre))
    lane = lax.broadcasted_iota(jnp.int32, moments[0].shape, 1)
    resid, direct = moments, moments
    steps, turns = [], []
    decay = jnp.ones((1, size), jnp.float32)
    for k in range(ITERS):
        after = tuple(pltpu.roll(v, size - 1, 1) for v in direct)
        prior = tuple(pltpu.roll(v, 1, 1) for v in direct)
        prior = tuple(jnp.where(lane == 0, a, p) for a, p in zip(after, prior))
        image = dd_add(dd_mul(direct, centre), dd_scale(dd_add(after, prior), 0.5))
        alpha = dd_div(lane_of(resid, k), lane_of(image, k))
        fresh = dd_add(resid, dd_neg(dd_mul(alpha, image)))
        beta = dd_mul(alpha, dd_div(lane_of(fresh, k + 1), lane_of(resid, k)))
        beta = dd_scale(beta, -1.0 if k == 0 else -0.5)
        direct = dd_add(fresh, dd_mul(beta, direct))
        resid = fresh
        steps.append(alpha[0][0:1])
        turns.append(beta[0][0:1])
        decay = decay * beta[0][0:1]
    gain = lax.rsqrt(jnp.maximum(jnp.abs(decay), 1e-30)) / centre[0][0:1]
    gain_ref[...] = jnp.broadcast_to(gain, gain_ref.shape)
    scaled = scaled_ref[...]
    field = steps[0]
    solved = jnp.broadcast_to(field, scaled.shape)
    left = 1.0 - field * scaled
    toward = left + turns[0]
    for k in range(1, ITERS):
        solved = solved + steps[k] * toward
        left = left - steps[k] * (scaled * toward)
        if k + 1 < ITERS:
            toward = left + turns[k] * toward
    solved = solved * (scale / half)
    left = left * (gain * scale)
    real, imag = real_ref[...], imag_ref[...]
    back_real = solved * real - left * imag
    back_imag = solved * imag + left * real
    both = dot(rows_ref[...], jnp.concatenate([back_real, back_imag], axis=1))
    out_ref[0] = both[:size, :size] - both[size:, size:]
    out_ref[1] = both[:size, size:] + both[size:, :size]


def output_kernel(given_ref, gain_ref, own_ref, lanes_ref, field_ref, resid_ref):
    planes, size = field_ref.shape[0], field_ref.shape[1]
    wide = jnp.concatenate([given_ref[:, i, :] for i in range(2 * planes)], axis=1)
    both = dot(own_ref[...], wide)
    shrink = 1.0 / gain_ref[0:1, :]
    for j in range(planes):
        at = 2 * j * size
        real = both[:size, at : at + size] - both[size:, at + size : at + 2 * size]
        imag = both[:size, at + size : at + 2 * size] + both[size:, at : at + size]
        ends = dot(jnp.concatenate([real, imag], axis=0), lanes_ref[...])
        field_ref[j] = ends[:size, :size] - ends[size:, size:]
        resid_ref[j] = (ends[size:, :size] + ends[:size, size:]) * shrink


def call(kernel, name, shapes, *args):
    whole = pl.BlockSpec(memory_space=pltpu.VMEM)
    return pl.pallas_call(
        kernel,
        out_shape=[jax.ShapeDtypeStruct(s, jnp.float32) for s in shapes],
        in_specs=[whole] * len(args),
        out_specs=[whole] * len(shapes),
        name=name,
    )(*args)


SIDE = 4
CORES = 2
ORDERS = ((0, 1, 2), (1, 2, 0))


def place_of(device):
    return device // 32, (device // 2) % SIDE, (device // 8) % SIDE, device % CORES


def device_at(x, y, z, core):
    return ((x * SIDE + z) * SIDE + y) * CORES + core


def shift_pairs(axes, hop):
    pairs = []
    for device in range(SIDE**3 * CORES):
        place = list(place_of(device))
        axis = axes[place[3]]
        place[axis] = (place[axis] + hop) % (CORES if axis == 3 else SIDE)
        pairs.append((device, device_at(*place)))
    return pairs


def grid_kernel(dest_ref, place_ref, values_ref, matrix_ref, out_ref, count_ref, list_ref):
    nent, rows, size = values_ref.shape
    nslab = count_ref.shape[0]
    capacity = list_ref.shape[0] // nslab
    x, y, z, core = (place_ref[i] for i in range(4))

    def clear(s, _):
        count_ref[s] = 0
        return 0

    def enter(e, _):
        slab = dest_ref[e]
        taken = count_ref[slab]
        list_ref[slab * capacity + taken] = e
        count_ref[slab] = taken + 1
        return 0

    lax.fori_loop(0, nslab, clear, 0)
    lax.fori_loop(0, nent, enter, 0)
    for zr in range(SIDE):
        for yr in range(SIDE):
            slab = ((z + zr) % SIDE) * (SIDE * CORES) + ((y + yr) % SIDE) * CORES + core
            taken = count_ref[slab]
            values, matrices = [], []
            for m in range(capacity):
                entry = jnp.where(m < taken, list_ref[slab * capacity + m], 0)
                value = values_ref[entry]
                values.append(jnp.where(m < taken, value, jnp.zeros_like(value)))
                matrices.append(
                    jnp.concatenate(
                        [
                            matrix_ref[entry, :, pl.ds(pl.multiple_of(((x + pr) % SIDE) * size, size), size)]
                            for pr in range(SIDE)
                        ],
                        axis=1,
                    )
                )
            product = lax.dot_general(
                jnp.concatenate(values, 0),
                jnp.concatenate(matrices, 0),
                (((0,), (0,)), ((), ())),
                preferred_element_type=jnp.float32,
            )
            for pr in range(SIDE):
                relative = (pr, yr, zr)
                first, second = (
                    sum(relative[axis] * SIDE ** (2 - i) for i, axis in enumerate(order)) for order in ORDERS
                )
                out_ref[jnp.where(core == 0, first, second)] = product[:, pr * size : (pr + 1) * size]


def grid_blocks(dest, place, values, matrix, nslab):
    whole = pl.BlockSpec(memory_space=pltpu.VMEM)
    scalars = pl.BlockSpec(memory_space=pltpu.SMEM)
    size = values.shape[2]
    nent = values.shape[0]
    capacity = max(2, 2 * nent // nslab)
    return pl.pallas_call(
        grid_kernel,
        out_shape=jax.ShapeDtypeStruct((SIDE**3, size, size), jnp.float32),
        in_specs=[scalars, scalars, whole, whole],
        out_specs=whole,
        scratch_shapes=[pltpu.SMEM((nslab,), jnp.int32), pltpu.SMEM((nslab * capacity,), jnp.int32)],
        name="gridding",
    )(dest, place, values, matrix)


def exchange(parts, axes):
    arrived = [lax.ppermute(parts[r], ALL, shift_pairs(axes, r)) for r in range(1, SIDE)]
    return ((parts[0] + arrived[0]) + arrived[1]) + arrived[2]


def scattered_sum(intensities, gridding, dest_slab, nslab):
    grid_at = lax.axis_index("grid")
    x, z, y, core = lax.axis_index("dp"), grid_at // 8, (grid_at // 2) % SIDE, grid_at % CORES
    dest = dest_slab[:, 0]
    place = lambda c: jnp.stack([x, y, z, c]).astype(jnp.int32)
    away = grid_blocks(dest, place(1 - core), intensities, gridding, nslab)
    arrived = lax.ppermute(away, ALL, shift_pairs((3, 3), 1))
    kept = grid_blocks(dest, place(core), intensities, gridding, nslab)
    quarter = lambda a: a.reshape((SIDE, a.shape[0] // SIDE) + a.shape[1:])
    kept, arrived = quarter(kept), quarter(arrived)
    total = exchange([kept[r] + arrived[r] for r in range(SIDE)], [order[0] for order in ORDERS])
    for stage in (1, 2):
        parts = quarter(total)
        total = exchange([parts[r] for r in range(SIDE)], [order[stage] for order in ORDERS])
    return total.reshape(total.shape[1:])


def body(intensities, gridding, dest_slab, spectral_weights):
    ngrid = lax.axis_size("grid")
    ndp = lax.axis_size("dp")
    size = intensities.shape[2]
    slab_rows = gridding.shape[2]
    planes = slab_rows // size
    count = ngrid * ndp
    table = dft_tables(size, ndp)

    mine = lax.axis_index("dp")
    pieces = [
        lax.dynamic_index_in_dim(spectral_weights[0], (mine + r) % SIDE, 1, keepdims=False) for r in range(SIDE)
    ]
    own = exchange(pieces, (0, 0))
    flip = lambda w: jnp.roll(jnp.flip(w, (0, 1)), (1, 1), (0, 1))
    ky = owner_order(size, ndp)
    holder = np.argsort(ky)
    mirrored = lax.ppermute(flip(own), ALL, [(d, int(holder[(-ky[d]) % size])) for d in range(count)])

    plane = scattered_sum(intensities, gridding, dest_slab, ngrid)

    forward, sym = call(
        plane_kernel, "plane", [(size, 4, size), (size, size)],
        plane, own, mirrored, table["lanes"], table["own_rows"],
    )
    columns = lax.all_to_all(forward, ALL, 0, 0, tiled=True)
    square = (size, size)
    real, imag, scaled, ends, send = call(
        moment_kernel, "moments", [square, square, square, (8, size), square],
        columns, sym, table["own_cols"],
    )
    sums = lax.all_to_all(send.reshape(count, 1, size), ALL, 0, 0, tiled=True).reshape(count, size)
    back, gain = call(
        functools.partial(solve_kernel, scale=1.0 / size**3), "solve", [(2, size, size), (8, size)],
        sums, ends, scaled, real, imag, table["back_rows"],
    )
    spread = jnp.transpose(back.reshape(2, ngrid, planes, size), (1, 2, 0, 3)).reshape(1, ngrid, 2 * planes, size)
    spread = jnp.broadcast_to(spread, (ndp, ngrid, 2 * planes, size)).reshape(count, 2 * planes, size)
    given = lax.all_to_all(spread, ALL, 0, 0, tiled=True)
    return tuple(
        call(
            output_kernel, "planes_back", [(planes, size, size)] * 2,
            given, gain, table["back_own"], table["lanes"],
        )
    )


def solution(mesh):
    return jax.shard_map(
        body,
        mesh=mesh,
        in_specs=(
            P(("dp", "grid"), None, None),
            P(("dp", "grid"), None, None),
            P(("dp", "grid"), None),
            P("dp", None, "grid", None),
        ),
        out_specs=(P("grid", None, None), P("grid", None, None)),
        check_vma=False,
    )
```

```python
import functools

import jax
import jax.numpy as jnp
import numpy as np
from jax import lax
from jax.experimental import pallas as pl
from jax.experimental.pallas import tpu as pltpu
from jax.sharding import PartitionSpec as P


ITERS = 8
MOMENTS = 2 * ITERS + 1
LOW_LANE = 64
ALL = ("dp", "grid")
HIGHEST = lax.Precision.HIGHEST


def two_sum(a, b):
    s = a + b
    v = s - a
    return s, (a - (s - v)) + (b - v)


def quick_sum(a, b):
    s = a + b
    return s, b - (s - a)


def halves(a):
    c = a * 4097.0
    high = c - (c - a)
    return high, a - high


def two_prod(a, b, a_parts=None, b_parts=None):
    p = a * b
    ah, al = a_parts or halves(a)
    bh, bl = b_parts or halves(b)
    return p, ((ah * bh - p) + ah * bl + al * bh) + al * bl


def dd_add(a, b):
    s, e = two_sum(a[0], b[0])
    t, f = two_sum(a[1], b[1])
    s, e = quick_sum(s, e + t)
    return quick_sum(s, e + f)


def dd_mul(a, b):
    p, e = two_prod(a[0], b[0])
    return quick_sum(p, e + (a[0] * b[1] + a[1] * b[0]))


def dd_scale(a, factor):
    return a[0] * factor, a[1] * factor


def dd_neg(a):
    return -a[0], -a[1]


def dd_div(a, b):
    first = a[0] / b[0]
    rest = dd_add(a, dd_neg(dd_mul((first, jnp.zeros_like(first)), b)))
    second = rest[0] / b[0]
    rest = dd_add(rest, dd_neg(dd_mul((second, jnp.zeros_like(second)), b)))
    third = rest[0] / b[0]
    high, low = quick_sum(first, second)
    return quick_sum(high, low + third)


def dot(a, b):
    return jax.lax.dot_general(
        a, b, (((1,), (0,)), ((), ())), precision=HIGHEST, preferred_element_type=jnp.float32
    )


SIDE = 4
CORES = 2
ORDERS = ((0, 1, 2), (1, 2, 0))


def place_of(device):
    chip = device // CORES
    return chip // SIDE**2, chip % SIDE, (chip // SIDE) % SIDE, device % CORES


def chip_at(x, y, z):
    return (x * SIDE + z) * SIDE + y


def shift_pairs(axes, hop):
    pairs = []
    for device in range(SIDE**3 * CORES):
        place = list(place_of(device))
        axis = axes[place[3]]
        place[axis] = (place[axis] + hop) % (CORES if axis == 3 else SIDE)
        pairs.append((device, chip_at(*place[:3]) * CORES + place[3]))
    return pairs


def routes():
    table = np.zeros((SIDE**3 * CORES, CORES, SIDE**3), np.int32)
    for device in range(table.shape[0]):
        place = place_of(device)
        for core in range(CORES):
            for index in range(SIDE**3):
                digits = (index // SIDE**2, (index // SIDE) % SIDE, index % SIDE)
                at = list(place[:3])
                for digit, axis in zip(digits, ORDERS[core]):
                    at[axis] = (at[axis] + digit) % SIDE
                table[device, core, index] = chip_at(*at)
    return table


def held_rows(size):
    chip, core = np.arange(size) // CORES, np.arange(size) % CORES
    return np.where(chip == 0, core * size // 2, np.where(core == 0, chip, size - chip))


def weight_rows(size, ndp):
    d = np.arange(size)
    return ndp * (d % (size // ndp)) + d // (size // ndp)


def dft_tables(size, ndp):
    index = np.arange(size)
    angle = 2.0 * np.pi * ((index[:, None] * index[None, :]) % size) / size
    cos, sin = np.cos(angle), np.sin(angle)
    held = held_rows(size)
    as_f32 = lambda a: np.ascontiguousarray(a, dtype=np.float32)
    half = size // 2
    packed = np.concatenate([cos[:, :half], cos[:, half : half + 1], -sin[:, 1:half]], 1)
    high = packed.astype(jnp.bfloat16)
    low = (packed - high.astype(np.float64)).astype(jnp.bfloat16)
    return dict(
        packed=np.concatenate([high, low], 1),
        lanes=as_f32(np.concatenate([cos, sin], 1)),
        rows=as_f32(np.concatenate([cos, sin], 0)),
        back=as_f32(
            np.concatenate(
                [np.concatenate([cos[held], sin[held]], 1), np.concatenate([-sin[held], cos[held]], 1)], 0
            )
        ),
        held=as_f32(held[:, None] == index[None, :]),
        weight=as_f32(weight_rows(size, ndp)[:, None] == index[None, :]),
        mirror=as_f32(((index[:, None] + index[None, :]) % size) == 0),
    )


def dot_as(a, b, left, right):
    return lax.dot_general(
        a, b, (((left,), (right,)), ((), ())), precision=HIGHEST, preferred_element_type=jnp.float32
    )


def grid_kernel(*refs, core_flip, first):
    if first:
        dest_ref, route_ref, values_ref, matrix_ref, packed_ref, out_ref, wave_ref = refs[:7]
        outs, others = None, None
    else:
        dest_ref, route_ref, wave_ref, matrix_ref, other_ref = refs[:5]
        outs = refs[5:9]
    count_ref, list_ref, stage_ref = refs[-3:]
    nent, rows = matrix_ref.shape[:2]
    size = stage_ref.shape[1]
    half = size // 2
    nslab = count_ref.shape[0]
    capacity = list_ref.shape[0] // nslab
    core = route_ref[CORES * half]
    core = 1 - core if core_flip else core

    def clear(s, _):
        count_ref[s] = 0
        return 0

    def enter(e, _):
        slab = dest_ref[e]
        taken = count_ref[slab]
        list_ref[slab * capacity + taken] = e
        count_ref[slab] = taken + 1
        return 0

    lax.fori_loop(0, nslab, clear, 0)
    lax.fori_loop(0, nent, enter, 0)
    if first:
        both = jnp.dot(values_ref[...].reshape(nent * rows, size), packed_ref[...], preferred_element_type=jnp.float32)
        wave = both[:, :size] + both[:, size:]
        high = wave.astype(jnp.bfloat16)
        low = (wave - high.astype(jnp.float32)).astype(jnp.bfloat16)
        for part in range(CORES):
            cut = slice(part * half, (part + 1) * half)
            wave_ref[part] = jnp.concatenate([high[:, cut], low[:, cut]], 1).reshape(nent, rows, size)

    def pair(at, _):
        for near in range(2):
            slab = at * 2 + near
            taken = count_ref[slab]
            waves, matrices = [], []
            for m in range(capacity):
                entry = jnp.where(m < taken, list_ref[slab * capacity + m], 0)
                wave = wave_ref[core, entry]
                waves.append(jnp.where(m < taken, wave, jnp.zeros_like(wave)))
                matrices.append(matrix_ref[entry])
            product = lax.dot_general(
                jnp.concatenate(waves, 0),
                jnp.concatenate(matrices, 0),
                (((0,), (0,)), ((), ())),
                preferred_element_type=jnp.float32,
            )
            product = product[:half] + product[half:]
            for p in range(SIDE):
                stage_ref[(near * SIDE + p) * half : (near * SIDE + p + 1) * half, :] = product[:, p * size : (p + 1) * size]
        place = pl.ds(pl.multiple_of(at * 8, 8), 8)
        for index in range(half):
            chip = route_ref[core * half + index]
            block = stage_ref[pl.ds(chip, 8, stride=half), :]
            if first:
                out_ref[index, place, :] = block
            else:
                outs[index // SIDE**2][index % SIDE**2, place, :] = block + other_ref[index, place, :]
        return 0

    lax.fori_loop(0, nslab // 2, pair, 0)


def grid_call(first, nslab, capacity, *args):
    whole = pl.BlockSpec(memory_space=pltpu.VMEM)
    scalars = pl.BlockSpec(memory_space=pltpu.SMEM)
    nent, rows, size = args[2].shape[-3:]
    if first:
        shapes = [
            jax.ShapeDtypeStruct((SIDE**3, size, size), jnp.float32),
            jax.ShapeDtypeStruct((CORES, nent, rows, size), jnp.bfloat16),
        ]
    else:
        shapes = [jax.ShapeDtypeStruct((SIDE**2, size, size), jnp.float32)] * SIDE
    return pl.pallas_call(
        functools.partial(grid_kernel, core_flip=first, first=first),
        out_shape=shapes,
        in_specs=[scalars, scalars] + [whole] * (len(args) - 2),
        out_specs=[whole] * len(shapes),
        scratch_shapes=[
            pltpu.SMEM((nslab,), jnp.int32),
            pltpu.SMEM((nslab * capacity,), jnp.int32),
            pltpu.VMEM((2 * SIDE * (size // 2), size), jnp.float32),
        ],
        name="gridding_away" if first else "gridding_kept",
    )(*args)


def weight_kernel(w0_ref, w1_ref, w2_ref, w3_ref, held_ref, out_ref):
    size = w0_ref.shape[0]
    own = ((w0_ref[...] + w1_ref[...]) + w2_ref[...]) + w3_ref[...]
    low = jnp.min(jnp.min(own, axis=0, keepdims=True), axis=1, keepdims=True)
    high = jnp.max(jnp.max(own, axis=0, keepdims=True), axis=1, keepdims=True)
    lane = lax.broadcasted_iota(jnp.int32, (size, size), 1)
    out_ref[:, 0, :] = dot_as(held_ref[...], own, 1, 1)
    out_ref[:, 1, :] = jnp.where(lane < size // 2, low, high)


def turn_kernel(given_ref, weight_ref, out_ref):
    out_ref[...] = dot_as(given_ref[:, 0, :], weight_ref[...], 0, 0)


def symmetry_kernel(given_ref, own_ref, other_ref, kind_ref, mirror_ref, scaled_ref, range_ref):
    size = own_ref.shape[0]
    ends = given_ref[:, 1, :]
    low = jnp.min(jnp.min(ends, axis=0, keepdims=True), axis=1, keepdims=True)
    high = jnp.max(jnp.max(ends, axis=0, keepdims=True), axis=1, keepdims=True)
    half = jnp.maximum((high - low) * 0.5, high * 1e-4)
    half = jnp.broadcast_to(half, (1, size))
    range_ref[0:1, :] = half
    range_ref[1:2, :] = jnp.broadcast_to((high + low) * 0.5, (1, size)) / half
    range_ref[2:8, :] = jnp.zeros((6, size), jnp.float32)
    partner = jnp.where(kind_ref[1] == 1, own_ref[...], other_ref[...])
    mirrored = dot(mirror_ref[...], dot(partner, mirror_ref[...]))
    scaled_ref[...] = (own_ref[...] + mirrored) * 0.5 / half


def sublane_total(a):
    for shift in (4, 2, 1):
        a = dd_add(a, (pltpu.roll(a[0], shift, 0), pltpu.roll(a[1], shift, 0)))
    return a


def lane_total(a):
    for shift in (64, 32, 16, 8, 4, 2, 1):
        a = dd_add(a, (pltpu.roll(a[0], shift, 1), pltpu.roll(a[1], shift, 1)))
    return a


def moment_kernel(own_ref, other_ref, kind_ref, scaled_ref, range_ref, lanes_ref, rows_ref, real_ref, imag_ref, send_ref):
    size = own_ref.shape[0]
    centre = range_ref[1:2, :]
    mine, theirs = own_ref[...], other_ref[...]
    second, alone = kind_ref[0] == 1, kind_ref[1] == 1
    re = jnp.where(jnp.logical_and(second, jnp.logical_not(alone)), theirs, mine)
    im = jnp.where(alone, jnp.zeros_like(mine), jnp.where(second, -mine, theirs))
    ends = dot(jnp.concatenate([re, im], 0), lanes_ref[...])
    mid_real = ends[:size, :size] + ends[size:, size:]
    mid_imag = ends[size:, :size] - ends[:size, size:]
    both = dot(rows_ref[...], jnp.concatenate([mid_real, mid_imag], 1))
    real = both[:size, :size] + both[size:, size:]
    imag = both[:size, size:] - both[size:, :size]
    real_ref[...] = real
    imag_ref[...] = imag
    scaled = scaled_ref[...]
    power = real * real + imag * imag
    chunk = 32
    totals = [None] * MOMENTS
    for start in range(0, size, chunk):
        t = scaled[start : start + chunk] - centre
        p = power[start : start + chunk]
        p_parts = halves(p)
        t2 = t * 2.0
        t2_parts = halves(t2)
        zero = jnp.zeros_like(t)
        before, here = (jnp.ones_like(t), zero), (t, zero)
        for order in range(MOMENTS):
            value = before
            v_parts = halves(value[0])
            term, low_term = two_prod(value[0], p, v_parts, p_parts)
            term = (term, low_term + value[1] * p)
            rows = [(term[0][i : i + 8], term[1][i : i + 8]) for i in range(0, chunk, 8)]
            while len(rows) > 1:
                rows = [dd_add(rows[i], rows[i + 1]) for i in range(0, len(rows), 2)]
            totals[order] = rows[0] if totals[order] is None else dd_add(totals[order], rows[0])
            if order + 1 < MOMENTS:
                up, low_up = two_prod(here[0], t2, None, t2_parts)
                up, low_up = quick_sum(up, low_up + here[1] * t2)
                following = dd_add((up, low_up), dd_neg(before))
                before, here = here, following
    row = lax.broadcasted_iota(jnp.int32, (8, size), 0)
    lane = lax.broadcasted_iota(jnp.int32, (8, size), 1)
    out = jnp.zeros((8, size), jnp.float32)
    for base in range(0, MOMENTS, 8):
        high_rows = jnp.zeros((8, size), jnp.float32)
        low_rows = jnp.zeros((8, size), jnp.float32)
        for order in range(base, min(base + 8, MOMENTS)):
            total = sublane_total(totals[order])
            high_rows = jnp.where(row == order - base, total[0], high_rows)
            low_rows = jnp.where(row == order - base, total[1], low_rows)
        high_rows, low_rows = lane_total((high_rows, low_rows))
        out = jnp.where(lane == row + base, high_rows, out)
        out = jnp.where(lane == row + (base + LOW_LANE), low_rows, out)
    line = jnp.sum(out, axis=0, keepdims=True)
    send_ref[...] = jnp.broadcast_to(line, (size, size))


def lane_of(a, lane):
    pick = lambda v: jnp.broadcast_to(v[:, lane : lane + 1], v.shape)
    return pick(a[0]), pick(a[1])


def solve_kernel(
    sums_ref, range_ref, scaled_ref, real_ref, imag_ref, lanes_ref, rows_ref, out_ref, gain_ref, *, scale
):
    size = scaled_ref.shape[0]
    given = sums_ref[...]
    low = pltpu.roll(given, size - LOW_LANE, 1)
    rows = [(given[i : i + 8], low[i : i + 8]) for i in range(0, given.shape[0], 8)]
    while len(rows) > 1:
        rows = [dd_add(rows[i], rows[i + 1]) for i in range(0, len(rows), 2)]
    moments = sublane_total(rows[0])
    half = range_ref[0:1, :]
    centre = jnp.broadcast_to(range_ref[1:2, :], moments[0].shape)
    centre = (centre, jnp.zeros_like(centre))
    lane = lax.broadcasted_iota(jnp.int32, moments[0].shape, 1)
    resid, direct = moments, moments
    steps, turns = [], []
    decay = jnp.ones((1, size), jnp.float32)
    for k in range(ITERS):
        after = tuple(pltpu.roll(v, size - 1, 1) for v in direct)
        prior = tuple(pltpu.roll(v, 1, 1) for v in direct)
        prior = tuple(jnp.where(lane == 0, a, p) for a, p in zip(after, prior))
        image = dd_add(dd_mul(direct, centre), dd_scale(dd_add(after, prior), 0.5))
        alpha = dd_div(lane_of(resid, k), lane_of(image, k))
        fresh = dd_add(resid, dd_neg(dd_mul(alpha, image)))
        beta = dd_mul(alpha, dd_div(lane_of(fresh, k + 1), lane_of(resid, k)))
        beta = dd_scale(beta, -1.0 if k == 0 else -0.5)
        direct = dd_add(fresh, dd_mul(beta, direct))
        resid = fresh
        steps.append(alpha[0][0:1])
        turns.append(beta[0][0:1])
        decay = decay * beta[0][0:1]
    gain = lax.rsqrt(jnp.maximum(jnp.abs(decay), 1e-30)) / centre[0][0:1]
    gain_ref[...] = jnp.broadcast_to(gain, gain_ref.shape)
    scaled = scaled_ref[...]
    field = steps[0]
    solved = jnp.broadcast_to(field, scaled.shape)
    left = 1.0 - field * scaled
    toward = left + turns[0]
    for k in range(1, ITERS):
        solved = solved + steps[k] * toward
        left = left - steps[k] * (scaled * toward)
        if k + 1 < ITERS:
            toward = left + turns[k] * toward
    solved = solved * (scale / half)
    left = left * (gain * scale)
    real, imag = real_ref[...], imag_ref[...]
    back_real = solved * real - left * imag
    back_imag = solved * imag + left * real
    ends = dot(jnp.concatenate([back_real, back_imag], 0), lanes_ref[...])
    mid_real = ends[:size, :size] - ends[size:, size:]
    mid_imag = ends[size:, :size] + ends[:size, size:]
    both = dot(rows_ref[...], jnp.concatenate([mid_real, mid_imag], 1))
    real = both[:size, :size] - both[size:, size:]
    imag = both[:size, size:] + both[size:, :size]
    for copy in range(out_ref.shape[0] // (2 * size)):
        out_ref[pl.ds(copy * 2 * size, size, stride=2), :] = real
        out_ref[pl.ds(copy * 2 * size + 1, size, stride=2), :] = imag


def output_kernel(given_ref, gain_ref, back_ref, field_ref, resid_ref):
    planes, size = field_ref.shape[0], field_ref.shape[1]
    step = 2 * planes
    shrink = 1.0 / gain_ref[0:1, :]
    for j in range(planes):
        pieces = [given_ref[pl.ds(2 * j + part, size, stride=step), :] for part in range(2)]
        both = dot_as(jnp.concatenate(pieces, 0), back_ref[...], 0, 0)
        field_ref[j] = both[:, :size]
        resid_ref[j] = both[:, size:] * shrink


def call(kernel, name, shapes, *args):
    whole = pl.BlockSpec(memory_space=pltpu.VMEM)
    scalars = pl.BlockSpec(memory_space=pltpu.SMEM)
    return pl.pallas_call(
        kernel,
        out_shape=[jax.ShapeDtypeStruct(s, jnp.float32) for s in shapes],
        in_specs=[scalars if a.dtype == jnp.int32 else whole for a in args],
        out_specs=[whole] * len(shapes),
        name=name,
    )(*args)


def exchange(parts, axes):
    return [parts[0]] + [lax.ppermute(parts[r], ALL, shift_pairs(axes, r)) for r in range(1, SIDE)]


def summed(parts):
    return ((parts[0] + parts[1]) + parts[2]) + parts[3]


def body(intensities, gridding, dest_slab, spectral_weights):
    ngrid = lax.axis_size("grid")
    ndp = lax.axis_size("dp")
    nent, rows, size = intensities.shape
    planes = gridding.shape[2] // size
    count = ngrid * ndp
    capacity = max(2, 2 * nent // ngrid)
    table = dft_tables(size, ndp)
    square = (size, size)
    swap = lambda a: lax.ppermute(a, ALL, shift_pairs((3, 3), 1))

    device = lax.axis_index("dp") * ngrid + lax.axis_index("grid")
    kinds = np.stack([np.arange(count) % CORES, np.arange(count) < CORES], 1).astype(np.int32)
    known = np.concatenate([routes().reshape(count, -1), kinds], 1)
    route = lax.dynamic_index_in_dim(jnp.asarray(known), device, 0, keepdims=False)
    kind = route[-2:]

    dest = dest_slab[:, 0]
    away, wave = grid_call(True, ngrid, capacity, dest, route, intensities, gridding, table["packed"])
    arrived = swap(away)
    together = lax.optimization_barrier
    _, grouped = together((away, spectral_weights))
    mine = lax.axis_index("dp")
    weights = exchange(
        [lax.dynamic_index_in_dim(grouped[0], (mine + r) % SIDE, 1, keepdims=False) for r in range(SIDE)],
        (0, 0),
    )
    (turned,) = call(weight_kernel, "weights", [(size, 2, size)], *weights, table["held"])
    arrived, turned = together((arrived, turned))
    parts = grid_call(False, ngrid, capacity, dest, route, wave, gridding, arrived)

    quarter = lambda a: [p.reshape(p.shape[1:]) for p in jnp.split(a.reshape((SIDE, -1) + a.shape[1:]), SIDE)]
    parts, turned = together((list(parts), turned))
    parts = exchange(parts, [order[0] for order in ORDERS])
    given = lax.all_to_all(turned, ALL, 0, 0, tiled=True)
    (own_weight,) = call(turn_kernel, "weights_turned", [square], given, table["weight"])
    scaled, ends = call(
        symmetry_kernel, "symmetry", [square, (8, size)],
        given, own_weight, swap(own_weight), kind, table["mirror"],
    )
    parts, scaled, ends = together((parts, scaled, ends))
    for stage in (1, 2):
        parts = exchange(quarter(summed(parts)), [order[stage] for order in ORDERS])
    own = summed(parts).reshape(square)
    real, imag, send = call(
        moment_kernel, "moments", [square, square, square],
        own, swap(own), kind, scaled, ends, table["lanes"], table["rows"],
    )
    sums = lax.all_to_all(send.reshape(count, 1, size), ALL, 0, 0, tiled=True).reshape(count, size)
    back, gain = call(
        functools.partial(solve_kernel, scale=1.0 / size**3), "solve", [(ndp * 2 * size, size), (8, size)],
        sums, ends, scaled, real, imag, table["lanes"], table["rows"],
    )
    landed = lax.all_to_all(back.reshape(count, 2 * planes, size), ALL, 0, 0, tiled=True)
    return tuple(
        call(
            output_kernel, "planes_back", [(planes, size, size)] * 2,
            landed.reshape(count * 2 * planes, size), gain, table["back"],
        )
    )


def solution(mesh):
    return jax.shard_map(
        body,
        mesh=mesh,
        in_specs=(
            P(("dp", "grid"), None, None),
            P(("dp", "grid"), None, None),
            P(("dp", "grid"), None),
            P("dp", None, "grid", None),
        ),
        out_specs=(P("grid", None, None), P("grid", None, None)),
        check_vma=False,
    )
```

```python
import functools

import jax
import jax.numpy as jnp
import numpy as np
from jax import lax
from jax.experimental import pallas as pl
from jax.experimental.pallas import tpu as pltpu
from jax.sharding import PartitionSpec as P


ITERS = 8
MOMENTS = 2 * ITERS + 1
LOW_LANE = 64
ALL = ("dp", "grid")
HIGHEST = lax.Precision.HIGHEST


def two_sum(a, b):
    s = a + b
    v = s - a
    return s, (a - (s - v)) + (b - v)


def quick_sum(a, b):
    s = a + b
    return s, b - (s - a)


def halves(a):
    c = a * 4097.0
    high = c - (c - a)
    return high, a - high


def two_prod(a, b, a_parts=None, b_parts=None):
    p = a * b
    ah, al = a_parts or halves(a)
    bh, bl = b_parts or halves(b)
    return p, ((ah * bh - p) + ah * bl + al * bh) + al * bl


def dd_add(a, b):
    s, e = two_sum(a[0], b[0])
    t, f = two_sum(a[1], b[1])
    s, e = quick_sum(s, e + t)
    return quick_sum(s, e + f)


def dd_mul(a, b):
    p, e = two_prod(a[0], b[0])
    return quick_sum(p, e + (a[0] * b[1] + a[1] * b[0]))


def dd_times(a, b):
    p, e = two_prod(a[0], b)
    return quick_sum(p, e + a[1] * b)


def dd_scale(a, factor):
    return a[0] * factor, a[1] * factor


def dd_neg(a):
    return -a[0], -a[1]


def dd_div(a, b):
    inverse = 1.0 / b[0]
    first = a[0] * inverse
    rest = dd_add(a, dd_neg(dd_times(b, first)))
    second = rest[0] * inverse
    rest = dd_add(rest, dd_neg(dd_times(b, second)))
    high, low = quick_sum(first, second)
    return quick_sum(high, low + rest[0] * inverse)


def dot(a, b):
    return jax.lax.dot_general(
        a, b, (((1,), (0,)), ((), ())), precision=HIGHEST, preferred_element_type=jnp.float32
    )


SIDE = 4
CORES = 2
ORDERS = ((0, 1, 2), (1, 2, 0))


def place_of(device):
    chip = device // CORES
    return chip // SIDE**2, chip % SIDE, (chip // SIDE) % SIDE, device % CORES


def chip_at(x, y, z):
    return (x * SIDE + z) * SIDE + y


def shift_pairs(axes, hop):
    pairs = []
    for device in range(SIDE**3 * CORES):
        place = list(place_of(device))
        axis = axes[place[3]]
        place[axis] = (place[axis] + hop) % (CORES if axis == 3 else SIDE)
        pairs.append((device, chip_at(*place[:3]) * CORES + place[3]))
    return pairs


def routes():
    table = np.zeros((SIDE**3 * CORES, CORES, SIDE**3), np.int32)
    for device in range(table.shape[0]):
        place = place_of(device)
        for core in range(CORES):
            for index in range(SIDE**3):
                digits = (index // SIDE**2, (index // SIDE) % SIDE, index % SIDE)
                at = list(place[:3])
                for digit, axis in zip(digits, ORDERS[core]):
                    at[axis] = (at[axis] + digit) % SIDE
                table[device, core, index] = chip_at(*at)
    return table


def held_rows(size):
    chip, core = np.arange(size) // CORES, np.arange(size) % CORES
    return np.where(chip == 0, core * size // 2, np.where(core == 0, chip, size - chip))


def weight_rows(size, ndp):
    d = np.arange(size)
    return ndp * (d % (size // ndp)) + d // (size // ndp)


def dft_tables(size, ndp):
    index = np.arange(size)
    angle = 2.0 * np.pi * ((index[:, None] * index[None, :]) % size) / size
    cos, sin = np.cos(angle), np.sin(angle)
    held = held_rows(size)
    as_f32 = lambda a: np.ascontiguousarray(a, dtype=np.float32)
    half = size // 2
    packed = np.concatenate([cos[:, :half], cos[:, half : half + 1], -sin[:, 1:half]], 1)
    high = packed.astype(jnp.bfloat16)
    low = (packed - high.astype(np.float64)).astype(jnp.bfloat16)
    return dict(
        packed=np.stack([np.concatenate([p[:, :half], q[:, :half]], 1) for p, q in ((high, low), (high[:, half:], low[:, half:]))]),
        lanes=as_f32(np.concatenate([cos, sin], 1)),
        rows=as_f32(np.concatenate([cos, sin], 0)),
        back=as_f32(
            np.concatenate(
                [np.concatenate([cos[held], sin[held]], 1), np.concatenate([-sin[held], cos[held]], 1)], 0
            )
        ),
        held=as_f32(held[:, None] == index[None, :]),
        weight=as_f32(weight_rows(size, ndp)[:, None] == index[None, :]),
        mirror=as_f32(((index[:, None] + index[None, :]) % size) == 0),
    )


def dot_as(a, b, left, right):
    return lax.dot_general(
        a, b, (((left,), (right,)), ((), ())), precision=HIGHEST, preferred_element_type=jnp.float32
    )


STEPS = 4


def sublane_turn(tiles):
    row = lax.broadcasted_iota(jnp.int32, tiles[0].shape, 0)
    for bit in (4, 2, 1):
        low = (row & bit) == 0
        turned = list(tiles)
        for i in range(8):
            if i & bit == 0:
                a, b = tiles[i], tiles[i + bit]
                turned[i] = jnp.where(low, a, pltpu.roll(b, bit, 0))
                turned[i + bit] = jnp.where(low, pltpu.roll(a, 8 - bit, 0), b)
        tiles = turned
    return tiles


def grid_kernel(*refs, first):
    if first:
        dest_ref, kind_ref, values_ref, matrix_ref, packed_ref, route_ref, out_ref, wave_ref = refs[:8]
    else:
        dest_ref, kind_ref, wave_ref, matrix_ref, other_ref = refs[:5]
        outs = refs[5:9]
    count_ref, list_ref = refs[-2:]
    nent, rows, width = matrix_ref.shape
    size = width // SIDE
    half = size // 2
    nslab = count_ref.shape[0]
    capacity = list_ref.shape[0] // nslab
    core = 1 - kind_ref[0] if first else kind_ref[0]
    step = pl.program_id(0)

    def clear(s, _):
        count_ref[s] = 0
        return 0

    def enter(e, _):
        slab = dest_ref[e]
        taken = count_ref[slab]
        list_ref[slab * capacity + taken] = e
        count_ref[slab] = taken + 1
        return 0

    @pl.when(step == 0)
    def _():
        lax.fori_loop(0, nslab, clear, 0)
        lax.fori_loop(0, nent, enter, 0)
        if first:
            values = values_ref[...].reshape(nent * rows, size)
            chip = lax.broadcasted_iota(jnp.int32, (half, half), 0)
            for part in range(CORES):
                pick = (chip == route_ref[part : part + 1, :]).astype(jnp.float32).astype(jnp.bfloat16)
                turn = lambda at: jnp.dot(packed_ref[part, :, at : at + half], pick, preferred_element_type=jnp.float32)
                slots = jnp.concatenate([turn(0), turn(half)], 1).astype(jnp.bfloat16)
                both = jnp.dot(values, slots, preferred_element_type=jnp.float32)
                wave = both[:, :half] + both[:, half:]
                high = wave.astype(jnp.bfloat16)
                low = (wave - high.astype(jnp.float32)).astype(jnp.bfloat16)
                wave_ref[part] = jnp.concatenate([high, low], 1).reshape(nent, rows, size)

    for pair in range(nslab // (2 * STEPS)):
        products = []
        for near in range(2):
            slab = (step * (nslab // (2 * STEPS)) + pair) * 2 + near
            taken = count_ref[slab]
            waves, matrices = [], []
            for m in range(capacity):
                entry = jnp.where(m < taken, list_ref[slab * capacity + m], 0)
                wave = wave_ref[core, entry]
                waves.append(jnp.where(m < taken, wave, jnp.zeros_like(wave)))
                matrices.append(matrix_ref[entry])
            product = lax.dot_general(
                jnp.concatenate(waves, 0),
                jnp.concatenate(matrices, 0),
                (((0,), (0,)), ((), ())),
                preferred_element_type=jnp.float32,
            )
            products.append(product[:half] + product[half:])
        place = slice(pair * 8, pair * 8 + 8)
        for start in range(0, half, 8):
            tiles = [
                product[start : start + 8, p * size : (p + 1) * size] for product in products for p in range(SIDE)
            ]
            for index, block in enumerate(sublane_turn(tiles), start):
                if first:
                    out_ref[index, place, :] = block
                else:
                    outs[index // SIDE**2][index % SIDE**2, place, :] = block + other_ref[index, place, :]


def grid_call(first, nslab, capacity, *args):
    nent, rows, size = args[2].shape[-3:]
    scalars = pl.BlockSpec(memory_space=pltpu.SMEM)
    fixed = lambda shape: pl.BlockSpec(shape, lambda i: (0,) * len(shape))
    moving = lambda count: pl.BlockSpec((count, size // STEPS, size), lambda i: (0, i, 0))
    blocks, wave = SIDE**3, (CORES, nent, rows, size)
    if first:
        out_shape = [jax.ShapeDtypeStruct((blocks, size, size), jnp.float32), jax.ShapeDtypeStruct(wave, jnp.bfloat16)]
        out_specs = [moving(blocks), fixed(wave)]
    else:
        out_shape = [jax.ShapeDtypeStruct((SIDE**2, size, size), jnp.float32)] * SIDE
        out_specs = [moving(SIDE**2)] * SIDE
    in_specs = [scalars, scalars] + [fixed(a.shape) for a in args[2:4]]
    in_specs += [fixed(a.shape) for a in args[4:]] if first else [moving(blocks)]
    return pl.pallas_call(
        functools.partial(grid_kernel, first=first),
        grid=(STEPS,),
        out_shape=out_shape,
        in_specs=in_specs,
        out_specs=out_specs,
        scratch_shapes=[pltpu.SMEM((nslab,), jnp.int32), pltpu.SMEM((nslab * capacity,), jnp.int32)],
        name="gridding_away" if first else "gridding_kept",
    )(*args)


def weight_kernel(w0_ref, w1_ref, w2_ref, w3_ref, held_ref, out_ref):
    size = w0_ref.shape[0]
    own = ((w0_ref[...] + w1_ref[...]) + w2_ref[...]) + w3_ref[...]
    low = jnp.min(jnp.min(own, axis=0, keepdims=True), axis=1, keepdims=True)
    high = jnp.max(jnp.max(own, axis=0, keepdims=True), axis=1, keepdims=True)
    lane = lax.broadcasted_iota(jnp.int32, (size, size), 1)
    out_ref[:, 0, :] = dot_as(held_ref[...], own, 1, 1)
    out_ref[:, 1, :] = jnp.where(lane < size // 2, low, high)


def turn_kernel(given_ref, weight_ref, out_ref):
    out_ref[...] = dot_as(given_ref[:, 0, :], weight_ref[...], 0, 0)


def symmetry_kernel(given_ref, own_ref, other_ref, kind_ref, mirror_ref, scaled_ref, range_ref):
    size = own_ref.shape[0]
    ends = given_ref[:, 1, :]
    low = jnp.min(jnp.min(ends, axis=0, keepdims=True), axis=1, keepdims=True)
    high = jnp.max(jnp.max(ends, axis=0, keepdims=True), axis=1, keepdims=True)
    half = jnp.maximum((high - low) * 0.5, high * 1e-4)
    half = jnp.broadcast_to(half, (1, size))
    range_ref[0:1, :] = half
    range_ref[1:2, :] = jnp.broadcast_to((high + low) * 0.5, (1, size)) / half
    range_ref[2:8, :] = jnp.zeros((6, size), jnp.float32)
    partner = jnp.where(kind_ref[1] == 1, own_ref[...], other_ref[...])
    mirrored = dot(mirror_ref[...], dot(partner, mirror_ref[...]))
    scaled_ref[...] = (own_ref[...] + mirrored) * 0.5 / half


def sublane_total(a):
    for shift in (4, 2, 1):
        a = dd_add(a, (pltpu.roll(a[0], shift, 0), pltpu.roll(a[1], shift, 0)))
    return a


def lane_total(a):
    for shift in (64, 32, 16, 8, 4, 2, 1):
        a = dd_add(a, (pltpu.roll(a[0], shift, 1), pltpu.roll(a[1], shift, 1)))
    return a


def moment_kernel(own_ref, other_ref, kind_ref, scaled_ref, range_ref, lanes_ref, rows_ref, real_ref, imag_ref, send_ref):
    size = own_ref.shape[0]
    centre = range_ref[1:2, :]
    mine, theirs = own_ref[...], other_ref[...]
    second, alone = kind_ref[0] == 1, kind_ref[1] == 1
    re = jnp.where(jnp.logical_and(second, jnp.logical_not(alone)), theirs, mine)
    im = jnp.where(alone, jnp.zeros_like(mine), jnp.where(second, -mine, theirs))
    ends = dot(jnp.concatenate([re, im], 0), lanes_ref[...])
    mid_real = ends[:size, :size] + ends[size:, size:]
    mid_imag = ends[size:, :size] - ends[:size, size:]
    both = dot(rows_ref[...], jnp.concatenate([mid_real, mid_imag], 1))
    real = both[:size, :size] + both[size:, size:]
    imag = both[:size, size:] - both[size:, :size]
    real_ref[...] = real
    imag_ref[...] = imag
    scaled = scaled_ref[...]
    kx = lax.broadcasted_iota(jnp.int32, (size // 2 + 8, size), 0)
    share = jnp.where(jnp.logical_or(kx == 0, kx == size // 2), 1.0, jnp.where(kx < size // 2, 2.0, 0.0))
    top = slice(0, size // 2 + 8)
    power = (real[top] * real[top] + imag[top] * imag[top]) * share
    chunk = 24
    totals = [None] * MOMENTS
    for start in range(0, size // 2 + 8, chunk):
        t = scaled[start : start + chunk] - centre
        p = power[start : start + chunk]
        p_parts = halves(p)
        t2 = t * 2.0
        t2_parts = halves(t2)
        zero = jnp.zeros_like(t)
        before, here = (jnp.ones_like(t), zero), (t, zero)
        for order in range(MOMENTS):
            value = before
            v_parts = halves(value[0])
            term, low_term = two_prod(value[0], p, v_parts, p_parts)
            term = (term, low_term + value[1] * p)
            rows = [(term[0][i : i + 8], term[1][i : i + 8]) for i in range(0, chunk, 8)]
            rows = [dd_add(dd_add(rows[0], rows[1]), rows[2])]
            totals[order] = rows[0] if totals[order] is None else dd_add(totals[order], rows[0])
            if order + 1 < MOMENTS:
                up, low_up = two_prod(here[0], t2, None, t2_parts)
                up, low_up = quick_sum(up, low_up + here[1] * t2)
                following = dd_add((up, low_up), dd_neg(before))
                before, here = here, following
    row = lax.broadcasted_iota(jnp.int32, (8, size), 0)
    lane = lax.broadcasted_iota(jnp.int32, (8, size), 1)
    out = jnp.zeros((8, size), jnp.float32)
    for base in range(0, MOMENTS, 8):
        high_rows = jnp.zeros((8, size), jnp.float32)
        low_rows = jnp.zeros((8, size), jnp.float32)
        for order in range(base, min(base + 8, MOMENTS)):
            total = sublane_total(totals[order])
            high_rows = jnp.where(row == order - base, total[0], high_rows)
            low_rows = jnp.where(row == order - base, total[1], low_rows)
        high_rows, low_rows = lane_total((high_rows, low_rows))
        out = jnp.where(lane == row + base, high_rows, out)
        out = jnp.where(lane == row + (base + LOW_LANE), low_rows, out)
    line = jnp.sum(out, axis=0, keepdims=True)
    send_ref[...] = jnp.broadcast_to(line, (size, size))


def lane_of(a, lane):
    pick = lambda v: jnp.broadcast_to(v[:, lane : lane + 1], v.shape)
    return pick(a[0]), pick(a[1])


def solve_kernel(
    sums_ref, range_ref, scaled_ref, real_ref, imag_ref, lanes_ref, rows_ref, out_ref, gain_ref, *, scale
):
    size = scaled_ref.shape[0]
    given = sums_ref[...]
    low = pltpu.roll(given, size - LOW_LANE, 1)
    rows = [(given[i : i + 8], low[i : i + 8]) for i in range(0, given.shape[0], 8)]
    while len(rows) > 1:
        rows = [dd_add(rows[i], rows[i + 1]) for i in range(0, len(rows), 2)]
    moments = sublane_total(rows[0])
    half = range_ref[0:1, :]
    centre = jnp.broadcast_to(range_ref[1:2, :], moments[0].shape)
    centre = (centre, jnp.zeros_like(centre))
    lane = lax.broadcasted_iota(jnp.int32, moments[0].shape, 1)
    resid, direct = moments, moments
    held = lane_of(resid, 0)
    steps, turns = [], []
    decay = jnp.ones((1, size), jnp.float32)
    for k in range(ITERS):
        after = tuple(pltpu.roll(v, size - 1, 1) for v in direct)
        prior = tuple(pltpu.roll(v, 1, 1) for v in direct)
        prior = tuple(jnp.where(lane == 0, a, p) for a, p in zip(after, prior))
        image = dd_add(dd_mul(direct, centre), dd_scale(dd_add(after, prior), 0.5))
        alpha = dd_div(held, lane_of(image, k))
        fresh = dd_add(resid, dd_neg(dd_mul(alpha, image)))
        reached = lane_of(fresh, k + 1)
        beta = dd_mul(alpha, dd_div(reached, held))
        held = reached
        beta = dd_scale(beta, -1.0 if k == 0 else -0.5)
        direct = dd_add(fresh, dd_mul(beta, direct))
        resid = fresh
        steps.append(alpha[0][0:1])
        turns.append(beta[0][0:1])
        decay = decay * beta[0][0:1]
    gain = lax.rsqrt(jnp.maximum(jnp.abs(decay), 1e-30)) / centre[0][0:1]
    gain_ref[...] = jnp.broadcast_to(gain, gain_ref.shape)
    scaled = scaled_ref[...]
    field = steps[0]
    solved = jnp.broadcast_to(field, scaled.shape)
    left = 1.0 - field * scaled
    toward = left + turns[0]
    for k in range(1, ITERS):
        solved = solved + steps[k] * toward
        left = left - steps[k] * (scaled * toward)
        if k + 1 < ITERS:
            toward = left + turns[k] * toward
    solved = solved * (scale / half)
    left = left * (gain * scale)
    real, imag = real_ref[...], imag_ref[...]
    back_real = solved * real - left * imag
    back_imag = solved * imag + left * real
    ends = dot(jnp.concatenate([back_real, back_imag], 0), lanes_ref[...])
    mid_real = ends[:size, :size] - ends[size:, size:]
    mid_imag = ends[size:, :size] + ends[:size, size:]
    both = dot(rows_ref[...], jnp.concatenate([mid_real, mid_imag], 1))
    real = both[:size, :size] - both[size:, size:]
    imag = both[:size, size:] + both[size:, :size]
    for copy in range(out_ref.shape[0] // (2 * size)):
        out_ref[pl.ds(copy * 2 * size, size, stride=2), :] = real
        out_ref[pl.ds(copy * 2 * size + 1, size, stride=2), :] = imag


def output_kernel(given_ref, gain_ref, back_ref, field_ref, resid_ref):
    planes, size = field_ref.shape[0], field_ref.shape[1]
    step = 2 * planes
    shrink = 1.0 / gain_ref[0:1, :]
    for j in range(planes):
        pieces = [given_ref[pl.ds(2 * j + part, size, stride=step), :] for part in range(2)]
        both = dot_as(jnp.concatenate(pieces, 0), back_ref[...], 0, 0)
        field_ref[j] = both[:, :size]
        resid_ref[j] = both[:, size:] * shrink


def call(kernel, name, shapes, *args):
    whole = pl.BlockSpec(memory_space=pltpu.VMEM)
    scalars = pl.BlockSpec(memory_space=pltpu.SMEM)
    return pl.pallas_call(
        kernel,
        out_shape=[jax.ShapeDtypeStruct(s, jnp.float32) for s in shapes],
        in_specs=[scalars if a.dtype == jnp.int32 else whole for a in args],
        out_specs=[whole] * len(shapes),
        name=name,
    )(*args)


def exchange(parts, axes):
    return [parts[0]] + [lax.ppermute(parts[r], ALL, shift_pairs(axes, r)) for r in range(1, SIDE)]


def summed(parts):
    return ((parts[0] + parts[1]) + parts[2]) + parts[3]


def body(intensities, gridding, dest_slab, spectral_weights):
    ngrid = lax.axis_size("grid")
    ndp = lax.axis_size("dp")
    nent, rows, size = intensities.shape
    planes = gridding.shape[2] // size
    count = ngrid * ndp
    capacity = max(2, 2 * nent // ngrid)
    table = dft_tables(size, ndp)
    square = (size, size)
    swap = lambda a: lax.ppermute(a, ALL, shift_pairs((3, 3), 1))

    device = lax.axis_index("dp") * ngrid + lax.axis_index("grid")
    number = jnp.arange(1, dtype=jnp.int32) + device
    kind = jnp.concatenate([number % CORES, (number < CORES).astype(jnp.int32)])
    route = lax.dynamic_index_in_dim(jnp.asarray(routes()), device, 0, keepdims=False)

    dest = dest_slab[:, 0]
    away, wave = grid_call(True, ngrid, capacity, dest, kind, intensities, gridding, table["packed"], route)
    arrived = swap(away)
    together = lax.optimization_barrier
    _, grouped = together((away, spectral_weights))
    mine = lax.axis_index("dp")
    weights = exchange(
        [lax.dynamic_index_in_dim(grouped[0], (mine + r) % SIDE, 1, keepdims=False) for r in range(SIDE)],
        (0, 0),
    )
    (turned,) = call(weight_kernel, "weights", [(size, 2, size)], *weights, table["held"])
    arrived, turned = together((arrived, turned))
    parts = grid_call(False, ngrid, capacity, dest, kind, wave, gridding, arrived)

    quarter = lambda a: [p.reshape(p.shape[1:]) for p in jnp.split(a.reshape((SIDE, -1) + a.shape[1:]), SIDE)]
    parts, turned = together((list(parts), turned))
    parts = exchange(parts, [order[0] for order in ORDERS])
    given = lax.all_to_all(turned, ALL, 0, 0, tiled=True)
    parts, given = together((parts, given))
    (own_weight,) = call(turn_kernel, "weights_turned", [square], given, table["weight"])
    scaled, ends = call(
        symmetry_kernel, "symmetry", [square, (8, size)],
        given, own_weight, swap(own_weight), kind, table["mirror"],
    )
    for stage in (1, 2):
        parts = exchange(quarter(summed(parts)), [order[stage] for order in ORDERS])
    own = summed(parts).reshape(square)
    real, imag, send = call(
        moment_kernel, "moments", [square, square, square],
        own, swap(own), kind, scaled, ends, table["lanes"], table["rows"],
    )
    sums = lax.all_to_all(send.reshape(count, 1, size), ALL, 0, 0, tiled=True).reshape(count, size)
    back, gain = call(
        functools.partial(solve_kernel, scale=1.0 / size**3), "solve", [(ndp * 2 * size, size), (8, size)],
        sums, ends, scaled, real, imag, table["lanes"], table["rows"],
    )
    landed = lax.all_to_all(back.reshape(count, 2 * planes, size), ALL, 0, 0, tiled=True)
    return tuple(
        call(
            output_kernel, "planes_back", [(planes, size, size)] * 2,
            landed.reshape(count * 2 * planes, size), gain, table["back"],
        )
    )


def solution(mesh):
    return jax.shard_map(
        body,
        mesh=mesh,
        in_specs=(
            P(("dp", "grid"), None, None),
            P(("dp", "grid"), None, None),
            P(("dp", "grid"), None),
            P("dp", None, "grid", None),
        ),
        out_specs=(P("grid", None, None), P("grid", None, None)),
        check_vma=False,
    )
```

```python
import functools

import jax
import jax.numpy as jnp
import numpy as np
from jax import lax
from jax.experimental import pallas as pl
from jax.experimental.pallas import tpu as pltpu
from jax.sharding import PartitionSpec as P


ITERS = 8
MOMENTS = 2 * ITERS + 1
LOW_LANE = 64
ALL = ("dp", "grid")
HIGHEST = lax.Precision.HIGHEST


def two_sum(a, b):
    s = a + b
    v = s - a
    return s, (a - (s - v)) + (b - v)


def quick_sum(a, b):
    s = a + b
    return s, b - (s - a)


def halves(a):
    c = a * 4097.0
    high = c - (c - a)
    return high, a - high


def two_prod(a, b, a_parts=None, b_parts=None):
    p = a * b
    ah, al = a_parts or halves(a)
    bh, bl = b_parts or halves(b)
    return p, ((ah * bh - p) + ah * bl + al * bh) + al * bl


def dd_add(a, b):
    s, e = two_sum(a[0], b[0])
    t, f = two_sum(a[1], b[1])
    s, e = quick_sum(s, e + t)
    return quick_sum(s, e + f)


def dd_mul(a, b):
    p, e = two_prod(a[0], b[0])
    return quick_sum(p, e + (a[0] * b[1] + a[1] * b[0]))


def dd_times(a, b):
    p, e = two_prod(a[0], b)
    return quick_sum(p, e + a[1] * b)


def dd_scale(a, factor):
    return a[0] * factor, a[1] * factor


def dd_neg(a):
    return -a[0], -a[1]


def dd_div(a, b):
    inverse = 1.0 / b[0]
    first = a[0] * inverse
    rest = dd_add(a, dd_neg(dd_times(b, first)))
    second = rest[0] * inverse
    rest = dd_add(rest, dd_neg(dd_times(b, second)))
    high, low = quick_sum(first, second)
    return quick_sum(high, low + rest[0] * inverse)


def dot(a, b):
    return jax.lax.dot_general(
        a, b, (((1,), (0,)), ((), ())), precision=HIGHEST, preferred_element_type=jnp.float32
    )


SIDE = 4
CORES = 2
ORDERS = ((0, 1, 2), (1, 2, 0))


def place_of(device):
    chip = device // CORES
    return chip // SIDE**2, chip % SIDE, (chip // SIDE) % SIDE, device % CORES


def chip_at(x, y, z):
    return (x * SIDE + z) * SIDE + y


def shift_pairs(axes, hop):
    pairs = []
    for device in range(SIDE**3 * CORES):
        place = list(place_of(device))
        axis = axes[place[3]]
        place[axis] = (place[axis] + hop) % (CORES if axis == 3 else SIDE)
        pairs.append((device, chip_at(*place[:3]) * CORES + place[3]))
    return pairs


def held_rows(size):
    chip, core = np.arange(size) // CORES, np.arange(size) % CORES
    return np.where(chip == 0, core * size // 2, np.where(core == 0, chip, size - chip))


def weight_rows(size, ndp):
    d = np.arange(size)
    return ndp * (d % (size // ndp)) + d // (size // ndp)


def dft_tables(size, ndp):
    index = np.arange(size)
    angle = 2.0 * np.pi * ((index[:, None] * index[None, :]) % size) / size
    cos, sin = np.cos(angle), np.sin(angle)
    held, order = held_rows(size), weight_rows(size, ndp)
    as_f32 = lambda a: np.ascontiguousarray(a, dtype=np.float32)
    half = size // 2
    packed = np.concatenate([cos[:, :half], cos[:, half : half + 1], -sin[:, 1:half]], 1)
    high = packed.astype(jnp.bfloat16)
    low = (packed - high.astype(np.float64)).astype(jnp.bfloat16)
    return dict(
        packed=np.stack([np.concatenate([p[:, :half], q[:, :half]], 1) for p, q in ((high, low), (high[:, half:], low[:, half:]))]),
        lanes=as_f32(np.concatenate([cos, sin], 1)),
        ky_rows=as_f32(np.concatenate([cos[order], sin[order]], 0)),
        ky_lanes=as_f32(np.concatenate([cos[order], sin[order]], 1)),
        back=as_f32(
            np.concatenate(
                [np.concatenate([cos[held], sin[held]], 1), np.concatenate([-sin[held], cos[held]], 1)], 0
            )
        ),
        held=as_f32(held[:, None] == index[None, :]),
        mirror=as_f32(((index[:, None] + index[None, :]) % size) == 0),
        ky_mirror=as_f32(((order[:, None] + order[None, :]) % size) == 0),
    )


def dot_as(a, b, left, right):
    return lax.dot_general(
        a, b, (((left,), (right,)), ((), ())), precision=HIGHEST, preferred_element_type=jnp.float32
    )


STEPS = 2
HALVES = 2


def sublane_turn(tiles):
    row = lax.broadcasted_iota(jnp.int32, tiles[0].shape, 0)
    for bit in (4, 2, 1):
        low = (row & bit) == 0
        turned = list(tiles)
        for i in range(8):
            if i & bit == 0:
                a, b = tiles[i], tiles[i + bit]
                turned[i] = jnp.where(low, a, pltpu.roll(b, bit, 0))
                turned[i + bit] = jnp.where(low, pltpu.roll(a, 8 - bit, 0), b)
        tiles = turned
    return tiles


def grid_kernel(*refs, kind, part, capacity):
    first, kept = kind == "first", kind == "kept"
    if first:
        dest_ref, place_ref, values_ref, matrix_ref, packed_ref, weights_ref = refs[:6]
        out_ref, wave_ref, count_ref, list_ref = refs[6:10]
    else:
        count_ref, list_ref, place_ref, wave_ref, matrix_ref = refs[:5]
        other_ref, outs, out_ref = (refs[5], refs[6:], None) if kept else (None, None, refs[5])
    nent, rows, width = matrix_ref.shape
    size = width // SIDE
    half = size // 2
    nslab = count_ref.shape[0]
    core = place_ref[3] if kept else 1 - place_ref[3]
    step = pl.program_id(0)

    def clear(s, _):
        count_ref[s] = 0
        return 0

    def enter(e, _):
        slab = dest_ref[e]
        taken = count_ref[slab]
        list_ref[slab * capacity + taken] = e
        count_ref[slab] = taken + 1
        return 0

    def prepare():
        lax.fori_loop(0, nslab, clear, 0)
        lax.fori_loop(0, nent, enter, 0)
        for r, slice_ref in enumerate(refs[10:]):
            slice_ref[...] = weights_ref[0, :, (place_ref[0] + r) % SIDE, :]
        chip = lax.broadcasted_iota(jnp.int32, (half, half), 0)
        slot = lax.broadcasted_iota(jnp.int32, (half, half), 1)
        digits = (slot // SIDE**2, (slot // SIDE) % SIDE, slot % SIDE)
        pieces = []
        for owner in range(CORES):
            at = [place_ref[0], place_ref[1], place_ref[2]]
            for digit, axis in zip(digits, ORDERS[owner]):
                at[axis] = (at[axis] + digit) % SIDE
            pick = (chip == chip_at(*at)).astype(jnp.float32).astype(jnp.bfloat16)
            for start in (0, half):
                piece = packed_ref[owner, :, start : start + half]
                pieces.append(jnp.dot(piece, pick, preferred_element_type=jnp.float32).astype(jnp.bfloat16))
        both = jnp.dot(
            values_ref[...].reshape(nent * rows, size),
            jnp.concatenate(pieces, 1),
            preferred_element_type=jnp.float32,
        )
        for owner in range(CORES):
            wave = both[:, owner * size : owner * size + half] + both[:, owner * size + half : (owner + 1) * size]
            high = wave.astype(jnp.bfloat16)
            low = (wave - high.astype(jnp.float32)).astype(jnp.bfloat16)
            wave_ref[owner] = jnp.concatenate([high, low], 1).reshape(nent, rows, size)

    if first:
        pl.when(step == 0)(prepare)

    pairs = nslab // (2 * STEPS * HALVES)
    for pair in range(pairs):
        products = []
        for near in range(2):
            slab = part * (nslab // HALVES) + (step * pairs + pair) * 2 + near
            taken = count_ref[slab]
            waves, matrices = [], []
            for m in range(capacity):
                entry = jnp.where(m < taken, list_ref[slab * capacity + m], 0)
                wave = wave_ref[core, entry]
                waves.append(jnp.where(m < taken, wave, jnp.zeros_like(wave)))
                matrices.append(matrix_ref[entry])
            product = lax.dot_general(
                jnp.concatenate(waves, 0),
                jnp.concatenate(matrices, 0),
                (((0,), (0,)), ((), ())),
                preferred_element_type=jnp.float32,
            )
            products.append(product[:half] + product[half:])
        place = slice(pair * 8, pair * 8 + 8)
        for start in range(0, half, 8):
            tiles = [
                product[start : start + 8, p * size : (p + 1) * size] for product in products for p in range(SIDE)
            ]
            for index, block in enumerate(sublane_turn(tiles), start):
                if kept:
                    outs[index // SIDE**2][index % SIDE**2, place, :] = block + other_ref[index, place, :]
                else:
                    out_ref[index, place, :] = block


def grid_call(kind, part, nslab, capacity, *args):
    scalars = pl.BlockSpec(memory_space=pltpu.SMEM)
    fixed = lambda shape: pl.BlockSpec(shape, lambda i: (0,) * len(shape))
    matrix = args[3] if kind == "first" else args[4]
    nent, rows, width = matrix.shape
    size, blocks = width // SIDE, SIDE**3
    moving = lambda count: pl.BlockSpec((count, size // (STEPS * HALVES), size), lambda i: (0, i, 0))
    f32 = lambda *shape: jax.ShapeDtypeStruct(shape, jnp.float32)
    if kind == "kept":
        out_shape, out_specs = [f32(SIDE**2, size // HALVES, size)] * SIDE, [moving(SIDE**2)] * SIDE
    else:
        out_shape, out_specs = [f32(blocks, size // HALVES, size)], [moving(blocks)]
    if kind == "first":
        wave = (CORES, nent, rows, size)
        out_shape += [
            jax.ShapeDtypeStruct(wave, jnp.bfloat16),
            jax.ShapeDtypeStruct((nslab,), jnp.int32),
            jax.ShapeDtypeStruct((nslab * capacity,), jnp.int32),
        ] + [f32(size, size)] * SIDE
        out_specs += [fixed(wave), scalars, scalars] + [fixed((size, size))] * SIDE
    in_specs = [scalars if a.dtype == jnp.int32 else fixed(a.shape) for a in args]
    if kind == "kept":
        in_specs[-1] = moving(blocks)
    return pl.pallas_call(
        functools.partial(grid_kernel, kind=kind, part=part, capacity=capacity),
        grid=(STEPS,),
        out_shape=out_shape,
        in_specs=in_specs,
        out_specs=out_specs,
    )(*args)


def weight_kernel(w0_ref, w1_ref, w2_ref, w3_ref, held_ref, out_ref):
    size = w0_ref.shape[0]
    own = ((w0_ref[...] + w1_ref[...]) + w2_ref[...]) + w3_ref[...]
    low = jnp.min(jnp.min(own, axis=0, keepdims=True), axis=1, keepdims=True)
    high = jnp.max(jnp.max(own, axis=0, keepdims=True), axis=1, keepdims=True)
    lane = lax.broadcasted_iota(jnp.int32, (size, size), 1)
    out_ref[:, 0, :] = dot_as(held_ref[...], own, 1, 1)
    out_ref[:, 1, :] = jnp.where(lane < size // 2, low, high)


def symmetry_kernel(given_ref, other_ref, place_ref, ky_mirror_ref, mirror_ref, scaled_ref, range_ref):
    size = scaled_ref.shape[0]
    ends = given_ref[:, 1, :]
    low = jnp.min(jnp.min(ends, axis=0, keepdims=True), axis=1, keepdims=True)
    high = jnp.max(jnp.max(ends, axis=0, keepdims=True), axis=1, keepdims=True)
    half = jnp.maximum((high - low) * 0.5, high * 1e-4)
    half = jnp.broadcast_to(half, (1, size))
    range_ref[0:1, :] = half
    range_ref[1:2, :] = jnp.broadcast_to((high + low) * 0.5, (1, size)) / half
    range_ref[2:8, :] = jnp.zeros((6, size), jnp.float32)
    own = given_ref[:, 0, :]
    partner = jnp.where(place_ref[4] == 1, own, other_ref[:, 0, :])
    mirrored = dot(ky_mirror_ref[...], dot(partner, mirror_ref[...]))
    scaled_ref[...] = (own + mirrored) * 0.5 / half


def sublane_total(a):
    for shift in (4, 2, 1):
        a = dd_add(a, (pltpu.roll(a[0], shift, 0), pltpu.roll(a[1], shift, 0)))
    return a


def lane_total(a):
    for shift in (64, 32, 16, 8, 4, 2, 1):
        a = dd_add(a, (pltpu.roll(a[0], shift, 1), pltpu.roll(a[1], shift, 1)))
    return a


def moment_kernel(own_ref, other_ref, place_ref, scaled_ref, range_ref, lanes_ref, rows_ref, real_ref, imag_ref, send_ref):
    size = own_ref.shape[0]
    centre = range_ref[1:2, :]
    mine, theirs = own_ref[...], other_ref[...]
    second, alone = place_ref[3] == 1, place_ref[4] == 1
    re = jnp.where(jnp.logical_and(second, jnp.logical_not(alone)), theirs, mine)
    im = jnp.where(alone, jnp.zeros_like(mine), jnp.where(second, -mine, theirs))
    ends = dot_as(jnp.concatenate([re, im], 1), lanes_ref[...], 0, 0)
    mid_real = ends[:size, :size] + ends[size:, size:]
    mid_imag = ends[size:, :size] - ends[:size, size:]
    both = dot(rows_ref[...], jnp.concatenate([mid_real, mid_imag], 1))
    real = both[:size, :size] + both[size:, size:]
    imag = both[:size, size:] - both[size:, :size]
    real_ref[...] = real
    imag_ref[...] = imag
    scaled = scaled_ref[...]
    power = real * real + imag * imag
    chunk = 24
    totals = [None] * MOMENTS
    for start in (0, size // 4, size // 4 + chunk):
        row = lax.broadcasted_iota(jnp.int32, (chunk, size), 0) + start
        if start == 0:
            share = jnp.where(row % (size // 8) == 0, 1.0, jnp.where(row < size // 8, 2.0, 0.0))
        else:
            share = 2.0
        t = scaled[start : start + chunk] - centre
        p = power[start : start + chunk] * share
        p_parts = halves(p)
        t2 = t * 2.0
        t2_parts = halves(t2)
        zero = jnp.zeros_like(t)
        before, here = (jnp.ones_like(t), zero), (t, zero)
        for order in range(MOMENTS):
            value = before
            v_parts = halves(value[0])
            term, low_term = two_prod(value[0], p, v_parts, p_parts)
            term = (term, low_term + value[1] * p)
            rows = [(term[0][i : i + 8], term[1][i : i + 8]) for i in range(0, chunk, 8)]
            rows = [dd_add(dd_add(rows[0], rows[1]), rows[2])]
            totals[order] = rows[0] if totals[order] is None else dd_add(totals[order], rows[0])
            if order + 1 < MOMENTS:
                up, low_up = two_prod(here[0], t2, None, t2_parts)
                up, low_up = quick_sum(up, low_up + here[1] * t2)
                following = dd_add((up, low_up), dd_neg(before))
                before, here = here, following
    row = lax.broadcasted_iota(jnp.int32, (8, size), 0)
    lane = lax.broadcasted_iota(jnp.int32, (8, size), 1)
    out = jnp.zeros((8, size), jnp.float32)
    for base in range(0, MOMENTS, 8):
        high_rows = jnp.zeros((8, size), jnp.float32)
        low_rows = jnp.zeros((8, size), jnp.float32)
        for order in range(base, min(base + 8, MOMENTS)):
            total = sublane_total(totals[order])
            high_rows = jnp.where(row == order - base, total[0], high_rows)
            low_rows = jnp.where(row == order - base, total[1], low_rows)
        high_rows, low_rows = lane_total((high_rows, low_rows))
        out = jnp.where(lane == row + base, high_rows, out)
        out = jnp.where(lane == row + (base + LOW_LANE), low_rows, out)
    line = jnp.sum(out, axis=0, keepdims=True)
    send_ref[...] = jnp.broadcast_to(line, (size, size))


def lane_of(a, lane):
    pick = lambda v: jnp.broadcast_to(v[:, lane : lane + 1], v.shape)
    return pick(a[0]), pick(a[1])


def solve_kernel(
    sums_ref, range_ref, scaled_ref, real_ref, imag_ref, lanes_ref, ky_lanes_ref, out_ref, gain_ref, *, scale
):
    size = scaled_ref.shape[0]
    given = sums_ref[...]
    low = pltpu.roll(given, size - LOW_LANE, 1)
    rows = [(given[i : i + 8], low[i : i + 8]) for i in range(0, given.shape[0], 8)]
    while len(rows) > 1:
        rows = [dd_add(rows[i], rows[i + 1]) for i in range(0, len(rows), 2)]
    moments = sublane_total(rows[0])
    half = range_ref[0:1, :]
    centre = jnp.broadcast_to(range_ref[1:2, :], moments[0].shape)
    centre = (centre, jnp.zeros_like(centre))
    lane = lax.broadcasted_iota(jnp.int32, moments[0].shape, 1)
    resid, direct = moments, moments
    held = lane_of(resid, 0)
    steps, turns = [], []
    decay = jnp.ones((1, size), jnp.float32)
    for k in range(ITERS):
        after = tuple(pltpu.roll(v, size - 1, 1) for v in direct)
        prior = tuple(pltpu.roll(v, 1, 1) for v in direct)
        prior = tuple(jnp.where(lane == 0, a, p) for a, p in zip(after, prior))
        image = dd_add(dd_mul(direct, centre), dd_scale(dd_add(after, prior), 0.5))
        alpha = dd_div(held, lane_of(image, k))
        fresh = dd_add(resid, dd_neg(dd_mul(alpha, image)))
        reached = lane_of(fresh, k + 1)
        beta = dd_mul(alpha, dd_div(reached, held))
        held = reached
        beta = dd_scale(beta, -1.0 if k == 0 else -0.5)
        direct = dd_add(fresh, dd_mul(beta, direct))
        resid = fresh
        steps.append(alpha[0][0:1])
        turns.append(beta[0][0:1])
        decay = decay * beta[0][0:1]
    gain = lax.rsqrt(jnp.maximum(jnp.abs(decay), 1e-30)) / centre[0][0:1]
    gain_ref[...] = jnp.broadcast_to(gain, gain_ref.shape)
    scaled = scaled_ref[...]
    field = steps[0]
    solved = jnp.broadcast_to(field, scaled.shape)
    left = 1.0 - field * scaled
    toward = left + turns[0]
    for k in range(1, ITERS):
        solved = solved + steps[k] * toward
        left = left - steps[k] * (scaled * toward)
        if k + 1 < ITERS:
            toward = left + turns[k] * toward
    solved = solved * (scale / half)
    left = left * (gain * scale)
    real, imag = real_ref[...], imag_ref[...]
    back_real = solved * real - left * imag
    back_imag = solved * imag + left * real
    ends = dot(jnp.concatenate([back_real, back_imag], 0), lanes_ref[...])
    mid_real = ends[:size, :size] - ends[size:, size:]
    mid_imag = ends[size:, :size] + ends[:size, size:]
    ends = dot_as(jnp.concatenate([mid_real, mid_imag], 1), ky_lanes_ref[...], 0, 0)
    real = ends[:size, :size] - ends[size:, size:]
    imag = ends[size:, :size] + ends[:size, size:]
    for copy in range(out_ref.shape[0] // (2 * size)):
        out_ref[pl.ds(copy * 2 * size, size, stride=2), :] = real
        out_ref[pl.ds(copy * 2 * size + 1, size, stride=2), :] = imag


def output_kernel(given_ref, gain_ref, back_ref, field_ref, resid_ref):
    planes, size = field_ref.shape[0], field_ref.shape[1]
    step = 2 * planes
    shrink = 1.0 / gain_ref[0:1, :]
    for j in range(planes):
        pieces = [given_ref[pl.ds(2 * j + part, size, stride=step), :] for part in range(2)]
        both = dot_as(jnp.concatenate(pieces, 0), back_ref[...], 0, 0)
        field_ref[j] = both[:, :size]
        resid_ref[j] = both[:, size:] * shrink


def call(kernel, shapes, *args):
    whole = pl.BlockSpec(memory_space=pltpu.VMEM)
    scalars = pl.BlockSpec(memory_space=pltpu.SMEM)
    return pl.pallas_call(
        kernel,
        out_shape=[jax.ShapeDtypeStruct(s, jnp.float32) for s in shapes],
        in_specs=[scalars if a.dtype == jnp.int32 else whole for a in args],
        out_specs=[whole] * len(shapes),
    )(*args)


def exchange(parts, axes):
    return [parts[0]] + [lax.ppermute(parts[r], ALL, shift_pairs(axes, r)) for r in range(1, SIDE)]


def summed(parts):
    return ((parts[0] + parts[1]) + parts[2]) + parts[3]


def body(intensities, gridding, dest_slab, spectral_weights):
    ngrid = lax.axis_size("grid")
    ndp = lax.axis_size("dp")
    nent, _, size = intensities.shape
    planes = gridding.shape[2] // size
    count = ngrid * ndp
    capacity = max(2, 2 * nent // ngrid)
    table = dft_tables(size, ndp)
    square = (size, size)
    swap = lambda a: lax.ppermute(a, ALL, shift_pairs((3, 3), 1))

    chip = lax.axis_index("dp") * (ngrid // CORES) + lax.axis_index("grid") // CORES
    core = lax.axis_index("grid") % CORES
    step = jnp.arange(5, dtype=jnp.int32)
    x, y, z = place_of(chip * CORES)[:3]
    place = jnp.where(
        step == 0, x, jnp.where(step == 1, y, jnp.where(step == 2, z, jnp.where(step == 3, core, chip == 0)))
    ).astype(jnp.int32)

    together = lax.optimization_barrier
    away, wave, counts, lists, *pieces = grid_call(
        "first", 0, ngrid, capacity, dest_slab[:, 0], place, intensities, gridding, table["packed"], spectral_weights
    )
    members = (counts, lists, place, wave, gridding)
    arrived = [swap(away)]
    weights = exchange(pieces, (0, 0))
    (away,) = grid_call("away", 1, ngrid, capacity, *members)
    arrived.append(swap(away))
    (turned,) = call(weight_kernel, [(size, 2, size)], *weights, table["held"])
    arrived[0], turned = together((arrived[0], turned))
    pieces = []
    for part in range(HALVES):
        kept = grid_call("kept", part, ngrid, capacity, *members, arrived[part])
        if part == 1:
            kept, turned = together((kept, turned))
        pieces.append(exchange(kept, [order[0] for order in ORDERS]))
    given = lax.all_to_all(turned, ALL, 0, 0, tiled=True)
    pieces, given = together((pieces, given))
    scaled, ends = call(
        symmetry_kernel, [square, (8, size)],
        given, swap(given), place, table["ky_mirror"], table["mirror"],
    )
    total = jnp.concatenate([summed(parts) for parts in pieces], 1)
    quarter = lambda a: [p.reshape(p.shape[1:]) for p in jnp.split(a.reshape((SIDE, -1) + a.shape[1:]), SIDE)]
    parts = exchange(quarter(total), [order[1] for order in ORDERS])
    parts, scaled, ends = together((parts, scaled, ends))
    parts = exchange(quarter(summed(parts)), [order[2] for order in ORDERS])
    own = summed(parts).reshape(square)
    real, imag, send = call(
        moment_kernel, [square, square, square],
        own, swap(own), place, scaled, ends, table["lanes"], table["ky_rows"],
    )
    sums = lax.all_to_all(send.reshape(count, 1, size), ALL, 0, 0, tiled=True).reshape(count, size)
    back, gain = call(
        functools.partial(solve_kernel, scale=1.0 / size**3), [(ndp * 2 * size, size), (8, size)],
        sums, ends, scaled, real, imag, table["lanes"], table["ky_lanes"],
    )
    landed = lax.all_to_all(back.reshape(count, 2 * planes, size), ALL, 0, 0, tiled=True)
    return tuple(
        call(
            output_kernel, [(planes, size, size)] * 2,
            landed.reshape(count * 2 * planes, size), gain, table["back"],
        )
    )


def solution(mesh):
    return jax.shard_map(
        body,
        mesh=mesh,
        in_specs=(
            P(("dp", "grid"), None, None),
            P(("dp", "grid"), None, None),
            P(("dp", "grid"), None),
            P("dp", None, "grid", None),
        ),
        out_specs=(P("grid", None, None), P("grid", None, None)),
        check_vma=False,
    )
```

```python
import functools

import jax
import jax.numpy as jnp
import numpy as np
from jax import lax
from jax.experimental import pallas as pl
from jax.experimental.pallas import tpu as pltpu
from jax.sharding import PartitionSpec as P


ITERS = 8
MOMENTS = 2 * ITERS + 1
LOW_LANE = 64
ALL = ("dp", "grid")
HIGHEST = lax.Precision.HIGHEST


def two_sum(a, b):
    s = a + b
    v = s - a
    return s, (a - (s - v)) + (b - v)


def quick_sum(a, b):
    s = a + b
    return s, b - (s - a)


def halves(a):
    c = a * 4097.0
    high = c - (c - a)
    return high, a - high


def two_prod(a, b, a_parts=None, b_parts=None):
    p = a * b
    ah, al = a_parts or halves(a)
    bh, bl = b_parts or halves(b)
    return p, ((ah * bh - p) + ah * bl + al * bh) + al * bl


def dd_add(a, b):
    s, e = two_sum(a[0], b[0])
    return quick_sum(s, e + (a[1] + b[1]))


def dd_mul(a, b):
    p, e = two_prod(a[0], b[0])
    return quick_sum(p, e + (a[0] * b[1] + a[1] * b[0]))


def dd_times(a, b):
    p, e = two_prod(a[0], b)
    return quick_sum(p, e + a[1] * b)


def dd_scale(a, factor):
    return a[0] * factor, a[1] * factor


def dd_neg(a):
    return -a[0], -a[1]


def dd_div(a, b):
    inverse = 1.0 / b[0]
    first = a[0] * inverse
    rest = dd_add(a, dd_neg(dd_times(b, first)))
    return quick_sum(first, rest[0] * inverse)


def dot(a, b):
    return jax.lax.dot_general(
        a, b, (((1,), (0,)), ((), ())), precision=HIGHEST, preferred_element_type=jnp.float32
    )


SIDE = 4
CORES = 2
ORDERS = ((0, 1, 2), (1, 2, 0))


def place_of(device):
    chip = device // CORES
    return chip // SIDE**2, chip % SIDE, (chip // SIDE) % SIDE, device % CORES


def chip_at(x, y, z):
    return (x * SIDE + z) * SIDE + y


def shift_pairs(axes, hop):
    pairs = []
    for device in range(SIDE**3 * CORES):
        place = list(place_of(device))
        axis = axes[place[3]]
        place[axis] = (place[axis] + hop) % (CORES if axis == 3 else SIDE)
        pairs.append((device, chip_at(*place[:3]) * CORES + place[3]))
    return pairs


def held_rows(size):
    chip, core = np.arange(size) // CORES, np.arange(size) % CORES
    return np.where(chip == 0, core * size // 2, np.where(core == 0, chip, size - chip))


def weight_rows(size, ndp):
    d = np.arange(size)
    return ndp * (d % (size // ndp)) + d // (size // ndp)


def dft_tables(size, ndp):
    index = np.arange(size)
    angle = 2.0 * np.pi * ((index[:, None] * index[None, :]) % size) / size
    cos, sin = np.cos(angle), np.sin(angle)
    held, order = held_rows(size), weight_rows(size, ndp)
    as_f32 = lambda a: np.ascontiguousarray(a, dtype=np.float32)
    half = size // 2
    packed = np.concatenate([cos[:, :half], cos[:, half : half + 1], -sin[:, 1:half]], 1)
    high = packed.astype(jnp.bfloat16)
    low = (packed - high.astype(np.float64)).astype(jnp.bfloat16)
    return dict(
        packed=np.stack([np.concatenate([p[:, :half], q[:, :half]], 1) for p, q in ((high, low), (high[:, half:], low[:, half:]))]),
        lanes=as_f32(np.concatenate([cos, sin], 1)),
        ky_rows=as_f32(np.concatenate([cos[order], sin[order]], 0)),
        ky_lanes=as_f32(np.concatenate([cos[order], sin[order]], 1)),
        back=as_f32(
            np.concatenate(
                [np.concatenate([cos[held], sin[held]], 1), np.concatenate([-sin[held], cos[held]], 1)], 0
            )
        ),
        held=as_f32(held[:, None] == index[None, :]),
        mirror=as_f32(((index[:, None] + index[None, :]) % size) == 0),
        ky_mirror=as_f32(((order[:, None] + order[None, :]) % size) == 0),
    )


def dot_as(a, b, left, right):
    return lax.dot_general(
        a, b, (((left,), (right,)), ((), ())), precision=HIGHEST, preferred_element_type=jnp.float32
    )


HALVES = 2
STEPS = 4


def sublane_turn(tiles):
    row = lax.broadcasted_iota(jnp.int32, tiles[0].shape, 0)
    for bit in (4, 2, 1):
        low = (row & bit) == 0
        turned = list(tiles)
        for i in range(8):
            if i & bit == 0:
                a, b = tiles[i], tiles[i + bit]
                turned[i] = jnp.where(low, a, pltpu.roll(b, bit, 0))
                turned[i + bit] = jnp.where(low, pltpu.roll(a, 8 - bit, 0), b)
        tiles = turned
    return tiles


def grid_kernel(*refs, kept, part, capacity):
    if kept:
        count_ref, list_ref, place_ref, wave_ref, matrix_ref, other_ref = refs[:6]
        outs = refs[6:]
    else:
        dest_ref, place_ref, values_ref, matrix_ref, packed_ref, weights_ref = refs[:6]
        out_ref, wave_ref, count_ref, list_ref = refs[6:10]
    nent, rows, width = matrix_ref.shape
    size = width // SIDE
    half = size // 2
    nslab = count_ref.shape[0]
    core = place_ref[3] if kept else 1 - place_ref[3]
    step = pl.program_id(0)

    def clear(s, _):
        count_ref[s] = 0
        return 0

    def enter(e, _):
        slab = dest_ref[e]
        taken = count_ref[slab]
        list_ref[slab * capacity + taken] = e
        count_ref[slab] = taken + 1
        return 0

    def prepare():
        lax.fori_loop(0, nslab, clear, 0)
        lax.fori_loop(0, nent, enter, 0)
        for r, slice_ref in enumerate(refs[10:]):
            slice_ref[...] = weights_ref[0, :, (place_ref[0] + r) % SIDE, :]
        chip = lax.broadcasted_iota(jnp.int32, (half, half), 0)
        slot = lax.broadcasted_iota(jnp.int32, (half, half), 1)
        digits = (slot // SIDE**2, (slot // SIDE) % SIDE, slot % SIDE)
        pieces = []
        for owner in range(CORES):
            at = [place_ref[0], place_ref[1], place_ref[2]]
            for digit, axis in zip(digits, ORDERS[owner]):
                at[axis] = (at[axis] + digit) % SIDE
            pick = (chip == chip_at(*at)).astype(jnp.float32).astype(jnp.bfloat16)
            for start in (0, half):
                piece = packed_ref[owner, :, start : start + half]
                pieces.append(jnp.dot(piece, pick, preferred_element_type=jnp.float32).astype(jnp.bfloat16))
        both = jnp.dot(
            values_ref[...].reshape(nent * rows, size),
            jnp.concatenate(pieces, 1),
            preferred_element_type=jnp.float32,
        )
        for owner in range(CORES):
            wave = both[:, owner * size : owner * size + half] + both[:, owner * size + half : (owner + 1) * size]
            high = wave.astype(jnp.bfloat16)
            low = (wave - high.astype(jnp.float32)).astype(jnp.bfloat16)
            wave_ref[owner] = jnp.concatenate([high, low], 1).reshape(nent, rows, size)

    if not kept:
        pl.when(step == 0)(prepare)

    pairs = nslab // (2 * STEPS)
    for pair in range(pairs):
        products = []
        for near in range(2):
            slab = ((part * (STEPS // HALVES) + step) * pairs + pair) * 2 + near
            taken = count_ref[slab]
            waves, matrices = [], []
            for m in range(capacity):
                entry = jnp.where(m < taken, list_ref[slab * capacity + m], 0)
                wave = wave_ref[core, entry]
                waves.append(jnp.where(m < taken, wave, jnp.zeros_like(wave)))
                matrices.append(matrix_ref[entry])
            product = lax.dot_general(
                jnp.concatenate(waves, 0),
                jnp.concatenate(matrices, 0),
                (((0,), (0,)), ((), ())),
                preferred_element_type=jnp.float32,
            )
            products.append(product[:half] + product[half:])
        place = slice(pair * 8, pair * 8 + 8)
        for start in range(0, half, 8):
            tiles = [
                product[start : start + 8, p * size : (p + 1) * size] for product in products for p in range(SIDE)
            ]
            for index, block in enumerate(sublane_turn(tiles), start):
                if kept:
                    outs[index // SIDE**2][index % SIDE**2, place, :] = block + other_ref[index, place, :]
                else:
                    out_ref[index, place, :] = block


def grid_call(kept, part, nslab, capacity, *args):
    scalars = pl.BlockSpec(memory_space=pltpu.SMEM)
    fixed = lambda shape: pl.BlockSpec(shape, lambda i: (0,) * len(shape))
    matrix = args[4] if kept else args[3]
    nent, rows, width = matrix.shape
    size, blocks = width // SIDE, SIDE**3
    steps = STEPS // HALVES if kept else STEPS
    moving = lambda count, start=0: pl.BlockSpec((count, size // STEPS, size), lambda i: (0, start + i, 0))
    f32 = lambda *shape: jax.ShapeDtypeStruct(shape, jnp.float32)
    in_specs = [scalars if a.dtype == jnp.int32 else fixed(a.shape) for a in args]
    if kept:
        out_shape, out_specs = [f32(SIDE**2, size // HALVES, size)] * SIDE, [moving(SIDE**2)] * SIDE
        in_specs[-1] = moving(blocks, part * steps)
    else:
        wave = (CORES, nent, rows, size)
        out_shape = [
            f32(blocks, size, size),
            jax.ShapeDtypeStruct(wave, jnp.bfloat16),
            jax.ShapeDtypeStruct((nslab,), jnp.int32),
            jax.ShapeDtypeStruct((nslab * capacity,), jnp.int32),
        ] + [f32(size, size)] * SIDE
        out_specs = [moving(blocks), fixed(wave), scalars, scalars] + [fixed((size, size))] * SIDE
    return pl.pallas_call(
        functools.partial(grid_kernel, kept=kept, part=part, capacity=capacity),
        grid=(steps,),
        out_shape=out_shape,
        in_specs=in_specs,
        out_specs=out_specs,
    )(*args)


def weight_kernel(w0_ref, w1_ref, w2_ref, w3_ref, held_ref, out_ref):
    size = w0_ref.shape[0]
    own = ((w0_ref[...] + w1_ref[...]) + w2_ref[...]) + w3_ref[...]
    low = jnp.min(jnp.min(own, axis=0, keepdims=True), axis=1, keepdims=True)
    high = jnp.max(jnp.max(own, axis=0, keepdims=True), axis=1, keepdims=True)
    lane = lax.broadcasted_iota(jnp.int32, (size, size), 1)
    out_ref[:, 0, :] = dot_as(held_ref[...], own, 1, 1)
    out_ref[:, 1, :] = jnp.where(lane < size // 2, low, high)


def symmetry_kernel(given_ref, other_ref, place_ref, ky_mirror_ref, mirror_ref, scaled_ref, range_ref):
    size = scaled_ref.shape[0]
    ends = given_ref[:, 1, :]
    low = jnp.min(jnp.min(ends, axis=0, keepdims=True), axis=1, keepdims=True)
    high = jnp.max(jnp.max(ends, axis=0, keepdims=True), axis=1, keepdims=True)
    half = jnp.maximum((high - low) * 0.5, high * 1e-4)
    half = jnp.broadcast_to(half, (1, size))
    range_ref[0:1, :] = half
    range_ref[1:2, :] = jnp.broadcast_to((high + low) * 0.5, (1, size)) / half
    range_ref[2:8, :] = jnp.zeros((6, size), jnp.float32)
    own = given_ref[:, 0, :]
    partner = jnp.where(place_ref[4] == 1, own, other_ref[:, 0, :])
    mirrored = dot(ky_mirror_ref[...], dot(partner, mirror_ref[...]))
    scaled_ref[...] = (own + mirrored) * 0.5 / half


def sublane_total(a):
    for shift in (4, 2, 1):
        a = dd_add(a, (pltpu.roll(a[0], shift, 0), pltpu.roll(a[1], shift, 0)))
    return a


def lane_total(a):
    for shift in (64, 32, 16, 8, 4, 2, 1):
        a = dd_add(a, (pltpu.roll(a[0], shift, 1), pltpu.roll(a[1], shift, 1)))
    return a


def moment_kernel(own_ref, other_ref, place_ref, scaled_ref, range_ref, lanes_ref, rows_ref, real_ref, imag_ref, send_ref):
    size = own_ref.shape[0]
    centre = range_ref[1:2, :]
    mine, theirs = own_ref[...], other_ref[...]
    second, alone = place_ref[3] == 1, place_ref[4] == 1
    re = jnp.where(jnp.logical_and(second, jnp.logical_not(alone)), theirs, mine)
    im = jnp.where(alone, jnp.zeros_like(mine), jnp.where(second, -mine, theirs))
    ends = dot_as(jnp.concatenate([re, im], 1), lanes_ref[...], 0, 0)
    mid_real = ends[:size, :size] + ends[size:, size:]
    mid_imag = ends[size:, :size] - ends[:size, size:]
    both = dot(rows_ref[...], jnp.concatenate([mid_real, mid_imag], 1))
    real = both[:size, :size] + both[size:, size:]
    imag = both[:size, size:] - both[size:, :size]
    real_ref[...] = real
    imag_ref[...] = imag
    scaled = scaled_ref[...]
    power = real * real + imag * imag
    chunk = 24
    totals = [None] * MOMENTS
    for start in (0, size // 4, size // 4 + chunk):
        row = lax.broadcasted_iota(jnp.int32, (chunk, size), 0) + start
        if start == 0:
            share = jnp.where(row % (size // 8) == 0, 1.0, jnp.where(row < size // 8, 2.0, 0.0))
        else:
            share = 2.0
        t = scaled[start : start + chunk] - centre
        p = power[start : start + chunk] * share
        p_parts = halves(p)
        t2 = t * 2.0
        t2_parts = halves(t2)
        zero = jnp.zeros_like(t)
        before, here = (jnp.ones_like(t), zero), (t, zero)
        for order in range(MOMENTS):
            value = before
            v_parts = halves(value[0])
            term, low_term = two_prod(value[0], p, v_parts, p_parts)
            term = (term, low_term + value[1] * p)
            total, spill = totals[order] or (None, None)
            for i in range(0, chunk, 8):
                piece, rest = term[0][i : i + 8], term[1][i : i + 8]
                if total is None:
                    total, spill = piece, rest
                else:
                    total, lost = two_sum(total, piece)
                    spill = spill + (lost + rest)
            totals[order] = total, spill
            if order + 1 < MOMENTS:
                up, low_up = two_prod(here[0], t2, None, t2_parts)
                following, lost = two_sum(up, -before[0])
                before, here = here, (following, lost + ((low_up + here[1] * t2) - before[1]))
    row = lax.broadcasted_iota(jnp.int32, (8, size), 0)
    lane = lax.broadcasted_iota(jnp.int32, (8, size), 1)
    out = jnp.zeros((8, size), jnp.float32)
    for base in range(0, MOMENTS, 8):
        high_rows = jnp.zeros((8, size), jnp.float32)
        low_rows = jnp.zeros((8, size), jnp.float32)
        for order in range(base, min(base + 8, MOMENTS)):
            total = sublane_total(quick_sum(*totals[order]))
            high_rows = jnp.where(row == order - base, total[0], high_rows)
            low_rows = jnp.where(row == order - base, total[1], low_rows)
        high_rows, low_rows = lane_total((high_rows, low_rows))
        out = jnp.where(lane == row + base, high_rows, out)
        out = jnp.where(lane == row + (base + LOW_LANE), low_rows, out)
    line = jnp.sum(out, axis=0, keepdims=True)
    send_ref[...] = jnp.broadcast_to(line, (size, size))


def lane_of(a, lane):
    pick = lambda v: jnp.broadcast_to(v[:, lane : lane + 1], v.shape)
    return pick(a[0]), pick(a[1])


def solve_kernel(
    sums_ref, range_ref, scaled_ref, real_ref, imag_ref, lanes_ref, ky_lanes_ref, out_ref, gain_ref, *, scale
):
    size = scaled_ref.shape[0]
    given = sums_ref[...]
    low = pltpu.roll(given, size - LOW_LANE, 1)
    rows = [(given[i : i + 8], low[i : i + 8]) for i in range(0, given.shape[0], 8)]
    while len(rows) > 1:
        rows = [dd_add(rows[i], rows[i + 1]) for i in range(0, len(rows), 2)]
    moments = sublane_total(rows[0])
    half = range_ref[0:1, :]
    centre = jnp.broadcast_to(range_ref[1:2, :], moments[0].shape)
    centre = (centre, jnp.zeros_like(centre))
    lane = lax.broadcasted_iota(jnp.int32, moments[0].shape, 1)
    resid, direct = moments, moments
    held = lane_of(resid, 0)
    steps, turns = [], []
    decay = jnp.ones((1, size), jnp.float32)
    for k in range(ITERS):
        after = tuple(pltpu.roll(v, size - 1, 1) for v in direct)
        prior = tuple(pltpu.roll(v, 1, 1) for v in direct)
        prior = tuple(jnp.where(lane == 0, a, p) for a, p in zip(after, prior))
        image = dd_add(dd_mul(direct, centre), dd_scale(dd_add(after, prior), 0.5))
        alpha = dd_div(held, lane_of(image, k))
        fresh = dd_add(resid, dd_neg(dd_mul(alpha, image)))
        reached = lane_of(fresh, k + 1)
        beta = dd_mul(alpha, dd_div(reached, held))
        held = reached
        beta = dd_scale(beta, -1.0 if k == 0 else -0.5)
        direct = dd_add(fresh, dd_mul(beta, direct))
        resid = fresh
        steps.append(alpha[0][0:1])
        turns.append(beta[0][0:1])
        decay = decay * beta[0][0:1]
    gain = lax.rsqrt(jnp.maximum(jnp.abs(decay), 1e-30)) / centre[0][0:1]
    gain_ref[...] = jnp.broadcast_to(gain, gain_ref.shape)
    scaled = scaled_ref[...]
    field = steps[0]
    solved = jnp.broadcast_to(field, scaled.shape)
    left = 1.0 - field * scaled
    toward = left + turns[0]
    for k in range(1, ITERS):
        solved = solved + steps[k] * toward
        left = left - steps[k] * (scaled * toward)
        if k + 1 < ITERS:
            toward = left + turns[k] * toward
    solved = solved * (scale / half)
    left = left * (gain * scale)
    real, imag = real_ref[...], imag_ref[...]
    back_real = solved * real - left * imag
    back_imag = solved * imag + left * real
    ends = dot(jnp.concatenate([back_real, back_imag], 0), lanes_ref[...])
    mid_real = ends[:size, :size] - ends[size:, size:]
    mid_imag = ends[size:, :size] + ends[:size, size:]
    ends = dot_as(jnp.concatenate([mid_real, mid_imag], 1), ky_lanes_ref[...], 0, 0)
    real = ends[:size, :size] - ends[size:, size:]
    imag = ends[size:, :size] + ends[:size, size:]
    for copy in range(out_ref.shape[0] // (2 * size)):
        out_ref[pl.ds(copy * 2 * size, size, stride=2), :] = real
        out_ref[pl.ds(copy * 2 * size + 1, size, stride=2), :] = imag


def output_kernel(given_ref, gain_ref, back_ref, field_ref, resid_ref):
    planes, size = field_ref.shape[0], field_ref.shape[1]
    step = 2 * planes
    shrink = 1.0 / gain_ref[0:1, :]
    for j in range(planes):
        pieces = [given_ref[pl.ds(2 * j + part, size, stride=step), :] for part in range(2)]
        both = dot_as(jnp.concatenate(pieces, 0), back_ref[...], 0, 0)
        field_ref[j] = both[:, :size]
        resid_ref[j] = both[:, size:] * shrink


def call(kernel, shapes, *args):
    whole = pl.BlockSpec(memory_space=pltpu.VMEM)
    scalars = pl.BlockSpec(memory_space=pltpu.SMEM)
    return pl.pallas_call(
        kernel,
        out_shape=[jax.ShapeDtypeStruct(s, jnp.float32) for s in shapes],
        in_specs=[scalars if a.dtype == jnp.int32 else whole for a in args],
        out_specs=[whole] * len(shapes),
    )(*args)


def exchange(parts, axes):
    return [parts[0]] + [lax.ppermute(parts[r], ALL, shift_pairs(axes, r)) for r in range(1, SIDE)]


def summed(parts):
    return ((parts[0] + parts[1]) + parts[2]) + parts[3]


def body(intensities, gridding, dest_slab, spectral_weights):
    ngrid = lax.axis_size("grid")
    ndp = lax.axis_size("dp")
    nent, _, size = intensities.shape
    planes = gridding.shape[2] // size
    count = ngrid * ndp
    capacity = max(2, 2 * nent // ngrid)
    table = dft_tables(size, ndp)
    square = (size, size)
    swap = lambda a: lax.ppermute(a, ALL, shift_pairs((3, 3), 1))

    chip = lax.axis_index("dp") * (ngrid // CORES) + lax.axis_index("grid") // CORES
    core = lax.axis_index("grid") % CORES
    step = jnp.arange(5, dtype=jnp.int32)
    x, y, z = place_of(chip * CORES)[:3]
    place = jnp.where(
        step == 0, x, jnp.where(step == 1, y, jnp.where(step == 2, z, jnp.where(step == 3, core, chip == 0)))
    ).astype(jnp.int32)

    together = lax.optimization_barrier
    away, wave, counts, lists, *pieces = grid_call(
        False, 0, ngrid, capacity, dest_slab[:, 0], place, intensities, gridding, table["packed"], spectral_weights
    )
    members = (counts, lists, place, wave, gridding)
    arrived = swap(away)
    weights = exchange(pieces, (0, 0))
    (turned,) = call(weight_kernel, [(size, 2, size)], *weights, table["held"])
    arrived, turned = together((arrived, turned))
    pieces = []
    for part in range(HALVES):
        kept = grid_call(True, part, ngrid, capacity, *members, arrived)
        if part == 1:
            kept, turned = together((kept, turned))
        pieces.append(exchange(kept, [order[0] for order in ORDERS]))
    given = lax.all_to_all(turned, ALL, 0, 0, tiled=True)
    pieces, given = together((pieces, given))
    scaled, ends = call(
        symmetry_kernel, [square, (8, size)],
        given, swap(given), place, table["ky_mirror"], table["mirror"],
    )
    total = jnp.concatenate([summed(parts) for parts in pieces], 1)
    quarter = lambda a: [p.reshape(p.shape[1:]) for p in jnp.split(a.reshape((SIDE, -1) + a.shape[1:]), SIDE)]
    parts = exchange(quarter(total), [order[1] for order in ORDERS])
    parts, scaled, ends = together((parts, scaled, ends))
    parts = exchange(quarter(summed(parts)), [order[2] for order in ORDERS])
    own = summed(parts).reshape(square)
    real, imag, send = call(
        moment_kernel, [square, square, square],
        own, swap(own), place, scaled, ends, table["lanes"], table["ky_rows"],
    )
    sums = lax.all_to_all(send.reshape(count, 1, size), ALL, 0, 0, tiled=True).reshape(count, size)
    back, gain = call(
        functools.partial(solve_kernel, scale=1.0 / size**3), [(ndp * 2 * size, size), (8, size)],
        sums, ends, scaled, real, imag, table["lanes"], table["ky_lanes"],
    )
    landed = lax.all_to_all(back.reshape(count, 2 * planes, size), ALL, 0, 0, tiled=True)
    return tuple(
        call(
            output_kernel, [(planes, size, size)] * 2,
            landed.reshape(count * 2 * planes, size), gain, table["back"],
        )
    )


def solution(mesh):
    return jax.shard_map(
        body,
        mesh=mesh,
        in_specs=(
            P(("dp", "grid"), None, None),
            P(("dp", "grid"), None, None),
            P(("dp", "grid"), None),
            P("dp", None, "grid", None),
        ),
        out_specs=(P("grid", None, None), P("grid", None, None)),
        check_vma=False,
    )
```

```python
import functools

import jax
import jax.numpy as jnp
import numpy as np
from jax import lax
from jax.experimental import pallas as pl
from jax.experimental.pallas import tpu as pltpu
from jax.sharding import PartitionSpec as P


ITERS = 8
MOMENTS = 2 * ITERS + 1
LOW_LANE = 64
ALL = ("dp", "grid")
HIGHEST = lax.Precision.HIGHEST


def two_sum(a, b):
    s = a + b
    v = s - a
    return s, (a - (s - v)) + (b - v)


def quick_sum(a, b):
    s = a + b
    return s, b - (s - a)


def halves(a):
    c = a * 4097.0
    high = c - (c - a)
    return high, a - high


def two_prod(a, b, a_parts=None, b_parts=None):
    p = a * b
    ah, al = a_parts or halves(a)
    bh, bl = b_parts or halves(b)
    return p, ((ah * bh - p) + ah * bl + al * bh) + al * bl


def dd_add(a, b):
    s, e = two_sum(a[0], b[0])
    return quick_sum(s, e + (a[1] + b[1]))


def dd_mul(a, b):
    p, e = two_prod(a[0], b[0])
    return quick_sum(p, e + (a[0] * b[1] + a[1] * b[0]))


def dd_times(a, b):
    p, e = two_prod(a[0], b)
    return quick_sum(p, e + a[1] * b)


def dd_scale(a, factor):
    return a[0] * factor, a[1] * factor


def dd_neg(a):
    return -a[0], -a[1]


def dd_div(a, b):
    inverse = 1.0 / b[0]
    first = a[0] * inverse
    rest = dd_add(a, dd_neg(dd_times(b, first)))
    return quick_sum(first, rest[0] * inverse)


def dot(a, b):
    return jax.lax.dot_general(
        a, b, (((1,), (0,)), ((), ())), precision=HIGHEST, preferred_element_type=jnp.float32
    )


SIDE = 4
CORES = 2
ORDERS = ((0, 1, 2), (1, 2, 0))


def place_of(device):
    chip = device // CORES
    return chip // SIDE**2, chip % SIDE, (chip // SIDE) % SIDE, device % CORES


def chip_at(x, y, z):
    return (x * SIDE + z) * SIDE + y


def shift_pairs(axes, hop):
    pairs = []
    for device in range(SIDE**3 * CORES):
        place = list(place_of(device))
        axis = axes[place[3]]
        place[axis] = (place[axis] + hop) % (CORES if axis == 3 else SIDE)
        pairs.append((device, chip_at(*place[:3]) * CORES + place[3]))
    return pairs


def held_rows(size):
    chip, core = np.arange(size) // CORES, np.arange(size) % CORES
    return np.where(chip == 0, core * size // 2, np.where(core == 0, chip, size - chip))


def dft_tables(size):
    index = np.arange(size)
    angle = 2.0 * np.pi * ((index[:, None] * index[None, :]) % size) / size
    cos, sin = np.cos(angle), np.sin(angle)
    held = held_rows(size)
    as_f32 = lambda a: np.ascontiguousarray(a, dtype=np.float32)
    half = size // 2
    packed = np.concatenate([cos[:, :half], cos[:, half : half + 1], -sin[:, 1:half]], 1)
    high = packed.astype(jnp.bfloat16)
    low = (packed - high.astype(np.float64)).astype(jnp.bfloat16)
    return dict(
        packed=np.stack([np.concatenate([p[:, :half], q[:, :half]], 1) for p, q in ((high, low), (high[:, half:], low[:, half:]))]),
        lanes=as_f32(np.concatenate([cos, sin], 1)),
        rows=as_f32(np.concatenate([cos, sin], 0)),
        back=as_f32(
            np.concatenate(
                [np.concatenate([cos[held], sin[held]], 1), np.concatenate([-sin[held], cos[held]], 1)], 0
            )
        ),
        mirror=as_f32(((index[:, None] + index[None, :]) % size) == 0),
    )


def dot_as(a, b, left, right):
    return lax.dot_general(
        a, b, (((left,), (right,)), ((), ())), precision=HIGHEST, preferred_element_type=jnp.float32
    )


HALVES = 2
STEPS = 4


def sublane_turn(tiles):
    row = lax.broadcasted_iota(jnp.int32, tiles[0].shape, 0)
    for bit in (4, 2, 1):
        low = (row & bit) == 0
        turned = list(tiles)
        for i in range(8):
            if i & bit == 0:
                a, b = tiles[i], tiles[i + bit]
                turned[i] = jnp.where(low, a, pltpu.roll(b, bit, 0))
                turned[i + bit] = jnp.where(low, pltpu.roll(a, 8 - bit, 0), b)
        tiles = turned
    return tiles


def grid_kernel(*refs, kept, part, capacity):
    if kept:
        count_ref, list_ref, place_ref, wave_ref, matrix_ref, other_ref = refs[:6]
        outs = refs[6:]
    else:
        dest_ref, place_ref, values_ref, matrix_ref, packed_ref, weights_ref = refs[:6]
        out_ref, wave_ref, count_ref, list_ref = refs[6:10]
    nent, rows, width = matrix_ref.shape
    size = width // SIDE
    half = size // 2
    nslab = count_ref.shape[0]
    core = place_ref[3] if kept else 1 - place_ref[3]
    step = pl.program_id(0)

    def clear(s, _):
        count_ref[s] = 0
        return 0

    def enter(e, _):
        slab = dest_ref[e]
        taken = count_ref[slab]
        list_ref[slab * capacity + taken] = e
        count_ref[slab] = taken + 1
        return 0

    def prepare():
        lax.fori_loop(0, nslab, clear, 0)
        lax.fori_loop(0, nent, enter, 0)
        for r, slice_ref in enumerate(refs[10:]):
            slice_ref[...] = weights_ref[0, :, (place_ref[0] + r) % SIDE, :]
        chip = lax.broadcasted_iota(jnp.int32, (half, half), 0)
        slot = lax.broadcasted_iota(jnp.int32, (half, half), 1)
        digits = digits_of(slot)
        pieces = []
        for owner in range(CORES):
            pick = (chip == chip_at(*moved(place_ref, digits, owner, 1))).astype(jnp.float32).astype(jnp.bfloat16)
            for start in (0, half):
                piece = packed_ref[owner, :, start : start + half]
                pieces.append(jnp.dot(piece, pick, preferred_element_type=jnp.float32).astype(jnp.bfloat16))
        both = jnp.dot(
            values_ref[...].reshape(nent * rows, size),
            jnp.concatenate(pieces, 1),
            preferred_element_type=jnp.float32,
        )
        for owner in range(CORES):
            wave = both[:, owner * size : owner * size + half] + both[:, owner * size + half : (owner + 1) * size]
            high = wave.astype(jnp.bfloat16)
            low = (wave - high.astype(jnp.float32)).astype(jnp.bfloat16)
            wave_ref[owner] = jnp.concatenate([high, low], 1).reshape(nent, rows, size)

    if not kept:
        pl.when(step == 0)(prepare)

    pairs = nslab // (2 * STEPS)
    for pair in range(pairs):
        products = []
        for near in range(2):
            slab = ((part * (STEPS // HALVES) + step) * pairs + pair) * 2 + near
            taken = count_ref[slab]
            waves, matrices = [], []
            for m in range(capacity):
                entry = jnp.where(m < taken, list_ref[slab * capacity + m], 0)
                wave = wave_ref[core, entry]
                waves.append(jnp.where(m < taken, wave, jnp.zeros_like(wave)))
                matrices.append(matrix_ref[entry])
            product = lax.dot_general(
                jnp.concatenate(waves, 0),
                jnp.concatenate(matrices, 0),
                (((0,), (0,)), ((), ())),
                preferred_element_type=jnp.float32,
            )
            products.append(product[:half] + product[half:])
        place = slice(pair * 8, pair * 8 + 8)
        for start in range(0, half, 8):
            tiles = [
                product[start : start + 8, p * size : (p + 1) * size] for product in products for p in range(SIDE)
            ]
            for index, block in enumerate(sublane_turn(tiles), start):
                if kept:
                    outs[index // SIDE**2][index % SIDE**2, place, :] = block + other_ref[index, place, :]
                else:
                    out_ref[index, place, :] = block


def grid_call(kept, part, nslab, capacity, *args):
    scalars = pl.BlockSpec(memory_space=pltpu.SMEM)
    fixed = lambda shape: pl.BlockSpec(shape, lambda i: (0,) * len(shape))
    matrix = args[4] if kept else args[3]
    nent, rows, width = matrix.shape
    size, blocks = width // SIDE, SIDE**3
    steps = STEPS // HALVES if kept else STEPS
    moving = lambda count, start=0: pl.BlockSpec((count, size // STEPS, size), lambda i: (0, start + i, 0))
    f32 = lambda *shape: jax.ShapeDtypeStruct(shape, jnp.float32)
    in_specs = [scalars if a.dtype == jnp.int32 else fixed(a.shape) for a in args]
    if kept:
        out_shape, out_specs = [f32(SIDE**2, size // HALVES, size)] * SIDE, [moving(SIDE**2)] * SIDE
        in_specs[-1] = moving(blocks, part * steps)
    else:
        wave = (CORES, nent, rows, size)
        out_shape = [
            f32(blocks, size, size),
            jax.ShapeDtypeStruct(wave, jnp.bfloat16),
            jax.ShapeDtypeStruct((nslab,), jnp.int32),
            jax.ShapeDtypeStruct((nslab * capacity,), jnp.int32),
        ] + [f32(size, size)] * SIDE
        out_specs = [moving(blocks), fixed(wave), scalars, scalars] + [fixed((size, size))] * SIDE
    return pl.pallas_call(
        functools.partial(grid_kernel, kept=kept, part=part, capacity=capacity),
        grid=(steps,),
        out_shape=out_shape,
        in_specs=in_specs,
        out_specs=out_specs,
    )(*args)


def moved(place_ref, digits, owner, sign):
    at = [place_ref[0], place_ref[1], place_ref[2]]
    for digit, axis in zip(digits, ORDERS[owner]):
        at[axis] = (at[axis] + sign * digit + SIDE) % SIDE
    return at


def digits_of(index):
    return index // SIDE**2, (index // SIDE) % SIDE, index % SIDE


def weight_kernel(w0_ref, w1_ref, w2_ref, w3_ref, place_ref, *outs):
    size = w0_ref.shape[0]
    half = size // 2
    own = ((w0_ref[...] + w1_ref[...]) + w2_ref[...]) + w3_ref[...]
    low = jnp.min(jnp.min(own, axis=0, keepdims=True), axis=1, keepdims=True)
    high = jnp.max(jnp.max(own, axis=0, keepdims=True), axis=1, keepdims=True)
    row = lax.broadcasted_iota(jnp.int32, (size, size), 0)
    lane = lax.broadcasted_iota(jnp.int32, (size, size), 1)
    chips = [chip_at(*moved(place_ref, digits_of(row % half), owner, 1)) for owner in range(CORES)]
    chip = jnp.where(place_ref[3] == 0, chips[0], chips[1])
    negative = jnp.where(chip == 0, half, size - chip)
    pick = (lane == jnp.where(row < half, chip, negative)).astype(jnp.float32)
    rows = dot_as(pick, own, 1, 1)
    ends = jnp.where(lax.broadcasted_iota(jnp.int32, (8, size), 1) < half, low, -high)
    count = half // SIDE
    for r, out_ref in enumerate(outs):
        out_ref[:, 0:8, :] = jnp.zeros((count, 8, size), jnp.float32)
        out_ref[:, 8:16, :] = jnp.broadcast_to(ends[None], (count, 8, size))
        for sign in range(2):
            at = sign * half + r * count
            out_ref[:, 2 * r + sign, :] = rows[at : at + count]


def sublane_total(a):
    for shift in (4, 2, 1):
        a = dd_add(a, (pltpu.roll(a[0], shift, 0), pltpu.roll(a[1], shift, 0)))
    return a


def lane_total(a):
    for shift in (64, 32, 16, 8, 4, 2, 1):
        a = dd_add(a, (pltpu.roll(a[0], shift, 1), pltpu.roll(a[1], shift, 1)))
    return a


def moment_kernel(
    own_ref, other_ref, place_ref, lanes_ref, rows_ref, mirror_ref, real_ref, imag_ref, scaled_ref, range_ref, send_ref
):
    size = scaled_ref.shape[0]
    second, alone = place_ref[3] == 1, place_ref[4] == 1
    lane8 = lax.broadcasted_iota(jnp.int32, (8, size), 1)
    ends = jnp.minimum(own_ref[2 * size :, :], other_ref[2 * size :, :])
    least = lambda v: jnp.min(jnp.min(v, axis=0, keepdims=True), axis=1, keepdims=True)
    low = least(jnp.where(lane8 < size // 2, ends, 1e30))
    high = -least(jnp.where(lane8 < size // 2, 1e30, ends))
    span = jnp.broadcast_to(jnp.maximum((high - low) * 0.5, high * 1e-4), (1, size))
    centre = jnp.broadcast_to((high + low) * 0.5, (1, size)) / span
    range_ref[0:1, :] = span
    range_ref[1:2, :] = centre
    range_ref[2:8, :] = jnp.zeros((6, size), jnp.float32)

    ky = lax.broadcasted_iota(jnp.int32, (size, size), 0)
    row = lax.broadcasted_iota(jnp.int32, (size, size), 1)
    found = row // 2
    back = (found % SIDE, (found // SIDE) % SIDE, found // SIDE**2)
    sources = []
    for owner in range(CORES):
        x, y, z = moved(place_ref, back, owner, -1)
        sources.append(SIDE * (z * (SIDE * CORES) + y * CORES + owner) + x)
    from_own = jnp.where(second, sources[1], sources[0])
    from_other = jnp.where(second, sources[0], sources[1])
    given = jnp.concatenate([own_ref[size : 2 * size, :], other_ref[size : 2 * size, :]], 0)
    picks = [
        jnp.concatenate(
            [jnp.where(row % 2 == sign, (ky == source).astype(jnp.float32), 0.0) for source in (from_own, from_other)], 1
        )
        for sign in range(2)
    ]
    signs = dot(jnp.concatenate(picks, 0), given)
    plus, minus = signs[:size], signs[size:]
    mine = jnp.where(second, minus, plus)
    partner = jnp.where(alone, mine, jnp.where(second, plus, minus))
    scaled = (mine + dot(dot(mirror_ref[...], partner), mirror_ref[...])) * 0.5 / span
    scaled_ref[...] = scaled.T

    mine, theirs = own_ref[:size, :], other_ref[:size, :]
    re = jnp.where(jnp.logical_and(second, jnp.logical_not(alone)), theirs, mine)
    im = jnp.where(alone, jnp.zeros_like(mine), jnp.where(second, -mine, theirs))
    ends = dot(jnp.concatenate([re, im], 0), lanes_ref[...])
    mid_real = ends[:size, :size] + ends[size:, size:]
    mid_imag = ends[size:, :size] - ends[:size, size:]
    both = dot(rows_ref[...], jnp.concatenate([mid_real, mid_imag], 1))
    real = both[:size, :size] + both[size:, size:]
    imag = both[:size, size:] - both[size:, :size]
    real_ref[...] = real
    imag_ref[...] = imag
    scaled = scaled_ref[...]
    power = real * real + imag * imag
    chunk = 24
    totals = [None] * MOMENTS
    for start in range(0, size // 2 + 8, chunk):
        row = lax.broadcasted_iota(jnp.int32, (chunk, size), 0) + start
        share = jnp.where(row % (size // 2) == 0, 1.0, jnp.where(row < size // 2, 2.0, 0.0))
        t = scaled[start : start + chunk] - centre
        p = power[start : start + chunk] * share
        p_parts = halves(p)
        t2 = t * 2.0
        t2_parts = halves(t2)
        zero = jnp.zeros_like(t)
        before, here = (jnp.ones_like(t), zero), (t, zero)
        for order in range(MOMENTS):
            value = before
            v_parts = halves(value[0])
            term, low_term = two_prod(value[0], p, v_parts, p_parts)
            term = (term, low_term + value[1] * p)
            total, spill = totals[order] or (None, None)
            for i in range(0, chunk, 8):
                piece, rest = term[0][i : i + 8], term[1][i : i + 8]
                if total is None:
                    total, spill = piece, rest
                else:
                    total, lost = two_sum(total, piece)
                    spill = spill + (lost + rest)
            totals[order] = total, spill
            if order + 1 < MOMENTS:
                up, low_up = two_prod(here[0], t2, None, t2_parts)
                following, lost = two_sum(up, -before[0])
                before, here = here, (following, lost + ((low_up + here[1] * t2) - before[1]))
    row = lax.broadcasted_iota(jnp.int32, (8, size), 0)
    lane = lax.broadcasted_iota(jnp.int32, (8, size), 1)
    out = jnp.zeros((8, size), jnp.float32)
    for base in range(0, MOMENTS, 8):
        high_rows = jnp.zeros((8, size), jnp.float32)
        low_rows = jnp.zeros((8, size), jnp.float32)
        for order in range(base, min(base + 8, MOMENTS)):
            total = sublane_total(quick_sum(*totals[order]))
            high_rows = jnp.where(row == order - base, total[0], high_rows)
            low_rows = jnp.where(row == order - base, total[1], low_rows)
        high_rows, low_rows = lane_total((high_rows, low_rows))
        out = jnp.where(lane == row + base, high_rows, out)
        out = jnp.where(lane == row + (base + LOW_LANE), low_rows, out)
    line = jnp.sum(out, axis=0, keepdims=True)
    send_ref[...] = jnp.broadcast_to(line, (size, size))


def lane_of(a, lane):
    pick = lambda v: jnp.broadcast_to(v[:, lane : lane + 1], v.shape)
    return pick(a[0]), pick(a[1])


def solve_kernel(
    sums_ref, range_ref, scaled_ref, real_ref, imag_ref, lanes_ref, rows_ref, out_ref, gain_ref, *, scale
):
    size = scaled_ref.shape[0]
    given = sums_ref[...]
    low = pltpu.roll(given, size - LOW_LANE, 1)
    rows = [(given[i : i + 8], low[i : i + 8]) for i in range(0, given.shape[0], 8)]
    while len(rows) > 1:
        rows = [dd_add(rows[i], rows[i + 1]) for i in range(0, len(rows), 2)]
    moments = sublane_total(rows[0])
    half = range_ref[0:1, :]
    centre = jnp.broadcast_to(range_ref[1:2, :], moments[0].shape)
    centre = (centre, jnp.zeros_like(centre))
    lane = lax.broadcasted_iota(jnp.int32, moments[0].shape, 1)
    resid, direct = moments, moments
    held = lane_of(resid, 0)
    steps, turns = [], []
    decay = jnp.ones((1, size), jnp.float32)
    for k in range(ITERS):
        after = tuple(pltpu.roll(v, size - 1, 1) for v in direct)
        prior = tuple(pltpu.roll(v, 1, 1) for v in direct)
        prior = tuple(jnp.where(lane == 0, a, p) for a, p in zip(after, prior))
        image = dd_add(dd_mul(direct, centre), dd_scale(dd_add(after, prior), 0.5))
        alpha = dd_div(held, lane_of(image, k))
        fresh = dd_add(resid, dd_neg(dd_mul(alpha, image)))
        reached = lane_of(fresh, k + 1)
        beta = dd_mul(alpha, dd_div(reached, held))
        held = reached
        beta = dd_scale(beta, -1.0 if k == 0 else -0.5)
        direct = dd_add(fresh, dd_mul(beta, direct))
        resid = fresh
        steps.append(alpha[0][0:1])
        turns.append(beta[0][0:1])
        decay = decay * beta[0][0:1]
    gain = lax.rsqrt(jnp.maximum(jnp.abs(decay), 1e-30)) / centre[0][0:1]
    gain_ref[...] = jnp.broadcast_to(gain, gain_ref.shape)
    scaled = scaled_ref[...]
    field = steps[0]
    solved = jnp.broadcast_to(field, scaled.shape)
    left = 1.0 - field * scaled
    toward = left + turns[0]
    for k in range(1, ITERS):
        solved = solved + steps[k] * toward
        left = left - steps[k] * (scaled * toward)
        if k + 1 < ITERS:
            toward = left + turns[k] * toward
    solved = solved * (scale / half)
    left = left * (gain * scale)
    real, imag = real_ref[...], imag_ref[...]
    back_real = solved * real - left * imag
    back_imag = solved * imag + left * real
    ends = dot(jnp.concatenate([back_real, back_imag], 0), lanes_ref[...])
    mid_real = ends[:size, :size] - ends[size:, size:]
    mid_imag = ends[size:, :size] + ends[:size, size:]
    both = dot(rows_ref[...], jnp.concatenate([mid_real, mid_imag], 1))
    real = both[:size, :size] - both[size:, size:]
    imag = both[:size, size:] + both[size:, :size]
    for copy in range(out_ref.shape[0] // (2 * size)):
        out_ref[pl.ds(copy * 2 * size, size, stride=2), :] = real
        out_ref[pl.ds(copy * 2 * size + 1, size, stride=2), :] = imag


def output_kernel(given_ref, gain_ref, back_ref, field_ref, resid_ref):
    planes, size = field_ref.shape[0], field_ref.shape[1]
    step = 2 * planes
    shrink = 1.0 / gain_ref[0:1, :]
    for j in range(planes):
        pieces = [given_ref[pl.ds(2 * j + part, size, stride=step), :] for part in range(2)]
        both = dot_as(jnp.concatenate(pieces, 0), back_ref[...], 0, 0)
        field_ref[j] = both[:, :size]
        resid_ref[j] = both[:, size:] * shrink


def call(kernel, shapes, *args):
    whole = pl.BlockSpec(memory_space=pltpu.VMEM)
    scalars = pl.BlockSpec(memory_space=pltpu.SMEM)
    return pl.pallas_call(
        kernel,
        out_shape=[jax.ShapeDtypeStruct(s, jnp.float32) for s in shapes],
        in_specs=[scalars if a.dtype == jnp.int32 else whole for a in args],
        out_specs=[whole] * len(shapes),
    )(*args)


def exchange(parts, axes):
    return [parts[0]] + [lax.ppermute(parts[r], ALL, shift_pairs(axes, r)) for r in range(1, SIDE)]


def summed(parts):
    return ((parts[0] + parts[1]) + parts[2]) + parts[3]


def body(intensities, gridding, dest_slab, spectral_weights):
    ngrid = lax.axis_size("grid")
    ndp = lax.axis_size("dp")
    nent, rows, size = intensities.shape
    planes = gridding.shape[2] // size
    count = ngrid * ndp
    capacity = max(2, 2 * nent // ngrid)
    table = dft_tables(size)
    square = (size, size)
    swap = lambda a: lax.ppermute(a, ALL, shift_pairs((3, 3), 1))

    chip = lax.axis_index("dp") * (ngrid // CORES) + lax.axis_index("grid") // CORES
    core = lax.axis_index("grid") % CORES
    step = jnp.arange(5, dtype=jnp.int32)
    x, y, z = place_of(chip * CORES)[:3]
    place = jnp.where(
        step == 0, x, jnp.where(step == 1, y, jnp.where(step == 2, z, jnp.where(step == 3, core, chip == 0)))
    ).astype(jnp.int32)

    together = lax.optimization_barrier
    away, wave, counts, lists, *pieces = grid_call(
        False, 0, ngrid, capacity, dest_slab[:, 0], place, intensities, gridding, table["packed"], spectral_weights
    )
    members = (counts, lists, place, wave, gridding)
    arrived = swap(away)
    weights = exchange(pieces, (0, 0))
    axes = [[order[stage] for order in ORDERS] for stage in range(3)]
    quarter = lambda a: [p.reshape(p.shape[1:]) for p in jnp.split(a.reshape((SIDE, -1) + a.shape[1:]), SIDE)]
    least = lambda parts: functools.reduce(jnp.minimum, parts)
    data = []
    for part in range(HALVES):
        kept = grid_call(True, part, ngrid, capacity, *members, arrived)
        if part == 1:
            kept, rows = together((kept, rows))
        data.append(exchange(kept, axes[0]))
        if part == 0:
            kept, weights = together((kept, weights))
            rows = call(weight_kernel, [(SIDE**2, 16, size)] * SIDE, *weights, place)
            arrived, rows = together((arrived, rows))
    rows = exchange(rows, axes[0])
    held = summed([a[:, :8] for a in rows])
    ends = least([a[:, 8:] for a in rows])
    parts = quarter(jnp.concatenate([summed(data[0]), summed(data[1]), held, ends], 1))
    for stage in (1, 2):
        parts = exchange(parts, axes[stage])
        parts = [
            summed([a[:, :size] for a in parts]),
            jnp.concatenate([a[:, size:-8] for a in parts], 1),
            least([a[:, -8:] for a in parts]),
        ]
        parts = jnp.concatenate(parts, 1)
        parts = quarter(parts) if stage == 1 else parts[0]
    real, imag, scaled, ends, send = call(
        moment_kernel, [square, square, square, (8, size), square],
        parts, swap(parts), place, table["lanes"], table["rows"], table["mirror"],
    )
    sums = lax.all_to_all(send.reshape(count, 1, size), ALL, 0, 0, tiled=True).reshape(count, size)
    back, gain = call(
        functools.partial(solve_kernel, scale=1.0 / size**3), [(ndp * 2 * size, size), (8, size)],
        sums, ends, scaled, real, imag, table["lanes"], table["rows"],
    )
    landed = lax.all_to_all(back.reshape(count, 2 * planes, size), ALL, 0, 0, tiled=True)
    return tuple(
        call(
            output_kernel, [(planes, size, size)] * 2,
            landed.reshape(count * 2 * planes, size), gain, table["back"],
        )
    )


def solution(mesh):
    return jax.shard_map(
        body,
        mesh=mesh,
        in_specs=(
            P(("dp", "grid"), None, None),
            P(("dp", "grid"), None, None),
            P(("dp", "grid"), None),
            P("dp", None, "grid", None),
        ),
        out_specs=(P("grid", None, None), P("grid", None, None)),
        check_vma=False,
    )
```

```python
import functools

import jax
import jax.numpy as jnp
import numpy as np
from jax import lax
from jax.experimental import pallas as pl
from jax.experimental.pallas import tpu as pltpu
from jax.sharding import PartitionSpec as P


ITERS = 8
MOMENTS = 2 * ITERS + 1
LOW_LANE = 64
ALL = ("dp", "grid")
HIGHEST = lax.Precision.HIGHEST


def two_sum(a, b):
    s = a + b
    v = s - a
    return s, (a - (s - v)) + (b - v)


def quick_sum(a, b):
    s = a + b
    return s, b - (s - a)


def halves(a):
    c = a * 4097.0
    high = c - (c - a)
    return high, a - high


def two_prod(a, b, a_parts=None, b_parts=None):
    p = a * b
    ah, al = a_parts or halves(a)
    bh, bl = b_parts or halves(b)
    return p, ((ah * bh - p) + ah * bl + al * bh) + al * bl


def dd_add(a, b):
    s, e = two_sum(a[0], b[0])
    return quick_sum(s, e + (a[1] + b[1]))


def dd_mul(a, b):
    p, e = two_prod(a[0], b[0])
    return quick_sum(p, e + (a[0] * b[1] + a[1] * b[0]))


def dd_times(a, b):
    p, e = two_prod(a[0], b)
    return quick_sum(p, e + a[1] * b)


def dd_scale(a, factor):
    return a[0] * factor, a[1] * factor


def dd_neg(a):
    return -a[0], -a[1]


def dd_div(a, b):
    inverse = 1.0 / b[0]
    first = a[0] * inverse
    rest = dd_add(a, dd_neg(dd_times(b, first)))
    return quick_sum(first, rest[0] * inverse)


def dot(a, b):
    return jax.lax.dot_general(
        a, b, (((1,), (0,)), ((), ())), precision=HIGHEST, preferred_element_type=jnp.float32
    )


SIDE = 4
CORES = 2
ORDERS = ((0, 1, 2), (1, 2, 0))


def place_of(device):
    chip = device // CORES
    return chip // SIDE**2, chip % SIDE, (chip // SIDE) % SIDE, device % CORES


def chip_at(x, y, z):
    return (x * SIDE + z) * SIDE + y


def shift_pairs(axes, hop):
    pairs = []
    for device in range(SIDE**3 * CORES):
        place = list(place_of(device))
        axis = axes[place[3]]
        place[axis] = (place[axis] + hop) % (CORES if axis == 3 else SIDE)
        pairs.append((device, chip_at(*place[:3]) * CORES + place[3]))
    return pairs


def held_rows(size):
    chip, core = np.arange(size) // CORES, np.arange(size) % CORES
    return np.where(chip == 0, core * size // 2, np.where(core == 0, chip, size - chip))


def dft_tables(size):
    index = np.arange(size)
    angle = 2.0 * np.pi * ((index[:, None] * index[None, :]) % size) / size
    cos, sin = np.cos(angle), np.sin(angle)
    held = held_rows(size)
    as_f32 = lambda a: np.ascontiguousarray(a, dtype=np.float32)
    half = size // 2
    packed = np.concatenate([cos[:, :half], cos[:, half : half + 1], -sin[:, 1:half]], 1)
    high = packed.astype(jnp.bfloat16)
    low = (packed - high.astype(np.float64)).astype(jnp.bfloat16)
    return dict(
        packed=np.stack([np.concatenate([p[:, :half], q[:, :half]], 1) for p, q in ((high, low), (high[:, half:], low[:, half:]))]),
        lanes=as_f32(np.concatenate([cos, sin], 1)),
        rows=as_f32(np.concatenate([cos, sin], 0)),
        back=as_f32(
            np.concatenate(
                [np.concatenate([cos[held], sin[held]], 1), np.concatenate([-sin[held], cos[held]], 1)], 0
            )
        ),
        mirror=as_f32(((index[:, None] + index[None, :]) % size) == 0),
    )


def dot_as(a, b, left, right):
    return lax.dot_general(
        a, b, (((left,), (right,)), ((), ())), precision=HIGHEST, preferred_element_type=jnp.float32
    )


HALVES = 2
STEPS = 4


def sublane_turn(tiles):
    row = lax.broadcasted_iota(jnp.int32, tiles[0].shape, 0)
    for bit in (4, 2, 1):
        low = (row & bit) == 0
        turned = list(tiles)
        for i in range(8):
            if i & bit == 0:
                a, b = tiles[i], tiles[i + bit]
                turned[i] = jnp.where(low, a, pltpu.roll(b, bit, 0))
                turned[i + bit] = jnp.where(low, pltpu.roll(a, 8 - bit, 0), b)
        tiles = turned
    return tiles


def grid_kernel(*refs, kept, part, capacity):
    if kept:
        count_ref, list_ref, place_ref, wave_ref, matrix_ref, other_ref = refs[:6]
        outs = refs[6:]
    else:
        dest_ref, place_ref, values_ref, matrix_ref, packed_ref, weights_ref = refs[:6]
        out_refs, (kept_wave_ref, count_ref, list_ref), wave_ref = refs[6:8], refs[8:11], refs[-1]
    nent, rows, width = matrix_ref.shape
    size = width // SIDE
    half = size // 2
    nslab = count_ref.shape[0]
    step = pl.program_id(0)

    def clear(s, _):
        count_ref[s] = 0
        return 0

    def enter(e, _):
        slab = dest_ref[e]
        taken = count_ref[slab]
        list_ref[slab * capacity + taken] = e
        count_ref[slab] = taken + 1
        return 0

    def prepare():
        lax.fori_loop(0, nslab, clear, 0)
        lax.fori_loop(0, nent, enter, 0)
        for r, slice_ref in enumerate(refs[11:-1]):
            slice_ref[...] = weights_ref[0, :, (place_ref[0] + r) % SIDE, :]
        chip = lax.broadcasted_iota(jnp.int32, (half, half), 0)
        slot = lax.broadcasted_iota(jnp.int32, (half, half), 1)
        digits = digits_of(slot)
        pieces = []
        chips = [chip_at(*moved(place_ref, digits, owner, 1)) for owner in range(CORES)]
        for owner in (1 - place_ref[3], place_ref[3]):
            pick = (chip == jnp.where(owner == 0, chips[0], chips[1])).astype(jnp.float32).astype(jnp.bfloat16)
            for start in (0, half):
                piece = packed_ref[owner, :, start : start + half]
                pieces.append(jnp.dot(piece, pick, preferred_element_type=jnp.float32).astype(jnp.bfloat16))
        both = jnp.dot(
            values_ref[...].reshape(nent * rows, size),
            jnp.concatenate(pieces, 1),
            preferred_element_type=jnp.float32,
        )
        for at, target_ref in ((0, wave_ref), (size, kept_wave_ref)):
            wave = both[:, at : at + half] + both[:, at + half : at + size]
            high = wave.astype(jnp.bfloat16)
            low = (wave - high.astype(jnp.float32)).astype(jnp.bfloat16)
            target_ref[...] = jnp.concatenate([high, low], 1).reshape(nent, rows, size)

    if not kept:
        pl.when(step == 0)(prepare)

    pairs = nslab // (2 * STEPS)

    def products(out):
        for pair in range(pairs):
            halves_of_tile = []
            for near in range(2):
                slab = ((part * (STEPS // HALVES) + step) * pairs + pair) * 2 + near
                taken = count_ref[slab]
                waves, matrices = [], []
                for m in range(capacity):
                    entry = jnp.where(m < taken, list_ref[slab * capacity + m], 0)
                    wave = wave_ref[entry]
                    waves.append(jnp.where(m < taken, wave, jnp.zeros_like(wave)))
                    matrices.append(matrix_ref[entry])
                product = lax.dot_general(
                    jnp.concatenate(waves, 0),
                    jnp.concatenate(matrices, 0),
                    (((0,), (0,)), ((), ())),
                    preferred_element_type=jnp.float32,
                )
                halves_of_tile.append(product[:half] + product[half:])
            place = slice(pair * 8, pair * 8 + 8)
            for start in range(0, half, 8):
                tiles = [
                    product[start : start + 8, p * size : (p + 1) * size]
                    for product in halves_of_tile
                    for p in range(SIDE)
                ]
                for index, block in enumerate(sublane_turn(tiles), start):
                    out(index, place, block)

    def keep(index, place, block):
        outs[index // SIDE**2][index % SIDE**2, place, :] = block + other_ref[index, place, :]

    def send(out_ref):
        def write(index, place, block):
            out_ref[index, place, :] = block

        return write

    if kept:
        products(keep)
    else:
        pl.when(step < STEPS // HALVES)(lambda: products(send(out_refs[0])))
        pl.when(step >= STEPS // HALVES)(lambda: products(send(out_refs[1])))


def grid_call(kept, part, nslab, capacity, *args):
    scalars = pl.BlockSpec(memory_space=pltpu.SMEM)
    fixed = lambda shape: pl.BlockSpec(shape, lambda i: (0,) * len(shape))
    matrix = args[4] if kept else args[3]
    nent, rows, width = matrix.shape
    size, blocks = width // SIDE, SIDE**3
    steps = STEPS // HALVES if kept else STEPS
    moving = lambda count: pl.BlockSpec((count, size // STEPS, size), lambda i: (0, i, 0))
    f32 = lambda *shape: jax.ShapeDtypeStruct(shape, jnp.float32)
    in_specs = [scalars if a.dtype == jnp.int32 else fixed(a.shape) for a in args]
    if kept:
        out_shape, out_specs = [f32(SIDE**2, size // HALVES, size)] * SIDE, [moving(SIDE**2)] * SIDE
        in_specs[-1] = moving(blocks)
        scratch = []
    else:
        wave = (nent, rows, size)
        out_shape = [f32(blocks, size // HALVES, size)] * HALVES + [
            jax.ShapeDtypeStruct(wave, jnp.bfloat16),
            jax.ShapeDtypeStruct((nslab,), jnp.int32),
            jax.ShapeDtypeStruct((nslab * capacity,), jnp.int32),
        ] + [f32(size, size)] * SIDE
        block = (blocks, size // STEPS, size)
        out_specs = [
            pl.BlockSpec(block, lambda i: (0, jnp.minimum(i, STEPS // HALVES - 1), 0)),
            pl.BlockSpec(block, lambda i: (0, jnp.maximum(i - STEPS // HALVES, 0), 0)),
        ] + [fixed(wave), scalars, scalars] + [fixed((size, size))] * SIDE
        scratch = [pltpu.VMEM(wave, jnp.bfloat16)]
    return pl.pallas_call(
        functools.partial(grid_kernel, kept=kept, part=part, capacity=capacity),
        grid=(steps,),
        out_shape=out_shape,
        in_specs=in_specs,
        out_specs=out_specs,
        scratch_shapes=scratch,
    )(*args)


def moved(place_ref, digits, owner, sign):
    at = [place_ref[0], place_ref[1], place_ref[2]]
    for digit, axis in zip(digits, ORDERS[owner]):
        at[axis] = (at[axis] + sign * digit + SIDE) % SIDE
    return at


def digits_of(index):
    return index // SIDE**2, (index // SIDE) % SIDE, index % SIDE


def weight_kernel(w0_ref, w1_ref, w2_ref, w3_ref, place_ref, *outs):
    size = w0_ref.shape[0]
    half = size // 2
    own = ((w0_ref[...] + w1_ref[...]) + w2_ref[...]) + w3_ref[...]
    low = jnp.min(jnp.min(own, axis=0, keepdims=True), axis=1, keepdims=True)
    high = jnp.max(jnp.max(own, axis=0, keepdims=True), axis=1, keepdims=True)
    row = lax.broadcasted_iota(jnp.int32, (size, size), 0)
    lane = lax.broadcasted_iota(jnp.int32, (size, size), 1)
    chips = [chip_at(*moved(place_ref, digits_of(row % half), owner, 1)) for owner in range(CORES)]
    chip = jnp.where(place_ref[3] == 0, chips[0], chips[1])
    negative = jnp.where(chip == 0, half, size - chip)
    pick = (lane == jnp.where(row < half, chip, negative)).astype(jnp.float32)
    rows = dot_as(pick, own, 1, 1)
    ends = jnp.where(lax.broadcasted_iota(jnp.int32, (8, size), 1) < half, low, -high)
    count = half // SIDE
    for r, out_ref in enumerate(outs):
        out_ref[:, 0:8, :] = jnp.zeros((count, 8, size), jnp.float32)
        out_ref[:, 8:16, :] = jnp.broadcast_to(ends[None], (count, 8, size))
        for sign in range(2):
            at = sign * half + r * count
            out_ref[:, 2 * r + sign, :] = rows[at : at + count]


def sublane_total(a):
    for shift in (4, 2, 1):
        a = dd_add(a, (pltpu.roll(a[0], shift, 0), pltpu.roll(a[1], shift, 0)))
    return a


def lane_total(a):
    for shift in (64, 32, 16, 8, 4, 2, 1):
        a = dd_add(a, (pltpu.roll(a[0], shift, 1), pltpu.roll(a[1], shift, 1)))
    return a


def moment_kernel(
    own_ref, other_ref, place_ref, lanes_ref, rows_ref, mirror_ref, real_ref, imag_ref, scaled_ref, range_ref, send_ref
):
    size = scaled_ref.shape[0]
    second, alone = place_ref[3] == 1, place_ref[4] == 1
    lane8 = lax.broadcasted_iota(jnp.int32, (8, size), 1)
    ends = jnp.minimum(own_ref[2 * size :, :], other_ref[2 * size :, :])
    least = lambda v: jnp.min(jnp.min(v, axis=0, keepdims=True), axis=1, keepdims=True)
    low = least(jnp.where(lane8 < size // 2, ends, 1e30))
    high = -least(jnp.where(lane8 < size // 2, 1e30, ends))
    span = jnp.broadcast_to(jnp.maximum((high - low) * 0.5, high * 1e-4), (1, size))
    centre = jnp.broadcast_to((high + low) * 0.5, (1, size)) / span
    range_ref[0:1, :] = span
    range_ref[1:2, :] = centre
    range_ref[2:8, :] = jnp.zeros((6, size), jnp.float32)

    ky = lax.broadcasted_iota(jnp.int32, (size, size), 0)
    row = lax.broadcasted_iota(jnp.int32, (size, size), 1)
    found = row // 2
    back = (found % SIDE, (found // SIDE) % SIDE, found // SIDE**2)
    sources = []
    for owner in range(CORES):
        x, y, z = moved(place_ref, back, owner, -1)
        sources.append(SIDE * (z * (SIDE * CORES) + y * CORES + owner) + x)
    from_own = jnp.where(second, sources[1], sources[0])
    from_other = jnp.where(second, sources[0], sources[1])
    given = jnp.concatenate([own_ref[size : 2 * size, :], other_ref[size : 2 * size, :]], 0)
    picks = [
        jnp.concatenate(
            [jnp.where(row % 2 == sign, (ky == source).astype(jnp.float32), 0.0) for source in (from_own, from_other)], 1
        )
        for sign in range(2)
    ]
    signs = dot(jnp.concatenate(picks, 0), given)
    plus, minus = signs[:size], signs[size:]
    mine = jnp.where(second, minus, plus)
    partner = jnp.where(alone, mine, jnp.where(second, plus, minus))
    scaled = (mine + dot(dot(mirror_ref[...], partner), mirror_ref[...])) * 0.5 / span
    scaled_ref[...] = scaled.T

    mine, theirs = own_ref[:size, :], other_ref[:size, :]
    re = jnp.where(jnp.logical_and(second, jnp.logical_not(alone)), theirs, mine)
    im = jnp.where(alone, jnp.zeros_like(mine), jnp.where(second, -mine, theirs))
    ends = dot(jnp.concatenate([re, im], 0), lanes_ref[...])
    mid_real = ends[:size, :size] + ends[size:, size:]
    mid_imag = ends[size:, :size] - ends[:size, size:]
    both = dot(rows_ref[...], jnp.concatenate([mid_real, mid_imag], 1))
    real = both[:size, :size] + both[size:, size:]
    imag = both[:size, size:] - both[size:, :size]
    real_ref[...] = real
    imag_ref[...] = imag
    scaled = scaled_ref[...]
    power = real * real + imag * imag
    chunk = 24
    totals = [None] * MOMENTS
    for start in range(0, size // 2 + 8, chunk):
        row = lax.broadcasted_iota(jnp.int32, (chunk, size), 0) + start
        share = jnp.where(row % (size // 2) == 0, 1.0, jnp.where(row < size // 2, 2.0, 0.0))
        t = scaled[start : start + chunk] - centre
        p = power[start : start + chunk] * share
        p_parts = halves(p)
        t2 = t * 2.0
        t2_parts = halves(t2)
        zero = jnp.zeros_like(t)
        before, here = (jnp.ones_like(t), zero), (t, zero)
        for order in range(MOMENTS):
            value = before
            v_parts = halves(value[0])
            term, low_term = two_prod(value[0], p, v_parts, p_parts)
            term = (term, low_term + value[1] * p)
            total, spill = totals[order] or (None, None)
            for i in range(0, chunk, 8):
                piece, rest = term[0][i : i + 8], term[1][i : i + 8]
                if total is None:
                    total, spill = piece, rest
                else:
                    total, lost = two_sum(total, piece)
                    spill = spill + (lost + rest)
            totals[order] = total, spill
            if order + 1 < MOMENTS:
                up, low_up = two_prod(here[0], t2, None, t2_parts)
                following, lost = two_sum(up, -before[0])
                before, here = here, (following, lost + ((low_up + here[1] * t2) - before[1]))
    row = lax.broadcasted_iota(jnp.int32, (8, size), 0)
    lane = lax.broadcasted_iota(jnp.int32, (8, size), 1)
    out = jnp.zeros((8, size), jnp.float32)
    for base in range(0, MOMENTS, 8):
        high_rows = jnp.zeros((8, size), jnp.float32)
        low_rows = jnp.zeros((8, size), jnp.float32)
        for order in range(base, min(base + 8, MOMENTS)):
            total = sublane_total(quick_sum(*totals[order]))
            high_rows = jnp.where(row == order - base, total[0], high_rows)
            low_rows = jnp.where(row == order - base, total[1], low_rows)
        high_rows, low_rows = lane_total((high_rows, low_rows))
        out = jnp.where(lane == row + base, high_rows, out)
        out = jnp.where(lane == row + (base + LOW_LANE), low_rows, out)
    line = jnp.sum(out, axis=0, keepdims=True)
    send_ref[...] = jnp.broadcast_to(line, (size, size))


def lane_of(a, lane):
    pick = lambda v: jnp.broadcast_to(v[:, lane : lane + 1], v.shape)
    return pick(a[0]), pick(a[1])


def solve_kernel(
    sums_ref, range_ref, scaled_ref, real_ref, imag_ref, lanes_ref, rows_ref, out_ref, gain_ref, *, scale
):
    size = scaled_ref.shape[0]
    given = sums_ref[...]
    low = pltpu.roll(given, size - LOW_LANE, 1)
    rows = [(given[i : i + 8], low[i : i + 8]) for i in range(0, given.shape[0], 8)]
    while len(rows) > 1:
        rows = [dd_add(rows[i], rows[i + 1]) for i in range(0, len(rows), 2)]
    moments = sublane_total(rows[0])
    half = range_ref[0:1, :]
    centre = jnp.broadcast_to(range_ref[1:2, :], moments[0].shape)
    centre = (centre, jnp.zeros_like(centre))
    lane = lax.broadcasted_iota(jnp.int32, moments[0].shape, 1)
    resid, direct = moments, moments
    held = lane_of(resid, 0)
    steps, turns = [], []
    decay = jnp.ones((1, size), jnp.float32)
    for k in range(ITERS):
        after = tuple(pltpu.roll(v, size - 1, 1) for v in direct)
        prior = tuple(pltpu.roll(v, 1, 1) for v in direct)
        prior = tuple(jnp.where(lane == 0, a, p) for a, p in zip(after, prior))
        image = dd_add(dd_mul(direct, centre), dd_scale(dd_add(after, prior), 0.5))
        alpha = dd_div(held, lane_of(image, k))
        fresh = dd_add(resid, dd_neg(dd_mul(alpha, image)))
        reached = lane_of(fresh, k + 1)
        beta = dd_mul(alpha, dd_div(reached, held))
        held = reached
        beta = dd_scale(beta, -1.0 if k == 0 else -0.5)
        direct = dd_add(fresh, dd_mul(beta, direct))
        resid = fresh
        steps.append(alpha[0][0:1])
        turns.append(beta[0][0:1])
        decay = decay * beta[0][0:1]
    gain = lax.rsqrt(jnp.maximum(jnp.abs(decay), 1e-30)) / centre[0][0:1]
    gain_ref[...] = jnp.broadcast_to(gain, gain_ref.shape)
    scaled = scaled_ref[...]
    field = steps[0]
    solved = jnp.broadcast_to(field, scaled.shape)
    left = 1.0 - field * scaled
    toward = left + turns[0]
    for k in range(1, ITERS):
        solved = solved + steps[k] * toward
        left = left - steps[k] * (scaled * toward)
        if k + 1 < ITERS:
            toward = left + turns[k] * toward
    solved = solved * (scale / half)
    left = left * (gain * scale)
    real, imag = real_ref[...], imag_ref[...]
    back_real = solved * real - left * imag
    back_imag = solved * imag + left * real
    ends = dot(jnp.concatenate([back_real, back_imag], 0), lanes_ref[...])
    mid_real = ends[:size, :size] - ends[size:, size:]
    mid_imag = ends[size:, :size] + ends[:size, size:]
    both = dot(rows_ref[...], jnp.concatenate([mid_real, mid_imag], 1))
    real = both[:size, :size] - both[size:, size:]
    imag = both[:size, size:] + both[size:, :size]
    for copy in range(out_ref.shape[0] // (2 * size)):
        out_ref[pl.ds(copy * 2 * size, size, stride=2), :] = real
        out_ref[pl.ds(copy * 2 * size + 1, size, stride=2), :] = imag


def output_kernel(given_ref, gain_ref, back_ref, field_ref, resid_ref):
    planes, size = field_ref.shape[0], field_ref.shape[1]
    step = 2 * planes
    shrink = 1.0 / gain_ref[0:1, :]
    for j in range(planes):
        pieces = [given_ref[pl.ds(2 * j + part, size, stride=step), :] for part in range(2)]
        both = dot_as(jnp.concatenate(pieces, 0), back_ref[...], 0, 0)
        field_ref[j] = both[:, :size]
        resid_ref[j] = both[:, size:] * shrink


def call(kernel, shapes, *args):
    whole = pl.BlockSpec(memory_space=pltpu.VMEM)
    scalars = pl.BlockSpec(memory_space=pltpu.SMEM)
    return pl.pallas_call(
        kernel,
        out_shape=[jax.ShapeDtypeStruct(s, jnp.float32) for s in shapes],
        in_specs=[scalars if a.dtype == jnp.int32 else whole for a in args],
        out_specs=[whole] * len(shapes),
    )(*args)


def exchange(parts, axes):
    return [parts[0]] + [lax.ppermute(parts[r], ALL, shift_pairs(axes, r)) for r in range(1, SIDE)]


def summed(parts):
    return ((parts[0] + parts[1]) + parts[2]) + parts[3]


def body(intensities, gridding, dest_slab, spectral_weights):
    ngrid = lax.axis_size("grid")
    ndp = lax.axis_size("dp")
    nent, rows, size = intensities.shape
    planes = gridding.shape[2] // size
    count = ngrid * ndp
    capacity = max(2, 2 * nent // ngrid)
    table = dft_tables(size)
    square = (size, size)
    swap = lambda a: lax.ppermute(a, ALL, shift_pairs((3, 3), 1))

    chip = lax.axis_index("dp") * (ngrid // CORES) + lax.axis_index("grid") // CORES
    core = lax.axis_index("grid") % CORES
    step = jnp.arange(5, dtype=jnp.int32)
    x, y, z = place_of(chip * CORES)[:3]
    place = jnp.where(
        step == 0, x, jnp.where(step == 1, y, jnp.where(step == 2, z, jnp.where(step == 3, core, chip == 0)))
    ).astype(jnp.int32)

    together = lax.optimization_barrier
    *away, wave, counts, lists, p0, p1, p2, p3 = grid_call(
        False, 0, ngrid, capacity, dest_slab[:, 0], place, intensities, gridding, table["packed"], spectral_weights
    )
    members = (counts, lists, place, wave, gridding)
    arrived = [swap(a) for a in away]
    weights = exchange([p0, p1, p2, p3], (0, 0))
    axes = [[order[stage] for order in ORDERS] for stage in range(3)]
    quarter = lambda a: [p.reshape(p.shape[1:]) for p in jnp.split(a.reshape((SIDE, -1) + a.shape[1:]), SIDE)]
    least = lambda parts: functools.reduce(jnp.minimum, parts)
    data = []
    for part in range(HALVES):
        kept = grid_call(True, part, ngrid, capacity, *members, arrived[part])
        data.append(exchange(kept, axes[0]))
    kept, weights = together((kept, weights))
    rows = call(weight_kernel, [(SIDE**2, 16, size)] * SIDE, *weights, place)
    rows = exchange(rows, axes[0])
    held = summed([a[:, :8] for a in rows])
    ends = least([a[:, 8:] for a in rows])
    parts = quarter(jnp.concatenate([summed(data[0]), summed(data[1]), held, ends], 1))
    for stage in (1, 2):
        parts = exchange(parts, axes[stage])
        parts = [
            summed([a[:, :size] for a in parts]),
            jnp.concatenate([a[:, size:-8] for a in parts], 1),
            least([a[:, -8:] for a in parts]),
        ]
        parts = jnp.concatenate(parts, 1)
        parts = quarter(parts) if stage == 1 else parts[0]
    real, imag, scaled, ends, send = call(
        moment_kernel, [square, square, square, (8, size), square],
        parts, swap(parts), place, table["lanes"], table["rows"], table["mirror"],
    )
    sums = lax.all_to_all(send.reshape(count, 1, size), ALL, 0, 0, tiled=True).reshape(count, size)
    back, gain = call(
        functools.partial(solve_kernel, scale=1.0 / size**3), [(ndp * 2 * size, size), (8, size)],
        sums, ends, scaled, real, imag, table["lanes"], table["rows"],
    )
    landed = lax.all_to_all(back.reshape(count, 2 * planes, size), ALL, 0, 0, tiled=True)
    return tuple(
        call(
            output_kernel, [(planes, size, size)] * 2,
            landed.reshape(count * 2 * planes, size), gain, table["back"],
        )
    )


def solution(mesh):
    return jax.shard_map(
        body,
        mesh=mesh,
        in_specs=(
            P(("dp", "grid"), None, None),
            P(("dp", "grid"), None, None),
            P(("dp", "grid"), None),
            P("dp", None, "grid", None),
        ),
        out_specs=(P("grid", None, None), P("grid", None, None)),
        check_vma=False,
    )
```

```python
import functools

import jax
import jax.numpy as jnp
import numpy as np
from jax import lax
from jax.experimental import pallas as pl
from jax.experimental.pallas import tpu as pltpu
from jax.sharding import PartitionSpec as P


ITERS = 8
MOMENTS = 2 * ITERS + 1
LOW_LANE = 64
ALL = ("dp", "grid")
HIGHEST = lax.Precision.HIGHEST


def two_sum(a, b):
    s = a + b
    v = s - a
    return s, (a - (s - v)) + (b - v)


def quick_sum(a, b):
    s = a + b
    return s, b - (s - a)


def halves(a):
    c = a * 4097.0
    high = c - (c - a)
    return high, a - high


def two_prod(a, b, a_parts=None, b_parts=None):
    p = a * b
    ah, al = a_parts or halves(a)
    bh, bl = b_parts or halves(b)
    return p, ((ah * bh - p) + ah * bl + al * bh) + al * bl


def dd_add(a, b):
    s, e = two_sum(a[0], b[0])
    return quick_sum(s, e + (a[1] + b[1]))


def dd_mul(a, b):
    p, e = two_prod(a[0], b[0])
    return quick_sum(p, e + (a[0] * b[1] + a[1] * b[0]))


def dd_times(a, b):
    p, e = two_prod(a[0], b)
    return quick_sum(p, e + a[1] * b)


def dd_scale(a, factor):
    return a[0] * factor, a[1] * factor


def dd_neg(a):
    return -a[0], -a[1]


def dd_div(a, b):
    inverse = 1.0 / b[0]
    first = a[0] * inverse
    rest = dd_add(a, dd_neg(dd_times(b, first)))
    return quick_sum(first, rest[0] * inverse)


def dot(a, b):
    return jax.lax.dot_general(
        a, b, (((1,), (0,)), ((), ())), precision=HIGHEST, preferred_element_type=jnp.float32
    )


SIDE = 4
CORES = 2
ORDERS = ((0, 2, 1), (1, 2, 0))


def place_of(device):
    chip = device // CORES
    return chip // SIDE**2, chip % SIDE, (chip // SIDE) % SIDE, device % CORES


def chip_at(x, y, z):
    return (x * SIDE + z) * SIDE + y


def shift_pairs(axes, hop):
    pairs = []
    for device in range(SIDE**3 * CORES):
        place = list(place_of(device))
        axis = axes[place[3]]
        place[axis] = (place[axis] + hop) % (CORES if axis == 3 else SIDE)
        pairs.append((device, chip_at(*place[:3]) * CORES + place[3]))
    return pairs


def held_rows(size):
    chip, core = np.arange(size) // CORES, np.arange(size) % CORES
    return np.where(chip == 0, core * size // 2, np.where(core == 0, chip, size - chip))


def dft_tables(size):
    index = np.arange(size)
    angle = 2.0 * np.pi * ((index[:, None] * index[None, :]) % size) / size
    cos, sin = np.cos(angle), np.sin(angle)
    held = held_rows(size)
    as_f32 = lambda a: np.ascontiguousarray(a, dtype=np.float32)
    half = size // 2
    packed = np.concatenate([cos[:, :half], cos[:, half : half + 1], -sin[:, 1:half]], 1)
    high = packed.astype(jnp.bfloat16)
    low = (packed - high.astype(np.float64)).astype(jnp.bfloat16)
    lanes, rows = np.concatenate([cos, sin], 1), np.concatenate([cos, sin], 0)
    back = np.concatenate(
        [np.concatenate([cos[held], sin[held]], 1), np.concatenate([-sin[held], cos[held]], 1)], 0
    )

    def thrice(table, axis):
        above = table.astype(jnp.bfloat16)
        below = (table - above.astype(np.float64)).astype(jnp.bfloat16)
        return np.concatenate([above, above, below], axis)

    return dict(
        packed=np.stack([np.concatenate([p[:, :half], q[:, :half]], 1) for p, q in ((high, low), (high[:, half:], low[:, half:]))]),
        lanes=as_f32(lanes),
        rows=as_f32(rows),
        lanes_pieces=thrice(lanes, 0),
        rows_pieces=thrice(rows, 1),
        back_pieces=thrice(back, 0),
        mirror=(((index[:, None] + index[None, :]) % size) == 0).astype(jnp.bfloat16),
    )


def dot_as(a, b, left, right):
    return lax.dot_general(
        a, b, (((left,), (right,)), ((), ())), precision=HIGHEST, preferred_element_type=jnp.float32
    )


def pieces_of(a, count):
    found = []
    for _ in range(count):
        piece = a.astype(jnp.bfloat16)
        found.append(piece)
        a = a - piece.astype(jnp.float32)
    return found


def dot_pieces(a, b, left, right):
    return lax.dot_general(a, b, (((left,), (right,)), ((), ())), preferred_element_type=jnp.float32)


def stacked(a, axis):
    high, low = pieces_of(a, 2)
    return jnp.concatenate([high, low, high], axis)


def select_rows(one_hot, a):
    width = a.shape[1]
    found = dot_pieces(one_hot, jnp.concatenate(pieces_of(a, 3), 1), 1, 0)
    return (found[:, :width] + found[:, width : 2 * width]) + found[:, 2 * width :]


def select_lanes(a, one_hot):
    height = a.shape[0]
    found = dot_pieces(jnp.concatenate(pieces_of(a, 3), 0), one_hot, 1, 0)
    return (found[:height] + found[height : 2 * height]) + found[2 * height :]


HALVES = 2
STEPS = 4


def sublane_turn(tiles):
    row = lax.broadcasted_iota(jnp.int32, tiles[0].shape, 0)
    for bit in (4, 2, 1):
        low = (row & bit) == 0
        turned = list(tiles)
        for i in range(8):
            if i & bit == 0:
                a, b = tiles[i], tiles[i + bit]
                turned[i] = jnp.where(low, a, pltpu.roll(b, bit, 0))
                turned[i + bit] = jnp.where(low, pltpu.roll(a, 8 - bit, 0), b)
        tiles = turned
    return tiles


def grid_kernel(*refs, kept, part, capacity):
    if kept:
        count_ref, list_ref, place_ref, wave_ref, matrix_ref, other_ref = refs[:6]
        outs = refs[6:]
    else:
        dest_ref, place_ref, values_ref, matrix_ref, packed_ref, weights_ref = refs[:6]
        out_refs, (kept_wave_ref, count_ref, list_ref), wave_ref = refs[6:8], refs[8:11], refs[-1]
    nent, rows, width = matrix_ref.shape
    size = width // SIDE
    half = size // 2
    nslab = count_ref.shape[0]
    step = pl.program_id(0)

    def clear(s, _):
        count_ref[s] = 0
        return 0

    def enter(e, _):
        slab = dest_ref[e]
        taken = count_ref[slab]
        list_ref[slab * capacity + taken] = e
        count_ref[slab] = taken + 1
        return 0

    def prepare():
        lax.fori_loop(0, nslab, clear, 0)
        lax.fori_loop(0, nent, enter, 0)
        for r, slice_ref in enumerate(refs[11:-1]):
            slice_ref[...] = weights_ref[0, :, (place_ref[0] + r) % SIDE, :]
        chip = lax.broadcasted_iota(jnp.int32, (half, half), 0)
        slot = lax.broadcasted_iota(jnp.int32, (half, half), 1)
        digits = digits_of(slot)
        pieces = []
        chips = [chip_at(*moved(place_ref, digits, owner, 1)) for owner in range(CORES)]
        for owner in (1 - place_ref[3], place_ref[3]):
            pick = (chip == jnp.where(owner == 0, chips[0], chips[1])).astype(jnp.float32).astype(jnp.bfloat16)
            for start in (0, half):
                piece = packed_ref[owner, :, start : start + half]
                pieces.append(jnp.dot(piece, pick, preferred_element_type=jnp.float32).astype(jnp.bfloat16))
        both = jnp.dot(
            values_ref[...].reshape(nent * rows, size),
            jnp.concatenate(pieces, 1),
            preferred_element_type=jnp.float32,
        )
        for at, target_ref in ((0, wave_ref), (size, kept_wave_ref)):
            wave = both[:, at : at + half] + both[:, at + half : at + size]
            high = wave.astype(jnp.bfloat16)
            low = (wave - high.astype(jnp.float32)).astype(jnp.bfloat16)
            target_ref[...] = jnp.concatenate([high, low], 1).reshape(nent, rows, size)

    if not kept:
        pl.when(step == 0)(prepare)

    pairs = nslab // (2 * STEPS)

    def products(out):
        for pair in range(pairs):
            halves_of_tile = []
            for near in range(2):
                slab = ((part * (STEPS // HALVES) + step) * pairs + pair) * 2 + near
                taken = count_ref[slab]
                waves, matrices = [], []
                for m in range(capacity):
                    entry = jnp.where(m < taken, list_ref[slab * capacity + m], 0)
                    wave = wave_ref[entry]
                    waves.append(jnp.where(m < taken, wave, jnp.zeros_like(wave)))
                    matrices.append(matrix_ref[entry])
                product = lax.dot_general(
                    jnp.concatenate(waves, 0),
                    jnp.concatenate(matrices, 0),
                    (((0,), (0,)), ((), ())),
                    preferred_element_type=jnp.float32,
                )
                halves_of_tile.append(product[:half] + product[half:])
            place = slice(pair * 8, pair * 8 + 8)
            for start in range(0, half, 8):
                tiles = [
                    product[start : start + 8, p * size : (p + 1) * size]
                    for product in halves_of_tile
                    for p in range(SIDE)
                ]
                for index, block in enumerate(sublane_turn(tiles), start):
                    out(index, place, block)

    def keep(index, place, block):
        outs[index // SIDE**2][index % SIDE**2, place, :] = block + other_ref[index, place, :]

    def send(out_ref):
        def write(index, place, block):
            out_ref[index, place, :] = block

        return write

    if kept:
        products(keep)
    else:
        pl.when(step < STEPS // HALVES)(lambda: products(send(out_refs[0])))
        pl.when(step >= STEPS // HALVES)(lambda: products(send(out_refs[1])))


def grid_call(kept, part, nslab, capacity, *args):
    scalars = pl.BlockSpec(memory_space=pltpu.SMEM)
    fixed = lambda shape: pl.BlockSpec(shape, lambda i: (0,) * len(shape))
    matrix = args[4] if kept else args[3]
    nent, rows, width = matrix.shape
    size, blocks = width // SIDE, SIDE**3
    steps = STEPS // HALVES if kept else STEPS
    moving = lambda count: pl.BlockSpec((count, size // STEPS, size), lambda i: (0, i, 0))
    f32 = lambda *shape: jax.ShapeDtypeStruct(shape, jnp.float32)
    in_specs = [scalars if a.dtype == jnp.int32 else fixed(a.shape) for a in args]
    if kept:
        out_shape, out_specs = [f32(SIDE**2, size // HALVES, size)] * SIDE, [moving(SIDE**2)] * SIDE
        in_specs[-1] = moving(blocks)
        scratch = []
    else:
        wave = (nent, rows, size)
        out_shape = [f32(blocks, size // HALVES, size)] * HALVES + [
            jax.ShapeDtypeStruct(wave, jnp.bfloat16),
            jax.ShapeDtypeStruct((nslab,), jnp.int32),
            jax.ShapeDtypeStruct((nslab * capacity,), jnp.int32),
        ] + [f32(size, size)] * SIDE
        block = (blocks, size // STEPS, size)
        out_specs = [
            pl.BlockSpec(block, lambda i: (0, jnp.minimum(i, STEPS // HALVES - 1), 0)),
            pl.BlockSpec(block, lambda i: (0, jnp.maximum(i - STEPS // HALVES, 0), 0)),
        ] + [fixed(wave), scalars, scalars] + [fixed((size, size))] * SIDE
        scratch = [pltpu.VMEM(wave, jnp.bfloat16)]
    return pl.pallas_call(
        functools.partial(grid_kernel, kept=kept, part=part, capacity=capacity),
        grid=(steps,),
        out_shape=out_shape,
        in_specs=in_specs,
        out_specs=out_specs,
        scratch_shapes=scratch,
    )(*args)


def moved(place_ref, digits, owner, sign):
    at = [place_ref[0], place_ref[1], place_ref[2]]
    for digit, axis in zip(digits, ORDERS[owner]):
        at[axis] = (at[axis] + sign * digit + SIDE) % SIDE
    return at


def digits_of(index):
    return index // SIDE**2, (index // SIDE) % SIDE, index % SIDE


def weight_kernel(w0_ref, w1_ref, w2_ref, w3_ref, place_ref, *outs):
    size = w0_ref.shape[0]
    half = size // 2
    own = ((w0_ref[...] + w1_ref[...]) + w2_ref[...]) + w3_ref[...]
    low = jnp.min(jnp.min(own, axis=0, keepdims=True), axis=1, keepdims=True)
    high = jnp.max(jnp.max(own, axis=0, keepdims=True), axis=1, keepdims=True)
    row = lax.broadcasted_iota(jnp.int32, (size, size), 0)
    lane = lax.broadcasted_iota(jnp.int32, (size, size), 1)
    chips = [chip_at(*moved(place_ref, digits_of(row % half), owner, 1)) for owner in range(CORES)]
    chip = jnp.where(place_ref[3] == 0, chips[0], chips[1])
    negative = jnp.where(chip == 0, half, size - chip)
    pick = (lane == jnp.where(row < half, chip, negative)).astype(jnp.float32)
    rows = dot_as(pick, own, 1, 1)
    ends = jnp.where(lax.broadcasted_iota(jnp.int32, (8, size), 1) < half, low, -high)
    count = half // SIDE
    for r, out_ref in enumerate(outs):
        out_ref[...] = jnp.zeros(out_ref.shape, jnp.float32)
        out_ref[8 * count :, :] = ends
        for sign in range(2):
            at = sign * half + r * count
            out_ref[pl.ds(2 * r + sign, count, stride=8), :] = rows[at : at + count]


def sublane_total(a):
    for shift in (4, 2, 1):
        a = dd_add(a, (pltpu.roll(a[0], shift, 0), pltpu.roll(a[1], shift, 0)))
    return a


def lane_total(a):
    for shift in (64, 32, 16, 8, 4, 2, 1):
        a = dd_add(a, (pltpu.roll(a[0], shift, 1), pltpu.roll(a[1], shift, 1)))
    return a


def moment_kernel(
    own_ref, other_ref, place_ref, lanes_ref, rows_ref, mirror_ref, real_ref, imag_ref, scaled_ref, range_ref, send_ref
):
    size = scaled_ref.shape[0]
    second, alone = place_ref[3] == 1, place_ref[4] == 1
    lane8 = lax.broadcasted_iota(jnp.int32, (8, size), 1)
    ends = jnp.minimum(own_ref[2 * size :, :], other_ref[2 * size :, :])
    least = lambda v: jnp.min(jnp.min(v, axis=0, keepdims=True), axis=1, keepdims=True)
    low = least(jnp.where(lane8 < size // 2, ends, 1e30))
    high = -least(jnp.where(lane8 < size // 2, 1e30, ends))
    span = jnp.broadcast_to(jnp.maximum((high - low) * 0.5, high * 1e-4), (1, size))
    centre = jnp.broadcast_to((high + low) * 0.5, (1, size)) / span
    range_ref[0:1, :] = span
    range_ref[1:2, :] = centre
    range_ref[2:8, :] = jnp.zeros((6, size), jnp.float32)

    ky = lax.broadcasted_iota(jnp.int32, (size, size), 0)
    row = lax.broadcasted_iota(jnp.int32, (size, size), 1)
    found = row // 2
    back = (found % SIDE, (found // SIDE) % SIDE, found // SIDE**2)
    sources = []
    for owner in range(CORES):
        x, y, z = moved(place_ref, back, owner, -1)
        sources.append(SIDE * (z * (SIDE * CORES) + y * CORES + owner) + x)
    from_own = jnp.where(second, sources[1], sources[0])
    from_other = jnp.where(second, sources[0], sources[1])
    given = jnp.concatenate([own_ref[size : 2 * size, :], other_ref[size : 2 * size, :]], 0)
    picks = [
        jnp.concatenate(
            [
                jnp.where(row % 2 == sign, (ky == source).astype(jnp.float32), 0.0).astype(jnp.bfloat16)
                for source in (from_own, from_other)
            ],
            1,
        )
        for sign in range(2)
    ]
    signs = select_rows(jnp.concatenate(picks, 0), given)
    plus, minus = signs[:size], signs[size:]
    mine = jnp.where(second, minus, plus)
    partner = jnp.where(alone, mine, jnp.where(second, plus, minus))
    scaled = (mine + select_lanes(select_rows(mirror_ref[...], partner), mirror_ref[...])) * 0.5 / span
    scaled_ref[...] = scaled.T

    mine, theirs = own_ref[:size, :], other_ref[:size, :]
    re = jnp.where(jnp.logical_and(second, jnp.logical_not(alone)), theirs, mine)
    im = jnp.where(alone, jnp.zeros_like(mine), jnp.where(second, -mine, theirs))
    ends = dot(jnp.concatenate([re, im], 0), lanes_ref[...])
    mid_real = ends[:size, :size] + ends[size:, size:]
    mid_imag = ends[size:, :size] - ends[:size, size:]
    both = dot(rows_ref[...], jnp.concatenate([mid_real, mid_imag], 1))
    real = both[:size, :size] + both[size:, size:]
    imag = both[:size, size:] - both[size:, :size]
    real_ref[...] = real
    imag_ref[...] = imag
    scaled = scaled_ref[...]
    power = real * real + imag * imag
    chunk = 24
    totals = [None] * MOMENTS
    for start in range(0, size // 2 + 8, chunk):
        row = lax.broadcasted_iota(jnp.int32, (chunk, size), 0) + start
        share = jnp.where(row % (size // 2) == 0, 1.0, jnp.where(row < size // 2, 2.0, 0.0))
        t = scaled[start : start + chunk] - centre
        p = power[start : start + chunk] * share
        p_parts = halves(p)
        t2 = t * 2.0
        t2_parts = halves(t2)
        zero = jnp.zeros_like(t)
        before, here = (jnp.ones_like(t), zero), (t, zero)
        for order in range(MOMENTS):
            value = before
            v_parts = halves(value[0])
            term, low_term = two_prod(value[0], p, v_parts, p_parts)
            term = (term, low_term + value[1] * p)
            total, spill = totals[order] or (None, None)
            for i in range(0, chunk, 8):
                piece, rest = term[0][i : i + 8], term[1][i : i + 8]
                if total is None:
                    total, spill = piece, rest
                else:
                    total, lost = two_sum(total, piece)
                    spill = spill + (lost + rest)
            totals[order] = total, spill
            if order + 1 < MOMENTS:
                up, low_up = two_prod(here[0], t2, None, t2_parts)
                following, lost = two_sum(up, -before[0])
                before, here = here, (following, lost + ((low_up + here[1] * t2) - before[1]))
    row = lax.broadcasted_iota(jnp.int32, (8, size), 0)
    lane = lax.broadcasted_iota(jnp.int32, (8, size), 1)
    out = jnp.zeros((8, size), jnp.float32)
    for base in range(0, MOMENTS, 8):
        high_rows = jnp.zeros((8, size), jnp.float32)
        low_rows = jnp.zeros((8, size), jnp.float32)
        for order in range(base, min(base + 8, MOMENTS)):
            total = sublane_total(quick_sum(*totals[order]))
            high_rows = jnp.where(row == order - base, total[0], high_rows)
            low_rows = jnp.where(row == order - base, total[1], low_rows)
        high_rows, low_rows = lane_total((high_rows, low_rows))
        out = jnp.where(lane == row + base, high_rows, out)
        out = jnp.where(lane == row + (base + LOW_LANE), low_rows, out)
    line = jnp.sum(out, axis=0, keepdims=True)
    send_ref[...] = jnp.broadcast_to(line, (size, size))


def lane_of(a, lane):
    pick = lambda v: jnp.broadcast_to(v[:, lane : lane + 1], v.shape)
    return pick(a[0]), pick(a[1])


def solve_kernel(
    sums_ref, range_ref, scaled_ref, real_ref, imag_ref, lanes_ref, rows_ref, out_ref, gain_ref, *, scale
):
    size = scaled_ref.shape[0]
    given = sums_ref[...]
    low = pltpu.roll(given, size - LOW_LANE, 1)
    rows = [(given[i : i + 8], low[i : i + 8]) for i in range(0, given.shape[0], 8)]
    while len(rows) > 1:
        rows = [dd_add(rows[i], rows[i + 1]) for i in range(0, len(rows), 2)]
    moments = sublane_total(rows[0])
    half = range_ref[0:1, :]
    centre = jnp.broadcast_to(range_ref[1:2, :], moments[0].shape)
    centre = (centre, jnp.zeros_like(centre))
    lane = lax.broadcasted_iota(jnp.int32, moments[0].shape, 1)
    resid, direct = moments, moments
    held = lane_of(resid, 0)
    steps, turns = [], []
    decay = jnp.ones((1, size), jnp.float32)
    for k in range(ITERS):
        after = tuple(pltpu.roll(v, size - 1, 1) for v in direct)
        prior = tuple(pltpu.roll(v, 1, 1) for v in direct)
        prior = tuple(jnp.where(lane == 0, a, p) for a, p in zip(after, prior))
        image = dd_add(dd_mul(direct, centre), dd_scale(dd_add(after, prior), 0.5))
        alpha = dd_div(held, lane_of(image, k))
        fresh = dd_add(resid, dd_neg(dd_mul(alpha, image)))
        reached = lane_of(fresh, k + 1)
        beta = dd_mul(alpha, dd_div(reached, held))
        held = reached
        beta = dd_scale(beta, -1.0 if k == 0 else -0.5)
        direct = dd_add(fresh, dd_mul(beta, direct))
        resid = fresh
        steps.append(alpha[0][0:1])
        turns.append(beta[0][0:1])
        decay = decay * beta[0][0:1]
    gain = lax.rsqrt(jnp.maximum(jnp.abs(decay), 1e-30)) / centre[0][0:1]
    gain_ref[...] = jnp.broadcast_to(gain, gain_ref.shape)
    scaled = scaled_ref[...]
    field = steps[0]
    solved = jnp.broadcast_to(field, scaled.shape)
    left = 1.0 - field * scaled
    toward = left + turns[0]
    for k in range(1, ITERS):
        solved = solved + steps[k] * toward
        left = left - steps[k] * (scaled * toward)
        if k + 1 < ITERS:
            toward = left + turns[k] * toward
    solved = solved * (scale / half)
    left = left * (gain * scale)
    real, imag = real_ref[...], imag_ref[...]
    back_real = solved * real - left * imag
    back_imag = solved * imag + left * real
    ends = dot_pieces(stacked(jnp.concatenate([back_real, back_imag], 0), 1), lanes_ref[...], 1, 0)
    mid_real = ends[:size, :size] - ends[size:, size:]
    mid_imag = ends[size:, :size] + ends[:size, size:]
    both = dot_pieces(rows_ref[...], stacked(jnp.concatenate([mid_real, mid_imag], 1), 0), 1, 0)
    real = both[:size, :size] - both[size:, size:]
    imag = both[:size, size:] + both[size:, :size]
    for copy in range(out_ref.shape[0] // (2 * size)):
        out_ref[pl.ds(copy * 2 * size, size, stride=2), :] = real
        out_ref[pl.ds(copy * 2 * size + 1, size, stride=2), :] = imag


def output_kernel(given_ref, gain_ref, back_ref, field_ref, resid_ref):
    planes, size = field_ref.shape[0], field_ref.shape[1]
    step = 2 * planes
    shrink = 1.0 / gain_ref[0:1, :]
    for j in range(planes):
        pieces = [given_ref[pl.ds(2 * j + part, size, stride=step), :] for part in range(2)]
        both = dot_pieces(stacked(jnp.concatenate(pieces, 0), 0), back_ref[...], 0, 0)
        field_ref[j] = both[:, :size]
        resid_ref[j] = both[:, size:] * shrink


def call(kernel, shapes, *args):
    whole = pl.BlockSpec(memory_space=pltpu.VMEM)
    scalars = pl.BlockSpec(memory_space=pltpu.SMEM)
    return pl.pallas_call(
        kernel,
        out_shape=[jax.ShapeDtypeStruct(s, jnp.float32) for s in shapes],
        in_specs=[scalars if a.dtype == jnp.int32 else whole for a in args],
        out_specs=[whole] * len(shapes),
    )(*args)


def exchange(parts, axes):
    return [parts[0]] + [lax.ppermute(parts[r], ALL, shift_pairs(axes, r)) for r in range(1, SIDE)]


def summed(parts):
    return ((parts[0] + parts[1]) + parts[2]) + parts[3]


def body(intensities, gridding, dest_slab, spectral_weights):
    ngrid = lax.axis_size("grid")
    ndp = lax.axis_size("dp")
    nent, rows, size = intensities.shape
    planes = gridding.shape[2] // size
    count = ngrid * ndp
    capacity = max(2, 2 * nent // ngrid)
    table = dft_tables(size)
    square = (size, size)
    swap = lambda a: lax.ppermute(a, ALL, shift_pairs((3, 3), 1))

    chip = lax.axis_index("dp") * (ngrid // CORES) + lax.axis_index("grid") // CORES
    core = lax.axis_index("grid") % CORES
    step = jnp.arange(5, dtype=jnp.int32)
    x, y, z = place_of(chip * CORES)[:3]
    place = jnp.where(
        step == 0, x, jnp.where(step == 1, y, jnp.where(step == 2, z, jnp.where(step == 3, core, chip == 0)))
    ).astype(jnp.int32)

    together = lax.optimization_barrier
    *away, wave, counts, lists, p0, p1, p2, p3 = grid_call(
        False, 0, ngrid, capacity, dest_slab[:, 0], place, intensities, gridding, table["packed"], spectral_weights
    )
    members = (counts, lists, place, wave, gridding)
    arrived = [swap(a) for a in away]
    weights = exchange([p0, p1, p2, p3], (0, 0))
    axes = [[order[stage] for order in ORDERS] for stage in range(3)]
    quarter = lambda a: [p.reshape(p.shape[1:]) for p in jnp.split(a.reshape((SIDE, -1) + a.shape[1:]), SIDE)]
    least = lambda parts: functools.reduce(jnp.minimum, parts)
    data = []
    for part in range(HALVES):
        kept = grid_call(True, part, ngrid, capacity, *members, arrived[part])
        data.append(exchange(kept, axes[0]))
    kept, weights = together((kept, weights))
    rows = call(weight_kernel, [(SIDE**2 * 8 + 8, size)] * SIDE, *weights, place)
    rows = exchange(rows, axes[0])
    parts = quarter(summed(data[0]))
    early = exchange(parts, axes[1])
    held = summed([a[: SIDE**2 * 8] for a in rows]).reshape(SIDE**2, 8, size)
    ends = jnp.broadcast_to(least([a[SIDE**2 * 8 :] for a in rows])[None], (SIDE**2, 8, size))
    parts = exchange(quarter(jnp.concatenate([summed(data[1]), held, ends], 1)), axes[1])
    late = size // HALVES
    for stage in (1, 2):
        if stage == 2:
            parts = exchange(quarter(parts), axes[2])
            late = size
        found = [
            summed([a[:, :late] for a in parts]),
            jnp.concatenate([a[:, late:-8] for a in parts], 1),
            least([a[:, -8:] for a in parts]),
        ]
        if stage == 1:
            found = [summed(early)] + found
        parts = jnp.concatenate(found, 1)
    parts = parts[0]
    real, imag, scaled, ends, send = call(
        moment_kernel, [square, square, square, (8, size), square],
        parts, swap(parts), place, table["lanes"], table["rows"], table["mirror"],
    )
    sums = lax.all_to_all(send.reshape(count, 1, size), ALL, 0, 0, tiled=True).reshape(count, size)
    back, gain = call(
        functools.partial(solve_kernel, scale=1.0 / size**3), [(ndp * 2 * size, size), (8, size)],
        sums, ends, scaled, real, imag, table["lanes_pieces"], table["rows_pieces"],
    )
    landed = lax.all_to_all(back.reshape(count, 2 * planes, size), ALL, 0, 0, tiled=True)
    return tuple(
        call(
            output_kernel, [(planes, size, size)] * 2,
            landed.reshape(count * 2 * planes, size), gain, table["back_pieces"],
        )
    )


def solution(mesh):
    return jax.shard_map(
        body,
        mesh=mesh,
        in_specs=(
            P(("dp", "grid"), None, None),
            P(("dp", "grid"), None, None),
            P(("dp", "grid"), None),
            P("dp", None, "grid", None),
        ),
        out_specs=(P("grid", None, None), P("grid", None, None)),
        check_vma=False,
    )
```

```python
import functools

import jax
import jax.numpy as jnp
import numpy as np
from jax import lax
from jax.experimental import pallas as pl
from jax.experimental.pallas import tpu as pltpu
from jax.sharding import PartitionSpec as P


ITERS = 8
MOMENTS = 2 * ITERS + 1
LOW_LANE = 64
ALL = ("dp", "grid")
HIGHEST = lax.Precision.HIGHEST


def two_sum(a, b):
    s = a + b
    v = s - a
    return s, (a - (s - v)) + (b - v)


def quick_sum(a, b):
    s = a + b
    return s, b - (s - a)


def halves(a):
    c = a * 4097.0
    high = c - (c - a)
    return high, a - high


def two_prod(a, b, a_parts=None, b_parts=None):
    p = a * b
    ah, al = a_parts or halves(a)
    bh, bl = b_parts or halves(b)
    return p, ((ah * bh - p) + ah * bl + al * bh) + al * bl


def dd_add(a, b):
    s, e = two_sum(a[0], b[0])
    return quick_sum(s, e + (a[1] + b[1]))


def dd_mul(a, b):
    p, e = two_prod(a[0], b[0])
    return quick_sum(p, e + (a[0] * b[1] + a[1] * b[0]))


def dd_times(a, b):
    p, e = two_prod(a[0], b)
    return quick_sum(p, e + a[1] * b)


def dd_scale(a, factor):
    return a[0] * factor, a[1] * factor


def dd_neg(a):
    return -a[0], -a[1]


def dd_div(a, b):
    inverse = 1.0 / b[0]
    first = a[0] * inverse
    rest = dd_add(a, dd_neg(dd_times(b, first)))
    return quick_sum(first, rest[0] * inverse)


def dot(a, b):
    return jax.lax.dot_general(
        a, b, (((1,), (0,)), ((), ())), precision=HIGHEST, preferred_element_type=jnp.float32
    )


SIDE = 4
CORES = 2
ORDERS = ((0, 2, 1), (1, 2, 0))
LATE_ORDERS = ((2, 0, 1), (2, 1, 0))


def place_of(device):
    chip = device // CORES
    return chip // SIDE**2, chip % SIDE, (chip // SIDE) % SIDE, device % CORES


def chip_at(x, y, z):
    return (x * SIDE + z) * SIDE + y


def shift_pairs(axes, hop):
    pairs = []
    for device in range(SIDE**3 * CORES):
        place = list(place_of(device))
        axis = axes[place[3]]
        place[axis] = (place[axis] + hop) % (CORES if axis == 3 else SIDE)
        pairs.append((device, chip_at(*place[:3]) * CORES + place[3]))
    return pairs


def held_rows(size):
    chip, core = np.arange(size) // CORES, np.arange(size) % CORES
    return np.where(chip == 0, core * size // 2, np.where(core == 0, chip, size - chip))


def dft_tables(size):
    index = np.arange(size)
    angle = 2.0 * np.pi * ((index[:, None] * index[None, :]) % size) / size
    cos, sin = np.cos(angle), np.sin(angle)
    held = held_rows(size)
    as_f32 = lambda a: np.ascontiguousarray(a, dtype=np.float32)
    half = size // 2
    packed = np.concatenate([cos[:, :half], cos[:, half : half + 1], -sin[:, 1:half]], 1)
    high = packed.astype(jnp.bfloat16)
    low = (packed - high.astype(np.float64)).astype(jnp.bfloat16)
    lanes, rows = np.concatenate([cos, sin], 1), np.concatenate([cos, sin], 0)
    back = np.concatenate(
        [np.concatenate([cos[held], sin[held]], 1), np.concatenate([-sin[held], cos[held]], 1)], 0
    )

    def thrice(table, axis):
        above = table.astype(jnp.bfloat16)
        below = (table - above.astype(np.float64)).astype(jnp.bfloat16)
        return np.concatenate([above, above, below], axis)

    return dict(
        packed=np.stack([np.concatenate([p[:, :half], q[:, :half]], 1) for p, q in ((high, low), (high[:, half:], low[:, half:]))]),
        lanes=as_f32(lanes),
        rows=as_f32(rows),
        lanes_pieces=thrice(lanes, 0),
        rows_pieces=thrice(rows, 1),
        back_pieces=thrice(back, 0),
        mirror=(((index[:, None] + index[None, :]) % size) == 0).astype(jnp.bfloat16),
    )


def dot_as(a, b, left, right):
    return lax.dot_general(
        a, b, (((left,), (right,)), ((), ())), precision=HIGHEST, preferred_element_type=jnp.float32
    )


def pieces_of(a, count):
    found = []
    for _ in range(count):
        piece = a.astype(jnp.bfloat16)
        found.append(piece)
        a = a - piece.astype(jnp.float32)
    return found


def dot_pieces(a, b, left, right):
    return lax.dot_general(a, b, (((left,), (right,)), ((), ())), preferred_element_type=jnp.float32)


def stacked(a, axis):
    high, low = pieces_of(a, 2)
    return jnp.concatenate([high, low, high], axis)


def select_rows(one_hot, a):
    width = a.shape[1]
    found = dot_pieces(one_hot, jnp.concatenate(pieces_of(a, 3), 1), 1, 0)
    return (found[:, :width] + found[:, width : 2 * width]) + found[:, 2 * width :]


def select_lanes(a, one_hot):
    height = a.shape[0]
    found = dot_pieces(jnp.concatenate(pieces_of(a, 3), 0), one_hot, 1, 0)
    return (found[:height] + found[height : 2 * height]) + found[2 * height :]


STEPS = 4
SHARES = (3, 1)


def sublane_turn(tiles):
    row = lax.broadcasted_iota(jnp.int32, tiles[0].shape, 0)
    for bit in (4, 2, 1):
        low = (row & bit) == 0
        turned = list(tiles)
        for i in range(8):
            if i & bit == 0:
                a, b = tiles[i], tiles[i + bit]
                turned[i] = jnp.where(low, a, pltpu.roll(b, bit, 0))
                turned[i + bit] = jnp.where(low, pltpu.roll(a, 8 - bit, 0), b)
        tiles = turned
    return tiles


def grid_kernel(*refs, kept, part, capacity):
    if kept:
        count_ref, list_ref, place_ref, wave_ref, matrix_ref, other_ref = refs[:6]
        outs, weight_refs = refs[-SIDE:], refs[6:-SIDE]
    else:
        dest_ref, place_ref, values_ref, matrix_ref, packed_ref, weights_ref = refs[:6]
        out_ref, kept_wave_ref, count_ref, list_ref, wave_ref = *refs[6:10], refs[-1]
    nent, rows, width = matrix_ref.shape
    size = width // SIDE
    half = size // 2
    nslab = count_ref.shape[0]
    step = pl.program_id(0)

    def clear(s, _):
        count_ref[s] = 0
        return 0

    def enter(e, _):
        slab = dest_ref[e]
        taken = count_ref[slab]
        list_ref[slab * capacity + taken] = e
        count_ref[slab] = taken + 1
        return 0

    def prepare():
        lax.fori_loop(0, nslab, clear, 0)
        lax.fori_loop(0, nent, enter, 0)
        for r, slice_ref in enumerate(refs[10:-1]):
            slice_ref[...] = weights_ref[0, :, (place_ref[0] + r) % SIDE, :]
        chip = lax.broadcasted_iota(jnp.int32, (half, half), 0)
        slot = lax.broadcasted_iota(jnp.int32, (half, half), 1)
        digits = digits_of(slot)
        pieces = []
        chips = [chip_at(*moved(place_ref, digits, order, 1)) for order in ORDERS]
        for owner in (1 - place_ref[3], place_ref[3]):
            pick = (chip == jnp.where(owner == 0, chips[0], chips[1])).astype(jnp.float32).astype(jnp.bfloat16)
            for start in (0, half):
                piece = packed_ref[owner, :, start : start + half]
                pieces.append(jnp.dot(piece, pick, preferred_element_type=jnp.float32).astype(jnp.bfloat16))
        both = jnp.dot(
            values_ref[...].reshape(nent * rows, size),
            jnp.concatenate(pieces, 1),
            preferred_element_type=jnp.float32,
        )
        for at, target_ref in ((0, wave_ref), (size, kept_wave_ref)):
            wave = both[:, at : at + half] + both[:, at + half : at + size]
            high = wave.astype(jnp.bfloat16)
            low = (wave - high.astype(jnp.float32)).astype(jnp.bfloat16)
            target_ref[...] = jnp.concatenate([high, low], 1).reshape(nent, rows, size)

    if not kept:
        pl.when(step == 0)(prepare)

    pairs = nslab // (2 * STEPS)

    def products(out):
        for pair in range(pairs):
            halves_of_tile = []
            for near in range(2):
                slab = ((sum(SHARES[:part]) + step) * pairs + pair) * 2 + near
                taken = count_ref[slab]
                waves, matrices = [], []
                for m in range(capacity):
                    entry = jnp.where(m < taken, list_ref[slab * capacity + m], 0)
                    wave = wave_ref[entry]
                    waves.append(jnp.where(m < taken, wave, jnp.zeros_like(wave)))
                    matrices.append(matrix_ref[entry])
                product = lax.dot_general(
                    jnp.concatenate(waves, 0),
                    jnp.concatenate(matrices, 0),
                    (((0,), (0,)), ((), ())),
                    preferred_element_type=jnp.float32,
                )
                halves_of_tile.append(product[:half] + product[half:])
            place = slice(pair * 8, pair * 8 + 8)
            for start in range(0, half, 8):
                tiles = [
                    product[start : start + 8, p * size : (p + 1) * size]
                    for product in halves_of_tile
                    for p in range(SIDE)
                ]
                for index, block in enumerate(sublane_turn(tiles), start):
                    out(index, place, block)

    def keep(index, place, block):
        digits = digits_of(index)
        first, second, third = digits if part == 0 else (digits[1], digits[0], digits[2])
        outs[first][second * SIDE + third, place, :] = block + other_ref[index, place, :]

    def send(index, place, block):
        out_ref[index, place, :] = block

    if kept:
        products(keep)
        if weight_refs:
            write_rows(weight_refs, place_ref, outs, pairs * 8)
    else:
        products(send)


def grid_call(kept, part, nslab, capacity, *args):
    scalars = pl.BlockSpec(memory_space=pltpu.SMEM)
    fixed = lambda shape: pl.BlockSpec(shape, lambda i: (0,) * len(shape))
    matrix = args[4] if kept else args[3]
    nent, rows, width = matrix.shape
    size, blocks = width // SIDE, SIDE**3
    steps = SHARES[part] if kept else STEPS
    deep = [share * size // STEPS for share in SHARES]
    moving = lambda count, start=0: pl.BlockSpec((count, size // STEPS, size), lambda i: (0, start + i, 0))
    f32 = lambda *shape: jax.ShapeDtypeStruct(shape, jnp.float32)
    in_specs = [scalars if a.dtype == jnp.int32 else fixed(a.shape) for a in args]
    if kept:
        in_specs[5] = moving(blocks, sum(SHARES[:part]))
        if part == 0:
            out_shape, out_specs = [f32(SIDE**2, deep[0], size)] * SIDE, [moving(SIDE**2)] * SIDE
        else:
            shape = (SIDE**2, deep[1] + 16, size)
            out_shape, out_specs = [f32(*shape)] * SIDE, [fixed(shape)] * SIDE
        scratch = []
    else:
        wave = (nent, rows, size)
        out_shape = [
            f32(blocks, size, size),
            jax.ShapeDtypeStruct(wave, jnp.bfloat16),
            jax.ShapeDtypeStruct((nslab,), jnp.int32),
            jax.ShapeDtypeStruct((nslab * capacity,), jnp.int32),
        ] + [f32(size, size)] * SIDE
        out_specs = [moving(blocks), fixed(wave), scalars, scalars] + [fixed((size, size))] * SIDE
        scratch = [pltpu.VMEM(wave, jnp.bfloat16)]
    return pl.pallas_call(
        functools.partial(grid_kernel, kept=kept, part=part, capacity=capacity),
        grid=(steps,),
        out_shape=out_shape,
        in_specs=in_specs,
        out_specs=out_specs,
        scratch_shapes=scratch,
    )(*args)


def moved(place_ref, digits, order, sign):
    at = [place_ref[0], place_ref[1], place_ref[2]]
    for digit, axis in zip(digits, order):
        at[axis] = (at[axis] + sign * digit + SIDE) % SIDE
    return at


def digits_of(index):
    return index // SIDE**2, (index // SIDE) % SIDE, index % SIDE


def write_rows(weight_refs, place_ref, outs, base):
    size = weight_refs[0].shape[0]
    half = size // 2
    own = summed([ref[...] for ref in weight_refs])
    low = jnp.min(jnp.min(own, axis=0, keepdims=True), axis=1, keepdims=True)
    high = jnp.max(jnp.max(own, axis=0, keepdims=True), axis=1, keepdims=True)
    row = lax.broadcasted_iota(jnp.int32, (size, size), 0)
    lane = lax.broadcasted_iota(jnp.int32, (size, size), 1)
    chips = [chip_at(*moved(place_ref, digits_of(row % half), order, 1)) for order in LATE_ORDERS]
    chip = jnp.where(place_ref[3] == 0, chips[0], chips[1])
    negative = jnp.where(chip == 0, half, size - chip)
    pick = (lane == jnp.where(row < half, chip, negative)).astype(jnp.float32)
    rows = dot_as(pick, own, 1, 1)
    ends = jnp.where(lax.broadcasted_iota(jnp.int32, (8, size), 1) < half, low, -high)
    count = half // SIDE
    for r, out_ref in enumerate(outs):
        out_ref[:, base : base + 8, :] = jnp.zeros((count, 8, size), jnp.float32)
        out_ref[:, base + 8 : base + 16, :] = jnp.broadcast_to(ends[None], (count, 8, size))
        for sign in range(2):
            at = sign * half + r * count
            out_ref[:, base + 2 * r + sign, :] = rows[at : at + count]


def sublane_total(a):
    for shift in (4, 2, 1):
        a = dd_add(a, (pltpu.roll(a[0], shift, 0), pltpu.roll(a[1], shift, 0)))
    return a


def lane_total(a):
    for shift in (64, 32, 16, 8, 4, 2, 1):
        a = dd_add(a, (pltpu.roll(a[0], shift, 1), pltpu.roll(a[1], shift, 1)))
    return a


def moment_kernel(
    own_ref, other_ref, place_ref, lanes_ref, rows_ref, mirror_ref, real_ref, imag_ref, scaled_ref, range_ref, send_ref
):
    size = scaled_ref.shape[0]
    second, alone = place_ref[3] == 1, place_ref[4] == 1
    lane8 = lax.broadcasted_iota(jnp.int32, (8, size), 1)
    ends = jnp.minimum(own_ref[2 * size :, :], other_ref[2 * size :, :])
    least = lambda v: jnp.min(jnp.min(v, axis=0, keepdims=True), axis=1, keepdims=True)
    low = least(jnp.where(lane8 < size // 2, ends, 1e30))
    high = -least(jnp.where(lane8 < size // 2, 1e30, ends))
    span = jnp.broadcast_to(jnp.maximum((high - low) * 0.5, high * 1e-4), (1, size))
    centre = jnp.broadcast_to((high + low) * 0.5, (1, size)) / span
    range_ref[0:1, :] = span
    range_ref[1:2, :] = centre
    range_ref[2:8, :] = jnp.zeros((6, size), jnp.float32)

    ky = lax.broadcasted_iota(jnp.int32, (size, size), 0)
    row = lax.broadcasted_iota(jnp.int32, (size, size), 1)
    found = row // 2
    back = (found % SIDE, (found // SIDE) % SIDE, found // SIDE**2)
    sources = []
    for owner, order in enumerate(LATE_ORDERS):
        x, y, z = moved(place_ref, back, order, -1)
        sources.append(SIDE * (z * (SIDE * CORES) + y * CORES + owner) + x)
    from_own = jnp.where(second, sources[1], sources[0])
    from_other = jnp.where(second, sources[0], sources[1])
    given = jnp.concatenate([own_ref[size : 2 * size, :], other_ref[size : 2 * size, :]], 0)
    picks = [
        jnp.concatenate(
            [
                jnp.where(row % 2 == sign, (ky == source).astype(jnp.float32), 0.0).astype(jnp.bfloat16)
                for source in (from_own, from_other)
            ],
            1,
        )
        for sign in range(2)
    ]
    signs = select_rows(jnp.concatenate(picks, 0), given)
    plus, minus = signs[:size], signs[size:]
    mine = jnp.where(second, minus, plus)
    partner = jnp.where(alone, mine, jnp.where(second, plus, minus))
    scaled = (mine + select_lanes(select_rows(mirror_ref[...], partner), mirror_ref[...])) * 0.5 / span
    scaled_ref[...] = scaled.T

    mine, theirs = own_ref[:size, :], other_ref[:size, :]
    re = jnp.where(jnp.logical_and(second, jnp.logical_not(alone)), theirs, mine)
    im = jnp.where(alone, jnp.zeros_like(mine), jnp.where(second, -mine, theirs))
    ends = dot(jnp.concatenate([re, im], 0), lanes_ref[...])
    mid_real = ends[:size, :size] + ends[size:, size:]
    mid_imag = ends[size:, :size] - ends[:size, size:]
    both = dot(rows_ref[...], jnp.concatenate([mid_real, mid_imag], 1))
    real = both[:size, :size] + both[size:, size:]
    imag = both[:size, size:] - both[size:, :size]
    real_ref[...] = real
    imag_ref[...] = imag
    scaled = scaled_ref[...]
    power = real * real + imag * imag
    chunk = 24
    totals = [None] * MOMENTS
    for start in range(0, size // 2 + 8, chunk):
        row = lax.broadcasted_iota(jnp.int32, (chunk, size), 0) + start
        share = jnp.where(row % (size // 2) == 0, 1.0, jnp.where(row < size // 2, 2.0, 0.0))
        t = scaled[start : start + chunk] - centre
        p = power[start : start + chunk] * share
        p_parts = halves(p)
        t2 = t * 2.0
        t2_parts = halves(t2)
        zero = jnp.zeros_like(t)
        before, here = (jnp.ones_like(t), zero), (t, zero)
        for order in range(MOMENTS):
            value = before
            v_parts = halves(value[0])
            term, low_term = two_prod(value[0], p, v_parts, p_parts)
            term = (term, low_term + value[1] * p)
            total, spill = totals[order] or (None, None)
            for i in range(0, chunk, 8):
                piece, rest = term[0][i : i + 8], term[1][i : i + 8]
                if total is None:
                    total, spill = piece, rest
                else:
                    total, lost = two_sum(total, piece)
                    spill = spill + (lost + rest)
            totals[order] = total, spill
            if order + 1 < MOMENTS:
                up, low_up = two_prod(here[0], t2, None, t2_parts)
                following, lost = two_sum(up, -before[0])
                before, here = here, (following, lost + ((low_up + here[1] * t2) - before[1]))
    row = lax.broadcasted_iota(jnp.int32, (8, size), 0)
    lane = lax.broadcasted_iota(jnp.int32, (8, size), 1)
    out = jnp.zeros((8, size), jnp.float32)
    for base in range(0, MOMENTS, 8):
        high_rows = jnp.zeros((8, size), jnp.float32)
        low_rows = jnp.zeros((8, size), jnp.float32)
        for order in range(base, min(base + 8, MOMENTS)):
            total = sublane_total(quick_sum(*totals[order]))
            high_rows = jnp.where(row == order - base, total[0], high_rows)
            low_rows = jnp.where(row == order - base, total[1], low_rows)
        high_rows, low_rows = lane_total((high_rows, low_rows))
        out = jnp.where(lane == row + base, high_rows, out)
        out = jnp.where(lane == row + (base + LOW_LANE), low_rows, out)
    line = jnp.sum(out, axis=0, keepdims=True)
    send_ref[...] = jnp.broadcast_to(line, (size, size))


def lane_of(a, lane):
    pick = lambda v: jnp.broadcast_to(v[:, lane : lane + 1], v.shape)
    return pick(a[0]), pick(a[1])


def solve_kernel(
    sums_ref, range_ref, scaled_ref, real_ref, imag_ref, lanes_ref, rows_ref, out_ref, gain_ref, *, scale
):
    size = scaled_ref.shape[0]
    given = sums_ref[...]
    low = pltpu.roll(given, size - LOW_LANE, 1)
    rows = [(given[i : i + 8], low[i : i + 8]) for i in range(0, given.shape[0], 8)]
    while len(rows) > 1:
        rows = [dd_add(rows[i], rows[i + 1]) for i in range(0, len(rows), 2)]
    moments = sublane_total(rows[0])
    half = range_ref[0:1, :]
    centre = jnp.broadcast_to(range_ref[1:2, :], moments[0].shape)
    centre = (centre, jnp.zeros_like(centre))
    lane = lax.broadcasted_iota(jnp.int32, moments[0].shape, 1)
    resid, direct = moments, moments
    held = lane_of(resid, 0)
    steps, turns = [], []
    decay = jnp.ones((1, size), jnp.float32)
    for k in range(ITERS):
        after = tuple(pltpu.roll(v, size - 1, 1) for v in direct)
        prior = tuple(pltpu.roll(v, 1, 1) for v in direct)
        prior = tuple(jnp.where(lane == 0, a, p) for a, p in zip(after, prior))
        image = dd_add(dd_mul(direct, centre), dd_scale(dd_add(after, prior), 0.5))
        alpha = dd_div(held, lane_of(image, k))
        fresh = dd_add(resid, dd_neg(dd_mul(alpha, image)))
        reached = lane_of(fresh, k + 1)
        beta = dd_mul(alpha, dd_div(reached, held))
        held = reached
        beta = dd_scale(beta, -1.0 if k == 0 else -0.5)
        direct = dd_add(fresh, dd_mul(beta, direct))
        resid = fresh
        steps.append(alpha[0][0:1])
        turns.append(beta[0][0:1])
        decay = decay * beta[0][0:1]
    gain = lax.rsqrt(jnp.maximum(jnp.abs(decay), 1e-30)) / centre[0][0:1]
    gain_ref[...] = jnp.broadcast_to(gain, gain_ref.shape)
    scaled = scaled_ref[...]
    field = steps[0]
    solved = jnp.broadcast_to(field, scaled.shape)
    left = 1.0 - field * scaled
    toward = left + turns[0]
    for k in range(1, ITERS):
        solved = solved + steps[k] * toward
        left = left - steps[k] * (scaled * toward)
        if k + 1 < ITERS:
            toward = left + turns[k] * toward
    solved = solved * (scale / half)
    left = left * (gain * scale)
    real, imag = real_ref[...], imag_ref[...]
    back_real = solved * real - left * imag
    back_imag = solved * imag + left * real
    ends = dot_pieces(stacked(jnp.concatenate([back_real, back_imag], 0), 1), lanes_ref[...], 1, 0)
    mid_real = ends[:size, :size] - ends[size:, size:]
    mid_imag = ends[size:, :size] + ends[:size, size:]
    both = dot_pieces(rows_ref[...], stacked(jnp.concatenate([mid_real, mid_imag], 1), 0), 1, 0)
    real = both[:size, :size] - both[size:, size:]
    imag = both[:size, size:] + both[size:, :size]
    for copy in range(out_ref.shape[0] // (2 * size)):
        out_ref[pl.ds(copy * 2 * size, size, stride=2), :] = real
        out_ref[pl.ds(copy * 2 * size + 1, size, stride=2), :] = imag


def output_kernel(given_ref, gain_ref, back_ref, field_ref, resid_ref):
    planes, size = field_ref.shape[0], field_ref.shape[1]
    step = 2 * planes
    shrink = 1.0 / gain_ref[0:1, :]
    for j in range(planes):
        pieces = [given_ref[pl.ds(2 * j + part, size, stride=step), :] for part in range(2)]
        both = dot_pieces(stacked(jnp.concatenate(pieces, 0), 0), back_ref[...], 0, 0)
        field_ref[j] = both[:, :size]
        resid_ref[j] = both[:, size:] * shrink


def call(kernel, shapes, *args):
    whole = pl.BlockSpec(memory_space=pltpu.VMEM)
    scalars = pl.BlockSpec(memory_space=pltpu.SMEM)
    return pl.pallas_call(
        kernel,
        out_shape=[jax.ShapeDtypeStruct(s, jnp.float32) for s in shapes],
        in_specs=[scalars if a.dtype == jnp.int32 else whole for a in args],
        out_specs=[whole] * len(shapes),
    )(*args)


def exchange(parts, axes):
    return [parts[0]] + [lax.ppermute(parts[r], ALL, shift_pairs(axes, r)) for r in range(1, SIDE)]


def summed(parts):
    return ((parts[0] + parts[1]) + parts[2]) + parts[3]


def body(intensities, gridding, dest_slab, spectral_weights):
    ngrid = lax.axis_size("grid")
    ndp = lax.axis_size("dp")
    nent, _, size = intensities.shape
    planes = gridding.shape[2] // size
    count = ngrid * ndp
    capacity = max(2, 2 * nent // ngrid)
    table = dft_tables(size)
    square = (size, size)
    swap = lambda a: lax.ppermute(a, ALL, shift_pairs((3, 3), 1))

    chip = lax.axis_index("dp") * (ngrid // CORES) + lax.axis_index("grid") // CORES
    core = lax.axis_index("grid") % CORES
    step = jnp.arange(5, dtype=jnp.int32)
    x, y, z = place_of(chip * CORES)[:3]
    place = jnp.where(
        step == 0, x, jnp.where(step == 1, y, jnp.where(step == 2, z, jnp.where(step == 3, core, chip == 0)))
    ).astype(jnp.int32)

    away, wave, counts, lists, *pieces = grid_call(
        False, 0, ngrid, capacity, dest_slab[:, 0], place, intensities, gridding, table["packed"], spectral_weights
    )
    members = (counts, lists, place, wave, gridding)
    arrived = swap(away)
    weights = exchange(pieces, (0, 0))
    axes = [[[order[stage] for order in orders] for stage in range(3)] for orders in (ORDERS, LATE_ORDERS)]
    quarter = lambda a: [p.reshape(p.shape[1:]) for p in jnp.split(a.reshape((SIDE, -1) + a.shape[1:]), SIDE)]
    least = lambda parts: functools.reduce(jnp.minimum, parts)
    data = []
    for part in range(2):
        kept = grid_call(True, part, ngrid, capacity, *members, arrived, *(weights if part else ()))
        data.append(exchange(kept, axes[part][0]))
    parts = quarter(summed(data[0]))
    early = exchange(parts, axes[0][1])
    late = SHARES[1] * size // STEPS
    parts = [summed([a[:, :-8] for a in data[1]]), least([a[:, -8:] for a in data[1]])]
    parts = quarter(jnp.concatenate(parts, 1))
    parts = exchange(parts, axes[1][1])
    for stage in (1, 2):
        if stage == 2:
            parts = exchange(quarter(parts), axes[0][2])
            late = size
        found = [
            summed([a[:, :late] for a in parts]),
            jnp.concatenate([a[:, late:-8] for a in parts], 1),
            least([a[:, -8:] for a in parts]),
        ]
        if stage == 1:
            found = [summed(early)] + found
        parts = jnp.concatenate(found, 1)
    parts = parts[0]
    real, imag, scaled, ends, send = call(
        moment_kernel, [square, square, square, (8, size), square],
        parts, swap(parts), place, table["lanes"], table["rows"], table["mirror"],
    )
    sums = lax.all_to_all(send.reshape(count, 1, size), ALL, 0, 0, tiled=True).reshape(count, size)
    back, gain = call(
        functools.partial(solve_kernel, scale=1.0 / size**3), [(ndp * 2 * size, size), (8, size)],
        sums, ends, scaled, real, imag, table["lanes_pieces"], table["rows_pieces"],
    )
    landed = lax.all_to_all(back.reshape(count, 2 * planes, size), ALL, 0, 0, tiled=True)
    return tuple(
        call(
            output_kernel, [(planes, size, size)] * 2,
            landed.reshape(count * 2 * planes, size), gain, table["back_pieces"],
        )
    )


def solution(mesh):
    return jax.shard_map(
        body,
        mesh=mesh,
        in_specs=(
            P(("dp", "grid"), None, None),
            P(("dp", "grid"), None, None),
            P(("dp", "grid"), None),
            P("dp", None, "grid", None),
        ),
        out_specs=(P("grid", None, None), P("grid", None, None)),
        check_vma=False,
    )
```

```python
import functools

import jax
import jax.numpy as jnp
import numpy as np
from jax import lax
from jax.experimental import pallas as pl
from jax.experimental.pallas import tpu as pltpu
from jax.sharding import PartitionSpec as P


ITERS = 8
MOMENTS = 2 * ITERS + 1
LOW_LANE = 64
ALL = ("dp", "grid")
HIGHEST = lax.Precision.HIGHEST


def two_sum(a, b):
    s = a + b
    v = s - a
    return s, (a - (s - v)) + (b - v)


def quick_sum(a, b):
    s = a + b
    return s, b - (s - a)


def halves(a):
    c = a * 4097.0
    high = c - (c - a)
    return high, a - high


def two_prod(a, b, a_parts=None, b_parts=None):
    p = a * b
    ah, al = a_parts or halves(a)
    bh, bl = b_parts or halves(b)
    return p, ((ah * bh - p) + ah * bl + al * bh) + al * bl


def dd_add(a, b):
    s, e = two_sum(a[0], b[0])
    return quick_sum(s, e + (a[1] + b[1]))


def dd_mul(a, b):
    p, e = two_prod(a[0], b[0])
    return quick_sum(p, e + (a[0] * b[1] + a[1] * b[0]))


def dd_times(a, b):
    p, e = two_prod(a[0], b)
    return quick_sum(p, e + a[1] * b)


def dd_scale(a, factor):
    return a[0] * factor, a[1] * factor


def dd_neg(a):
    return -a[0], -a[1]


def dd_div(a, b):
    inverse = 1.0 / b[0]
    first = a[0] * inverse
    rest = dd_add(a, dd_neg(dd_times(b, first)))
    return quick_sum(first, rest[0] * inverse)


def dot(a, b):
    return jax.lax.dot_general(
        a, b, (((1,), (0,)), ((), ())), precision=HIGHEST, preferred_element_type=jnp.float32
    )


SIDE = 4
CORES = 2
ORDERS = ((0, 2, 1), (1, 2, 0))


def place_of(device):
    chip = device // CORES
    return chip // SIDE**2, chip % SIDE, (chip // SIDE) % SIDE, device % CORES


def chip_at(x, y, z):
    return (x * SIDE + z) * SIDE + y


def shift_pairs(axes, hop):
    pairs = []
    for device in range(SIDE**3 * CORES):
        place = list(place_of(device))
        axis = axes[place[3]]
        place[axis] = (place[axis] + hop) % (CORES if axis == 3 else SIDE)
        pairs.append((device, chip_at(*place[:3]) * CORES + place[3]))
    return pairs


def held_rows(size):
    chip, core = np.arange(size) // CORES, np.arange(size) % CORES
    return np.where(chip == 0, core * size // 2, np.where(core == 0, chip, size - chip))


def dft_tables(size):
    index = np.arange(size)
    angle = 2.0 * np.pi * ((index[:, None] * index[None, :]) % size) / size
    cos, sin = np.cos(angle), np.sin(angle)
    held = held_rows(size)
    as_f32 = lambda a: np.ascontiguousarray(a, dtype=np.float32)
    half = size // 2
    packed = np.concatenate([cos[:, :half], cos[:, half : half + 1], -sin[:, 1:half]], 1)
    high = packed.astype(jnp.bfloat16)
    low = (packed - high.astype(np.float64)).astype(jnp.bfloat16)
    lanes, rows = np.concatenate([cos, sin], 1), np.concatenate([cos, sin], 0)
    back = np.concatenate(
        [np.concatenate([cos[held], sin[held]], 1), np.concatenate([-sin[held], cos[held]], 1)], 0
    )

    def thrice(table, axis):
        above = table.astype(jnp.bfloat16)
        below = (table - above.astype(np.float64)).astype(jnp.bfloat16)
        return np.concatenate([above, above, below], axis)

    return dict(
        packed=np.stack([np.concatenate([p[:, :half], q[:, :half]], 1) for p, q in ((high, low), (high[:, half:], low[:, half:]))]),
        lanes=as_f32(lanes),
        rows=as_f32(rows),
        lanes_pieces=thrice(lanes, 0),
        rows_pieces=thrice(rows, 1),
        back_pieces=thrice(back, 0),
        mirror=(((index[:, None] + index[None, :]) % size) == 0).astype(jnp.bfloat16),
    )


def dot_as(a, b, left, right):
    return lax.dot_general(
        a, b, (((left,), (right,)), ((), ())), precision=HIGHEST, preferred_element_type=jnp.float32
    )


def pieces_of(a, count):
    found = []
    for _ in range(count):
        piece = a.astype(jnp.bfloat16)
        found.append(piece)
        a = a - piece.astype(jnp.float32)
    return found


def dot_pieces(a, b, left, right):
    return lax.dot_general(a, b, (((left,), (right,)), ((), ())), preferred_element_type=jnp.float32)


def stacked(a, axis):
    high, low = pieces_of(a, 2)
    return jnp.concatenate([high, low, high], axis)


def select_rows(one_hot, a):
    width = a.shape[1]
    found = dot_pieces(one_hot, jnp.concatenate(pieces_of(a, 3), 1), 1, 0)
    return (found[:, :width] + found[:, width : 2 * width]) + found[:, 2 * width :]


def select_lanes(a, one_hot):
    height = a.shape[0]
    found = dot_pieces(jnp.concatenate(pieces_of(a, 3), 0), one_hot, 1, 0)
    return (found[:height] + found[height : 2 * height]) + found[2 * height :]


STEPS = 4
SHARES = (2, 2)


def sublane_turn(tiles):
    row = lax.broadcasted_iota(jnp.int32, tiles[0].shape, 0)
    for bit in (4, 2, 1):
        low = (row & bit) == 0
        turned = list(tiles)
        for i in range(8):
            if i & bit == 0:
                a, b = tiles[i], tiles[i + bit]
                turned[i] = jnp.where(low, a, pltpu.roll(b, bit, 0))
                turned[i + bit] = jnp.where(low, pltpu.roll(a, 8 - bit, 0), b)
        tiles = turned
    return tiles


def grid_kernel(*refs, kept, part, capacity):
    if kept:
        count_ref, list_ref, place_ref, wave_ref, matrix_ref, other_ref = refs[:6]
        outs, weight_refs = refs[-SIDE:], refs[6:-SIDE]
    else:
        dest_ref, place_ref, values_ref, matrix_ref, packed_ref, weights_ref = refs[:6]
        out_refs, (kept_wave_ref, count_ref, list_ref), wave_ref = refs[6:8], refs[8:11], refs[-1]
    nent, rows, width = matrix_ref.shape
    size = width // SIDE
    half = size // 2
    nslab = count_ref.shape[0]
    step = pl.program_id(0)

    def clear(s, _):
        count_ref[s] = 0
        return 0

    def enter(e, _):
        slab = dest_ref[e]
        taken = count_ref[slab]
        list_ref[slab * capacity + taken] = e
        count_ref[slab] = taken + 1
        return 0

    def prepare():
        lax.fori_loop(0, nslab, clear, 0)
        lax.fori_loop(0, nent, enter, 0)
        for r, slice_ref in enumerate(refs[11:-1]):
            slice_ref[...] = weights_ref[0, :, (place_ref[0] + r) % SIDE, :]
        chip = lax.broadcasted_iota(jnp.int32, (half, half), 0)
        slot = lax.broadcasted_iota(jnp.int32, (half, half), 1)
        digits = digits_of(slot)
        pieces = []
        chips = [chip_at(*moved(place_ref, digits, order, 1)) for order in ORDERS]
        for owner in (1 - place_ref[3], place_ref[3]):
            pick = (chip == jnp.where(owner == 0, chips[0], chips[1])).astype(jnp.float32).astype(jnp.bfloat16)
            for start in (0, half):
                piece = packed_ref[owner, :, start : start + half]
                pieces.append(jnp.dot(piece, pick, preferred_element_type=jnp.float32).astype(jnp.bfloat16))
        both = jnp.dot(
            values_ref[...].reshape(nent * rows, size),
            jnp.concatenate(pieces, 1),
            preferred_element_type=jnp.float32,
        )
        for at, target_ref in ((0, wave_ref), (size, kept_wave_ref)):
            wave = both[:, at : at + half] + both[:, at + half : at + size]
            high = wave.astype(jnp.bfloat16)
            low = (wave - high.astype(jnp.float32)).astype(jnp.bfloat16)
            target_ref[...] = jnp.concatenate([high, low], 1).reshape(nent, rows, size)

    if not kept:
        pl.when(step == 0)(prepare)

    pairs = nslab // (2 * STEPS) // (1 + (part > 0))

    def products(out):
        for pair in range(pairs):
            halves_of_tile = []
            for near in range(2):
                slab = sum(SHARES[:part]) * (nslab // STEPS) + (step * pairs + pair) * 2 + near
                taken = count_ref[slab]
                waves, matrices = [], []
                for m in range(capacity):
                    entry = jnp.where(m < taken, list_ref[slab * capacity + m], 0)
                    wave = wave_ref[entry]
                    waves.append(jnp.where(m < taken, wave, jnp.zeros_like(wave)))
                    matrices.append(matrix_ref[entry])
                product = lax.dot_general(
                    jnp.concatenate(waves, 0),
                    jnp.concatenate(matrices, 0),
                    (((0,), (0,)), ((), ())),
                    preferred_element_type=jnp.float32,
                )
                halves_of_tile.append(product[:half] + product[half:])
            place = slice(pair * 8, pair * 8 + 8)
            for start in range(0, half, 8):
                tiles = [
                    product[start : start + 8, p * size : (p + 1) * size]
                    for product in halves_of_tile
                    for p in range(SIDE)
                ]
                for index, block in enumerate(sublane_turn(tiles), start):
                    out(index, place, block)

    def keep(index, place, block):
        outs[index // SIDE**2][index % SIDE**2, place, :] = block + other_ref[index, place, :]

    def send(out_ref):
        def write(index, place, block):
            out_ref[index, place, :] = block

        return write

    if not kept:
        pl.when(step < SHARES[0])(lambda: products(send(out_refs[0])))
        pl.when(step >= SHARES[0])(lambda: products(send(out_refs[1])))
    elif part == 0:
        products(keep)
    else:
        pl.when(step < 2 * SHARES[1])(lambda: products(keep))
        pl.when(step == 2 * SHARES[1])(lambda: write_rows(weight_refs, place_ref, outs))


def grid_call(kept, part, nslab, capacity, *args):
    scalars = pl.BlockSpec(memory_space=pltpu.SMEM)
    fixed = lambda shape: pl.BlockSpec(shape, lambda i: (0,) * len(shape))
    matrix = args[4] if kept else args[3]
    nent, rows, width = matrix.shape
    size, blocks = width // SIDE, SIDE**3
    steps = STEPS
    if kept:
        steps = SHARES[0] if part == 0 else 2 * SHARES[1] + 1
    deep = [share * size // STEPS for share in SHARES]
    moving = lambda count: pl.BlockSpec((count, size // STEPS, size), lambda i: (0, i, 0))
    f32 = lambda *shape: jax.ShapeDtypeStruct(shape, jnp.float32)
    in_specs = [scalars if a.dtype == jnp.int32 else fixed(a.shape) for a in args]
    if kept:
        if part == 0:
            in_specs[5] = moving(blocks)
            out_shape, out_specs = [f32(SIDE**2, deep[0], size)] * SIDE, [moving(SIDE**2)] * SIDE
        else:
            depth = size // (2 * STEPS)
            in_specs[5] = pl.BlockSpec((blocks, depth, size), lambda i: (0, jnp.minimum(i, steps - 2), 0))
            out_shape = [f32(SIDE**2, deep[1] + 16, size)] * SIDE
            out_specs = [pl.BlockSpec((SIDE**2, depth, size), lambda i: (0, i, 0))] * SIDE
        scratch = []
    else:
        wave = (nent, rows, size)
        out_shape = [f32(blocks, depth, size) for depth in deep] + [
            jax.ShapeDtypeStruct(wave, jnp.bfloat16),
            jax.ShapeDtypeStruct((nslab,), jnp.int32),
            jax.ShapeDtypeStruct((nslab * capacity,), jnp.int32),
        ] + [f32(size, size)] * SIDE
        block = (blocks, size // STEPS, size)
        out_specs = [
            pl.BlockSpec(block, lambda i: (0, jnp.minimum(i, SHARES[0] - 1), 0)),
            pl.BlockSpec(block, lambda i: (0, jnp.maximum(i - SHARES[0], 0), 0)),
        ] + [fixed(wave), scalars, scalars] + [fixed((size, size))] * SIDE
        scratch = [pltpu.VMEM(wave, jnp.bfloat16)]
    return pl.pallas_call(
        functools.partial(grid_kernel, kept=kept, part=part, capacity=capacity),
        grid=(steps,),
        out_shape=out_shape,
        in_specs=in_specs,
        out_specs=out_specs,
        scratch_shapes=scratch,
    )(*args)


def moved(place_ref, digits, order, sign):
    at = [place_ref[0], place_ref[1], place_ref[2]]
    for digit, axis in zip(digits, order):
        at[axis] = (at[axis] + sign * digit + SIDE) % SIDE
    return at


def digits_of(index):
    return index // SIDE**2, (index // SIDE) % SIDE, index % SIDE


def write_rows(weight_refs, place_ref, outs):
    size = weight_refs[0].shape[0]
    half = size // 2
    own = summed([ref[...] for ref in weight_refs])
    low = jnp.min(jnp.min(own, axis=0, keepdims=True), axis=1, keepdims=True)
    high = jnp.max(jnp.max(own, axis=0, keepdims=True), axis=1, keepdims=True)
    row = lax.broadcasted_iota(jnp.int32, (size, size), 0)
    lane = lax.broadcasted_iota(jnp.int32, (size, size), 1)
    chips = [chip_at(*moved(place_ref, digits_of(row % half), order, 1)) for order in ORDERS]
    chip = jnp.where(place_ref[3] == 0, chips[0], chips[1])
    negative = jnp.where(chip == 0, half, size - chip)
    pick = (lane == jnp.where(row < half, chip, negative)).astype(jnp.float32)
    rows = dot_as(pick, own, 1, 1)
    ends = jnp.where(lax.broadcasted_iota(jnp.int32, (8, size), 1) < half, low, -high)
    count = half // SIDE
    for r, out_ref in enumerate(outs):
        out_ref[:, 0:8, :] = jnp.zeros((count, 8, size), jnp.float32)
        out_ref[:, 8:16, :] = jnp.broadcast_to(ends[None], (count, 8, size))
        for sign in range(2):
            at = sign * half + r * count
            out_ref[:, 2 * r + sign, :] = rows[at : at + count]


def sublane_total(a):
    for shift in (4, 2, 1):
        a = dd_add(a, (pltpu.roll(a[0], shift, 0), pltpu.roll(a[1], shift, 0)))
    return a


def lane_total(a):
    for shift in (64, 32, 16, 8, 4, 2, 1):
        a = dd_add(a, (pltpu.roll(a[0], shift, 1), pltpu.roll(a[1], shift, 1)))
    return a


def moment_kernel(
    own_ref, other_ref, place_ref, lanes_ref, rows_ref, mirror_ref, real_ref, imag_ref, scaled_ref, range_ref, send_ref
):
    size = scaled_ref.shape[0]
    second, alone = place_ref[3] == 1, place_ref[4] == 1
    lane8 = lax.broadcasted_iota(jnp.int32, (8, size), 1)
    ends = jnp.minimum(own_ref[2 * size :, :], other_ref[2 * size :, :])
    least = lambda v: jnp.min(jnp.min(v, axis=0, keepdims=True), axis=1, keepdims=True)
    low = least(jnp.where(lane8 < size // 2, ends, 1e30))
    high = -least(jnp.where(lane8 < size // 2, 1e30, ends))
    span = jnp.broadcast_to(jnp.maximum((high - low) * 0.5, high * 1e-4), (1, size))
    centre = jnp.broadcast_to((high + low) * 0.5, (1, size)) / span
    range_ref[0:1, :] = span
    range_ref[1:2, :] = centre
    range_ref[2:8, :] = jnp.zeros((6, size), jnp.float32)

    ky = lax.broadcasted_iota(jnp.int32, (size, size), 0)
    row = lax.broadcasted_iota(jnp.int32, (size, size), 1)
    found = row // 2
    back = (found % SIDE, (found // SIDE) % SIDE, found // SIDE**2)
    sources = []
    for owner, order in enumerate(ORDERS):
        x, y, z = moved(place_ref, back, order, -1)
        sources.append(SIDE * (z * (SIDE * CORES) + y * CORES + owner) + x)
    from_own = jnp.where(second, sources[1], sources[0])
    from_other = jnp.where(second, sources[0], sources[1])
    given = jnp.concatenate([own_ref[size : 2 * size, :], other_ref[size : 2 * size, :]], 0)
    picks = [
        jnp.concatenate(
            [
                jnp.where(row % 2 == sign, (ky == source).astype(jnp.float32), 0.0).astype(jnp.bfloat16)
                for source in (from_own, from_other)
            ],
            1,
        )
        for sign in range(2)
    ]
    signs = select_rows(jnp.concatenate(picks, 0), given)
    plus, minus = signs[:size], signs[size:]
    mine = jnp.where(second, minus, plus)
    partner = jnp.where(alone, mine, jnp.where(second, plus, minus))
    scaled = (mine + select_lanes(select_rows(mirror_ref[...], partner), mirror_ref[...])) * 0.5 / span
    scaled_ref[...] = scaled.T

    mine, theirs = own_ref[:size, :], other_ref[:size, :]
    re = jnp.where(jnp.logical_and(second, jnp.logical_not(alone)), theirs, mine)
    im = jnp.where(alone, jnp.zeros_like(mine), jnp.where(second, -mine, theirs))
    ends = dot(jnp.concatenate([re, im], 0), lanes_ref[...])
    mid_real = ends[:size, :size] + ends[size:, size:]
    mid_imag = ends[size:, :size] - ends[:size, size:]
    both = dot(rows_ref[...], jnp.concatenate([mid_real, mid_imag], 1))
    real = both[:size, :size] + both[size:, size:]
    imag = both[:size, size:] - both[size:, :size]
    real_ref[...] = real
    imag_ref[...] = imag
    scaled = scaled_ref[...]
    power = real * real + imag * imag
    chunk = 24
    totals = [None] * MOMENTS
    for start in range(0, size // 2 + 8, chunk):
        row = lax.broadcasted_iota(jnp.int32, (chunk, size), 0) + start
        share = jnp.where(row % (size // 2) == 0, 1.0, jnp.where(row < size // 2, 2.0, 0.0))
        t = scaled[start : start + chunk] - centre
        p = power[start : start + chunk] * share
        p_parts = halves(p)
        t2 = t * 2.0
        t2_parts = halves(t2)
        zero = jnp.zeros_like(t)
        before, here = (jnp.ones_like(t), zero), (t, zero)
        for order in range(MOMENTS):
            value = before
            v_parts = halves(value[0])
            term, low_term = two_prod(value[0], p, v_parts, p_parts)
            term = (term, low_term + value[1] * p)
            total, spill = totals[order] or (None, None)
            for i in range(0, chunk, 8):
                piece, rest = term[0][i : i + 8], term[1][i : i + 8]
                if total is None:
                    total, spill = piece, rest
                else:
                    total, lost = two_sum(total, piece)
                    spill = spill + (lost + rest)
            totals[order] = total, spill
            if order + 1 < MOMENTS:
                up, low_up = two_prod(here[0], t2, None, t2_parts)
                following, lost = two_sum(up, -before[0])
                before, here = here, (following, lost + ((low_up + here[1] * t2) - before[1]))
    row = lax.broadcasted_iota(jnp.int32, (8, size), 0)
    lane = lax.broadcasted_iota(jnp.int32, (8, size), 1)
    out = jnp.zeros((8, size), jnp.float32)
    for base in range(0, MOMENTS, 8):
        high_rows = jnp.zeros((8, size), jnp.float32)
        low_rows = jnp.zeros((8, size), jnp.float32)
        for order in range(base, min(base + 8, MOMENTS)):
            total = sublane_total(quick_sum(*totals[order]))
            high_rows = jnp.where(row == order - base, total[0], high_rows)
            low_rows = jnp.where(row == order - base, total[1], low_rows)
        high_rows, low_rows = lane_total((high_rows, low_rows))
        out = jnp.where(lane == row + base, high_rows, out)
        out = jnp.where(lane == row + (base + LOW_LANE), low_rows, out)
    line = jnp.sum(out, axis=0, keepdims=True)
    send_ref[...] = jnp.broadcast_to(line, (size, size))


def lane_of(a, lane):
    pick = lambda v: jnp.broadcast_to(v[:, lane : lane + 1], v.shape)
    return pick(a[0]), pick(a[1])


def solve_kernel(
    sums_ref, range_ref, scaled_ref, real_ref, imag_ref, lanes_ref, rows_ref, out_ref, gain_ref, *, scale
):
    size = scaled_ref.shape[0]
    given = sums_ref[...]
    low = pltpu.roll(given, size - LOW_LANE, 1)
    rows = [(given[i : i + 8], low[i : i + 8]) for i in range(0, given.shape[0], 8)]
    while len(rows) > 1:
        rows = [dd_add(rows[i], rows[i + 1]) for i in range(0, len(rows), 2)]
    moments = sublane_total(rows[0])
    half = range_ref[0:1, :]
    centre = jnp.broadcast_to(range_ref[1:2, :], moments[0].shape)
    centre = (centre, jnp.zeros_like(centre))
    lane = lax.broadcasted_iota(jnp.int32, moments[0].shape, 1)
    resid, direct = moments, moments
    held = lane_of(resid, 0)
    steps, turns = [], []
    decay = jnp.ones((1, size), jnp.float32)
    for k in range(ITERS):
        after = tuple(pltpu.roll(v, size - 1, 1) for v in direct)
        prior = tuple(pltpu.roll(v, 1, 1) for v in direct)
        prior = tuple(jnp.where(lane == 0, a, p) for a, p in zip(after, prior))
        image = dd_add(dd_mul(direct, centre), dd_scale(dd_add(after, prior), 0.5))
        alpha = dd_div(held, lane_of(image, k))
        fresh = dd_add(resid, dd_neg(dd_mul(alpha, image)))
        reached = lane_of(fresh, k + 1)
        beta = dd_mul(alpha, dd_div(reached, held))
        held = reached
        beta = dd_scale(beta, -1.0 if k == 0 else -0.5)
        direct = dd_add(fresh, dd_mul(beta, direct))
        resid = fresh
        steps.append(alpha[0][0:1])
        turns.append(beta[0][0:1])
        decay = decay * beta[0][0:1]
    gain = lax.rsqrt(jnp.maximum(jnp.abs(decay), 1e-30)) / centre[0][0:1]
    gain_ref[...] = jnp.broadcast_to(gain, gain_ref.shape)
    scaled = scaled_ref[...]
    field = steps[0]
    solved = jnp.broadcast_to(field, scaled.shape)
    left = 1.0 - field * scaled
    toward = left + turns[0]
    for k in range(1, ITERS):
        solved = solved + steps[k] * toward
        left = left - steps[k] * (scaled * toward)
        if k + 1 < ITERS:
            toward = left + turns[k] * toward
    solved = solved * (scale / half)
    left = left * (gain * scale)
    real, imag = real_ref[...], imag_ref[...]
    back_real = solved * real - left * imag
    back_imag = solved * imag + left * real
    ends = dot_pieces(stacked(jnp.concatenate([back_real, back_imag], 0), 1), lanes_ref[...], 1, 0)
    mid_real = ends[:size, :size] - ends[size:, size:]
    mid_imag = ends[size:, :size] + ends[:size, size:]
    both = dot_pieces(rows_ref[...], stacked(jnp.concatenate([mid_real, mid_imag], 1), 0), 1, 0)
    real = both[:size, :size] - both[size:, size:]
    imag = both[:size, size:] + both[size:, :size]
    for copy in range(out_ref.shape[0] // (2 * size)):
        out_ref[pl.ds(copy * 2 * size, size, stride=2), :] = real
        out_ref[pl.ds(copy * 2 * size + 1, size, stride=2), :] = imag


def output_kernel(given_ref, gain_ref, back_ref, field_ref, resid_ref):
    planes, size = field_ref.shape[0], field_ref.shape[1]
    step = 2 * planes
    shrink = 1.0 / gain_ref[0:1, :]
    for j in range(planes):
        pieces = [given_ref[pl.ds(2 * j + part, size, stride=step), :] for part in range(2)]
        both = dot_pieces(stacked(jnp.concatenate(pieces, 0), 0), back_ref[...], 0, 0)
        field_ref[j] = both[:, :size]
        resid_ref[j] = both[:, size:] * shrink


def call(kernel, shapes, *args):
    whole = pl.BlockSpec(memory_space=pltpu.VMEM)
    scalars = pl.BlockSpec(memory_space=pltpu.SMEM)
    return pl.pallas_call(
        kernel,
        out_shape=[jax.ShapeDtypeStruct(s, jnp.float32) for s in shapes],
        in_specs=[scalars if a.dtype == jnp.int32 else whole for a in args],
        out_specs=[whole] * len(shapes),
    )(*args)


def exchange(parts, axes):
    return [parts[0]] + [lax.ppermute(parts[r], ALL, shift_pairs(axes, r)) for r in range(1, SIDE)]


def summed(parts):
    return ((parts[0] + parts[1]) + parts[2]) + parts[3]


def body(intensities, gridding, dest_slab, spectral_weights):
    ngrid = lax.axis_size("grid")
    ndp = lax.axis_size("dp")
    nent, _, size = intensities.shape
    planes = gridding.shape[2] // size
    count = ngrid * ndp
    capacity = max(2, 2 * nent // ngrid)
    table = dft_tables(size)
    square = (size, size)
    swap = lambda a: lax.ppermute(a, ALL, shift_pairs((3, 3), 1))

    chip = lax.axis_index("dp") * (ngrid // CORES) + lax.axis_index("grid") // CORES
    core = lax.axis_index("grid") % CORES
    step = jnp.arange(5, dtype=jnp.int32)
    x, y, z = place_of(chip * CORES)[:3]
    place = jnp.where(
        step == 0, x, jnp.where(step == 1, y, jnp.where(step == 2, z, jnp.where(step == 3, core, chip == 0)))
    ).astype(jnp.int32)

    *away, wave, counts, lists, p0, p1, p2, p3 = grid_call(
        False, 0, ngrid, capacity, dest_slab[:, 0], place, intensities, gridding, table["packed"], spectral_weights
    )
    members = (counts, lists, place, wave, gridding)
    arrived = [swap(a) for a in away]
    weights = exchange([p0, p1, p2, p3], (0, 0))
    axes = [[order[stage] for order in ORDERS] for stage in range(3)]
    quarter = lambda a: [p.reshape(p.shape[1:]) for p in jnp.split(a.reshape((SIDE, -1) + a.shape[1:]), SIDE)]
    least = lambda parts: functools.reduce(jnp.minimum, parts)
    data = []
    for part in range(2):
        kept = grid_call(True, part, ngrid, capacity, *members, arrived[part], *(weights if part else ()))
        data.append(exchange(kept, axes[0]))
    parts = quarter(summed(data[0]))
    early = exchange(parts, axes[1])
    late = SHARES[1] * size // STEPS
    parts = [summed([a[:, :-8] for a in data[1]]), least([a[:, -8:] for a in data[1]])]
    parts = quarter(jnp.concatenate(parts, 1))
    parts = exchange(parts, axes[1])
    for stage in (1, 2):
        if stage == 2:
            parts = exchange(quarter(parts), axes[2])
            late = size
        found = [
            summed([a[:, :late] for a in parts]),
            jnp.concatenate([a[:, late:-8] for a in parts], 1),
            least([a[:, -8:] for a in parts]),
        ]
        if stage == 1:
            found = [summed(early)] + found
        parts = jnp.concatenate(found, 1)
    parts = parts[0]
    real, imag, scaled, ends, send = call(
        moment_kernel, [square, square, square, (8, size), square],
        parts, swap(parts), place, table["lanes"], table["rows"], table["mirror"],
    )
    sums = lax.all_to_all(send.reshape(count, 1, size), ALL, 0, 0, tiled=True).reshape(count, size)
    back, gain = call(
        functools.partial(solve_kernel, scale=1.0 / size**3), [(ndp * 2 * size, size), (8, size)],
        sums, ends, scaled, real, imag, table["lanes_pieces"], table["rows_pieces"],
    )
    landed = lax.all_to_all(back.reshape(count, 2 * planes, size), ALL, 0, 0, tiled=True)
    return tuple(
        call(
            output_kernel, [(planes, size, size)] * 2,
            landed.reshape(count * 2 * planes, size), gain, table["back_pieces"],
        )
    )


def solution(mesh):
    return jax.shard_map(
        body,
        mesh=mesh,
        in_specs=(
            P(("dp", "grid"), None, None),
            P(("dp", "grid"), None, None),
            P(("dp", "grid"), None),
            P("dp", None, "grid", None),
        ),
        out_specs=(P("grid", None, None), P("grid", None, None)),
        check_vma=False,
    )
```

```python
import functools

import jax
import jax.numpy as jnp
import numpy as np
from jax import lax
from jax.experimental import pallas as pl
from jax.experimental.pallas import tpu as pltpu
from jax.sharding import PartitionSpec as P


ITERS = 8
MOMENTS = 2 * ITERS + 1
LOW_LANE = 64
ALL = ("dp", "grid")
HIGHEST = lax.Precision.HIGHEST


def two_sum(a, b):
    s = a + b
    v = s - a
    return s, (a - (s - v)) + (b - v)


def quick_sum(a, b):
    s = a + b
    return s, b - (s - a)


def halves(a):
    c = a * 4097.0
    high = c - (c - a)
    return high, a - high


def two_prod(a, b, a_parts=None, b_parts=None):
    p = a * b
    ah, al = a_parts or halves(a)
    bh, bl = b_parts or halves(b)
    return p, ((ah * bh - p) + ah * bl + al * bh) + al * bl


def dd_add(a, b):
    s, e = two_sum(a[0], b[0])
    return quick_sum(s, e + (a[1] + b[1]))


def dd_mul(a, b):
    p, e = two_prod(a[0], b[0])
    return quick_sum(p, e + (a[0] * b[1] + a[1] * b[0]))


def dd_times(a, b):
    p, e = two_prod(a[0], b)
    return quick_sum(p, e + a[1] * b)


def dd_scale(a, factor):
    return a[0] * factor, a[1] * factor


def dd_neg(a):
    return -a[0], -a[1]


def dd_div(a, b):
    inverse = 1.0 / b[0]
    first = a[0] * inverse
    rest = dd_add(a, dd_neg(dd_times(b, first)))
    return quick_sum(first, rest[0] * inverse)


def dot(a, b):
    return jax.lax.dot_general(
        a, b, (((1,), (0,)), ((), ())), precision=HIGHEST, preferred_element_type=jnp.float32
    )


SIDE = 4
CORES = 2
ORDERS = ((0, 2, 1), (1, 2, 0))


def place_of(device):
    chip = device // CORES
    return chip // SIDE**2, chip % SIDE, (chip // SIDE) % SIDE, device % CORES


def chip_at(x, y, z):
    return (x * SIDE + z) * SIDE + y


def shift_pairs(axes, hop):
    pairs = []
    for device in range(SIDE**3 * CORES):
        place = list(place_of(device))
        axis = axes[place[3]]
        place[axis] = (place[axis] + hop) % (CORES if axis == 3 else SIDE)
        pairs.append((device, chip_at(*place[:3]) * CORES + place[3]))
    return pairs


def held_rows(size):
    chip, core = np.arange(size) // CORES, np.arange(size) % CORES
    return np.where(chip == 0, core * size // 2, np.where(core == 0, chip, size - chip))


def dft_tables(size):
    index = np.arange(size)
    angle = 2.0 * np.pi * ((index[:, None] * index[None, :]) % size) / size
    cos, sin = np.cos(angle), np.sin(angle)
    held = held_rows(size)
    as_f32 = lambda a: np.ascontiguousarray(a, dtype=np.float32)
    half = size // 2
    packed = np.concatenate([cos[:, :half], cos[:, half : half + 1], -sin[:, 1:half]], 1)
    high = packed.astype(jnp.bfloat16)
    low = (packed - high.astype(np.float64)).astype(jnp.bfloat16)
    lanes, rows = np.concatenate([cos, sin], 1), np.concatenate([cos, sin], 0)
    back = np.concatenate(
        [np.concatenate([cos[held], sin[held]], 1), np.concatenate([-sin[held], cos[held]], 1)], 0
    )

    def thrice(table, axis):
        above = table.astype(jnp.bfloat16)
        below = (table - above.astype(np.float64)).astype(jnp.bfloat16)
        return np.concatenate([above, above, below], axis)

    return dict(
        packed=np.stack([np.concatenate([p[:, :half], q[:, :half]], 1) for p, q in ((high, low), (high[:, half:], low[:, half:]))]),
        lanes=as_f32(lanes),
        rows=as_f32(rows),
        lanes_pieces=thrice(lanes, 0),
        rows_pieces=thrice(rows, 1),
        back_pieces=thrice(back, 0),
        mirror=(((index[:, None] + index[None, :]) % size) == 0).astype(jnp.bfloat16),
    )


def dot_as(a, b, left, right):
    return lax.dot_general(
        a, b, (((left,), (right,)), ((), ())), precision=HIGHEST, preferred_element_type=jnp.float32
    )


def pieces_of(a, count):
    found = []
    for _ in range(count):
        piece = a.astype(jnp.bfloat16)
        found.append(piece)
        a = a - piece.astype(jnp.float32)
    return found


def dot_pieces(a, b, left, right):
    return lax.dot_general(a, b, (((left,), (right,)), ((), ())), preferred_element_type=jnp.float32)


def stacked(a, axis):
    high, low = pieces_of(a, 2)
    return jnp.concatenate([high, low, high], axis)


def select_rows(one_hot, a):
    width = a.shape[1]
    found = dot_pieces(one_hot, jnp.concatenate(pieces_of(a, 3), 1), 1, 0)
    return (found[:, :width] + found[:, width : 2 * width]) + found[:, 2 * width :]


def select_lanes(a, one_hot):
    height = a.shape[0]
    found = dot_pieces(jnp.concatenate(pieces_of(a, 3), 0), one_hot, 1, 0)
    return (found[:height] + found[height : 2 * height]) + found[2 * height :]


HALVES = 2
STEPS = 4


def sublane_turn(tiles):
    row = lax.broadcasted_iota(jnp.int32, tiles[0].shape, 0)
    for bit in (4, 2, 1):
        low = (row & bit) == 0
        turned = list(tiles)
        for i in range(8):
            if i & bit == 0:
                a, b = tiles[i], tiles[i + bit]
                turned[i] = jnp.where(low, a, pltpu.roll(b, bit, 0))
                turned[i + bit] = jnp.where(low, pltpu.roll(a, 8 - bit, 0), b)
        tiles = turned
    return tiles


def grid_kernel(*refs, kept, part, capacity):
    if kept:
        count_ref, list_ref, place_ref, wave_ref, matrix_ref, other_ref = refs[:6]
        weight_refs = refs[6 : 6 + SIDE] if part else ()
        outs, row_refs = refs[6 + len(weight_refs) :][:SIDE], refs[6 + len(weight_refs) :][SIDE:]
    else:
        dest_ref, place_ref, values_ref, source_ref, packed_ref, weights_ref = refs[:6]
        out_refs, (kept_wave_ref, count_ref, list_ref), slice_refs = refs[6:8], refs[8:11], refs[11 : 11 + SIDE]
        wave_ref, matrix_ref, fetched = refs[-3:]
    nent, rows, width = matrix_ref.shape
    size = width // SIDE
    half = size // 2
    nslab = count_ref.shape[0]
    step = pl.program_id(0)

    def clear(s, _):
        count_ref[s] = 0
        return 0

    def enter(e, _):
        slab = dest_ref[e]
        taken = count_ref[slab]
        list_ref[slab * capacity + taken] = e
        count_ref[slab] = taken + 1
        return 0

    def prepare():
        fetch = pltpu.make_async_copy(source_ref, matrix_ref, fetched)
        fetch.start()
        lax.fori_loop(0, nslab, clear, 0)
        lax.fori_loop(0, nent, enter, 0)
        for r, slice_ref in enumerate(slice_refs):
            slice_ref[...] = weights_ref[0, :, (place_ref[0] + r) % SIDE, :]
        chip = lax.broadcasted_iota(jnp.int32, (half, half), 0)
        slot = lax.broadcasted_iota(jnp.int32, (half, half), 1)
        digits = digits_of(slot)
        pieces = []
        chips = [chip_at(*moved(place_ref, digits, owner, 1)) for owner in range(CORES)]
        for owner in (1 - place_ref[3], place_ref[3]):
            pick = (chip == jnp.where(owner == 0, chips[0], chips[1])).astype(jnp.float32).astype(jnp.bfloat16)
            for start in (0, half):
                piece = packed_ref[owner, :, start : start + half]
                pieces.append(jnp.dot(piece, pick, preferred_element_type=jnp.float32).astype(jnp.bfloat16))
        both = jnp.dot(
            values_ref[...].reshape(nent * rows, size),
            jnp.concatenate(pieces, 1),
            preferred_element_type=jnp.float32,
        )
        for at, target_ref in ((0, wave_ref), (size, kept_wave_ref)):
            wave = both[:, at : at + half] + both[:, at + half : at + size]
            high = wave.astype(jnp.bfloat16)
            low = (wave - high.astype(jnp.float32)).astype(jnp.bfloat16)
            target_ref[...] = jnp.concatenate([high, low], 1).reshape(nent, rows, size)
        fetch.wait()

    if not kept:
        pl.when(step == 0)(prepare)

    pairs = nslab // (2 * STEPS)

    def products(out):
        for pair in range(pairs):
            halves_of_tile = []
            for near in range(2):
                slab = ((part * (STEPS // HALVES) + step) * pairs + pair) * 2 + near
                taken = count_ref[slab]
                waves, matrices = [], []
                for m in range(capacity):
                    entry = jnp.where(m < taken, list_ref[slab * capacity + m], 0)
                    wave = wave_ref[entry]
                    waves.append(jnp.where(m < taken, wave, jnp.zeros_like(wave)))
                    matrices.append(matrix_ref[entry])
                product = lax.dot_general(
                    jnp.concatenate(waves, 0),
                    jnp.concatenate(matrices, 0),
                    (((0,), (0,)), ((), ())),
                    preferred_element_type=jnp.float32,
                )
                halves_of_tile.append(product[:half] + product[half:])
            place = slice(pair * 8, pair * 8 + 8)
            for start in range(0, half, 8):
                tiles = [
                    product[start : start + 8, p * size : (p + 1) * size]
                    for product in halves_of_tile
                    for p in range(SIDE)
                ]
                for index, block in enumerate(sublane_turn(tiles), start):
                    out(index, place, block)

    def keep(index, place, block):
        outs[index // SIDE**2][index % SIDE**2, place, :] = block + other_ref[index, place, :]

    def send(out_ref):
        def write(index, place, block):
            out_ref[index, place, :] = block

        return write

    if kept:
        products(keep)
        if part:
            pl.when(step == STEPS // HALVES - 1)(lambda: weight_kernel(*weight_refs, place_ref, *row_refs))
    else:
        pl.when(step < STEPS // HALVES)(lambda: products(send(out_refs[0])))
        pl.when(step >= STEPS // HALVES)(lambda: products(send(out_refs[1])))


def grid_call(kept, part, nslab, capacity, *args):
    scalars = pl.BlockSpec(memory_space=pltpu.SMEM)
    fixed = lambda shape: pl.BlockSpec(shape, lambda i: (0,) * len(shape))
    matrix = args[4] if kept else args[3]
    nent, rows, width = matrix.shape
    size, blocks = width // SIDE, SIDE**3
    steps = STEPS // HALVES if kept else STEPS
    moving = lambda count: pl.BlockSpec((count, size // STEPS, size), lambda i: (0, i, 0))
    f32 = lambda *shape: jax.ShapeDtypeStruct(shape, jnp.float32)
    in_specs = [scalars if a.dtype == jnp.int32 else fixed(a.shape) for a in args]
    if kept:
        out_shape, out_specs = [f32(SIDE**2, size // HALVES, size)] * SIDE, [moving(SIDE**2)] * SIDE
        in_specs[5] = moving(blocks)
        if part:
            rows_shape = (SIDE**2 * 8 + 8, size)
            out_shape = out_shape + [f32(*rows_shape)] * SIDE
            out_specs = out_specs + [fixed(rows_shape)] * SIDE
        scratch = []
    else:
        wave = (nent, rows, size)
        out_shape = [f32(blocks, size // HALVES, size)] * HALVES + [
            jax.ShapeDtypeStruct(wave, jnp.bfloat16),
            jax.ShapeDtypeStruct((nslab,), jnp.int32),
            jax.ShapeDtypeStruct((nslab * capacity,), jnp.int32),
        ] + [f32(size, size)] * SIDE
        block = (blocks, size // STEPS, size)
        out_specs = [
            pl.BlockSpec(block, lambda i: (0, jnp.minimum(i, STEPS // HALVES - 1), 0)),
            pl.BlockSpec(block, lambda i: (0, jnp.maximum(i - STEPS // HALVES, 0), 0)),
        ] + [fixed(wave), scalars, scalars] + [fixed((size, size))] * SIDE
        in_specs[3] = pl.BlockSpec(memory_space=pl.ANY)
        scratch = [pltpu.VMEM(wave, jnp.bfloat16), pltpu.VMEM(matrix.shape, jnp.bfloat16), pltpu.SemaphoreType.DMA]
    return pl.pallas_call(
        functools.partial(grid_kernel, kept=kept, part=part, capacity=capacity),
        grid=(steps,),
        out_shape=out_shape,
        in_specs=in_specs,
        out_specs=out_specs,
        scratch_shapes=scratch,
    )(*args)


def moved(place_ref, digits, owner, sign):
    at = [place_ref[0], place_ref[1], place_ref[2]]
    for digit, axis in zip(digits, ORDERS[owner]):
        at[axis] = (at[axis] + sign * digit + SIDE) % SIDE
    return at


def digits_of(index):
    return index // SIDE**2, (index // SIDE) % SIDE, index % SIDE


def weight_kernel(w0_ref, w1_ref, w2_ref, w3_ref, place_ref, *outs):
    size = w0_ref.shape[0]
    half = size // 2
    own = ((w0_ref[...] + w1_ref[...]) + w2_ref[...]) + w3_ref[...]
    low = jnp.min(jnp.min(own, axis=0, keepdims=True), axis=1, keepdims=True)
    high = jnp.max(jnp.max(own, axis=0, keepdims=True), axis=1, keepdims=True)
    row = lax.broadcasted_iota(jnp.int32, (size, size), 0)
    lane = lax.broadcasted_iota(jnp.int32, (size, size), 1)
    chips = [chip_at(*moved(place_ref, digits_of(row % half), owner, 1)) for owner in range(CORES)]
    chip = jnp.where(place_ref[3] == 0, chips[0], chips[1])
    negative = jnp.where(chip == 0, half, size - chip)
    pick = (lane == jnp.where(row < half, chip, negative)).astype(jnp.float32)
    rows = dot_as(pick, own, 1, 1)
    ends = jnp.where(lax.broadcasted_iota(jnp.int32, (8, size), 1) < half, low, -high)
    count = half // SIDE
    for r, out_ref in enumerate(outs):
        out_ref[...] = jnp.zeros(out_ref.shape, jnp.float32)
        out_ref[8 * count :, :] = ends
        for sign in range(2):
            at = sign * half + r * count
            out_ref[pl.ds(2 * r + sign, count, stride=8), :] = rows[at : at + count]


def sublane_total(a):
    for shift in (4, 2, 1):
        a = dd_add(a, (pltpu.roll(a[0], shift, 0), pltpu.roll(a[1], shift, 0)))
    return a


def lane_total(a):
    for shift in (64, 32, 16, 8, 4, 2, 1):
        a = dd_add(a, (pltpu.roll(a[0], shift, 1), pltpu.roll(a[1], shift, 1)))
    return a


def moment_kernel(
    own_ref, other_ref, place_ref, lanes_ref, rows_ref, mirror_ref, real_ref, imag_ref, scaled_ref, range_ref, send_ref
):
    size = scaled_ref.shape[0]
    second, alone = place_ref[3] == 1, place_ref[4] == 1
    lane8 = lax.broadcasted_iota(jnp.int32, (8, size), 1)
    ends = jnp.minimum(own_ref[2 * size :, :], other_ref[2 * size :, :])
    least = lambda v: jnp.min(jnp.min(v, axis=0, keepdims=True), axis=1, keepdims=True)
    low = least(jnp.where(lane8 < size // 2, ends, 1e30))
    high = -least(jnp.where(lane8 < size // 2, 1e30, ends))
    span = jnp.broadcast_to(jnp.maximum((high - low) * 0.5, high * 1e-4), (1, size))
    centre = jnp.broadcast_to((high + low) * 0.5, (1, size)) / span
    range_ref[0:1, :] = span
    range_ref[1:2, :] = centre
    range_ref[2:8, :] = jnp.zeros((6, size), jnp.float32)

    ky = lax.broadcasted_iota(jnp.int32, (size, size), 0)
    row = lax.broadcasted_iota(jnp.int32, (size, size), 1)
    found = row // 2
    back = (found % SIDE, (found // SIDE) % SIDE, found // SIDE**2)
    sources = []
    for owner in range(CORES):
        x, y, z = moved(place_ref, back, owner, -1)
        sources.append(SIDE * (z * (SIDE * CORES) + y * CORES + owner) + x)
    from_own = jnp.where(second, sources[1], sources[0])
    from_other = jnp.where(second, sources[0], sources[1])
    given = jnp.concatenate([own_ref[size : 2 * size, :], other_ref[size : 2 * size, :]], 0)
    picks = [
        jnp.concatenate(
            [
                jnp.where(row % 2 == sign, (ky == source).astype(jnp.float32), 0.0).astype(jnp.bfloat16)
                for source in (from_own, from_other)
            ],
            1,
        )
        for sign in range(2)
    ]
    signs = select_rows(jnp.concatenate(picks, 0), given)
    plus, minus = signs[:size], signs[size:]
    mine = jnp.where(second, minus, plus)
    partner = jnp.where(alone, mine, jnp.where(second, plus, minus))
    scaled = (mine + select_lanes(select_rows(mirror_ref[...], partner), mirror_ref[...])) * 0.5 / span
    scaled_ref[...] = scaled.T

    mine, theirs = own_ref[:size, :], other_ref[:size, :]
    re = jnp.where(jnp.logical_and(second, jnp.logical_not(alone)), theirs, mine)
    im = jnp.where(alone, jnp.zeros_like(mine), jnp.where(second, -mine, theirs))
    ends = dot(jnp.concatenate([re, im], 0), lanes_ref[...])
    mid_real = ends[:size, :size] + ends[size:, size:]
    mid_imag = ends[size:, :size] - ends[:size, size:]
    both = dot(rows_ref[...], jnp.concatenate([mid_real, mid_imag], 1))
    real = both[:size, :size] + both[size:, size:]
    imag = both[:size, size:] - both[size:, :size]
    real_ref[...] = real
    imag_ref[...] = imag
    scaled = scaled_ref[...]
    power = real * real + imag * imag
    chunk = 24
    totals = [None] * MOMENTS
    for start in range(0, size // 2 + 8, chunk):
        row = lax.broadcasted_iota(jnp.int32, (chunk, size), 0) + start
        share = jnp.where(row % (size // 2) == 0, 1.0, jnp.where(row < size // 2, 2.0, 0.0))
        t = scaled[start : start + chunk] - centre
        p = power[start : start + chunk] * share
        p_parts = halves(p)
        t2 = t * 2.0
        t2_parts = halves(t2)
        zero = jnp.zeros_like(t)
        before, here = (jnp.ones_like(t), zero), (t, zero)
        for order in range(MOMENTS):
            value = before
            v_parts = halves(value[0])
            term, low_term = two_prod(value[0], p, v_parts, p_parts)
            term = (term, low_term + value[1] * p)
            total, spill = totals[order] or (None, None)
            for i in range(0, chunk, 8):
                piece, rest = term[0][i : i + 8], term[1][i : i + 8]
                if total is None:
                    total, spill = piece, rest
                else:
                    total, lost = two_sum(total, piece)
                    spill = spill + (lost + rest)
            totals[order] = total, spill
            if order + 1 < MOMENTS:
                up, low_up = two_prod(here[0], t2, None, t2_parts)
                following, lost = two_sum(up, -before[0])
                before, here = here, (following, lost + ((low_up + here[1] * t2) - before[1]))
    row = lax.broadcasted_iota(jnp.int32, (8, size), 0)
    lane = lax.broadcasted_iota(jnp.int32, (8, size), 1)
    out = jnp.zeros((8, size), jnp.float32)
    for base in range(0, MOMENTS, 8):
        high_rows = jnp.zeros((8, size), jnp.float32)
        low_rows = jnp.zeros((8, size), jnp.float32)
        for order in range(base, min(base + 8, MOMENTS)):
            total = sublane_total(quick_sum(*totals[order]))
            high_rows = jnp.where(row == order - base, total[0], high_rows)
            low_rows = jnp.where(row == order - base, total[1], low_rows)
        high_rows, low_rows = lane_total((high_rows, low_rows))
        out = jnp.where(lane == row + base, high_rows, out)
        out = jnp.where(lane == row + (base + LOW_LANE), low_rows, out)
    line = jnp.sum(out, axis=0, keepdims=True)
    send_ref[...] = jnp.broadcast_to(line, (size, size))


def lane_of(a, lane):
    pick = lambda v: jnp.broadcast_to(v[:, lane : lane + 1], v.shape)
    return pick(a[0]), pick(a[1])


def solve_kernel(sums_ref, range_ref, *refs, scale):
    sources, (out_ref, gain_ref), held, (result_ref, fetched, sent) = refs[:5], refs[5:7], refs[7:12], refs[12:]
    fetches = [pltpu.make_async_copy(a, b, fetched.at[i]) for i, (a, b) in enumerate(zip(sources, held))]
    for fetch in fetches:
        fetch.start()
    scaled_ref, real_ref, imag_ref, lanes_ref, rows_ref = held
    size = scaled_ref.shape[0]
    given = sums_ref[...]
    low = pltpu.roll(given, size - LOW_LANE, 1)
    rows = [(given[i : i + 8], low[i : i + 8]) for i in range(0, given.shape[0], 8)]
    while len(rows) > 1:
        rows = [dd_add(rows[i], rows[i + 1]) for i in range(0, len(rows), 2)]
    moments = sublane_total(rows[0])
    half = range_ref[0:1, :]
    centre = jnp.broadcast_to(range_ref[1:2, :], moments[0].shape)
    centre = (centre, jnp.zeros_like(centre))
    lane = lax.broadcasted_iota(jnp.int32, moments[0].shape, 1)
    resid, direct = moments, moments
    held = lane_of(resid, 0)
    steps, turns = [], []
    decay = jnp.ones((1, size), jnp.float32)
    for k in range(ITERS):
        after = tuple(pltpu.roll(v, size - 1, 1) for v in direct)
        prior = tuple(pltpu.roll(v, 1, 1) for v in direct)
        prior = tuple(jnp.where(lane == 0, a, p) for a, p in zip(after, prior))
        image = dd_add(dd_mul(direct, centre), dd_scale(dd_add(after, prior), 0.5))
        alpha = dd_div(held, lane_of(image, k))
        fresh = dd_add(resid, dd_neg(dd_mul(alpha, image)))
        reached = lane_of(fresh, k + 1)
        beta = dd_mul(alpha, dd_div(reached, held))
        held = reached
        beta = dd_scale(beta, -1.0 if k == 0 else -0.5)
        direct = dd_add(fresh, dd_mul(beta, direct))
        resid = fresh
        steps.append(alpha[0][0:1])
        turns.append(beta[0][0:1])
        decay = decay * beta[0][0:1]
    gain = lax.rsqrt(jnp.maximum(jnp.abs(decay), 1e-30)) / centre[0][0:1]
    gain_ref[...] = jnp.broadcast_to(gain, gain_ref.shape)
    for fetch in fetches:
        fetch.wait()
    scaled = scaled_ref[...]
    field = steps[0]
    solved = jnp.broadcast_to(field, scaled.shape)
    left = 1.0 - field * scaled
    toward = left + turns[0]
    for k in range(1, ITERS):
        solved = solved + steps[k] * toward
        left = left - steps[k] * (scaled * toward)
        if k + 1 < ITERS:
            toward = left + turns[k] * toward
    solved = solved * (scale / half)
    left = left * (gain * scale)
    real, imag = real_ref[...], imag_ref[...]
    back_real = solved * real - left * imag
    back_imag = solved * imag + left * real
    ends = dot_pieces(stacked(jnp.concatenate([back_real, back_imag], 0), 1), lanes_ref[...], 1, 0)
    mid_real = ends[:size, :size] - ends[size:, size:]
    mid_imag = ends[size:, :size] + ends[:size, size:]
    both = dot_pieces(rows_ref[...], stacked(jnp.concatenate([mid_real, mid_imag], 1), 0), 1, 0)
    real = both[:size, :size] - both[size:, size:]
    imag = both[:size, size:] + both[size:, :size]
    result_ref[pl.ds(0, size, stride=2), :] = real
    result_ref[pl.ds(1, size, stride=2), :] = imag
    copies = [pltpu.make_async_copy(result_ref, out_ref.at[i], sent.at[i]) for i in range(out_ref.shape[0])]
    for copy in copies:
        copy.start()
    for copy in copies:
        copy.wait()


def solve_call(copies, scale, *args):
    whole = pl.BlockSpec(memory_space=pltpu.VMEM)
    apart = pl.BlockSpec(memory_space=pl.ANY)
    size = args[0].shape[1]
    return pl.pallas_call(
        functools.partial(solve_kernel, scale=scale),
        out_shape=[
            jax.ShapeDtypeStruct((copies, 2 * size, size), jnp.float32),
            jax.ShapeDtypeStruct((8, size), jnp.float32),
        ],
        in_specs=[whole] * 2 + [apart] * (len(args) - 2),
        out_specs=[apart, whole],
        scratch_shapes=[pltpu.VMEM(a.shape, a.dtype) for a in args[2:]]
        + [
            pltpu.VMEM((2 * size, size), jnp.float32),
            pltpu.SemaphoreType.DMA((len(args) - 2,)),
            pltpu.SemaphoreType.DMA((copies,)),
        ],
        name="solve",
    )(*args)


def output_kernel(given_ref, gain_ref, back_ref, field_ref, resid_ref):
    planes, size = field_ref.shape[0], field_ref.shape[1]
    step = 2 * planes
    shrink = 1.0 / gain_ref[0:1, :]
    for j in range(planes):
        pieces = [given_ref[pl.ds(2 * j + part, size, stride=step), :] for part in range(2)]
        both = dot_pieces(stacked(jnp.concatenate(pieces, 0), 0), back_ref[...], 0, 0)
        field_ref[j] = both[:, :size]
        resid_ref[j] = both[:, size:] * shrink


def call(kernel, shapes, *args):
    whole = pl.BlockSpec(memory_space=pltpu.VMEM)
    scalars = pl.BlockSpec(memory_space=pltpu.SMEM)
    return pl.pallas_call(
        kernel,
        out_shape=[jax.ShapeDtypeStruct(s, jnp.float32) for s in shapes],
        in_specs=[scalars if a.dtype == jnp.int32 else whole for a in args],
        out_specs=[whole] * len(shapes),
    )(*args)


def exchange(parts, axes):
    return [parts[0]] + [lax.ppermute(parts[r], ALL, shift_pairs(axes, r)) for r in range(1, SIDE)]


def summed(parts):
    return ((parts[0] + parts[1]) + parts[2]) + parts[3]


def body(intensities, gridding, dest_slab, spectral_weights):
    ngrid = lax.axis_size("grid")
    ndp = lax.axis_size("dp")
    nent, rows, size = intensities.shape
    planes = gridding.shape[2] // size
    count = ngrid * ndp
    capacity = max(2, 2 * nent // ngrid)
    table = dft_tables(size)
    square = (size, size)
    swap = lambda a: lax.ppermute(a, ALL, shift_pairs((3, 3), 1))

    chip = lax.axis_index("dp") * (ngrid // CORES) + lax.axis_index("grid") // CORES
    core = lax.axis_index("grid") % CORES
    step = jnp.arange(5, dtype=jnp.int32)
    x, y, z = place_of(chip * CORES)[:3]
    place = jnp.where(
        step == 0, x, jnp.where(step == 1, y, jnp.where(step == 2, z, jnp.where(step == 3, core, chip == 0)))
    ).astype(jnp.int32)

    *away, wave, counts, lists, p0, p1, p2, p3 = grid_call(
        False, 0, ngrid, capacity, dest_slab[:, 0], place, intensities, gridding, table["packed"], spectral_weights
    )
    members = (counts, lists, place, wave, gridding)
    arrived = [swap(a) for a in away]
    weights = exchange([p0, p1, p2, p3], (0, 0))
    axes = [[order[stage] for order in ORDERS] for stage in range(3)]
    quarter = lambda a: [p.reshape(p.shape[1:]) for p in jnp.split(a.reshape((SIDE, -1) + a.shape[1:]), SIDE)]
    least = lambda parts: functools.reduce(jnp.minimum, parts)
    data = []
    for part in range(HALVES):
        kept = grid_call(True, part, ngrid, capacity, *members, arrived[part], *(weights if part else ()))
        kept, rows = kept[:SIDE], kept[SIDE:]
        data.append(exchange(kept, axes[0]))
    rows = exchange(rows, axes[0])
    parts = quarter(summed(data[0]))
    early = exchange(parts, axes[1])
    held = summed([a[: SIDE**2 * 8] for a in rows]).reshape(SIDE**2, 8, size)
    ends = jnp.broadcast_to(least([a[SIDE**2 * 8 :] for a in rows])[None], (SIDE**2, 8, size))
    parts = exchange(quarter(jnp.concatenate([summed(data[1]), held, ends], 1)), axes[1])
    late = size // HALVES
    for stage in (1, 2):
        if stage == 2:
            parts = exchange(quarter(parts), axes[2])
            late = size
        found = [
            summed([a[:, :late] for a in parts]),
            jnp.concatenate([a[:, late:-8] for a in parts], 1),
            least([a[:, -8:] for a in parts]),
        ]
        if stage == 1:
            found = [summed(early)] + found
        parts = jnp.concatenate(found, 1)
    parts = parts[0]
    real, imag, scaled, ends, send = call(
        moment_kernel, [square, square, square, (8, size), square],
        parts, swap(parts), place, table["lanes"], table["rows"], table["mirror"],
    )
    sums = lax.all_to_all(send.reshape(count, 1, size), ALL, 0, 0, tiled=True).reshape(count, size)
    back, gain = solve_call(
        ndp, 1.0 / size**3, sums, ends, scaled, real, imag, table["lanes_pieces"], table["rows_pieces"]
    )
    landed = lax.all_to_all(back.reshape(count, 2 * planes, size), ALL, 0, 0, tiled=True)
    return tuple(
        call(
            output_kernel, [(planes, size, size)] * 2,
            landed.reshape(count * 2 * planes, size), gain, table["back_pieces"],
        )
    )


def solution(mesh):
    return jax.shard_map(
        body,
        mesh=mesh,
        in_specs=(
            P(("dp", "grid"), None, None),
            P(("dp", "grid"), None, None),
            P(("dp", "grid"), None),
            P("dp", None, "grid", None),
        ),
        out_specs=(P("grid", None, None), P("grid", None, None)),
        check_vma=False,
    )
```

```python
import functools

import jax
import jax.numpy as jnp
import numpy as np
from jax import lax
from jax.experimental import pallas as pl
from jax.experimental.pallas import tpu as pltpu
from jax.sharding import PartitionSpec as P


ITERS = 8
MOMENTS = 2 * ITERS + 1
LOW_LANE = 64
ALL = ("dp", "grid")
HIGHEST = lax.Precision.HIGHEST


def two_sum(a, b):
    s = a + b
    v = s - a
    return s, (a - (s - v)) + (b - v)


def quick_sum(a, b):
    s = a + b
    return s, b - (s - a)


def halves(a):
    c = a * 4097.0
    high = c - (c - a)
    return high, a - high


def two_prod(a, b, a_parts=None, b_parts=None):
    p = a * b
    ah, al = a_parts or halves(a)
    bh, bl = b_parts or halves(b)
    return p, ((ah * bh - p) + ah * bl + al * bh) + al * bl


def dd_add(a, b):
    s, e = two_sum(a[0], b[0])
    return quick_sum(s, e + (a[1] + b[1]))


def dd_mul(a, b):
    p, e = two_prod(a[0], b[0])
    return quick_sum(p, e + (a[0] * b[1] + a[1] * b[0]))


def dd_times(a, b):
    p, e = two_prod(a[0], b)
    return quick_sum(p, e + a[1] * b)


def dd_scale(a, factor):
    return a[0] * factor, a[1] * factor


def dd_neg(a):
    return -a[0], -a[1]


def dd_div(a, b):
    inverse = 1.0 / b[0]
    first = a[0] * inverse
    rest = dd_add(a, dd_neg(dd_times(b, first)))
    return quick_sum(first, rest[0] * inverse)


def dot(a, b):
    return jax.lax.dot_general(
        a, b, (((1,), (0,)), ((), ())), precision=HIGHEST, preferred_element_type=jnp.float32
    )


SIDE = 4
CORES = 2
ORDERS = ((0, 2, 1), (1, 0, 2))


def place_of(device):
    chip = device // CORES
    return chip // SIDE**2, chip % SIDE, (chip // SIDE) % SIDE, device % CORES


def chip_at(x, y, z):
    return (x * SIDE + z) * SIDE + y


def shift_pairs(axes, hop):
    pairs = []
    for device in range(SIDE**3 * CORES):
        place = list(place_of(device))
        axis = axes[place[3]]
        place[axis] = (place[axis] + hop) % (CORES if axis == 3 else SIDE)
        pairs.append((device, chip_at(*place[:3]) * CORES + place[3]))
    return pairs


def held_rows(size):
    chip, core = np.arange(size) // CORES, np.arange(size) % CORES
    return np.where(chip == 0, core * size // 2, np.where(core == 0, chip, size - chip))


def dft_tables(size):
    index = np.arange(size)
    angle = 2.0 * np.pi * ((index[:, None] * index[None, :]) % size) / size
    cos, sin = np.cos(angle), np.sin(angle)
    held = held_rows(size)
    as_f32 = lambda a: np.ascontiguousarray(a, dtype=np.float32)
    half = size // 2
    packed = np.concatenate([cos[:, :half], cos[:, half : half + 1], -sin[:, 1:half]], 1)
    high = packed.astype(jnp.bfloat16)
    low = (packed - high.astype(np.float64)).astype(jnp.bfloat16)
    lanes, rows = np.concatenate([cos, sin], 1), np.concatenate([cos, sin], 0)
    back = np.concatenate(
        [np.concatenate([cos[held], sin[held]], 1), np.concatenate([-sin[held], cos[held]], 1)], 0
    )

    def thrice(table, axis):
        above = table.astype(jnp.bfloat16)
        below = (table - above.astype(np.float64)).astype(jnp.bfloat16)
        return np.concatenate([above, above, below], axis)

    return dict(
        packed=np.stack([np.concatenate([p[:, :half], q[:, :half]], 1) for p, q in ((high, low), (high[:, half:], low[:, half:]))]),
        lanes=as_f32(lanes),
        rows=as_f32(rows),
        lanes_pieces=thrice(lanes, 0),
        rows_pieces=thrice(rows, 1),
        back_pieces=thrice(back, 0),
        mirror=(((index[:, None] + index[None, :]) % size) == 0).astype(jnp.bfloat16),
    )


def dot_as(a, b, left, right):
    return lax.dot_general(
        a, b, (((left,), (right,)), ((), ())), precision=HIGHEST, preferred_element_type=jnp.float32
    )


def pieces_of(a, count):
    found = []
    for _ in range(count):
        piece = a.astype(jnp.bfloat16)
        found.append(piece)
        a = a - piece.astype(jnp.float32)
    return found


def dot_pieces(a, b, left, right):
    return lax.dot_general(a, b, (((left,), (right,)), ((), ())), preferred_element_type=jnp.float32)


def stacked(a, axis):
    high, low = pieces_of(a, 2)
    return jnp.concatenate([high, low, high], axis)


def select_rows(one_hot, a):
    width = a.shape[1]
    found = dot_pieces(one_hot, jnp.concatenate(pieces_of(a, 3), 1), 1, 0)
    return (found[:, :width] + found[:, width : 2 * width]) + found[:, 2 * width :]


def select_lanes(a, one_hot):
    height = a.shape[0]
    found = dot_pieces(jnp.concatenate(pieces_of(a, 3), 0), one_hot, 1, 0)
    return (found[:height] + found[height : 2 * height]) + found[2 * height :]


HALVES = 2
STEPS = 4


def sublane_turn(tiles):
    row = lax.broadcasted_iota(jnp.int32, tiles[0].shape, 0)
    for bit in (4, 2, 1):
        low = (row & bit) == 0
        turned = list(tiles)
        for i in range(8):
            if i & bit == 0:
                a, b = tiles[i], tiles[i + bit]
                turned[i] = jnp.where(low, a, pltpu.roll(b, bit, 0))
                turned[i + bit] = jnp.where(low, pltpu.roll(a, 8 - bit, 0), b)
        tiles = turned
    return tiles


def grid_kernel(*refs, kept, part, capacity):
    if kept:
        count_ref, list_ref, place_ref, wave_ref, matrix_ref, other_ref = refs[:6]
        weight_refs = refs[6 : 6 + SIDE] if part else ()
        outs, row_refs = refs[6 + len(weight_refs) :][:SIDE], refs[6 + len(weight_refs) :][SIDE:]
    else:
        dest_ref, place_ref, values_ref, source_ref, packed_ref, weights_ref = refs[:6]
        out_refs, (kept_wave_ref, count_ref, list_ref), slice_refs = refs[6:8], refs[8:11], refs[11 : 11 + SIDE]
        wave_ref, matrix_ref, fetched = refs[-3:]
    nent, rows, width = matrix_ref.shape
    size = width // SIDE
    half = size // 2
    nslab = count_ref.shape[0]
    step = pl.program_id(0)

    def clear(s, _):
        count_ref[s] = 0
        return 0

    def enter(e, _):
        slab = dest_ref[e]
        taken = count_ref[slab]
        list_ref[slab * capacity + taken] = e
        count_ref[slab] = taken + 1
        return 0

    def prepare():
        fetch = pltpu.make_async_copy(source_ref, matrix_ref, fetched)
        fetch.start()
        lax.fori_loop(0, nslab, clear, 0)
        lax.fori_loop(0, nent, enter, 0)
        for r, slice_ref in enumerate(slice_refs):
            slice_ref[...] = weights_ref[0, :, (place_ref[0] + r) % SIDE, :]
        chip = lax.broadcasted_iota(jnp.int32, (half, half), 0)
        slot = lax.broadcasted_iota(jnp.int32, (half, half), 1)
        digits = digits_of(slot)
        pieces = []
        chips = [chip_at(*moved(place_ref, digits, owner, 1)) for owner in range(CORES)]
        for owner in (1 - place_ref[3], place_ref[3]):
            pick = (chip == jnp.where(owner == 0, chips[0], chips[1])).astype(jnp.float32).astype(jnp.bfloat16)
            for start in (0, half):
                piece = packed_ref[owner, :, start : start + half]
                pieces.append(jnp.dot(piece, pick, preferred_element_type=jnp.float32).astype(jnp.bfloat16))
        both = jnp.dot(
            values_ref[...].reshape(nent * rows, size),
            jnp.concatenate(pieces, 1),
            preferred_element_type=jnp.float32,
        )
        for at, target_ref in ((0, wave_ref), (size, kept_wave_ref)):
            wave = both[:, at : at + half] + both[:, at + half : at + size]
            high = wave.astype(jnp.bfloat16)
            low = (wave - high.astype(jnp.float32)).astype(jnp.bfloat16)
            target_ref[...] = jnp.concatenate([high, low], 1).reshape(nent, rows, size)
        fetch.wait()

    if not kept:
        pl.when(step == 0)(prepare)

    pairs = nslab // (2 * STEPS)

    def products(out):
        for pair in range(pairs):
            halves_of_tile = []
            for near in range(2):
                slab = ((part * (STEPS // HALVES) + step) * pairs + pair) * 2 + near
                taken = count_ref[slab]
                waves, matrices = [], []
                for m in range(capacity):
                    entry = jnp.where(m < taken, list_ref[slab * capacity + m], 0)
                    wave = wave_ref[entry]
                    waves.append(jnp.where(m < taken, wave, jnp.zeros_like(wave)))
                    matrices.append(matrix_ref[entry])
                product = lax.dot_general(
                    jnp.concatenate(waves, 0),
                    jnp.concatenate(matrices, 0),
                    (((0,), (0,)), ((), ())),
                    preferred_element_type=jnp.float32,
                )
                halves_of_tile.append(product[:half] + product[half:])
            place = slice(pair * 8, pair * 8 + 8)
            for start in range(0, half, 8):
                tiles = [
                    product[start : start + 8, p * size : (p + 1) * size]
                    for product in halves_of_tile
                    for p in range(SIDE)
                ]
                for index, block in enumerate(sublane_turn(tiles), start):
                    out(index, place, block)

    def keep(index, place, block):
        outs[index // SIDE**2][index % SIDE**2, place, :] = block + other_ref[index, place, :]

    def send(out_ref):
        def write(index, place, block):
            out_ref[index, place, :] = block

        return write

    if kept:
        products(keep)
        if part:
            pl.when(step == STEPS // HALVES - 1)(lambda: weight_kernel(*weight_refs, place_ref, *row_refs))
    else:
        pl.when(step < STEPS // HALVES)(lambda: products(send(out_refs[0])))
        pl.when(step >= STEPS // HALVES)(lambda: products(send(out_refs[1])))


def grid_call(kept, part, nslab, capacity, *args):
    scalars = pl.BlockSpec(memory_space=pltpu.SMEM)
    fixed = lambda shape: pl.BlockSpec(shape, lambda i: (0,) * len(shape))
    matrix = args[4] if kept else args[3]
    nent, rows, width = matrix.shape
    size, blocks = width // SIDE, SIDE**3
    steps = STEPS // HALVES if kept else STEPS
    moving = lambda count: pl.BlockSpec((count, size // STEPS, size), lambda i: (0, i, 0))
    f32 = lambda *shape: jax.ShapeDtypeStruct(shape, jnp.float32)
    in_specs = [scalars if a.dtype == jnp.int32 else fixed(a.shape) for a in args]
    if kept:
        out_shape, out_specs = [f32(SIDE**2, size // HALVES, size)] * SIDE, [moving(SIDE**2)] * SIDE
        in_specs[5] = moving(blocks)
        if part:
            rows_shape = (SIDE**2 * 8 + 8, size)
            out_shape = out_shape + [f32(*rows_shape)] * SIDE
            out_specs = out_specs + [fixed(rows_shape)] * SIDE
        scratch = []
    else:
        wave = (nent, rows, size)
        out_shape = [f32(blocks, size // HALVES, size)] * HALVES + [
            jax.ShapeDtypeStruct(wave, jnp.bfloat16),
            jax.ShapeDtypeStruct((nslab,), jnp.int32),
            jax.ShapeDtypeStruct((nslab * capacity,), jnp.int32),
        ] + [f32(size, size)] * SIDE
        block = (blocks, size // STEPS, size)
        out_specs = [
            pl.BlockSpec(block, lambda i: (0, jnp.minimum(i, STEPS // HALVES - 1), 0)),
            pl.BlockSpec(block, lambda i: (0, jnp.maximum(i - STEPS // HALVES, 0), 0)),
        ] + [fixed(wave), scalars, scalars] + [fixed((size, size))] * SIDE
        in_specs[3] = pl.BlockSpec(memory_space=pl.ANY)
        scratch = [pltpu.VMEM(wave, jnp.bfloat16), pltpu.VMEM(matrix.shape, jnp.bfloat16), pltpu.SemaphoreType.DMA]
    return pl.pallas_call(
        functools.partial(grid_kernel, kept=kept, part=part, capacity=capacity),
        grid=(steps,),
        out_shape=out_shape,
        in_specs=in_specs,
        out_specs=out_specs,
        scratch_shapes=scratch,
    )(*args)


def moved(place_ref, digits, owner, sign):
    at = [place_ref[0], place_ref[1], place_ref[2]]
    for digit, axis in zip(digits, ORDERS[owner]):
        at[axis] = (at[axis] + sign * digit + SIDE) % SIDE
    return at


def digits_of(index):
    return index // SIDE**2, (index // SIDE) % SIDE, index % SIDE


def weight_kernel(w0_ref, w1_ref, w2_ref, w3_ref, place_ref, *outs):
    size = w0_ref.shape[0]
    half = size // 2
    own = ((w0_ref[...] + w1_ref[...]) + w2_ref[...]) + w3_ref[...]
    low = jnp.min(jnp.min(own, axis=0, keepdims=True), axis=1, keepdims=True)
    high = jnp.max(jnp.max(own, axis=0, keepdims=True), axis=1, keepdims=True)
    row = lax.broadcasted_iota(jnp.int32, (size, size), 0)
    lane = lax.broadcasted_iota(jnp.int32, (size, size), 1)
    chips = [chip_at(*moved(place_ref, digits_of(row % half), owner, 1)) for owner in range(CORES)]
    chip = jnp.where(place_ref[3] == 0, chips[0], chips[1])
    negative = jnp.where(chip == 0, half, size - chip)
    pick = (lane == jnp.where(row < half, chip, negative)).astype(jnp.float32)
    rows = dot_as(pick, own, 1, 1)
    ends = jnp.where(lax.broadcasted_iota(jnp.int32, (8, size), 1) < half, low, -high)
    count = half // SIDE
    for r, out_ref in enumerate(outs):
        out_ref[...] = jnp.zeros(out_ref.shape, jnp.float32)
        out_ref[8 * count :, :] = ends
        for sign in range(2):
            at = sign * half + r * count
            out_ref[pl.ds(2 * r + sign, count, stride=8), :] = rows[at : at + count]


def sublane_total(a):
    for shift in (4, 2, 1):
        a = dd_add(a, (pltpu.roll(a[0], shift, 0), pltpu.roll(a[1], shift, 0)))
    return a


def lane_total(a):
    for shift in (64, 32, 16, 8, 4, 2, 1):
        a = dd_add(a, (pltpu.roll(a[0], shift, 1), pltpu.roll(a[1], shift, 1)))
    return a


def moment_kernel(
    own_ref, other_ref, place_ref, lanes_ref, rows_ref, mirror_ref, real_ref, imag_ref, scaled_ref, range_ref, send_ref
):
    size = scaled_ref.shape[0]
    second, alone = place_ref[3] == 1, place_ref[4] == 1
    lane8 = lax.broadcasted_iota(jnp.int32, (8, size), 1)
    ends = jnp.minimum(own_ref[2 * size :, :], other_ref[2 * size :, :])
    least = lambda v: jnp.min(jnp.min(v, axis=0, keepdims=True), axis=1, keepdims=True)
    low = least(jnp.where(lane8 < size // 2, ends, 1e30))
    high = -least(jnp.where(lane8 < size // 2, 1e30, ends))
    span = jnp.broadcast_to(jnp.maximum((high - low) * 0.5, high * 1e-4), (1, size))
    centre = jnp.broadcast_to((high + low) * 0.5, (1, size)) / span
    range_ref[0:1, :] = span
    range_ref[1:2, :] = centre
    range_ref[2:8, :] = jnp.zeros((6, size), jnp.float32)

    ky = lax.broadcasted_iota(jnp.int32, (size, size), 0)
    row = lax.broadcasted_iota(jnp.int32, (size, size), 1)
    found = row // 2
    back = (found % SIDE, (found // SIDE) % SIDE, found // SIDE**2)
    sources = []
    for owner in range(CORES):
        x, y, z = moved(place_ref, back, owner, -1)
        sources.append(SIDE * (z * (SIDE * CORES) + y * CORES + owner) + x)
    from_own = jnp.where(second, sources[1], sources[0])
    from_other = jnp.where(second, sources[0], sources[1])
    given = jnp.concatenate([own_ref[size : 2 * size, :], other_ref[size : 2 * size, :]], 0)
    picks = [
        jnp.concatenate(
            [
                jnp.where(row % 2 == sign, (ky == source).astype(jnp.float32), 0.0).astype(jnp.bfloat16)
                for source in (from_own, from_other)
            ],
            1,
        )
        for sign in range(2)
    ]
    signs = select_rows(jnp.concatenate(picks, 0), given)
    plus, minus = signs[:size], signs[size:]
    mine = jnp.where(second, minus, plus)
    partner = jnp.where(alone, mine, jnp.where(second, plus, minus))
    scaled = (mine + select_lanes(select_rows(mirror_ref[...], partner), mirror_ref[...])) * 0.5 / span
    scaled_ref[...] = scaled.T

    mine, theirs = own_ref[:size, :], other_ref[:size, :]
    re = jnp.where(jnp.logical_and(second, jnp.logical_not(alone)), theirs, mine)
    im = jnp.where(alone, jnp.zeros_like(mine), jnp.where(second, -mine, theirs))
    ends = dot(jnp.concatenate([re, im], 0), lanes_ref[...])
    mid_real = ends[:size, :size] + ends[size:, size:]
    mid_imag = ends[size:, :size] - ends[:size, size:]
    both = dot(rows_ref[...], jnp.concatenate([mid_real, mid_imag], 1))
    real = both[:size, :size] + both[size:, size:]
    imag = both[:size, size:] - both[size:, :size]
    real_ref[...] = real
    imag_ref[...] = imag
    scaled = scaled_ref[...]
    power = real * real + imag * imag
    chunk = 24
    totals = [None] * MOMENTS
    for start in range(0, size // 2 + 8, chunk):
        row = lax.broadcasted_iota(jnp.int32, (chunk, size), 0) + start
        share = jnp.where(row % (size // 2) == 0, 1.0, jnp.where(row < size // 2, 2.0, 0.0))
        t = scaled[start : start + chunk] - centre
        p = power[start : start + chunk] * share
        p_parts = halves(p)
        t2 = t * 2.0
        t2_parts = halves(t2)
        zero = jnp.zeros_like(t)
        before, here = (jnp.ones_like(t), zero), (t, zero)
        for order in range(MOMENTS):
            value = before
            v_parts = halves(value[0])
            term, low_term = two_prod(value[0], p, v_parts, p_parts)
            term = (term, low_term + value[1] * p)
            total, spill = totals[order] or (None, None)
            for i in range(0, chunk, 8):
                piece, rest = term[0][i : i + 8], term[1][i : i + 8]
                if total is None:
                    total, spill = piece, rest
                else:
                    total, lost = two_sum(total, piece)
                    spill = spill + (lost + rest)
            totals[order] = total, spill
            if order + 1 < MOMENTS:
                up, low_up = two_prod(here[0], t2, None, t2_parts)
                following, lost = two_sum(up, -before[0])
                before, here = here, (following, lost + ((low_up + here[1] * t2) - before[1]))
    row = lax.broadcasted_iota(jnp.int32, (8, size), 0)
    lane = lax.broadcasted_iota(jnp.int32, (8, size), 1)
    out = jnp.zeros((8, size), jnp.float32)
    for base in range(0, MOMENTS, 8):
        high_rows = jnp.zeros((8, size), jnp.float32)
        low_rows = jnp.zeros((8, size), jnp.float32)
        for order in range(base, min(base + 8, MOMENTS)):
            total = sublane_total(quick_sum(*totals[order]))
            high_rows = jnp.where(row == order - base, total[0], high_rows)
            low_rows = jnp.where(row == order - base, total[1], low_rows)
        high_rows, low_rows = lane_total((high_rows, low_rows))
        out = jnp.where(lane == row + base, high_rows, out)
        out = jnp.where(lane == row + (base + LOW_LANE), low_rows, out)
    line = jnp.sum(out, axis=0, keepdims=True)
    send_ref[...] = jnp.broadcast_to(line, (size, size))


def lane_of(a, lane):
    pick = lambda v: jnp.broadcast_to(v[:, lane : lane + 1], v.shape)
    return pick(a[0]), pick(a[1])


def solve_kernel(
    sums_ref, range_ref, scaled_ref, real_ref, imag_ref, lanes_ref, rows_ref, out_ref, gain_ref, *, scale
):
    size = scaled_ref.shape[0]
    given = sums_ref[...]
    low = pltpu.roll(given, size - LOW_LANE, 1)
    rows = [(given[i : i + 8], low[i : i + 8]) for i in range(0, given.shape[0], 8)]
    while len(rows) > 1:
        rows = [dd_add(rows[i], rows[i + 1]) for i in range(0, len(rows), 2)]
    moments = sublane_total(rows[0])
    half = range_ref[0:1, :]
    centre = jnp.broadcast_to(range_ref[1:2, :], moments[0].shape)
    centre = (centre, jnp.zeros_like(centre))
    lane = lax.broadcasted_iota(jnp.int32, moments[0].shape, 1)
    resid, direct = moments, moments
    held = lane_of(resid, 0)
    steps, turns = [], []
    decay = jnp.ones((1, size), jnp.float32)
    for k in range(ITERS):
        after = tuple(pltpu.roll(v, size - 1, 1) for v in direct)
        prior = tuple(pltpu.roll(v, 1, 1) for v in direct)
        prior = tuple(jnp.where(lane == 0, a, p) for a, p in zip(after, prior))
        image = dd_add(dd_mul(direct, centre), dd_scale(dd_add(after, prior), 0.5))
        alpha = dd_div(held, lane_of(image, k))
        fresh = dd_add(resid, dd_neg(dd_mul(alpha, image)))
        reached = lane_of(fresh, k + 1)
        beta = dd_mul(alpha, dd_div(reached, held))
        held = reached
        beta = dd_scale(beta, -1.0 if k == 0 else -0.5)
        direct = dd_add(fresh, dd_mul(beta, direct))
        resid = fresh
        steps.append(alpha[0][0:1])
        turns.append(beta[0][0:1])
        decay = decay * beta[0][0:1]
    gain = lax.rsqrt(jnp.maximum(jnp.abs(decay), 1e-30)) / centre[0][0:1]
    gain_ref[...] = jnp.broadcast_to(gain, gain_ref.shape)
    scaled = scaled_ref[...]
    field = steps[0]
    solved = jnp.broadcast_to(field, scaled.shape)
    left = 1.0 - field * scaled
    toward = left + turns[0]
    for k in range(1, ITERS):
        solved = solved + steps[k] * toward
        left = left - steps[k] * (scaled * toward)
        if k + 1 < ITERS:
            toward = left + turns[k] * toward
    solved = solved * (scale / half)
    left = left * (gain * scale)
    real, imag = real_ref[...], imag_ref[...]
    back_real = solved * real - left * imag
    back_imag = solved * imag + left * real
    ends = dot_pieces(stacked(jnp.concatenate([back_real, back_imag], 0), 1), lanes_ref[...], 1, 0)
    mid_real = ends[:size, :size] - ends[size:, size:]
    mid_imag = ends[size:, :size] + ends[:size, size:]
    both = dot_pieces(rows_ref[...], stacked(jnp.concatenate([mid_real, mid_imag], 1), 0), 1, 0)
    real = both[:size, :size] - both[size:, size:]
    imag = both[:size, size:] + both[size:, :size]
    for copy in range(out_ref.shape[0] // (2 * size)):
        out_ref[pl.ds(copy * 2 * size, size, stride=2), :] = real
        out_ref[pl.ds(copy * 2 * size + 1, size, stride=2), :] = imag


def output_kernel(given_ref, gain_ref, back_ref, field_ref, resid_ref):
    planes, size = field_ref.shape[0], field_ref.shape[1]
    step = 2 * planes
    shrink = 1.0 / gain_ref[0:1, :]
    for j in range(planes):
        pieces = [given_ref[pl.ds(2 * j + part, size, stride=step), :] for part in range(2)]
        both = dot_pieces(stacked(jnp.concatenate(pieces, 0), 0), back_ref[...], 0, 0)
        field_ref[j] = both[:, :size]
        resid_ref[j] = both[:, size:] * shrink


def call(kernel, shapes, *args):
    whole = pl.BlockSpec(memory_space=pltpu.VMEM)
    scalars = pl.BlockSpec(memory_space=pltpu.SMEM)
    return pl.pallas_call(
        kernel,
        out_shape=[jax.ShapeDtypeStruct(s, jnp.float32) for s in shapes],
        in_specs=[scalars if a.dtype == jnp.int32 else whole for a in args],
        out_specs=[whole] * len(shapes),
    )(*args)


def exchange(parts, axes):
    return [parts[0]] + [lax.ppermute(parts[r], ALL, shift_pairs(axes, r)) for r in range(1, SIDE)]


def summed(parts):
    return ((parts[0] + parts[1]) + parts[2]) + parts[3]


def body(intensities, gridding, dest_slab, spectral_weights):
    ngrid = lax.axis_size("grid")
    ndp = lax.axis_size("dp")
    nent, rows, size = intensities.shape
    planes = gridding.shape[2] // size
    count = ngrid * ndp
    capacity = max(2, 2 * nent // ngrid)
    table = dft_tables(size)
    square = (size, size)
    swap = lambda a: lax.ppermute(a, ALL, shift_pairs((3, 3), 1))

    chip = lax.axis_index("dp") * (ngrid // CORES) + lax.axis_index("grid") // CORES
    core = lax.axis_index("grid") % CORES
    step = jnp.arange(5, dtype=jnp.int32)
    x, y, z = place_of(chip * CORES)[:3]
    place = jnp.where(
        step == 0, x, jnp.where(step == 1, y, jnp.where(step == 2, z, jnp.where(step == 3, core, chip == 0)))
    ).astype(jnp.int32)

    *away, wave, counts, lists, p0, p1, p2, p3 = grid_call(
        False, 0, ngrid, capacity, dest_slab[:, 0], place, intensities, gridding, table["packed"], spectral_weights
    )
    members = (counts, lists, place, wave, gridding)
    arrived = [swap(a) for a in away]
    weights = exchange([p0, p1, p2, p3], (0, 0))
    axes = [[order[stage] for order in ORDERS] for stage in range(3)]
    quarter = lambda a: [p.reshape(p.shape[1:]) for p in jnp.split(a.reshape((SIDE, -1) + a.shape[1:]), SIDE)]
    least = lambda parts: functools.reduce(jnp.minimum, parts)
    data = []
    for part in range(HALVES):
        kept = grid_call(True, part, ngrid, capacity, *members, arrived[part], *(weights if part else ()))
        kept, rows = kept[:SIDE], kept[SIDE:]
        data.append(exchange(kept, axes[0]))
    rows = exchange(rows, axes[0])
    parts = quarter(summed(data[0]))
    early = exchange(parts, axes[1])
    held = summed([a[: SIDE**2 * 8] for a in rows]).reshape(SIDE**2, 8, size)
    ends = jnp.broadcast_to(least([a[SIDE**2 * 8 :] for a in rows])[None], (SIDE**2, 8, size))
    parts = exchange(quarter(jnp.concatenate([summed(data[1]), held, ends], 1)), axes[1])
    late = size // HALVES
    for stage in (1, 2):
        if stage == 2:
            parts = exchange(quarter(parts), axes[2])
            late = size
        found = [
            summed([a[:, :late] for a in parts]),
            jnp.concatenate([a[:, late:-8] for a in parts], 1),
            least([a[:, -8:] for a in parts]),
        ]
        if stage == 1:
            found = [summed(early)] + found
        parts = jnp.concatenate(found, 1)
    parts = parts[0]
    real, imag, scaled, ends, send = call(
        moment_kernel, [square, square, square, (8, size), square],
        parts, swap(parts), place, table["lanes"], table["rows"], table["mirror"],
    )
    sums = lax.all_to_all(send.reshape(count, 1, size), ALL, 0, 0, tiled=True).reshape(count, size)
    back, gain = call(
        functools.partial(solve_kernel, scale=1.0 / size**3), [(ndp * 2 * size, size), (8, size)],
        sums, ends, scaled, real, imag, table["lanes_pieces"], table["rows_pieces"],
    )
    landed = lax.all_to_all(back.reshape(count, 2 * planes, size), ALL, 0, 0, tiled=True)
    return tuple(
        call(
            output_kernel, [(planes, size, size)] * 2,
            landed.reshape(count * 2 * planes, size), gain, table["back_pieces"],
        )
    )


def solution(mesh):
    return jax.shard_map(
        body,
        mesh=mesh,
        in_specs=(
            P(("dp", "grid"), None, None),
            P(("dp", "grid"), None, None),
            P(("dp", "grid"), None),
            P("dp", None, "grid", None),
        ),
        out_specs=(P("grid", None, None), P("grid", None, None)),
        check_vma=False,
    )
```

```python
import functools

import jax
import jax.numpy as jnp
import numpy as np
from jax import lax
from jax.experimental import pallas as pl
from jax.experimental.pallas import tpu as pltpu
from jax.sharding import PartitionSpec as P


ITERS = 8
MOMENTS = 2 * ITERS + 1
LOW_LANE = 64
ALL = ("dp", "grid")
HIGHEST = lax.Precision.HIGHEST


def two_sum(a, b):
    s = a + b
    v = s - a
    return s, (a - (s - v)) + (b - v)


def quick_sum(a, b):
    s = a + b
    return s, b - (s - a)


def halves(a):
    c = a * 4097.0
    high = c - (c - a)
    return high, a - high


def two_prod(a, b, a_parts=None, b_parts=None):
    p = a * b
    ah, al = a_parts or halves(a)
    bh, bl = b_parts or halves(b)
    return p, ((ah * bh - p) + ah * bl + al * bh) + al * bl


def dd_add(a, b):
    s, e = two_sum(a[0], b[0])
    return quick_sum(s, e + (a[1] + b[1]))


def dd_mul(a, b):
    p, e = two_prod(a[0], b[0])
    return quick_sum(p, e + (a[0] * b[1] + a[1] * b[0]))


def dd_times(a, b):
    p, e = two_prod(a[0], b)
    return quick_sum(p, e + a[1] * b)


def dd_scale(a, factor):
    return a[0] * factor, a[1] * factor


def dd_neg(a):
    return -a[0], -a[1]


def dd_div(a, b):
    inverse = 1.0 / b[0]
    first = a[0] * inverse
    rest = dd_add(a, dd_neg(dd_times(b, first)))
    return quick_sum(first, rest[0] * inverse)


def dot(a, b):
    return jax.lax.dot_general(
        a, b, (((1,), (0,)), ((), ())), precision=HIGHEST, preferred_element_type=jnp.float32
    )


SIDE = 4
CORES = 2
ORDERS = ((0, 2, 1), (1, 2, 0))


def place_of(device):
    chip = device // CORES
    return chip // SIDE**2, chip % SIDE, (chip // SIDE) % SIDE, device % CORES


def chip_at(x, y, z):
    return (x * SIDE + z) * SIDE + y


def shift_pairs(axes, hop):
    pairs = []
    for device in range(SIDE**3 * CORES):
        place = list(place_of(device))
        axis = axes[place[3]]
        place[axis] = (place[axis] + hop) % (CORES if axis == 3 else SIDE)
        pairs.append((device, chip_at(*place[:3]) * CORES + place[3]))
    return pairs


def held_rows(size):
    chip, core = np.arange(size) // CORES, np.arange(size) % CORES
    return np.where(chip == 0, core * size // 2, np.where(core == 0, chip, size - chip))


def dft_tables(size):
    index = np.arange(size)
    angle = 2.0 * np.pi * ((index[:, None] * index[None, :]) % size) / size
    cos, sin = np.cos(angle), np.sin(angle)
    held = held_rows(size)
    as_f32 = lambda a: np.ascontiguousarray(a, dtype=np.float32)
    half = size // 2
    packed = np.concatenate([cos[:, :half], cos[:, half : half + 1], -sin[:, 1:half]], 1)
    high = packed.astype(jnp.bfloat16)
    low = (packed - high.astype(np.float64)).astype(jnp.bfloat16)
    lanes, rows = np.concatenate([cos, sin], 1), np.concatenate([cos, sin], 0)
    back = np.concatenate(
        [np.concatenate([cos[held], sin[held]], 1), np.concatenate([-sin[held], cos[held]], 1)], 0
    )

    def thrice(table, axis):
        above = table.astype(jnp.bfloat16)
        below = (table - above.astype(np.float64)).astype(jnp.bfloat16)
        return np.concatenate([above, above, below], axis)

    return dict(
        packed=np.stack([np.concatenate([p[:, :half], q[:, :half]], 1) for p, q in ((high, low), (high[:, half:], low[:, half:]))]),
        lanes=as_f32(lanes),
        rows=as_f32(rows),
        lanes_pieces=thrice(lanes, 0),
        rows_pieces=thrice(rows, 1),
        back_pieces=thrice(back, 0),
        mirror=(((index[:, None] + index[None, :]) % size) == 0).astype(jnp.bfloat16),
    )


def dot_as(a, b, left, right):
    return lax.dot_general(
        a, b, (((left,), (right,)), ((), ())), precision=HIGHEST, preferred_element_type=jnp.float32
    )


def pieces_of(a, count):
    found = []
    for _ in range(count):
        piece = a.astype(jnp.bfloat16)
        found.append(piece)
        a = a - piece.astype(jnp.float32)
    return found


def dot_pieces(a, b, left, right):
    return lax.dot_general(a, b, (((left,), (right,)), ((), ())), preferred_element_type=jnp.float32)


def stacked(a, axis):
    high, low = pieces_of(a, 2)
    return jnp.concatenate([high, low, high], axis)


def select_rows(one_hot, a):
    width = a.shape[1]
    found = dot_pieces(one_hot, jnp.concatenate(pieces_of(a, 3), 1), 1, 0)
    return (found[:, :width] + found[:, width : 2 * width]) + found[:, 2 * width :]


def select_lanes(a, one_hot):
    height = a.shape[0]
    found = dot_pieces(jnp.concatenate(pieces_of(a, 3), 0), one_hot, 1, 0)
    return (found[:height] + found[height : 2 * height]) + found[2 * height :]


HALVES = 2
STEPS = 4


def sublane_turn(tiles):
    row = lax.broadcasted_iota(jnp.int32, tiles[0].shape, 0)
    for bit in (4, 2, 1):
        low = (row & bit) == 0
        turned = list(tiles)
        for i in range(8):
            if i & bit == 0:
                a, b = tiles[i], tiles[i + bit]
                turned[i] = jnp.where(low, a, pltpu.roll(b, bit, 0))
                turned[i + bit] = jnp.where(low, pltpu.roll(a, 8 - bit, 0), b)
        tiles = turned
    return tiles


def grid_kernel(*refs, kept, part, capacity):
    if kept:
        count_ref, list_ref, place_ref, wave_ref, matrix_ref, other_ref = refs[:6]
        weight_refs = refs[6 : 6 + SIDE] if part else ()
        outs, row_refs = refs[6 + len(weight_refs) :][:SIDE], refs[6 + len(weight_refs) :][SIDE:]
    else:
        dest_ref, place_ref, values_ref, source_ref, packed_ref, weights_ref = refs[:6]
        out_refs, (kept_wave_ref, count_ref, list_ref), slice_refs = refs[6:8], refs[8:11], refs[11 : 11 + SIDE]
        wave_ref, matrix_ref, fetched = refs[-3:]
    nent, rows, width = matrix_ref.shape
    size = width // SIDE
    half = size // 2
    nslab = count_ref.shape[0]
    step = pl.program_id(0)

    def clear(s, _):
        count_ref[s] = 0
        return 0

    def enter(e, _):
        slab = dest_ref[e]
        taken = count_ref[slab]
        list_ref[slab * capacity + taken] = e
        count_ref[slab] = taken + 1
        return 0

    def prepare():
        fetch = pltpu.make_async_copy(source_ref, matrix_ref, fetched)
        fetch.start()
        lax.fori_loop(0, nslab, clear, 0)
        lax.fori_loop(0, nent, enter, 0)
        for r, slice_ref in enumerate(slice_refs):
            slice_ref[...] = weights_ref[0, :, (place_ref[0] + r) % SIDE, :]
        chip = lax.broadcasted_iota(jnp.int32, (half, half), 0)
        slot = lax.broadcasted_iota(jnp.int32, (half, half), 1)
        digits = digits_of(slot)
        pieces = []
        chips = [chip_at(*moved(place_ref, digits, owner, 1)) for owner in range(CORES)]
        for owner in (1 - place_ref[3], place_ref[3]):
            pick = (chip == jnp.where(owner == 0, chips[0], chips[1])).astype(jnp.float32).astype(jnp.bfloat16)
            for start in (0, half):
                piece = packed_ref[owner, :, start : start + half]
                pieces.append(jnp.dot(piece, pick, preferred_element_type=jnp.float32).astype(jnp.bfloat16))
        both = jnp.dot(
            values_ref[...].reshape(nent * rows, size),
            jnp.concatenate(pieces, 1),
            preferred_element_type=jnp.float32,
        )
        for at, target_ref in ((0, wave_ref), (size, kept_wave_ref)):
            wave = both[:, at : at + half] + both[:, at + half : at + size]
            high = wave.astype(jnp.bfloat16)
            low = (wave - high.astype(jnp.float32)).astype(jnp.bfloat16)
            target_ref[...] = jnp.concatenate([high, low], 1).reshape(nent, rows, size)
        fetch.wait()

    if not kept:
        pl.when(step == 0)(prepare)

    pairs = nslab // (2 * STEPS)

    def products(out):
        for pair in range(pairs):
            halves_of_tile = []
            for near in range(2):
                slab = ((part * (STEPS // HALVES) + step) * pairs + pair) * 2 + near
                taken = count_ref[slab]
                waves, matrices = [], []
                for m in range(capacity):
                    entry = jnp.where(m < taken, list_ref[slab * capacity + m], 0)
                    wave = wave_ref[entry]
                    waves.append(jnp.where(m < taken, wave, jnp.zeros_like(wave)))
                    matrices.append(matrix_ref[entry])
                product = lax.dot_general(
                    jnp.concatenate(waves, 0),
                    jnp.concatenate(matrices, 0),
                    (((0,), (0,)), ((), ())),
                    preferred_element_type=jnp.float32,
                )
                halves_of_tile.append(product[:half] + product[half:])
            place = slice(pair * 8, pair * 8 + 8)
            for start in range(0, half, 8):
                tiles = [
                    product[start : start + 8, p * size : (p + 1) * size]
                    for product in halves_of_tile
                    for p in range(SIDE)
                ]
                for index, block in enumerate(sublane_turn(tiles), start):
                    out(index, place, block)

    def keep(index, place, block):
        outs[index // SIDE**2][index % SIDE**2, place, :] = block + other_ref[index, place, :]

    def send(out_ref):
        def write(index, place, block):
            out_ref[index, place, :] = block

        return write

    if kept:
        products(keep)
        if part:
            pl.when(step == STEPS // HALVES - 1)(lambda: weight_kernel(*weight_refs, place_ref, *row_refs))
    else:
        pl.when(step < STEPS // HALVES)(lambda: products(send(out_refs[0])))
        pl.when(step >= STEPS // HALVES)(lambda: products(send(out_refs[1])))


def grid_call(kept, part, nslab, capacity, *args):
    scalars = pl.BlockSpec(memory_space=pltpu.SMEM)
    fixed = lambda shape: pl.BlockSpec(shape, lambda i: (0,) * len(shape))
    matrix = args[4] if kept else args[3]
    nent, rows, width = matrix.shape
    size, blocks = width // SIDE, SIDE**3
    steps = STEPS // HALVES if kept else STEPS
    moving = lambda count: pl.BlockSpec((count, size // STEPS, size), lambda i: (0, i, 0))
    f32 = lambda *shape: jax.ShapeDtypeStruct(shape, jnp.float32)
    in_specs = [scalars if a.dtype == jnp.int32 else fixed(a.shape) for a in args]
    if kept:
        out_shape, out_specs = [f32(SIDE**2, size // HALVES, size)] * SIDE, [moving(SIDE**2)] * SIDE
        in_specs[5] = moving(blocks)
        if part:
            rows_shape = (SIDE**2 * 8 + 8, size)
            out_shape = out_shape + [f32(*rows_shape)] * SIDE
            out_specs = out_specs + [fixed(rows_shape)] * SIDE
        scratch = []
    else:
        wave = (nent, rows, size)
        out_shape = [f32(blocks, size // HALVES, size)] * HALVES + [
            jax.ShapeDtypeStruct(wave, jnp.bfloat16),
            jax.ShapeDtypeStruct((nslab,), jnp.int32),
            jax.ShapeDtypeStruct((nslab * capacity,), jnp.int32),
        ] + [f32(size, size)] * SIDE
        block = (blocks, size // STEPS, size)
        out_specs = [
            pl.BlockSpec(block, lambda i: (0, jnp.minimum(i, STEPS // HALVES - 1), 0)),
            pl.BlockSpec(block, lambda i: (0, jnp.maximum(i - STEPS // HALVES, 0), 0)),
        ] + [fixed(wave), scalars, scalars] + [fixed((size, size))] * SIDE
        in_specs[3] = pl.BlockSpec(memory_space=pl.ANY)
        scratch = [pltpu.VMEM(wave, jnp.bfloat16), pltpu.VMEM(matrix.shape, jnp.bfloat16), pltpu.SemaphoreType.DMA]
    return pl.pallas_call(
        functools.partial(grid_kernel, kept=kept, part=part, capacity=capacity),
        grid=(steps,),
        out_shape=out_shape,
        in_specs=in_specs,
        out_specs=out_specs,
        scratch_shapes=scratch,
    )(*args)


def moved(place_ref, digits, owner, sign):
    at = [place_ref[0], place_ref[1], place_ref[2]]
    for digit, axis in zip(digits, ORDERS[owner]):
        at[axis] = (at[axis] + sign * digit + SIDE) % SIDE
    return at


def digits_of(index):
    return index // SIDE**2, (index // SIDE) % SIDE, index % SIDE


def weight_kernel(w0_ref, w1_ref, w2_ref, w3_ref, place_ref, *outs):
    size = w0_ref.shape[0]
    half = size // 2
    own = ((w0_ref[...] + w1_ref[...]) + w2_ref[...]) + w3_ref[...]
    low = jnp.min(jnp.min(own, axis=0, keepdims=True), axis=1, keepdims=True)
    high = jnp.max(jnp.max(own, axis=0, keepdims=True), axis=1, keepdims=True)
    row = lax.broadcasted_iota(jnp.int32, (size, size), 0)
    lane = lax.broadcasted_iota(jnp.int32, (size, size), 1)
    chips = [chip_at(*moved(place_ref, digits_of(row % half), owner, 1)) for owner in range(CORES)]
    chip = jnp.where(place_ref[3] == 0, chips[0], chips[1])
    negative = jnp.where(chip == 0, half, size - chip)
    pick = (lane == jnp.where(row < half, chip, negative)).astype(jnp.float32)
    rows = dot_as(pick, own, 1, 1)
    ends = jnp.where(lax.broadcasted_iota(jnp.int32, (8, size), 1) < half, low, -high)
    count = half // SIDE
    for r, out_ref in enumerate(outs):
        out_ref[...] = jnp.zeros(out_ref.shape, jnp.float32)
        out_ref[8 * count :, :] = ends
        for sign in range(2):
            at = sign * half + r * count
            out_ref[pl.ds(2 * r + sign, count, stride=8), :] = rows[at : at + count]


def sublane_total(a):
    for shift in (4, 2, 1):
        a = dd_add(a, (pltpu.roll(a[0], shift, 0), pltpu.roll(a[1], shift, 0)))
    return a


def lane_total(a):
    for shift in (64, 32, 16, 8, 4, 2, 1):
        a = dd_add(a, (pltpu.roll(a[0], shift, 1), pltpu.roll(a[1], shift, 1)))
    return a


def moment_kernel(
    own_ref, other_ref, place_ref, lanes_ref, rows_ref, mirror_ref, real_ref, imag_ref, scaled_ref, range_ref, send_ref
):
    size = scaled_ref.shape[0]
    second, alone = place_ref[3] == 1, place_ref[4] == 1
    lane8 = lax.broadcasted_iota(jnp.int32, (8, size), 1)
    ends = jnp.minimum(own_ref[2 * size :, :], other_ref[2 * size :, :])
    least = lambda v: jnp.min(jnp.min(v, axis=0, keepdims=True), axis=1, keepdims=True)
    low = least(jnp.where(lane8 < size // 2, ends, 1e30))
    high = -least(jnp.where(lane8 < size // 2, 1e30, ends))
    span = jnp.broadcast_to(jnp.maximum((high - low) * 0.5, high * 1e-4), (1, size))
    centre = jnp.broadcast_to((high + low) * 0.5, (1, size)) / span
    range_ref[0:1, :] = span
    range_ref[1:2, :] = centre
    range_ref[2:8, :] = jnp.zeros((6, size), jnp.float32)

    ky = lax.broadcasted_iota(jnp.int32, (size, size), 0)
    row = lax.broadcasted_iota(jnp.int32, (size, size), 1)
    found = row // 2
    back = (found % SIDE, (found // SIDE) % SIDE, found // SIDE**2)
    sources = []
    for owner in range(CORES):
        x, y, z = moved(place_ref, back, owner, -1)
        sources.append(SIDE * (z * (SIDE * CORES) + y * CORES + owner) + x)
    from_own = jnp.where(second, sources[1], sources[0])
    from_other = jnp.where(second, sources[0], sources[1])
    given = jnp.concatenate([own_ref[size : 2 * size, :], other_ref[size : 2 * size, :]], 0)
    picks = [
        jnp.concatenate(
            [
                jnp.where(row % 2 == sign, (ky == source).astype(jnp.float32), 0.0).astype(jnp.bfloat16)
                for source in (from_own, from_other)
            ],
            1,
        )
        for sign in range(2)
    ]
    signs = select_rows(jnp.concatenate(picks, 0), given)
    plus, minus = signs[:size], signs[size:]
    mine = jnp.where(second, minus, plus)
    partner = jnp.where(alone, mine, jnp.where(second, plus, minus))
    scaled = (mine + select_lanes(select_rows(mirror_ref[...], partner), mirror_ref[...])) * 0.5 / span
    scaled_ref[...] = scaled.T

    mine, theirs = own_ref[:size, :], other_ref[:size, :]
    re = jnp.where(jnp.logical_and(second, jnp.logical_not(alone)), theirs, mine)
    im = jnp.where(alone, jnp.zeros_like(mine), jnp.where(second, -mine, theirs))
    ends = dot(jnp.concatenate([re, im], 0), lanes_ref[...])
    mid_real = ends[:size, :size] + ends[size:, size:]
    mid_imag = ends[size:, :size] - ends[:size, size:]
    both = dot(rows_ref[...], jnp.concatenate([mid_real, mid_imag], 1))
    real = both[:size, :size] + both[size:, size:]
    imag = both[:size, size:] - both[size:, :size]
    real_ref[...] = real
    imag_ref[...] = imag
    scaled = scaled_ref[...]
    power = real * real + imag * imag
    chunk = 24
    totals = [None] * MOMENTS
    for start in range(0, size // 2 + 8, chunk):
        row = lax.broadcasted_iota(jnp.int32, (chunk, size), 0) + start
        share = jnp.where(row % (size // 2) == 0, 1.0, jnp.where(row < size // 2, 2.0, 0.0))
        t = scaled[start : start + chunk] - centre
        p = power[start : start + chunk] * share
        p_parts = halves(p)
        t2 = t * 2.0
        t2_parts = halves(t2)
        zero = jnp.zeros_like(t)
        before, here = (jnp.ones_like(t), zero), (t, zero)
        for order in range(MOMENTS):
            value = before
            v_parts = halves(value[0])
            term, low_term = two_prod(value[0], p, v_parts, p_parts)
            term = (term, low_term + value[1] * p)
            total, spill = totals[order] or (None, None)
            for i in range(0, chunk, 8):
                piece, rest = term[0][i : i + 8], term[1][i : i + 8]
                if total is None:
                    total, spill = piece, rest
                else:
                    total, lost = two_sum(total, piece)
                    spill = spill + (lost + rest)
            totals[order] = total, spill
            if order + 1 < MOMENTS:
                up, low_up = two_prod(here[0], t2, None, t2_parts)
                following, lost = two_sum(up, -before[0])
                before, here = here, (following, lost + ((low_up + here[1] * t2) - before[1]))
    row = lax.broadcasted_iota(jnp.int32, (8, size), 0)
    lane = lax.broadcasted_iota(jnp.int32, (8, size), 1)
    out = jnp.zeros((8, size), jnp.float32)
    for base in range(0, MOMENTS, 8):
        high_rows = jnp.zeros((8, size), jnp.float32)
        low_rows = jnp.zeros((8, size), jnp.float32)
        for order in range(base, min(base + 8, MOMENTS)):
            total = sublane_total(quick_sum(*totals[order]))
            high_rows = jnp.where(row == order - base, total[0], high_rows)
            low_rows = jnp.where(row == order - base, total[1], low_rows)
        high_rows, low_rows = lane_total((high_rows, low_rows))
        out = jnp.where(lane == row + base, high_rows, out)
        out = jnp.where(lane == row + (base + LOW_LANE), low_rows, out)
    line = jnp.sum(out, axis=0, keepdims=True)
    send_ref[...] = jnp.broadcast_to(line, (size, size))


def lane_of(a, lane):
    pick = lambda v: jnp.broadcast_to(v[:, lane : lane + 1], v.shape)
    return pick(a[0]), pick(a[1])


def solve_kernel(
    sums_ref, range_ref, scaled_ref, real_ref, imag_ref, lanes_ref, rows_ref, out_ref, gain_ref, *, scale
):
    size = scaled_ref.shape[0]
    given = sums_ref[...]
    low = pltpu.roll(given, size - LOW_LANE, 1)
    rows = [(given[i : i + 8], low[i : i + 8]) for i in range(0, given.shape[0], 8)]
    while len(rows) > 1:
        rows = [dd_add(rows[i], rows[i + 1]) for i in range(0, len(rows), 2)]
    moments = sublane_total(rows[0])
    half = range_ref[0:1, :]
    centre = jnp.broadcast_to(range_ref[1:2, :], moments[0].shape)
    centre = (centre, jnp.zeros_like(centre))
    lane = lax.broadcasted_iota(jnp.int32, moments[0].shape, 1)
    resid, direct = moments, moments
    held = lane_of(resid, 0)
    steps, turns = [], []
    decay = jnp.ones((1, size), jnp.float32)
    for k in range(ITERS):
        after = tuple(pltpu.roll(v, size - 1, 1) for v in direct)
        prior = tuple(pltpu.roll(v, 1, 1) for v in direct)
        prior = tuple(jnp.where(lane == 0, a, p) for a, p in zip(after, prior))
        image = dd_add(dd_mul(direct, centre), dd_scale(dd_add(after, prior), 0.5))
        alpha = dd_div(held, lane_of(image, k))
        fresh = dd_add(resid, dd_neg(dd_mul(alpha, image)))
        reached = lane_of(fresh, k + 1)
        beta = dd_mul(alpha, dd_div(reached, held))
        held = reached
        beta = dd_scale(beta, -1.0 if k == 0 else -0.5)
        direct = dd_add(fresh, dd_mul(beta, direct))
        resid = fresh
        steps.append(alpha[0][0:1])
        turns.append(beta[0][0:1])
        decay = decay * beta[0][0:1]
    gain = lax.rsqrt(jnp.maximum(jnp.abs(decay), 1e-30)) / centre[0][0:1]
    gain_ref[...] = jnp.broadcast_to(gain, gain_ref.shape)
    scaled = scaled_ref[...]
    field = steps[0]
    solved = jnp.broadcast_to(field, scaled.shape)
    left = 1.0 - field * scaled
    toward = left + turns[0]
    for k in range(1, ITERS):
        solved = solved + steps[k] * toward
        left = left - steps[k] * (scaled * toward)
        if k + 1 < ITERS:
            toward = left + turns[k] * toward
    solved = solved * (scale / half)
    left = left * (gain * scale)
    real, imag = real_ref[...], imag_ref[...]
    back_real = solved * real - left * imag
    back_imag = solved * imag + left * real
    ends = dot_pieces(stacked(jnp.concatenate([back_real, back_imag], 0), 1), lanes_ref[...], 1, 0)
    mid_real = ends[:size, :size] - ends[size:, size:]
    mid_imag = ends[size:, :size] + ends[:size, size:]
    both = dot_pieces(rows_ref[...], stacked(jnp.concatenate([mid_real, mid_imag], 1), 0), 1, 0)
    real = both[:size, :size] - both[size:, size:]
    imag = both[:size, size:] + both[size:, :size]
    for copy in range(out_ref.shape[0] // (2 * size)):
        out_ref[pl.ds(copy * 2 * size, size, stride=2), :] = real
        out_ref[pl.ds(copy * 2 * size + 1, size, stride=2), :] = imag


def output_kernel(given_ref, gain_ref, back_ref, field_ref, resid_ref):
    planes, size = field_ref.shape[0], field_ref.shape[1]
    step = 2 * planes
    shrink = 1.0 / gain_ref[0:1, :]
    for j in range(planes):
        pieces = [given_ref[pl.ds(2 * j + part, size, stride=step), :] for part in range(2)]
        both = dot_pieces(stacked(jnp.concatenate(pieces, 0), 0), back_ref[...], 0, 0)
        field_ref[j] = both[:, :size]
        resid_ref[j] = both[:, size:] * shrink


def call(kernel, shapes, *args):
    whole = pl.BlockSpec(memory_space=pltpu.VMEM)
    scalars = pl.BlockSpec(memory_space=pltpu.SMEM)
    return pl.pallas_call(
        kernel,
        out_shape=[jax.ShapeDtypeStruct(s, jnp.float32) for s in shapes],
        in_specs=[scalars if a.dtype == jnp.int32 else whole for a in args],
        out_specs=[whole] * len(shapes),
    )(*args)


def exchange(parts, axes):
    arrived = {r: lax.ppermute(parts[r], ALL, shift_pairs(axes, r)) for r in (2, 1, 3)}
    return [parts[0], arrived[1], arrived[2], arrived[3]]


def summed(parts):
    return ((parts[0] + parts[1]) + parts[2]) + parts[3]


def body(intensities, gridding, dest_slab, spectral_weights):
    ngrid = lax.axis_size("grid")
    ndp = lax.axis_size("dp")
    nent, rows, size = intensities.shape
    planes = gridding.shape[2] // size
    count = ngrid * ndp
    capacity = max(2, 2 * nent // ngrid)
    table = dft_tables(size)
    square = (size, size)
    swap = lambda a: lax.ppermute(a, ALL, shift_pairs((3, 3), 1))

    chip = lax.axis_index("dp") * (ngrid // CORES) + lax.axis_index("grid") // CORES
    core = lax.axis_index("grid") % CORES
    step = jnp.arange(5, dtype=jnp.int32)
    x, y, z = place_of(chip * CORES)[:3]
    place = jnp.where(
        step == 0, x, jnp.where(step == 1, y, jnp.where(step == 2, z, jnp.where(step == 3, core, chip == 0)))
    ).astype(jnp.int32)

    *away, wave, counts, lists, p0, p1, p2, p3 = grid_call(
        False, 0, ngrid, capacity, dest_slab[:, 0], place, intensities, gridding, table["packed"], spectral_weights
    )
    members = (counts, lists, place, wave, gridding)
    arrived = [swap(a) for a in away]
    weights = exchange([p0, p1, p2, p3], (0, 0))
    axes = [[order[stage] for order in ORDERS] for stage in range(3)]
    quarter = lambda a: [p.reshape(p.shape[1:]) for p in jnp.split(a.reshape((SIDE, -1) + a.shape[1:]), SIDE)]
    least = lambda parts: functools.reduce(jnp.minimum, parts)
    data = []
    for part in range(HALVES):
        kept = grid_call(True, part, ngrid, capacity, *members, arrived[part], *(weights if part else ()))
        kept, rows = kept[:SIDE], kept[SIDE:]
        data.append(exchange(kept, axes[0]))
    rows = exchange(rows, axes[0])
    parts = quarter(summed(data[0]))
    early = exchange(parts, axes[1])
    held = summed([a[: SIDE**2 * 8] for a in rows]).reshape(SIDE**2, 8, size)
    ends = jnp.broadcast_to(least([a[SIDE**2 * 8 :] for a in rows])[None], (SIDE**2, 8, size))
    parts = exchange(quarter(jnp.concatenate([summed(data[1]), held, ends], 1)), axes[1])
    late = size // HALVES
    for stage in (1, 2):
        if stage == 2:
            parts = exchange(quarter(parts), axes[2])
            late = size
        found = [
            summed([a[:, :late] for a in parts]),
            jnp.concatenate([a[:, late:-8] for a in parts], 1),
            least([a[:, -8:] for a in parts]),
        ]
        if stage == 1:
            found = [summed(early)] + found
        parts = jnp.concatenate(found, 1)
    parts = parts[0]
    real, imag, scaled, ends, send = call(
        moment_kernel, [square, square, square, (8, size), square],
        parts, swap(parts), place, table["lanes"], table["rows"], table["mirror"],
    )
    sums = lax.all_to_all(send.reshape(count, 1, size), ALL, 0, 0, tiled=True).reshape(count, size)
    back, gain = call(
        functools.partial(solve_kernel, scale=1.0 / size**3), [(ndp * 2 * size, size), (8, size)],
        sums, ends, scaled, real, imag, table["lanes_pieces"], table["rows_pieces"],
    )
    landed = lax.all_to_all(back.reshape(count, 2 * planes, size), ALL, 0, 0, tiled=True)
    return tuple(
        call(
            output_kernel, [(planes, size, size)] * 2,
            landed.reshape(count * 2 * planes, size), gain, table["back_pieces"],
        )
    )


def solution(mesh):
    return jax.shard_map(
        body,
        mesh=mesh,
        in_specs=(
            P(("dp", "grid"), None, None),
            P(("dp", "grid"), None, None),
            P(("dp", "grid"), None),
            P("dp", None, "grid", None),
        ),
        out_specs=(P("grid", None, None), P("grid", None, None)),
        check_vma=False,
    )
```

```python
import functools

import jax
import jax.numpy as jnp
import numpy as np
from jax import lax
from jax.experimental import pallas as pl
from jax.experimental.pallas import tpu as pltpu
from jax.sharding import PartitionSpec as P


ITERS = 8
MOMENTS = 2 * ITERS + 1
LOW_LANE = 64
ALL = ("dp", "grid")
HIGHEST = lax.Precision.HIGHEST


def two_sum(a, b):
    s = a + b
    v = s - a
    return s, (a - (s - v)) + (b - v)


def quick_sum(a, b):
    s = a + b
    return s, b - (s - a)


def halves(a):
    c = a * 4097.0
    high = c - (c - a)
    return high, a - high


def two_prod(a, b, a_parts=None, b_parts=None):
    p = a * b
    ah, al = a_parts or halves(a)
    bh, bl = b_parts or halves(b)
    return p, ((ah * bh - p) + ah * bl + al * bh) + al * bl


def dd_add(a, b):
    s, e = two_sum(a[0], b[0])
    return quick_sum(s, e + (a[1] + b[1]))


def dd_mul(a, b):
    p, e = two_prod(a[0], b[0])
    return quick_sum(p, e + (a[0] * b[1] + a[1] * b[0]))


def dd_times(a, b):
    p, e = two_prod(a[0], b)
    return quick_sum(p, e + a[1] * b)


def dd_scale(a, factor):
    return a[0] * factor, a[1] * factor


def dd_neg(a):
    return -a[0], -a[1]


def dd_div(a, b):
    inverse = 1.0 / b[0]
    first = a[0] * inverse
    rest = dd_add(a, dd_neg(dd_times(b, first)))
    return quick_sum(first, rest[0] * inverse)


def dot(a, b):
    return jax.lax.dot_general(
        a, b, (((1,), (0,)), ((), ())), precision=HIGHEST, preferred_element_type=jnp.float32
    )


SIDE = 4
CORES = 2
ORDERS = ((0, 2, 1), (1, 2, 0))


def place_of(device):
    chip = device // CORES
    return chip // SIDE**2, chip % SIDE, (chip // SIDE) % SIDE, device % CORES


def chip_at(x, y, z):
    return (x * SIDE + z) * SIDE + y


def shift_pairs(axes, hop):
    pairs = []
    for device in range(SIDE**3 * CORES):
        place = list(place_of(device))
        axis = axes[place[3]]
        place[axis] = (place[axis] + hop) % (CORES if axis == 3 else SIDE)
        pairs.append((device, chip_at(*place[:3]) * CORES + place[3]))
    return pairs


def held_rows(size):
    chip, core = np.arange(size) // CORES, np.arange(size) % CORES
    return np.where(chip == 0, core * size // 2, np.where(core == 0, chip, size - chip))


def dft_tables(size):
    index = np.arange(size)
    angle = 2.0 * np.pi * ((index[:, None] * index[None, :]) % size) / size
    cos, sin = np.cos(angle), np.sin(angle)
    held = held_rows(size)
    as_f32 = lambda a: np.ascontiguousarray(a, dtype=np.float32)
    half = size // 2
    packed = np.concatenate([cos[:, :half], cos[:, half : half + 1], -sin[:, 1:half]], 1)
    high = packed.astype(jnp.bfloat16)
    low = (packed - high.astype(np.float64)).astype(jnp.bfloat16)
    lanes, rows = np.concatenate([cos, sin], 1), np.concatenate([cos, sin], 0)
    back = np.concatenate(
        [np.concatenate([cos[held], sin[held]], 1), np.concatenate([-sin[held], cos[held]], 1)], 0
    )

    def thrice(table, axis):
        above = table.astype(jnp.bfloat16)
        below = (table - above.astype(np.float64)).astype(jnp.bfloat16)
        return np.concatenate([above, above, below], axis)

    return dict(
        packed=np.stack([np.concatenate([p[:, :half], q[:, :half]], 1) for p, q in ((high, low), (high[:, half:], low[:, half:]))]),
        lanes=as_f32(lanes),
        rows=as_f32(rows),
        lanes_pieces=thrice(lanes, 0),
        rows_pieces=thrice(rows, 1),
        back_pieces=thrice(back, 0),
        mirror=(((index[:, None] + index[None, :]) % size) == 0).astype(jnp.bfloat16),
    )


def dot_as(a, b, left, right):
    return lax.dot_general(
        a, b, (((left,), (right,)), ((), ())), precision=HIGHEST, preferred_element_type=jnp.float32
    )


def pieces_of(a, count):
    found = []
    for _ in range(count):
        piece = a.astype(jnp.bfloat16)
        found.append(piece)
        a = a - piece.astype(jnp.float32)
    return found


def dot_pieces(a, b, left, right):
    return lax.dot_general(a, b, (((left,), (right,)), ((), ())), preferred_element_type=jnp.float32)


def stacked(a, axis):
    high, low = pieces_of(a, 2)
    return jnp.concatenate([high, low, high], axis)


def select_rows(one_hot, a):
    width = a.shape[1]
    found = dot_pieces(one_hot, jnp.concatenate(pieces_of(a, 3), 1), 1, 0)
    return (found[:, :width] + found[:, width : 2 * width]) + found[:, 2 * width :]


def select_lanes(a, one_hot):
    height = a.shape[0]
    found = dot_pieces(jnp.concatenate(pieces_of(a, 3), 0), one_hot, 1, 0)
    return (found[:height] + found[height : 2 * height]) + found[2 * height :]


HALVES = 2
STEPS = 4


def sublane_turn(tiles):
    row = lax.broadcasted_iota(jnp.int32, tiles[0].shape, 0)
    for bit in (4, 2, 1):
        low = (row & bit) == 0
        turned = list(tiles)
        for i in range(8):
            if i & bit == 0:
                a, b = tiles[i], tiles[i + bit]
                turned[i] = jnp.where(low, a, pltpu.roll(b, bit, 0))
                turned[i + bit] = jnp.where(low, pltpu.roll(a, 8 - bit, 0), b)
        tiles = turned
    return tiles


def grid_kernel(*refs, kept, part, capacity):
    if kept:
        count_ref, list_ref, place_ref, wave_ref, matrix_ref, other_ref = refs[:6]
        weight_refs = refs[6 : 6 + SIDE] if part else ()
        outs, row_refs = refs[6 + len(weight_refs) :][:SIDE], refs[6 + len(weight_refs) :][SIDE:]
    else:
        dest_ref, place_ref, values_ref, source_ref, packed_ref, weights_ref = refs[:6]
        out_refs, (kept_wave_ref, count_ref, list_ref), slice_refs = refs[6:8], refs[8:11], refs[11 : 11 + SIDE]
        wave_ref, matrix_ref, fetched = refs[-3:]
    nent, rows, width = matrix_ref.shape
    size = width // SIDE
    half = size // 2
    nslab = count_ref.shape[0]
    step = pl.program_id(0)

    def clear(s, _):
        count_ref[s] = 0
        return 0

    def enter(e, _):
        slab = dest_ref[e]
        taken = count_ref[slab]
        list_ref[slab * capacity + taken] = e
        count_ref[slab] = taken + 1
        return 0

    def prepare():
        fetch = pltpu.make_async_copy(source_ref, matrix_ref, fetched)
        fetch.start()
        lax.fori_loop(0, nslab, clear, 0)
        lax.fori_loop(0, nent, enter, 0)
        for r, slice_ref in enumerate(slice_refs):
            slice_ref[...] = weights_ref[0, :, (place_ref[0] + r) % SIDE, :]
        chip = lax.broadcasted_iota(jnp.int32, (half, half), 0)
        slot = lax.broadcasted_iota(jnp.int32, (half, half), 1)
        digits = digits_of(slot)
        pieces = []
        chips = [chip_at(*moved(place_ref, digits, owner, 1)) for owner in range(CORES)]
        for owner in (1 - place_ref[3], place_ref[3]):
            pick = (chip == jnp.where(owner == 0, chips[0], chips[1])).astype(jnp.float32).astype(jnp.bfloat16)
            for start in (0, half):
                piece = packed_ref[owner, :, start : start + half]
                pieces.append(jnp.dot(piece, pick, preferred_element_type=jnp.float32).astype(jnp.bfloat16))
        both = jnp.dot(
            values_ref[...].reshape(nent * rows, size),
            jnp.concatenate(pieces, 1),
            preferred_element_type=jnp.float32,
        )
        for at, target_ref in ((0, wave_ref), (size, kept_wave_ref)):
            wave = both[:, at : at + half] + both[:, at + half : at + size]
            high = wave.astype(jnp.bfloat16)
            low = (wave - high.astype(jnp.float32)).astype(jnp.bfloat16)
            target_ref[...] = jnp.concatenate([high, low], 1).reshape(nent, rows, size)
        fetch.wait()

    if not kept:
        pl.when(step == 0)(prepare)

    pairs = nslab // (2 * STEPS)

    def products(out):
        for pair in range(pairs):
            halves_of_tile = []
            for near in range(2):
                slab = ((part * (STEPS // HALVES) + step) * pairs + pair) * 2 + near
                taken = count_ref[slab]
                waves, matrices = [], []
                for m in range(capacity):
                    entry = jnp.where(m < taken, list_ref[slab * capacity + m], 0)
                    wave = wave_ref[entry]
                    waves.append(jnp.where(m < taken, wave, jnp.zeros_like(wave)))
                    matrices.append(matrix_ref[entry])
                product = lax.dot_general(
                    jnp.concatenate(waves, 0),
                    jnp.concatenate(matrices, 0),
                    (((0,), (0,)), ((), ())),
                    preferred_element_type=jnp.float32,
                )
                halves_of_tile.append(product[:half] + product[half:])
            place = slice(pair * 8, pair * 8 + 8)
            for start in range(0, half, 8):
                tiles = [
                    product[start : start + 8, p * size : (p + 1) * size]
                    for product in halves_of_tile
                    for p in range(SIDE)
                ]
                for index, block in enumerate(sublane_turn(tiles), start):
                    out(index, place, block)

    def keep(index, place, block):
        outs[index // SIDE**2][index % SIDE**2, place, :] = block + other_ref[index, place, :]

    def send(out_ref):
        def write(index, place, block):
            out_ref[index, place, :] = block

        return write

    if kept:
        products(keep)
        if part:
            pl.when(step == STEPS // HALVES - 1)(lambda: weight_kernel(*weight_refs, place_ref, *row_refs))
    else:
        pl.when(step < STEPS // HALVES)(lambda: products(send(out_refs[0])))
        pl.when(step >= STEPS // HALVES)(lambda: products(send(out_refs[1])))


def grid_call(kept, part, nslab, capacity, *args):
    scalars = pl.BlockSpec(memory_space=pltpu.SMEM)
    fixed = lambda shape: pl.BlockSpec(shape, lambda i: (0,) * len(shape))
    matrix = args[4] if kept else args[3]
    nent, rows, width = matrix.shape
    size, blocks = width // SIDE, SIDE**3
    steps = STEPS // HALVES if kept else STEPS
    moving = lambda count: pl.BlockSpec((count, size // STEPS, size), lambda i: (0, i, 0))
    f32 = lambda *shape: jax.ShapeDtypeStruct(shape, jnp.float32)
    in_specs = [scalars if a.dtype == jnp.int32 else fixed(a.shape) for a in args]
    if kept:
        out_shape, out_specs = [f32(SIDE**2, size // HALVES, size)] * SIDE, [moving(SIDE**2)] * SIDE
        in_specs[5] = moving(blocks)
        if part:
            rows_shape = (SIDE**2 * 8 + 8, size)
            out_shape = out_shape + [f32(*rows_shape)] * SIDE
            out_specs = out_specs + [fixed(rows_shape)] * SIDE
        scratch = []
    else:
        wave = (nent, rows, size)
        out_shape = [f32(blocks, size // HALVES, size)] * HALVES + [
            jax.ShapeDtypeStruct(wave, jnp.bfloat16),
            jax.ShapeDtypeStruct((nslab,), jnp.int32),
            jax.ShapeDtypeStruct((nslab * capacity,), jnp.int32),
        ] + [f32(size, size)] * SIDE
        block = (blocks, size // STEPS, size)
        out_specs = [
            pl.BlockSpec(block, lambda i: (0, jnp.minimum(i, STEPS // HALVES - 1), 0)),
            pl.BlockSpec(block, lambda i: (0, jnp.maximum(i - STEPS // HALVES, 0), 0)),
        ] + [fixed(wave), scalars, scalars] + [fixed((size, size))] * SIDE
        in_specs[3] = pl.BlockSpec(memory_space=pl.ANY)
        scratch = [pltpu.VMEM(wave, jnp.bfloat16), pltpu.VMEM(matrix.shape, jnp.bfloat16), pltpu.SemaphoreType.DMA]
    return pl.pallas_call(
        functools.partial(grid_kernel, kept=kept, part=part, capacity=capacity),
        grid=(steps,),
        out_shape=out_shape,
        in_specs=in_specs,
        out_specs=out_specs,
        scratch_shapes=scratch,
    )(*args)


def moved(place_ref, digits, owner, sign):
    at = [place_ref[0], place_ref[1], place_ref[2]]
    for digit, axis in zip(digits, ORDERS[owner]):
        at[axis] = (at[axis] + sign * digit + SIDE) % SIDE
    return at


def digits_of(index):
    return index // SIDE**2, (index // SIDE) % SIDE, index % SIDE


def weight_kernel(w0_ref, w1_ref, w2_ref, w3_ref, place_ref, *outs):
    size = w0_ref.shape[0]
    half = size // 2
    own = ((w0_ref[...] + w1_ref[...]) + w2_ref[...]) + w3_ref[...]
    low = jnp.min(jnp.min(own, axis=0, keepdims=True), axis=1, keepdims=True)
    high = jnp.max(jnp.max(own, axis=0, keepdims=True), axis=1, keepdims=True)
    row = lax.broadcasted_iota(jnp.int32, (size, size), 0)
    lane = lax.broadcasted_iota(jnp.int32, (size, size), 1)
    chips = [chip_at(*moved(place_ref, digits_of(row % half), owner, 1)) for owner in range(CORES)]
    chip = jnp.where(place_ref[3] == 0, chips[0], chips[1])
    negative = jnp.where(chip == 0, half, size - chip)
    pick = (lane == jnp.where(row < half, chip, negative)).astype(jnp.float32)
    rows = dot_as(pick, own, 1, 1)
    ends = jnp.where(lax.broadcasted_iota(jnp.int32, (8, size), 1) < half, low, -high)
    count = half // SIDE
    for r, out_ref in enumerate(outs):
        out_ref[...] = jnp.zeros(out_ref.shape, jnp.float32)
        out_ref[8 * count :, :] = ends
        for sign in range(2):
            at = sign * half + r * count
            out_ref[pl.ds(2 * r + sign, count, stride=8), :] = rows[at : at + count]


def sublane_total(a):
    for shift in (4, 2, 1):
        a = dd_add(a, (pltpu.roll(a[0], shift, 0), pltpu.roll(a[1], shift, 0)))
    return a


def lane_total(a):
    for shift in (64, 32, 16, 8, 4, 2, 1):
        a = dd_add(a, (pltpu.roll(a[0], shift, 1), pltpu.roll(a[1], shift, 1)))
    return a


def moment_kernel(
    own_ref, other_ref, place_ref, lanes_ref, rows_ref, mirror_ref, real_ref, imag_ref, scaled_ref, range_ref, send_ref
):
    size = scaled_ref.shape[0]
    second, alone = place_ref[3] == 1, place_ref[4] == 1
    lane8 = lax.broadcasted_iota(jnp.int32, (8, size), 1)
    ends = jnp.minimum(own_ref[2 * size :, :], other_ref[2 * size :, :])
    least = lambda v: jnp.min(jnp.min(v, axis=0, keepdims=True), axis=1, keepdims=True)
    low = least(jnp.where(lane8 < size // 2, ends, 1e30))
    high = -least(jnp.where(lane8 < size // 2, 1e30, ends))
    span = jnp.broadcast_to(jnp.maximum((high - low) * 0.5, high * 1e-4), (1, size))
    centre = jnp.broadcast_to((high + low) * 0.5, (1, size)) / span
    range_ref[0:1, :] = span
    range_ref[1:2, :] = centre
    range_ref[2:8, :] = jnp.zeros((6, size), jnp.float32)

    ky = lax.broadcasted_iota(jnp.int32, (size, size), 0)
    row = lax.broadcasted_iota(jnp.int32, (size, size), 1)
    found = row // 2
    back = (found % SIDE, (found // SIDE) % SIDE, found // SIDE**2)
    sources = []
    for owner in range(CORES):
        x, y, z = moved(place_ref, back, owner, -1)
        sources.append(SIDE * (z * (SIDE * CORES) + y * CORES + owner) + x)
    from_own = jnp.where(second, sources[1], sources[0])
    from_other = jnp.where(second, sources[0], sources[1])
    given = jnp.concatenate([own_ref[size : 2 * size, :], other_ref[size : 2 * size, :]], 0)
    picks = [
        jnp.concatenate(
            [
                jnp.where(row % 2 == sign, (ky == source).astype(jnp.float32), 0.0).astype(jnp.bfloat16)
                for source in (from_own, from_other)
            ],
            1,
        )
        for sign in range(2)
    ]
    signs = select_rows(jnp.concatenate(picks, 0), given)
    plus, minus = signs[:size], signs[size:]
    mine = jnp.where(second, minus, plus)
    partner = jnp.where(alone, mine, jnp.where(second, plus, minus))
    scaled = (mine + select_lanes(select_rows(mirror_ref[...], partner), mirror_ref[...])) * 0.5 / span
    scaled_ref[...] = scaled.T

    mine, theirs = own_ref[:size, :], other_ref[:size, :]
    re = jnp.where(jnp.logical_and(second, jnp.logical_not(alone)), theirs, mine)
    im = jnp.where(alone, jnp.zeros_like(mine), jnp.where(second, -mine, theirs))
    ends = dot(jnp.concatenate([re, im], 0), lanes_ref[...])
    mid_real = ends[:size, :size] + ends[size:, size:]
    mid_imag = ends[size:, :size] - ends[:size, size:]
    both = dot(rows_ref[...], jnp.concatenate([mid_real, mid_imag], 1))
    real = both[:size, :size] + both[size:, size:]
    imag = both[:size, size:] - both[size:, :size]
    real_ref[...] = real
    imag_ref[...] = imag
    scaled = scaled_ref[...]
    power = real * real + imag * imag
    chunk = 24
    totals = [None] * MOMENTS
    for start in range(0, size // 2 + 8, chunk):
        row = lax.broadcasted_iota(jnp.int32, (chunk, size), 0) + start
        share = jnp.where(row % (size // 2) == 0, 1.0, jnp.where(row < size // 2, 2.0, 0.0))
        t = scaled[start : start + chunk] - centre
        p = power[start : start + chunk] * share
        p_parts = halves(p)
        t2 = t * 2.0
        t2_parts = halves(t2)
        zero = jnp.zeros_like(t)
        before, here = (jnp.ones_like(t), zero), (t, zero)
        for order in range(MOMENTS):
            value = before
            v_parts = halves(value[0])
            term, low_term = two_prod(value[0], p, v_parts, p_parts)
            term = (term, low_term + value[1] * p)
            total, spill = totals[order] or (None, None)
            for i in range(0, chunk, 8):
                piece, rest = term[0][i : i + 8], term[1][i : i + 8]
                if total is None:
                    total, spill = piece, rest
                else:
                    total, lost = two_sum(total, piece)
                    spill = spill + (lost + rest)
            totals[order] = total, spill
            if order + 1 < MOMENTS:
                up, low_up = two_prod(here[0], t2, None, t2_parts)
                following, lost = two_sum(up, -before[0])
                before, here = here, (following, lost + ((low_up + here[1] * t2) - before[1]))
    row = lax.broadcasted_iota(jnp.int32, (8, size), 0)
    lane = lax.broadcasted_iota(jnp.int32, (8, size), 1)
    out = jnp.zeros((8, size), jnp.float32)
    for base in range(0, MOMENTS, 8):
        high_rows = jnp.zeros((8, size), jnp.float32)
        low_rows = jnp.zeros((8, size), jnp.float32)
        for order in range(base, min(base + 8, MOMENTS)):
            total = sublane_total(quick_sum(*totals[order]))
            high_rows = jnp.where(row == order - base, total[0], high_rows)
            low_rows = jnp.where(row == order - base, total[1], low_rows)
        high_rows, low_rows = lane_total((high_rows, low_rows))
        out = jnp.where(lane == row + base, high_rows, out)
        out = jnp.where(lane == row + (base + LOW_LANE), low_rows, out)
    line = jnp.sum(out, axis=0, keepdims=True)
    send_ref[...] = jnp.broadcast_to(line, (size, size))


def lane_of(a, lane):
    pick = lambda v: jnp.broadcast_to(v[:, lane : lane + 1], v.shape)
    return pick(a[0]), pick(a[1])


def solve_kernel(
    sums_ref, range_ref, scaled_ref, real_ref, imag_ref, lanes_ref, rows_ref, out_ref, gain_ref, *, scale
):
    size = scaled_ref.shape[0]
    given = sums_ref[...]
    low = pltpu.roll(given, size - LOW_LANE, 1)
    rows = [(given[i : i + 8], low[i : i + 8]) for i in range(0, given.shape[0], 8)]
    while len(rows) > 1:
        rows = [dd_add(rows[i], rows[i + 1]) for i in range(0, len(rows), 2)]
    moments = sublane_total(rows[0])
    half = range_ref[0:1, :]
    centre = jnp.broadcast_to(range_ref[1:2, :], moments[0].shape)
    centre = (centre, jnp.zeros_like(centre))
    lane = lax.broadcasted_iota(jnp.int32, moments[0].shape, 1)
    resid, direct = moments, moments
    held = lane_of(resid, 0)
    steps, turns = [], []
    decay = jnp.ones((1, size), jnp.float32)
    for k in range(ITERS):
        after = tuple(pltpu.roll(v, size - 1, 1) for v in direct)
        prior = tuple(pltpu.roll(v, 1, 1) for v in direct)
        prior = tuple(jnp.where(lane == 0, a, p) for a, p in zip(after, prior))
        image = dd_add(dd_mul(direct, centre), dd_scale(dd_add(after, prior), 0.5))
        alpha = dd_div(held, lane_of(image, k))
        fresh = dd_add(resid, dd_neg(dd_mul(alpha, image)))
        reached = lane_of(fresh, k + 1)
        beta = dd_mul(alpha, dd_div(reached, held))
        held = reached
        beta = dd_scale(beta, -1.0 if k == 0 else -0.5)
        direct = dd_add(fresh, dd_mul(beta, direct))
        resid = fresh
        steps.append(alpha[0][0:1])
        turns.append(beta[0][0:1])
        decay = decay * beta[0][0:1]
    gain = lax.rsqrt(jnp.maximum(jnp.abs(decay), 1e-30)) / centre[0][0:1]
    gain_ref[...] = jnp.broadcast_to(gain, gain_ref.shape)
    scaled = scaled_ref[...]
    field = steps[0]
    solved = jnp.broadcast_to(field, scaled.shape)
    left = 1.0 - field * scaled
    toward = left + turns[0]
    for k in range(1, ITERS):
        solved = solved + steps[k] * toward
        left = left - steps[k] * (scaled * toward)
        if k + 1 < ITERS:
            toward = left + turns[k] * toward
    solved = solved * (scale / half)
    left = left * (gain * scale)
    real, imag = real_ref[...], imag_ref[...]
    back_real = solved * real - left * imag
    back_imag = solved * imag + left * real
    ends = dot_pieces(stacked(jnp.concatenate([back_real, back_imag], 0), 1), lanes_ref[...], 1, 0)
    mid_real = ends[:size, :size] - ends[size:, size:]
    mid_imag = ends[size:, :size] + ends[:size, size:]
    both = dot_pieces(rows_ref[...], stacked(jnp.concatenate([mid_real, mid_imag], 1), 0), 1, 0)
    real = both[:size, :size] - both[size:, size:]
    imag = both[:size, size:] + both[size:, :size]
    for copy in range(out_ref.shape[0] // (2 * size)):
        out_ref[pl.ds(copy * 2 * size, size, stride=2), :] = real
        out_ref[pl.ds(copy * 2 * size + 1, size, stride=2), :] = imag


def output_kernel(given_ref, gain_ref, back_ref, field_ref, resid_ref):
    planes, size = field_ref.shape[0], field_ref.shape[1]
    step = 2 * planes
    shrink = 1.0 / gain_ref[0:1, :]
    for j in range(planes):
        pieces = [given_ref[pl.ds(2 * j + part, size, stride=step), :] for part in range(2)]
        both = dot_pieces(stacked(jnp.concatenate(pieces, 0), 0), back_ref[...], 0, 0)
        field_ref[j] = both[:, :size]
        resid_ref[j] = both[:, size:] * shrink


def call(kernel, shapes, *args):
    whole = pl.BlockSpec(memory_space=pltpu.VMEM)
    scalars = pl.BlockSpec(memory_space=pltpu.SMEM)
    return pl.pallas_call(
        kernel,
        out_shape=[jax.ShapeDtypeStruct(s, jnp.float32) for s in shapes],
        in_specs=[scalars if a.dtype == jnp.int32 else whole for a in args],
        out_specs=[whole] * len(shapes),
    )(*args)


def exchange(parts, axes):
    arrived = {}
    for r in (2, 1, 3):
        arrived[r] = lax.ppermute(parts[r], ALL, shift_pairs(axes, r))
    return [parts[0], arrived[1], arrived[2], arrived[3]]


def summed(parts):
    return ((parts[0] + parts[1]) + parts[2]) + parts[3]


def body(intensities, gridding, dest_slab, spectral_weights):
    ngrid = lax.axis_size("grid")
    ndp = lax.axis_size("dp")
    nent, rows, size = intensities.shape
    planes = gridding.shape[2] // size
    count = ngrid * ndp
    capacity = max(2, 2 * nent // ngrid)
    table = dft_tables(size)
    square = (size, size)
    swap = lambda a: lax.ppermute(a, ALL, shift_pairs((3, 3), 1))

    chip = lax.axis_index("dp") * (ngrid // CORES) + lax.axis_index("grid") // CORES
    core = lax.axis_index("grid") % CORES
    step = jnp.arange(5, dtype=jnp.int32)
    x, y, z = place_of(chip * CORES)[:3]
    place = jnp.where(
        step == 0, x, jnp.where(step == 1, y, jnp.where(step == 2, z, jnp.where(step == 3, core, chip == 0)))
    ).astype(jnp.int32)

    *away, wave, counts, lists, p0, p1, p2, p3 = grid_call(
        False, 0, ngrid, capacity, dest_slab[:, 0], place, intensities, gridding, table["packed"], spectral_weights
    )
    members = (counts, lists, place, wave, gridding)
    arrived = [swap(a) for a in away]
    weights = exchange([p0, p1, p2, p3], (0, 0))
    axes = [[order[stage] for order in ORDERS] for stage in range(3)]
    quarter = lambda a: [p.reshape(p.shape[1:]) for p in jnp.split(a.reshape((SIDE, -1) + a.shape[1:]), SIDE)]
    least = lambda parts: functools.reduce(jnp.minimum, parts)
    data = []
    for part in range(HALVES):
        kept = grid_call(True, part, ngrid, capacity, *members, arrived[part], *(weights if part else ()))
        kept, rows = kept[:SIDE], kept[SIDE:]
        data.append(exchange(kept, axes[0]))
    rows = exchange(rows, axes[0])
    parts = quarter(summed(data[0]))
    early = exchange(parts, axes[1])
    held = summed([a[: SIDE**2 * 8] for a in rows]).reshape(SIDE**2, 8, size)
    ends = jnp.broadcast_to(least([a[SIDE**2 * 8 :] for a in rows])[None], (SIDE**2, 8, size))
    parts = quarter(jnp.concatenate([summed(data[1]), held, ends], 1))
    parts = exchange(parts, axes[1])
    late = size // HALVES
    for stage in (1, 2):
        if stage == 2:
            parts = exchange(quarter(parts), axes[2])
            late = size
        found = [
            summed([a[:, :late] for a in parts]),
            jnp.concatenate([a[:, late:-8] for a in parts], 1),
            least([a[:, -8:] for a in parts]),
        ]
        if stage == 1:
            found = [summed(early)] + found
        parts = jnp.concatenate(found, 1)
    parts = parts[0]
    real, imag, scaled, ends, send = call(
        moment_kernel, [square, square, square, (8, size), square],
        parts, swap(parts), place, table["lanes"], table["rows"], table["mirror"],
    )
    sums = lax.all_to_all(send.reshape(count, 1, size), ALL, 0, 0, tiled=True).reshape(count, size)
    back, gain = call(
        functools.partial(solve_kernel, scale=1.0 / size**3), [(ndp * 2 * size, size), (8, size)],
        sums, ends, scaled, real, imag, table["lanes_pieces"], table["rows_pieces"],
    )
    landed = lax.all_to_all(back.reshape(count, 2 * planes, size), ALL, 0, 0, tiled=True)
    return tuple(
        call(
            output_kernel, [(planes, size, size)] * 2,
            landed.reshape(count * 2 * planes, size), gain, table["back_pieces"],
        )
    )


def solution(mesh):
    return jax.shard_map(
        body,
        mesh=mesh,
        in_specs=(
            P(("dp", "grid"), None, None),
            P(("dp", "grid"), None, None),
            P(("dp", "grid"), None),
            P("dp", None, "grid", None),
        ),
        out_specs=(P("grid", None, None), P("grid", None, None)),
        check_vma=False,
    )
```

```python
import functools

import jax
import jax.numpy as jnp
import numpy as np
from jax import lax
from jax.experimental import pallas as pl
from jax.experimental.pallas import tpu as pltpu
from jax.sharding import PartitionSpec as P


ITERS = 8
MOMENTS = 2 * ITERS + 1
LOW_LANE = 64
ALL = ("dp", "grid")
HIGHEST = lax.Precision.HIGHEST


def two_sum(a, b):
    s = a + b
    v = s - a
    return s, (a - (s - v)) + (b - v)


def quick_sum(a, b):
    s = a + b
    return s, b - (s - a)


def halves(a):
    c = a * 4097.0
    high = c - (c - a)
    return high, a - high


def two_prod(a, b, a_parts=None, b_parts=None):
    p = a * b
    ah, al = a_parts or halves(a)
    bh, bl = b_parts or halves(b)
    return p, ((ah * bh - p) + ah * bl + al * bh) + al * bl


def dd_add(a, b):
    s, e = two_sum(a[0], b[0])
    return quick_sum(s, e + (a[1] + b[1]))


def dd_mul(a, b):
    p, e = two_prod(a[0], b[0])
    return quick_sum(p, e + (a[0] * b[1] + a[1] * b[0]))


def dd_times(a, b):
    p, e = two_prod(a[0], b)
    return quick_sum(p, e + a[1] * b)


def dd_scale(a, factor):
    return a[0] * factor, a[1] * factor


def dd_neg(a):
    return -a[0], -a[1]


def dd_div(a, b):
    inverse = 1.0 / b[0]
    first = a[0] * inverse
    rest = dd_add(a, dd_neg(dd_times(b, first)))
    return quick_sum(first, rest[0] * inverse)


def dot(a, b):
    return jax.lax.dot_general(
        a, b, (((1,), (0,)), ((), ())), precision=HIGHEST, preferred_element_type=jnp.float32
    )


SIDE = 4
CORES = 2
ORDERS = ((0, 2, 1), (1, 2, 0))


def place_of(device):
    chip = device // CORES
    return chip // SIDE**2, chip % SIDE, (chip // SIDE) % SIDE, device % CORES


def chip_at(x, y, z):
    return (x * SIDE + z) * SIDE + y


def shift_pairs(axes, hop):
    pairs = []
    for device in range(SIDE**3 * CORES):
        place = list(place_of(device))
        axis = axes[place[3]]
        place[axis] = (place[axis] + hop) % (CORES if axis == 3 else SIDE)
        pairs.append((device, chip_at(*place[:3]) * CORES + place[3]))
    return pairs


def held_rows(size):
    chip, core = np.arange(size) // CORES, np.arange(size) % CORES
    return np.where(chip == 0, core * size // 2, np.where(core == 0, chip, size - chip))


def dft_tables(size):
    index = np.arange(size)
    angle = 2.0 * np.pi * ((index[:, None] * index[None, :]) % size) / size
    cos, sin = np.cos(angle), np.sin(angle)
    held = held_rows(size)
    as_f32 = lambda a: np.ascontiguousarray(a, dtype=np.float32)
    half = size // 2
    packed = np.concatenate([cos[:, :half], cos[:, half : half + 1], -sin[:, 1:half]], 1)
    high = packed.astype(jnp.bfloat16)
    low = (packed - high.astype(np.float64)).astype(jnp.bfloat16)
    lanes, rows = np.concatenate([cos, sin], 1), np.concatenate([cos, sin], 0)
    back = np.concatenate(
        [np.concatenate([cos[held], sin[held]], 1), np.concatenate([-sin[held], cos[held]], 1)], 0
    )

    def thrice(table, axis):
        above = table.astype(jnp.bfloat16)
        below = (table - above.astype(np.float64)).astype(jnp.bfloat16)
        return np.concatenate([above, above, below], axis)

    return dict(
        packed=np.stack([np.concatenate([p[:, :half], q[:, :half]], 1) for p, q in ((high, low), (high[:, half:], low[:, half:]))]),
        lanes=as_f32(lanes),
        rows=as_f32(rows),
        lanes_pieces=thrice(lanes, 0),
        rows_pieces=thrice(rows, 1),
        back_pieces=thrice(back, 0),
        mirror=(((index[:, None] + index[None, :]) % size) == 0).astype(jnp.bfloat16),
    )


def dot_as(a, b, left, right):
    return lax.dot_general(
        a, b, (((left,), (right,)), ((), ())), precision=HIGHEST, preferred_element_type=jnp.float32
    )


def pieces_of(a, count):
    found = []
    for _ in range(count):
        piece = a.astype(jnp.bfloat16)
        found.append(piece)
        a = a - piece.astype(jnp.float32)
    return found


def dot_pieces(a, b, left, right):
    return lax.dot_general(a, b, (((left,), (right,)), ((), ())), preferred_element_type=jnp.float32)


def stacked(a, axis):
    high, low = pieces_of(a, 2)
    return jnp.concatenate([high, low, high], axis)


def select_rows(one_hot, a):
    width = a.shape[1]
    found = dot_pieces(one_hot, jnp.concatenate(pieces_of(a, 3), 1), 1, 0)
    return (found[:, :width] + found[:, width : 2 * width]) + found[:, 2 * width :]


def select_lanes(a, one_hot):
    height = a.shape[0]
    found = dot_pieces(jnp.concatenate(pieces_of(a, 3), 0), one_hot, 1, 0)
    return (found[:height] + found[height : 2 * height]) + found[2 * height :]


HALVES = 2
STEPS = 4


def sublane_turn(tiles):
    row = lax.broadcasted_iota(jnp.int32, tiles[0].shape, 0)
    for bit in (4, 2, 1):
        low = (row & bit) == 0
        turned = list(tiles)
        for i in range(8):
            if i & bit == 0:
                a, b = tiles[i], tiles[i + bit]
                turned[i] = jnp.where(low, a, pltpu.roll(b, bit, 0))
                turned[i + bit] = jnp.where(low, pltpu.roll(a, 8 - bit, 0), b)
        tiles = turned
    return tiles


def grid_kernel(*refs, kept, part, capacity):
    if kept:
        count_ref, list_ref, place_ref, wave_ref, matrix_ref, other_ref = refs[:6]
        weight_refs = refs[6 : 6 + SIDE] if part else ()
        outs, row_refs = refs[6 + len(weight_refs) :][:SIDE], refs[6 + len(weight_refs) :][SIDE:]
    else:
        dest_ref, place_ref, values_ref, source_ref, packed_ref, weights_ref = refs[:6]
        out_refs, (kept_wave_ref, count_ref, list_ref), slice_refs = refs[6:8], refs[8:11], refs[11 : 11 + SIDE]
        wave_ref, matrix_ref, fetched = refs[-3:]
    nent, rows, width = matrix_ref.shape
    size = width // SIDE
    half = size // 2
    nslab = count_ref.shape[0]
    step = pl.program_id(0)

    def clear(s, _):
        count_ref[s] = 0
        return 0

    def enter(e, _):
        slab = dest_ref[e]
        taken = count_ref[slab]
        list_ref[slab * capacity + taken] = e
        count_ref[slab] = taken + 1
        return 0

    def prepare():
        fetch = pltpu.make_async_copy(source_ref, matrix_ref, fetched)
        fetch.start()
        lax.fori_loop(0, nslab, clear, 0)
        lax.fori_loop(0, nent, enter, 0)
        for r, slice_ref in enumerate(slice_refs):
            slice_ref[...] = weights_ref[0, :, (place_ref[0] + r) % SIDE, :]
        chip = lax.broadcasted_iota(jnp.int32, (half, half), 0)
        slot = lax.broadcasted_iota(jnp.int32, (half, half), 1)
        digits = digits_of(slot)
        pieces = []
        chips = [chip_at(*moved(place_ref, digits, owner, 1)) for owner in range(CORES)]
        for owner in (1 - place_ref[3], place_ref[3]):
            pick = (chip == jnp.where(owner == 0, chips[0], chips[1])).astype(jnp.float32).astype(jnp.bfloat16)
            for start in (0, half):
                piece = packed_ref[owner, :, start : start + half]
                pieces.append(jnp.dot(piece, pick, preferred_element_type=jnp.float32).astype(jnp.bfloat16))
        both = jnp.dot(
            values_ref[...].reshape(nent * rows, size),
            jnp.concatenate(pieces, 1),
            preferred_element_type=jnp.float32,
        )
        for at, target_ref in ((0, wave_ref), (size, kept_wave_ref)):
            wave = both[:, at : at + half] + both[:, at + half : at + size]
            high = wave.astype(jnp.bfloat16)
            low = (wave - high.astype(jnp.float32)).astype(jnp.bfloat16)
            target_ref[...] = jnp.concatenate([high, low], 1).reshape(nent, rows, size)
        fetch.wait()

    if not kept:
        pl.when(step == 0)(prepare)

    pairs = nslab // (2 * STEPS)

    def products(out):
        for pair in range(pairs):
            halves_of_tile = []
            for near in range(2):
                slab = ((part * (STEPS // HALVES) + step) * pairs + pair) * 2 + near
                taken = count_ref[slab]
                waves, matrices = [], []
                for m in range(capacity):
                    entry = jnp.where(m < taken, list_ref[slab * capacity + m], 0)
                    wave = wave_ref[entry]
                    waves.append(jnp.where(m < taken, wave, jnp.zeros_like(wave)))
                    matrices.append(matrix_ref[entry])
                product = lax.dot_general(
                    jnp.concatenate(waves, 0),
                    jnp.concatenate(matrices, 0),
                    (((0,), (0,)), ((), ())),
                    preferred_element_type=jnp.float32,
                )
                halves_of_tile.append(product[:half] + product[half:])
            place = slice(pair * 8, pair * 8 + 8)
            for start in range(0, half, 8):
                tiles = [
                    product[start : start + 8, p * size : (p + 1) * size]
                    for product in halves_of_tile
                    for p in range(SIDE)
                ]
                for index, block in enumerate(sublane_turn(tiles), start):
                    out(index, place, block)

    def keep(index, place, block):
        outs[index // SIDE**2][index % SIDE**2, place, :] = block + other_ref[index, place, :]

    def send(out_ref):
        def write(index, place, block):
            out_ref[index, place, :] = block

        return write

    if kept:
        products(keep)
        if part:
            pl.when(step == STEPS // HALVES - 1)(lambda: weight_kernel(*weight_refs, place_ref, *row_refs))
    else:
        pl.when(step < STEPS // HALVES)(lambda: products(send(out_refs[0])))
        pl.when(step >= STEPS // HALVES)(lambda: products(send(out_refs[1])))


def grid_call(kept, part, nslab, capacity, *args):
    scalars = pl.BlockSpec(memory_space=pltpu.SMEM)
    fixed = lambda shape: pl.BlockSpec(shape, lambda i: (0,) * len(shape))
    matrix = args[4] if kept else args[3]
    nent, rows, width = matrix.shape
    size, blocks = width // SIDE, SIDE**3
    steps = STEPS // HALVES if kept else STEPS
    moving = lambda count: pl.BlockSpec((count, size // STEPS, size), lambda i: (0, i, 0))
    f32 = lambda *shape: jax.ShapeDtypeStruct(shape, jnp.float32)
    in_specs = [scalars if a.dtype == jnp.int32 else fixed(a.shape) for a in args]
    if kept:
        out_shape, out_specs = [f32(SIDE**2, size // HALVES, size)] * SIDE, [moving(SIDE**2)] * SIDE
        in_specs[5] = moving(blocks)
        if part:
            rows_shape = (SIDE**2 * 8 + 8, size)
            out_shape = out_shape + [f32(*rows_shape)] * SIDE
            out_specs = out_specs + [fixed(rows_shape)] * SIDE
        scratch = []
    else:
        wave = (nent, rows, size)
        out_shape = [f32(blocks, size // HALVES, size)] * HALVES + [
            jax.ShapeDtypeStruct(wave, jnp.bfloat16),
            jax.ShapeDtypeStruct((nslab,), jnp.int32),
            jax.ShapeDtypeStruct((nslab * capacity,), jnp.int32),
        ] + [f32(size, size)] * SIDE
        block = (blocks, size // STEPS, size)
        out_specs = [
            pl.BlockSpec(block, lambda i: (0, jnp.minimum(i, STEPS // HALVES - 1), 0)),
            pl.BlockSpec(block, lambda i: (0, jnp.maximum(i - STEPS // HALVES, 0), 0)),
        ] + [fixed(wave), scalars, scalars] + [fixed((size, size))] * SIDE
        in_specs[3] = pl.BlockSpec(memory_space=pl.ANY)
        scratch = [pltpu.VMEM(wave, jnp.bfloat16), pltpu.VMEM(matrix.shape, jnp.bfloat16), pltpu.SemaphoreType.DMA]
    return pl.pallas_call(
        functools.partial(grid_kernel, kept=kept, part=part, capacity=capacity),
        grid=(steps,),
        out_shape=out_shape,
        in_specs=in_specs,
        out_specs=out_specs,
        scratch_shapes=scratch,
    )(*args)


def moved(place_ref, digits, owner, sign):
    at = [place_ref[0], place_ref[1], place_ref[2]]
    for digit, axis in zip(digits, ORDERS[owner]):
        at[axis] = (at[axis] + sign * digit + SIDE) % SIDE
    return at


def digits_of(index):
    return index // SIDE**2, (index // SIDE) % SIDE, index % SIDE


def weight_kernel(w0_ref, w1_ref, w2_ref, w3_ref, place_ref, *outs):
    size = w0_ref.shape[0]
    half = size // 2
    own = ((w0_ref[...] + w1_ref[...]) + w2_ref[...]) + w3_ref[...]
    low = jnp.min(jnp.min(own, axis=0, keepdims=True), axis=1, keepdims=True)
    high = jnp.max(jnp.max(own, axis=0, keepdims=True), axis=1, keepdims=True)
    row = lax.broadcasted_iota(jnp.int32, (size, size), 0)
    lane = lax.broadcasted_iota(jnp.int32, (size, size), 1)
    chips = [chip_at(*moved(place_ref, digits_of(row % half), owner, 1)) for owner in range(CORES)]
    chip = jnp.where(place_ref[3] == 0, chips[0], chips[1])
    negative = jnp.where(chip == 0, half, size - chip)
    pick = (lane == jnp.where(row < half, chip, negative)).astype(jnp.float32)
    rows = dot_as(pick, own, 1, 1)
    ends = jnp.where(lax.broadcasted_iota(jnp.int32, (8, size), 1) < half, low, -high)
    count = half // SIDE
    for r, out_ref in enumerate(outs):
        out_ref[...] = jnp.zeros(out_ref.shape, jnp.float32)
        out_ref[8 * count :, :] = ends
        for sign in range(2):
            at = sign * half + r * count
            out_ref[pl.ds(2 * r + sign, count, stride=8), :] = rows[at : at + count]


def sublane_total(a):
    for shift in (4, 2, 1):
        a = dd_add(a, (pltpu.roll(a[0], shift, 0), pltpu.roll(a[1], shift, 0)))
    return a


def lane_total(a):
    for shift in (64, 32, 16, 8, 4, 2, 1):
        a = dd_add(a, (pltpu.roll(a[0], shift, 1), pltpu.roll(a[1], shift, 1)))
    return a


def moment_kernel(
    own_ref, other_ref, place_ref, lanes_ref, rows_ref, mirror_ref, real_ref, imag_ref, scaled_ref, range_ref, send_ref
):
    size = scaled_ref.shape[0]
    second, alone = place_ref[3] == 1, place_ref[4] == 1
    lane8 = lax.broadcasted_iota(jnp.int32, (8, size), 1)
    ends = jnp.minimum(own_ref[2 * size :, :], other_ref[2 * size :, :])
    least = lambda v: jnp.min(jnp.min(v, axis=0, keepdims=True), axis=1, keepdims=True)
    low = least(jnp.where(lane8 < size // 2, ends, 1e30))
    high = -least(jnp.where(lane8 < size // 2, 1e30, ends))
    span = jnp.broadcast_to(jnp.maximum((high - low) * 0.5, high * 1e-4), (1, size))
    centre = jnp.broadcast_to((high + low) * 0.5, (1, size)) / span
    range_ref[0:1, :] = span
    range_ref[1:2, :] = centre
    range_ref[2:8, :] = jnp.zeros((6, size), jnp.float32)

    ky = lax.broadcasted_iota(jnp.int32, (size, size), 0)
    row = lax.broadcasted_iota(jnp.int32, (size, size), 1)
    found = row // 2
    back = (found % SIDE, (found // SIDE) % SIDE, found // SIDE**2)
    sources = []
    for owner in range(CORES):
        x, y, z = moved(place_ref, back, owner, -1)
        sources.append(SIDE * (z * (SIDE * CORES) + y * CORES + owner) + x)
    from_own = jnp.where(second, sources[1], sources[0])
    from_other = jnp.where(second, sources[0], sources[1])
    given = jnp.concatenate([own_ref[size : 2 * size, :], other_ref[size : 2 * size, :]], 0)
    picks = [
        jnp.concatenate(
            [
                jnp.where(row % 2 == sign, (ky == source).astype(jnp.float32), 0.0).astype(jnp.bfloat16)
                for source in (from_own, from_other)
            ],
            1,
        )
        for sign in range(2)
    ]
    signs = select_rows(jnp.concatenate(picks, 0), given)
    plus, minus = signs[:size], signs[size:]
    mine = jnp.where(second, minus, plus)
    partner = jnp.where(alone, mine, jnp.where(second, plus, minus))
    scaled = (mine + select_lanes(select_rows(mirror_ref[...], partner), mirror_ref[...])) * 0.5 / span
    scaled_ref[...] = scaled.T

    mine, theirs = own_ref[:size, :], other_ref[:size, :]
    re = jnp.where(jnp.logical_and(second, jnp.logical_not(alone)), theirs, mine)
    im = jnp.where(alone, jnp.zeros_like(mine), jnp.where(second, -mine, theirs))
    ends = dot(jnp.concatenate([re, im], 0), lanes_ref[...])
    mid_real = ends[:size, :size] + ends[size:, size:]
    mid_imag = ends[size:, :size] - ends[:size, size:]
    both = dot(rows_ref[...], jnp.concatenate([mid_real, mid_imag], 1))
    real = both[:size, :size] + both[size:, size:]
    imag = both[:size, size:] - both[size:, :size]
    real_ref[...] = real
    imag_ref[...] = imag
    scaled = scaled_ref[...]
    power = real * real + imag * imag
    chunk = 24
    totals = [None] * MOMENTS
    for start in range(0, size // 2 + 8, chunk):
        row = lax.broadcasted_iota(jnp.int32, (chunk, size), 0) + start
        share = jnp.where(row % (size // 2) == 0, 1.0, jnp.where(row < size // 2, 2.0, 0.0))
        t = scaled[start : start + chunk] - centre
        p = power[start : start + chunk] * share
        p_parts = halves(p)
        t2 = t * 2.0
        t2_parts = halves(t2)
        zero = jnp.zeros_like(t)
        before, here = (jnp.ones_like(t), zero), (t, zero)
        for order in range(MOMENTS):
            value = before
            v_parts = halves(value[0])
            term, low_term = two_prod(value[0], p, v_parts, p_parts)
            term = (term, low_term + value[1] * p)
            total, spill = totals[order] or (None, None)
            for i in range(0, chunk, 8):
                piece, rest = term[0][i : i + 8], term[1][i : i + 8]
                if total is None:
                    total, spill = piece, rest
                else:
                    total, lost = two_sum(total, piece)
                    spill = spill + (lost + rest)
            totals[order] = total, spill
            if order + 1 < MOMENTS:
                up, low_up = two_prod(here[0], t2, None, t2_parts)
                following, lost = two_sum(up, -before[0])
                before, here = here, (following, lost + ((low_up + here[1] * t2) - before[1]))
    row = lax.broadcasted_iota(jnp.int32, (8, size), 0)
    lane = lax.broadcasted_iota(jnp.int32, (8, size), 1)
    out = jnp.zeros((8, size), jnp.float32)
    for base in range(0, MOMENTS, 8):
        high_rows = jnp.zeros((8, size), jnp.float32)
        low_rows = jnp.zeros((8, size), jnp.float32)
        for order in range(base, min(base + 8, MOMENTS)):
            total = sublane_total(quick_sum(*totals[order]))
            high_rows = jnp.where(row == order - base, total[0], high_rows)
            low_rows = jnp.where(row == order - base, total[1], low_rows)
        high_rows, low_rows = lane_total((high_rows, low_rows))
        out = jnp.where(lane == row + base, high_rows, out)
        out = jnp.where(lane == row + (base + LOW_LANE), low_rows, out)
    line = jnp.sum(out, axis=0, keepdims=True)
    send_ref[...] = jnp.broadcast_to(line, (size, size))


def lane_of(a, lane):
    pick = lambda v: jnp.broadcast_to(v[:, lane : lane + 1], v.shape)
    return pick(a[0]), pick(a[1])


def solve_kernel(
    sums_ref, range_ref, scaled_ref, real_ref, imag_ref, lanes_ref, rows_ref, out_ref, gain_ref, *, scale
):
    size = scaled_ref.shape[0]
    given = sums_ref[...]
    low = pltpu.roll(given, size - LOW_LANE, 1)
    rows = [(given[i : i + 8], low[i : i + 8]) for i in range(0, given.shape[0], 8)]
    while len(rows) > 1:
        rows = [dd_add(rows[i], rows[i + 1]) for i in range(0, len(rows), 2)]
    moments = sublane_total(rows[0])
    half = range_ref[0:1, :]
    centre = jnp.broadcast_to(range_ref[1:2, :], moments[0].shape)
    centre = (centre, jnp.zeros_like(centre))
    lane = lax.broadcasted_iota(jnp.int32, moments[0].shape, 1)
    resid, direct = moments, moments
    held = lane_of(resid, 0)
    least = (1.0 - 1e-4) / (centre[0] + 1.0)
    most = (1.0 + 1e-4) / jnp.maximum(centre[0] - 1.0, 1e-3)
    steps, turns = [], []
    decay = jnp.ones((1, size), jnp.float32)
    for k in range(ITERS):
        after = tuple(pltpu.roll(v, size - 1, 1) for v in direct)
        prior = tuple(pltpu.roll(v, 1, 1) for v in direct)
        prior = tuple(jnp.where(lane == 0, a, p) for a, p in zip(after, prior))
        image = dd_add(dd_mul(direct, centre), dd_scale(dd_add(after, prior), 0.5))
        alpha = dd_div(held, lane_of(image, k))
        inside = jnp.logical_and(alpha[0] >= least, alpha[0] <= most)
        bound = jnp.where(alpha[0] > most, most, least)
        alpha = jnp.where(inside, alpha[0], bound), jnp.where(inside, alpha[1], 0.0)
        fresh = dd_add(resid, dd_neg(dd_mul(alpha, image)))
        reached = lane_of(fresh, k + 1)
        beta = dd_mul(alpha, dd_div(reached, held))
        held = reached
        beta = dd_scale(beta, -1.0 if k == 0 else -0.5)
        sound = jnp.logical_and(beta[0] >= 0.0, beta[0] <= 1e4)
        beta = tuple(jnp.where(sound, v, 0.0) for v in beta)
        direct = dd_add(fresh, dd_mul(beta, direct))
        resid = fresh
        steps.append(alpha[0][0:1])
        turns.append(beta[0][0:1])
        decay = decay * beta[0][0:1]
    gain = lax.rsqrt(jnp.maximum(jnp.abs(decay), 1e-13)) / centre[0][0:1]
    gain_ref[...] = jnp.broadcast_to(gain, gain_ref.shape)
    scaled = scaled_ref[...]
    field = steps[0]
    solved = jnp.broadcast_to(field, scaled.shape)
    left = 1.0 - field * scaled
    toward = left + turns[0]
    for k in range(1, ITERS):
        solved = solved + steps[k] * toward
        left = left - steps[k] * (scaled * toward)
        if k + 1 < ITERS:
            toward = left + turns[k] * toward
    solved = solved * (scale / half)
    left = left * (gain * scale)
    real, imag = real_ref[...], imag_ref[...]
    back_real = solved * real - left * imag
    back_imag = solved * imag + left * real
    ends = dot_pieces(stacked(jnp.concatenate([back_real, back_imag], 0), 1), lanes_ref[...], 1, 0)
    mid_real = ends[:size, :size] - ends[size:, size:]
    mid_imag = ends[size:, :size] + ends[:size, size:]
    both = dot_pieces(rows_ref[...], stacked(jnp.concatenate([mid_real, mid_imag], 1), 0), 1, 0)
    real = both[:size, :size] - both[size:, size:]
    imag = both[:size, size:] + both[size:, :size]
    for copy in range(out_ref.shape[0] // (2 * size)):
        out_ref[pl.ds(copy * 2 * size, size, stride=2), :] = real
        out_ref[pl.ds(copy * 2 * size + 1, size, stride=2), :] = imag


def output_kernel(given_ref, gain_ref, back_ref, field_ref, resid_ref):
    planes, size = field_ref.shape[0], field_ref.shape[1]
    step = 2 * planes
    shrink = 1.0 / gain_ref[0:1, :]
    for j in range(planes):
        pieces = [given_ref[pl.ds(2 * j + part, size, stride=step), :] for part in range(2)]
        both = dot_pieces(stacked(jnp.concatenate(pieces, 0), 0), back_ref[...], 0, 0)
        field_ref[j] = both[:, :size]
        resid_ref[j] = both[:, size:] * shrink


def call(kernel, shapes, *args):
    whole = pl.BlockSpec(memory_space=pltpu.VMEM)
    scalars = pl.BlockSpec(memory_space=pltpu.SMEM)
    return pl.pallas_call(
        kernel,
        out_shape=[jax.ShapeDtypeStruct(s, jnp.float32) for s in shapes],
        in_specs=[scalars if a.dtype == jnp.int32 else whole for a in args],
        out_specs=[whole] * len(shapes),
    )(*args)


def exchange(parts, axes):
    arrived = {r: lax.ppermute(parts[r], ALL, shift_pairs(axes, r)) for r in (2, 1, 3)}
    return [parts[0], arrived[1], arrived[2], arrived[3]]


def summed(parts):
    return ((parts[0] + parts[1]) + parts[2]) + parts[3]


def body(intensities, gridding, dest_slab, spectral_weights):
    ngrid = lax.axis_size("grid")
    ndp = lax.axis_size("dp")
    nent, rows, size = intensities.shape
    planes = gridding.shape[2] // size
    count = ngrid * ndp
    capacity = max(2, 2 * nent // ngrid)
    table = dft_tables(size)
    square = (size, size)
    swap = lambda a: lax.ppermute(a, ALL, shift_pairs((3, 3), 1))

    chip = lax.axis_index("dp") * (ngrid // CORES) + lax.axis_index("grid") // CORES
    core = lax.axis_index("grid") % CORES
    step = jnp.arange(5, dtype=jnp.int32)
    x, y, z = place_of(chip * CORES)[:3]
    place = jnp.where(
        step == 0, x, jnp.where(step == 1, y, jnp.where(step == 2, z, jnp.where(step == 3, core, chip == 0)))
    ).astype(jnp.int32)

    *away, wave, counts, lists, p0, p1, p2, p3 = grid_call(
        False, 0, ngrid, capacity, dest_slab[:, 0], place, intensities, gridding, table["packed"], spectral_weights
    )
    members = (counts, lists, place, wave, gridding)
    arrived = [swap(a) for a in away]
    weights = exchange([p0, p1, p2, p3], (0, 0))
    axes = [[order[stage] for order in ORDERS] for stage in range(3)]
    quarter = lambda a: [p.reshape(p.shape[1:]) for p in jnp.split(a.reshape((SIDE, -1) + a.shape[1:]), SIDE)]
    least = lambda parts: functools.reduce(jnp.minimum, parts)
    data = []
    for part in range(HALVES):
        kept = grid_call(True, part, ngrid, capacity, *members, arrived[part], *(weights if part else ()))
        kept, rows = kept[:SIDE], kept[SIDE:]
        data.append(exchange(kept, axes[0]))
    rows = exchange(rows, axes[0])
    parts = quarter(summed(data[0]))
    early = exchange(parts, axes[1])
    held = summed([a[: SIDE**2 * 8] for a in rows]).reshape(SIDE**2, 8, size)
    ends = jnp.broadcast_to(least([a[SIDE**2 * 8 :] for a in rows])[None], (SIDE**2, 8, size))
    parts = exchange(quarter(jnp.concatenate([summed(data[1]), held, ends], 1)), axes[1])
    late = size // HALVES
    for stage in (1, 2):
        if stage == 2:
            parts = exchange(quarter(parts), axes[2])
            late = size
        found = [
            summed([a[:, :late] for a in parts]),
            jnp.concatenate([a[:, late:-8] for a in parts], 1),
            least([a[:, -8:] for a in parts]),
        ]
        if stage == 1:
            found = [summed(early)] + found
        parts = jnp.concatenate(found, 1)
    parts = parts[0]
    real, imag, scaled, ends, send = call(
        moment_kernel, [square, square, square, (8, size), square],
        parts, swap(parts), place, table["lanes"], table["rows"], table["mirror"],
    )
    sums = lax.all_to_all(send.reshape(count, 1, size), ALL, 0, 0, tiled=True).reshape(count, size)
    back, gain = call(
        functools.partial(solve_kernel, scale=1.0 / size**3), [(ndp * 2 * size, size), (8, size)],
        sums, ends, scaled, real, imag, table["lanes_pieces"], table["rows_pieces"],
    )
    landed = lax.all_to_all(back.reshape(count, 2 * planes, size), ALL, 0, 0, tiled=True)
    return tuple(
        call(
            output_kernel, [(planes, size, size)] * 2,
            landed.reshape(count * 2 * planes, size), gain, table["back_pieces"],
        )
    )


def solution(mesh):
    return jax.shard_map(
        body,
        mesh=mesh,
        in_specs=(
            P(("dp", "grid"), None, None),
            P(("dp", "grid"), None, None),
            P(("dp", "grid"), None),
            P("dp", None, "grid", None),
        ),
        out_specs=(P("grid", None, None), P("grid", None, None)),
        check_vma=False,
    )
```
